32 devices in a mesh: seq: 8 (over z, core), fsdp: 4 (over y, x).
Axes of the slice: x: 2, y: 2, z: 4, core: 2. Of those that a mesh axis runs over, the one named last changes fastest.
Arguments:
- tokens: bfloat16 [4, 4, 1024, 768], P(None, 'fsdp', 'seq'), may hold values from -6 to 6
- segments: int32 [4, 4, 1024], P(None, 'fsdp', 'seq'), may hold values from 0 to 3, never falling along the last dimension, each value on 1 to 512 neighbouring positions
- w_query: bfloat16 [768, 768], P('fsdp'), may hold values from -0.4375 to 0.4375
- w_key: bfloat16 [768, 768], P('fsdp'), may hold values from -0.21875 to 0.21875
- w_value: bfloat16 [768, 768], P('fsdp'), may hold values from -0.21875 to 0.21875
- w_out: bfloat16 [768, 768], P('fsdp'), may hold values from -0.625 to 0.625
- w_gate: bfloat16 [768, 2048], P('fsdp'), may hold values from -0.21875 to 0.21875
- w_up: bfloat16 [768, 2048], P('fsdp'), may hold values from -0.21875 to 0.21875
- w_down: bfloat16 [2048, 768], P('fsdp'), may hold values from -0.125 to 0.125
- gain_attn: bfloat16 [768], P('fsdp'), may hold values from 0.099609375 to 1.8984375
- gain_ffn: bfloat16 [768], P('fsdp'), may hold values from 0.099609375 to 1.8984375
- cotangent: bfloat16 [4, 4, 1024, 768], P(None, 'fsdp', 'seq'), may hold values from -6 to 6
Outputs:
- output: bfloat16 [4, 4, 1024, 768], P(None, 'fsdp', 'seq')
- input_grad: bfloat16 [4, 4, 1024, 768], P(None, 'fsdp', 'seq')
- w_query_grad: float32 [768, 768], P('fsdp')
- w_key_grad: float32 [768, 768], P('fsdp')
- w_value_grad: float32 [768, 768], P('fsdp')
- w_out_grad: float32 [768, 768], P('fsdp')
- w_gate_grad: float32 [768, 2048], P('fsdp')
- w_up_grad: float32 [768, 2048], P('fsdp')
- w_down_grad: float32 [2048, 768], P('fsdp')
- gain_attn_grad: float32 [768], P('fsdp')
- gain_ffn_grad: float32 [768], P('fsdp')
The draws below stay inside these ranges and needn't reach their ends.
Inputs may be any that keep to these rules, and one draw needn't show every extreme that they name: `segments`: along each sequence the document number never falls; every document of 0 to 3 holds 1 to 512 tokens, and one holds exactly 512.
All inputs are finite; a program needn't handle non-finite values.
Results may differ from the reference program's by a relative error of at most 0.024.
Values may be sent and summed in bfloat16 or wider, within the bound.
No kernel may reach another device: no remote copies, remote signals or barrier semaphores. Data moves between devices by JAX's collectives and lax.ppermute only.
A program may use at most 192 MiB of HBM per device.

```python
import math
import jax
import jax.numpy as jnp
import numpy as np
from jax import lax

D = 768
HEADS = 12
HEAD = 64
FF = 2048
MICRO = 4
DOCS = 4
LENGTH = 1024
SEQS = 4


def block_levels(rng, dims, shards, low, high):
    gain = 1.0
    for position, parts in shards:
        steps = jax.random.uniform(jax.random.fold_in(jax.random.fold_in(rng, 6), position), (parts,), jnp.float32, low / len(shards), high / len(shards))
        gain = gain * jnp.repeat(jnp.exp(steps), dims[position] // parts).reshape((-1,) + (1,) * (len(dims) - 1 - position))
    return gain


def split_up(amount, total, bound, slope):
    loads = [(1 << 20) // math.isqrt(rank ** slope) + 1 for rank in range(2, amount + 1)]
    spare, given = total - bound - (amount - 1), [1] * (amount - 1)
    while spare > 0:
        free = [i for i in range(amount - 1) if given[i] < bound]
        whole, remaining = sum([loads[i] for i in free]), spare
        for i in free:
            extra = min(bound - given[i], max(1, remaining * loads[i] // whole), spare)
            given[i] = given[i] + extra
            spare = spare - extra
    return np.array([bound] + given)


def ragged_sizes(key, count, total, most, lean):
    if count == 2:
        one = jax.random.randint(key, (), max(1, total - most), min(most, total - 1) + 1)
        return jnp.stack([one, total - one])
    tallies = jnp.asarray(split_up(count, total, most, lean), jnp.int32)
    pairs = (count - 1) // 2
    source_of, sink = tallies[1:1 + 2 * pairs:2], tallies[2:2 + 2 * pairs:2]
    slack = jnp.minimum(source_of - 1, most - sink)
    shifted = jax.random.randint(jax.random.fold_in(key, 1), (pairs,), 0, 1 << 20) % (slack + 1)
    tallies = tallies.at[1:1 + 2 * pairs:2].set(source_of - shifted).at[2:2 + 2 * pairs:2].set(sink + shifted)
    return tallies[jax.random.permutation(jax.random.fold_in(key, 2), count)]


def noise(own_key, shape, scale, most, pieces=(), kind=jnp.bfloat16):
    array = jax.random.normal(own_key, shape, jnp.float32) * scale
    if len(pieces) > 0:
        array = block_levels(own_key, shape, pieces, -0.22, 0.18) * array
    return jnp.clip(array, min=-most, max=most).astype(kind)


def setup_inputs(seed: int = 0) -> dict:
    seeds = jax.random.split(jax.random.key(seed), 13)
    return {
        "tokens": noise(seeds[0], (MICRO, SEQS, LENGTH, D), 1.0, 6.0, ((1, 4), (2, 8))),
        "segments": jax.vmap(lambda own: jnp.searchsorted(jnp.cumsum(ragged_sizes(own, DOCS, LENGTH, LENGTH // 2, 1)), jnp.arange(LENGTH), side="right"))(jax.random.split(seeds[1], MICRO * SEQS)).reshape((MICRO, SEQS, LENGTH)).astype(jnp.int32),
        "w_query": noise(seeds[2], (D, D), (D // 4) ** -0.5, 0.4375, ((0, 4),)),
        "w_key": noise(seeds[3], (D, D), D ** -0.5, 0.21875, ((0, 4),)),
        "w_value": noise(seeds[4], (D, D), D ** -0.5, 0.21875, ((0, 4),)),
        "w_out": noise(seeds[5], (D, D), (D // 8) ** -0.5, 0.625, ((0, 4),)),
        "w_gate": noise(seeds[6], (D, FF), D ** -0.5, 0.21875, ((0, 4),)),
        "w_up": noise(seeds[7], (D, FF), D ** -0.5, 0.21875, ((0, 4),)),
        "w_down": noise(seeds[8], (FF, D), FF ** -0.5, 0.125, ((0, 4),)),
        "gain_attn": jnp.clip(1.0 + 0.18 * jax.random.normal(seeds[9], (D,), jnp.float32), 0.099609375, 1.8984375).astype(jnp.bfloat16),
        "gain_ffn": jnp.clip(1.0 + 0.18 * jax.random.normal(seeds[10], (D,), jnp.float32), 0.099609375, 1.8984375).astype(jnp.bfloat16),
        "cotangent": noise(seeds[11], (MICRO, SEQS, LENGTH, D), 1.0, 6.0, ((1, 4), (2, 8))),
    }


@jax.custom_vjp
def low(v):
    return lax.optimization_barrier(v.astype(jnp.bfloat16)).astype(jnp.float32)

@jax.custom_vjp
def low_back(v):
    return v

def low_keep(v):
    return (low(v), None)

def low_pass(kept, grad):
    return (grad,)

def back_keep(v):
    return (v, None)

def back_low(kept, grad):
    return (low(grad),)
low.defvjp(low_keep, low_pass)
low_back.defvjp(back_keep, back_low)
EPS = 1e-06
best_precision = lax.Precision.HIGHEST

def matmul(left_rows, right_rows):
    return jnp.dot(left_rows, right_rows, precision=best_precision)

def angles(positions):
    half_size = HEAD // 2
    frequency = 10000.0 ** (-jnp.arange(half_size, dtype=jnp.float32) / half_size)
    angle_rows = positions.astype(jnp.float32)[:, None] * frequency[None, :]
    angle_rows = jnp.concatenate([angle_rows, angle_rows], axis=-1)
    return (jnp.cos(angle_rows)[:, None, :], jnp.sin(angle_rows)[:, None, :])

def rotate(field_rows, cosine_rows, sine_rows):
    half_size = field_rows.shape[-1] // 2
    turned = jnp.concatenate([-field_rows[..., half_size:], field_rows[..., :half_size]], axis=-1)
    return field_rows * cosine_rows + turned * sine_rows

def normalize(value_rows, gain_vector):
    factor = lax.rsqrt(lax.optimization_barrier(jnp.mean(value_rows * value_rows, axis=-1, keepdims=True)) + EPS)
    return value_rows * factor * gain_vector

def layer(hidden_in, w_query, w_key, w_value, w_out, w_gate, w_up, w_down, gain_attn, gain_ffn, starts, positions):
    seq_tokens = hidden_in.shape[0]
    model_width = hidden_in.shape[1]
    cosine_rows, sine_rows = angles(positions - starts)
    query_lin = low_back(matmul(hidden_in, w_query)).reshape(seq_tokens, HEADS, HEAD)
    key_lin = low_back(matmul(hidden_in, w_key)).reshape(seq_tokens, HEADS, HEAD)
    queries = low(rotate(query_lin, cosine_rows, sine_rows))
    keys_rot = low(rotate(key_lin, cosine_rows, sine_rows))
    values_all = low(low_back(matmul(hidden_in, w_value))).reshape(seq_tokens, HEADS, HEAD)
    block_count = max(1, seq_tokens // 512)
    block_rows = seq_tokens // block_count
    score_scale = 1.0 / math.sqrt(HEAD)

    def attend_block(query_rows, query_index, query_start):
        scores = low_back(jnp.einsum('qhd,khd->hqk', query_rows, keys_rot, precision=best_precision) * score_scale)
        visible = (positions[None, :] <= query_index[:, None]) & (positions[None, :] >= query_start[:, None])
        weight_rows = jax.nn.softmax(jnp.where(visible[None], scores, -jnp.inf), axis=-1)
        return jnp.einsum('hqk,khd->qhd', low(weight_rows), values_all, precision=best_precision)
    checked = jax.checkpoint(attend_block)
    attended = lax.map(lambda block_item: checked(block_item[0], block_item[1], block_item[2]), (queries.reshape(block_count, block_rows, HEADS, HEAD), positions.reshape(block_count, block_rows), starts.reshape(block_count, block_rows)))
    attended = attended.reshape(seq_tokens, model_width)
    attended_low = low(low_back(attended))
    branch = low_back(matmul(attended_low, w_out))
    middle = normalize(hidden_in + branch, gain_attn)
    middle_low = low(middle)
    gate_pre = low_back(matmul(middle_low, w_gate))
    up_pre = low_back(matmul(middle_low, w_up))
    hidden_low = low(jax.nn.silu(gate_pre) * up_pre)
    ffn_out = low_back(matmul(hidden_low, w_down))
    return normalize(middle + ffn_out, gain_ffn)

def doc_starts(segment_row):
    membership = (segment_row[:, None] == jnp.arange(DOCS, dtype=jnp.int32)[None, :]).astype(jnp.int32)
    doc_totals = lax.optimization_barrier(jnp.sum(membership, axis=0)).astype(jnp.int32)
    before = (jnp.cumsum(doc_totals) - doc_totals).astype(jnp.int32)
    return lax.optimization_barrier(jnp.sum(membership * before[None, :], axis=1)).astype(jnp.int32)

def reference(tokens, segments, w_query, w_key, w_value, w_out, w_gate, w_up, w_down, gain_attn, gain_ffn, cotangent):
    micro_count, seq_count, seq_tokens, model_width = tokens.shape
    weight_list = tuple((item_w.astype(jnp.float32) for item_w in (w_query, w_key, w_value, w_out, w_gate, w_up, w_down, gain_attn, gain_ffn)))
    inputs_all = tokens.reshape(micro_count * seq_count, seq_tokens, model_width).astype(jnp.float32)
    cot_all = cotangent.reshape(micro_count * seq_count, seq_tokens, model_width).astype(jnp.float32)
    seg_all = segments.reshape(micro_count * seq_count, seq_tokens)
    positions = jnp.arange(seq_tokens, dtype=jnp.int32)

    def one_sequence(carry_sums, seq_item):
        hidden_in, segment_row, cot_rows = seq_item
        starts = doc_starts(segment_row)

        def forward(input_rows, *weight_args):
            return layer(input_rows, *weight_args, starts, positions)
        result, pullback = jax.vjp(forward, hidden_in, *weight_list)
        grads_all = pullback(cot_rows)
        new_sums = tuple((earlier + current for earlier, current in zip(carry_sums, grads_all[1:])))
        return (new_sums, (result.astype(jnp.bfloat16), grads_all[0].astype(jnp.bfloat16)))
    start_sums = tuple((jnp.zeros(item_w.shape, jnp.float32) for item_w in weight_list))
    sums_all, (results, input_grads) = lax.scan(one_sequence, start_sums, (inputs_all, seg_all, cot_all))
    output = results.reshape(micro_count, seq_count, seq_tokens, model_width)
    input_grad = input_grads.reshape(micro_count, seq_count, seq_tokens, model_width)
    return (output, input_grad, sums_all[0], sums_all[1], sums_all[2], sums_all[3], sums_all[4], sums_all[5], sums_all[6], sums_all[7], sums_all[8])
```

```python
import math

import jax
import jax.numpy as jnp
from jax import lax
from jax.experimental import pallas as pl
from jax.experimental.pallas import tpu as pltpu
from jax.sharding import Mesh, PartitionSpec as P

HEADS = 12
DOCS = 4
EPS = 1e-06
NEGATIVE = -1e30
BF = jnp.bfloat16
F32 = jnp.float32


def dot(left, right, dims=((1,), (0,))):
    return lax.dot_general(left, right, (dims, ((), ())), preferred_element_type=F32)


def rotary_tables(seq_tokens, head_size, copies):
    half = head_size // 2
    frequency = 10000.0 ** (-jnp.arange(half, dtype=F32) / half)
    angle = jnp.arange(seq_tokens, dtype=jnp.int32).astype(F32)[:, None] * frequency[None, :]
    cosine, sine = jnp.cos(angle), jnp.sin(angle)
    return (
        jnp.concatenate([cosine, cosine] * copies, axis=1),
        jnp.concatenate([-sine, sine] * copies, axis=1),
    )


def turn(rows, half):
    lanes = rows.shape[1]
    lane = lax.broadcasted_iota(jnp.int32, (1, lanes), 1)
    low = (lane // half) % 2 == 0
    return jnp.where(low, pltpu.roll(rows, lanes - half, 1), pltpu.roll(rows, half, 1))


def first_key(query_first, block, window):
    return max(0, (query_first - window + 1) // block * block)


def start_row(seg_ref):
    seg = seg_ref[...]
    starts = jnp.zeros_like(seg)
    for doc in range(1, DOCS):
        before = jnp.sum(jnp.where(seg < doc, 1.0, 0.0), axis=1, keepdims=True)
        starts = jnp.maximum(starts, jnp.where(seg >= doc, before, 0.0))
    return starts


def attend_kernel(seg_ref, x_ref, w_ref, cos_ref, sin_ref, q_ref, k_ref, v_ref, att_ref, lse_ref,
                  col_ref, *, block, window, scale, head_size):
    tokens = x_ref.shape[0]
    lane = lax.broadcasted_iota(jnp.int32, (1, 2 * head_size), 1)
    first = lane < head_size

    @pl.when(pl.program_id(0) == 0)
    def _():
        starts = start_row(seg_ref)
        col_ref[...] = jnp.broadcast_to(starts, (128, tokens)).T

    for low in range(0, tokens, block):
        rows = pl.ds(low, block)
        lin = [dot(x_ref[rows, :], w_ref[n]) for n in range(3)]
        cosine, sine = cos_ref[rows, :], sin_ref[rows, :]
        half = head_size // 2
        q_ref[rows, :] = (lin[0] * cosine + turn(lin[0], half) * sine).astype(BF)
        k_ref[rows, :] = (lin[1] * cosine + turn(lin[1], half) * sine).astype(BF)
        v_ref[rows, :] = lin[2].astype(BF)
    for low in range(0, tokens, block):
        begin = first_key(low, block, window)
        end = low + block
        q = q_ref[low:end, :] * jnp.asarray(scale, BF)
        zero = jnp.zeros_like(q)
        stacked = jnp.concatenate([jnp.where(first, q, zero), jnp.where(first, zero, q)], axis=0)
        scores = dot(stacked, k_ref[begin:end, :], ((1,), (1,)))
        key_index = lax.broadcasted_iota(jnp.int32, (block, end - begin), 1) + begin
        query_index = lax.broadcasted_iota(jnp.int32, (block, end - begin), 0) + low
        visible = (key_index.astype(F32) >= col_ref[low:end, 0:1]) & (key_index <= query_index)
        parts = []
        for head in range(2):
            own = jnp.where(visible, scores[head * block:(head + 1) * block], NEGATIVE)
            top = jnp.max(own, axis=1, keepdims=True)
            weights = jnp.exp(own - top)
            total = jnp.sum(weights, axis=1, keepdims=True)
            out = dot(weights.astype(BF), v_ref[begin:end, :]) / total
            parts.append(out)
            lse = jnp.broadcast_to(top + jnp.log(total), (block, 128))
            lse_ref[0, head:head + 1, low:end] = lse.T[0:1, :]
        att_ref[low:end, :] = jnp.where(first, parts[0], parts[1]).astype(BF)


def attend(seg, x, w, cosine, sine, window, head_size):
    tokens, width = x.shape
    pairs = w.shape[2] // (2 * head_size)
    lanes = 2 * head_size
    block = 256
    kernel = lambda *refs: attend_kernel(
        *refs, block=block, window=window, scale=1.0 / math.sqrt(head_size), head_size=head_size)
    whole = lambda p: (0, 0)
    column = pl.BlockSpec((tokens, lanes), lambda p: (0, p))
    flops = 2 * tokens * (width * 3 + 4 * window) * lanes * pairs
    return pl.pallas_call(
        kernel,
        grid=(pairs,),
        in_specs=[
            pl.BlockSpec((1, tokens), whole),
            pl.BlockSpec((tokens, width), whole),
            pl.BlockSpec((3, width, lanes), lambda p: (0, 0, p)),
            pl.BlockSpec((tokens, lanes), whole),
            pl.BlockSpec((tokens, lanes), whole),
        ],
        out_specs=[column, column, column, column, pl.BlockSpec((1, 8, tokens), lambda p: (p, 0, 0))],
        out_shape=[jax.ShapeDtypeStruct((tokens, lanes * pairs), BF)] * 4
        + [jax.ShapeDtypeStruct((pairs, 8, tokens), F32)],
        scratch_shapes=[pltpu.VMEM((tokens, 128), F32)],
        compiler_params=pltpu.CompilerParams(vmem_limit_bytes=40 << 20),
        cost_estimate=pl.CostEstimate(flops=flops, bytes_accessed=8 << 20, transcendentals=0),
        name="attend",
    )(seg, x, w, cosine, sine)


def attend_back_kernel(seg_ref, g_ref, w_ref, q_ref, k_ref, v_ref, att_ref, lse_ref, cos_ref, sin_ref,
                       dq_ref, dk_ref, dv_ref, grad_ref, k_sum, v_sum, *, block, window, scale, head_size):
    tokens = g_ref.shape[0]
    half = head_size // 2
    lane = lax.broadcasted_iota(jnp.int32, (1, 2 * head_size), 1)
    first = lane < head_size
    starts = start_row(seg_ref)
    k_sum[...] = jnp.zeros_like(k_sum)
    v_sum[...] = jnp.zeros_like(v_sum)
    for low in range(0, tokens, block):
        rows = pl.ds(low, block)
        grad_ref[rows, :] = dot(g_ref[rows, :], w_ref[...], ((1,), (1,))).astype(BF)
    for low in range(0, tokens, block):
        begin = first_key(low, block, window)
        end = low + block
        count = end - begin
        q = q_ref[low:end, :] * jnp.asarray(scale, BF)
        grad = grad_ref[low:end, :]
        product = (grad.astype(F32) * att_ref[low:end, :].astype(F32)).T
        k = k_ref[begin:end, :]
        v = v_ref[begin:end, :]
        zero = jnp.zeros_like(k)
        k_two = jnp.concatenate([jnp.where(first, k, zero), jnp.where(first, zero, k)], axis=0)
        v_two = jnp.concatenate([jnp.where(first, v, zero), jnp.where(first, zero, v)], axis=0)
        scores = dot(k_two, q, ((1,), (1,)))
        prob_grad = dot(v_two, grad, ((1,), (1,)))
        key_index = lax.broadcasted_iota(jnp.int32, (count, block), 0) + begin
        query_index = lax.broadcasted_iota(jnp.int32, (count, block), 1) + low
        visible = (key_index.astype(F32) >= starts[:, low:end]) & (key_index <= query_index)
        weights_low, score_low = [], []
        for head in range(2):
            part = slice(head * count, (head + 1) * count)
            weights = jnp.where(
                visible, jnp.exp(scores[part] - lse_ref[0, head:head + 1, low:end]), 0.0)
            row_dots = jnp.sum(
                product[head * head_size:(head + 1) * head_size], axis=0, keepdims=True)
            weights_low.append(weights.astype(BF))
            score_low.append((weights * (prob_grad[part] - row_dots)).astype(BF))
        weights_low = jnp.concatenate(weights_low, axis=0)
        score_low = jnp.concatenate(score_low, axis=0)
        v_part = dot(weights_low, grad)
        k_part = dot(score_low, q)
        v_sum[begin:end, :] += jnp.where(first, v_part[:count], v_part[count:])
        k_sum[begin:end, :] += jnp.where(first, k_part[:count], k_part[count:])
        dq = dot(score_low, k_two, ((0,), (0,))) * scale
        dq_ref[low:end, :] = (
            dq * cos_ref[low:end, :] - turn(dq, half) * sin_ref[low:end, :]).astype(BF)
    for low in range(0, tokens, block):
        rows = pl.ds(low, block)
        dk = k_sum[rows, :]
        dk_ref[rows, :] = (dk * cos_ref[rows, :] - turn(dk, half) * sin_ref[rows, :]).astype(BF)
        dv_ref[rows, :] = v_sum[rows, :].astype(BF)


def attend_back(seg, g, w_out, q, k, v, att, lse, cosine, sine, window, head_size):
    tokens, width = g.shape
    lanes = 2 * head_size
    pairs = q.shape[1] // lanes
    block = 256
    kernel = lambda *refs: attend_back_kernel(
        *refs, block=block, window=window, scale=1.0 / math.sqrt(head_size), head_size=head_size)
    whole = lambda p: (0, 0)
    column = pl.BlockSpec((tokens, lanes), lambda p: (0, p))
    flops = 2 * tokens * (width + 10 * window) * lanes * pairs
    return pl.pallas_call(
        kernel,
        grid=(pairs,),
        in_specs=[
            pl.BlockSpec((1, tokens), whole),
            pl.BlockSpec((tokens, width), whole),
            pl.BlockSpec((lanes, width), lambda p: (p, 0)),
            column, column, column, column,
            pl.BlockSpec((1, 8, tokens), lambda p: (p, 0, 0)),
            pl.BlockSpec((tokens, lanes), whole),
            pl.BlockSpec((tokens, lanes), whole),
        ],
        out_specs=[column, column, column],
        out_shape=[jax.ShapeDtypeStruct((tokens, lanes * pairs), BF)] * 3,
        scratch_shapes=[
            pltpu.VMEM((tokens, lanes), BF),
            pltpu.VMEM((tokens, lanes), F32),
            pltpu.VMEM((tokens, lanes), F32),
        ],
        compiler_params=pltpu.CompilerParams(vmem_limit_bytes=48 << 20),
        cost_estimate=pl.CostEstimate(flops=flops, bytes_accessed=8 << 20, transcendentals=0),
        name="attend_back",
    )(seg, g, w_out, q, k, v, att, lse, cosine, sine)


def normalize(rows, gain):
    factor = lax.rsqrt(jnp.mean(rows * rows, axis=-1, keepdims=True) + EPS)
    unit = rows * factor
    return unit * gain, unit, factor


def normalize_back(grad, unit, factor, gain):
    scaled = grad * gain
    inner = jnp.mean(scaled * unit, axis=-1, keepdims=True)
    return factor * (scaled - unit * inner), jnp.sum(grad * unit, axis=0)


def make_body(groups, ranks, fsdp, square):
    F = ("y", "x") if square else ("f",)
    swap = [(0, 1), (1, 0)]

    def spread(slabs):
        me = lax.axis_index("m")
        out = jnp.zeros_like(slabs)
        for k in range(groups):
            slab = lax.dynamic_index_in_dim(slabs, me ^ k, 0, keepdims=False)
            if k:
                slab = lax.ppermute(slab, "m", [(i, i ^ k) for i in range(groups)])
            out = lax.dynamic_update_index_in_dim(out, slab, me ^ k, 0)
        return out

    def share(part):
        if ranks == 2:
            other = lax.ppermute(part, "r", swap)
            mine_first = lax.axis_index("r") == 0
            return jnp.stack(
                [jnp.where(mine_first, part, other), jnp.where(mine_first, other, part)], axis=1)
        return lax.all_gather(part, "r", axis=1)

    def total(part):
        if ranks == 2:
            return part + lax.ppermute(part.astype(BF), "r", swap).astype(F32)
        return lax.psum(part.astype(BF), "r").astype(F32)

    def gather_rows(part):
        if not square:
            return lax.all_gather(part, F, axis=0)
        rows = part.shape[0] // 2
        me = lax.axis_index(F)
        from_x = lax.ppermute(part, "x", swap)
        from_y = lax.ppermute(part, "y", swap)
        far_a = lax.ppermute(from_y[:rows], "x", swap)
        far_b = lax.ppermute(from_x[rows:], "y", swap)
        out = jnp.zeros((fsdp,) + part.shape, part.dtype)
        out = lax.dynamic_update_index_in_dim(out, part, me, 0)
        out = lax.dynamic_update_index_in_dim(out, from_x, me ^ 1, 0)
        out = lax.dynamic_update_index_in_dim(out, from_y, me ^ 2, 0)
        out = lax.dynamic_update_slice(out, far_a[None], (me ^ 3, 0, 0))
        return lax.dynamic_update_slice(out, far_b[None], (me ^ 3, rows, 0))

    def body(tokens, segments, w_query, w_key, w_value, w_out, w_gate, w_up, w_down,
             gain_attn, gain_ffn, cotangent):
        micro, _, span, width = tokens.shape
        head_size = width // HEADS
        seq_tokens = span * groups * ranks
        window = seq_tokens // 2
        rank = lax.axis_index("r")
        own_cols = width // ranks
        shard = w_query.shape[0]
        down_rows = w_down.shape[0]
        part_rows = down_rows // ranks
        ff = w_gate.shape[1]

        def columns(w):
            return lax.dynamic_slice_in_dim(w, rank * own_cols, own_cols, 1)

        def ff_columns(w):
            return lax.dynamic_slice_in_dim(
                w.reshape(shard, fsdp, down_rows), rank * part_rows, part_rows, 2
            ).reshape(shard, ff // ranks)

        small = jnp.concatenate([columns(w) for w in (w_query, w_key, w_value, w_out)], axis=1)
        seg_rows = jnp.pad(segments[:, 0, None, :].astype(BF), ((0, 0), (0, 15), (0, width - span)))
        token_slabs = jnp.concatenate([tokens[:, 0], seg_rows], axis=1)

        mine = spread(token_slabs)
        small_all = gather_rows(small).reshape(width, 4 * own_cols)
        gate_up = jnp.concatenate([ff_columns(w_gate), ff_columns(w_up)], axis=1)
        down = lax.dynamic_slice_in_dim(w_down, rank * part_rows, part_rows, 0)
        gu_all = lax.all_gather(gate_up, F, axis=0, tiled=True)
        down_all = lax.all_gather(down, F, axis=0, tiled=True)
        gains = lax.all_gather(jnp.stack([gain_attn, gain_ffn]), F, axis=1, tiled=True).astype(F32)
        gain_one, gain_two = gains[0], gains[1]
        cot_mine = spread(cotangent[:, 0])

        both = share(mine)
        x = both[:, :, :span].reshape(seq_tokens, width)
        seg = both[:, :, span, :span].reshape(1, seq_tokens).astype(F32)
        cosine, sine = rotary_tables(seq_tokens, head_size, 2)
        w_qkv = jnp.stack([small_all[:, n * own_cols:(n + 1) * own_cols] for n in range(3)])
        spare = -own_cols % (2 * head_size)
        out_cols = small_all[:, 3 * own_cols:]
        if ranks == 2:
            give = lax.dynamic_slice_in_dim(out_cols, (1 - rank) * own_cols, own_cols, 0)
            keep = lax.dynamic_slice_in_dim(out_cols, rank * own_cols, own_cols, 0)
            got = lax.ppermute(give, "r", swap)
            w_out_own = jnp.where(rank == 0, jnp.concatenate([keep, got], 1),
                                  jnp.concatenate([got, keep], 1))
        else:
            pieces = lax.all_to_all(out_cols, "r", 0, 0, tiled=True)
            pieces = pieces.reshape(ranks, own_cols, own_cols)
            w_out_own = jnp.concatenate([pieces[i] for i in range(ranks)], axis=1)

        w_qkv_even = jnp.pad(w_qkv, ((0, 0), (0, 0), (0, spare)))
        w_out_even = jnp.pad(w_out_own, ((0, spare), (0, 0)))
        q, k, v, att_even, lse = attend(seg, x, w_qkv_even, cosine, sine, window, head_size)
        att = att_even[:, :own_cols]
        branch = total(dot(att, w_out_own))
        middle, unit_one, factor_one = normalize(x.astype(F32) + branch, gain_one)
        middle_low = middle.astype(BF)
        half_ff = ff // ranks
        gate_up_pre = dot(middle_low, gu_all)
        gate_pre, up_pre = gate_up_pre[:, :half_ff], gate_up_pre[:, half_ff:]
        gate_sig = jax.nn.sigmoid(gate_pre)
        gate_silu = gate_pre * gate_sig
        hidden_low = (gate_silu * up_pre).astype(BF)
        ffn_out = total(dot(hidden_low, down_all))
        result, unit_two, factor_two = normalize(middle + ffn_out, gain_two)

        def own_tokens(rows):
            rows = rows.reshape(groups, ranks, span, width)
            return lax.dynamic_index_in_dim(rows, rank, 1, keepdims=False)

        output = spread(own_tokens(result.astype(BF)))
        cot = share(cot_mine).reshape(seq_tokens, width).astype(F32)
        ffn_grad, gain_ffn_grad = normalize_back(cot, unit_two, factor_two, gain_two)
        ffn_grad_low = ffn_grad.astype(BF)
        down_w_grad = dot(hidden_low, ffn_grad_low, ((0,), (0,)))
        hidden_grad = dot(ffn_grad_low, down_all, ((1,), (1,)))
        gate_grad = hidden_grad * up_pre * gate_sig * (1.0 + gate_pre * (1.0 - gate_sig))
        up_grad = hidden_grad * gate_silu
        gu_grad_low = jnp.concatenate([gate_grad.astype(BF), up_grad.astype(BF)], axis=1)
        gu_w_grad = dot(middle_low, gu_grad_low, ((0,), (0,)))
        middle_grad = ffn_grad + total(dot(gu_grad_low, gu_all, ((1,), (1,))))
        branch_grad, gain_attn_grad = normalize_back(middle_grad, unit_one, factor_one, gain_one)
        branch_grad_low = branch_grad.astype(BF)
        out_w_grad = dot(att, branch_grad_low, ((0,), (0,)))
        dq, dk, dv = (d[:, :own_cols] for d in attend_back(
            seg, branch_grad_low, w_out_even, q, k, v, att_even, lse, cosine, sine,
            window, head_size))
        part = sum(dot(d, w_qkv[n], ((1,), (1,))) for n, d in enumerate((dq, dk, dv)))
        qkv_w_grad = [dot(x, d, ((0,), (0,))) for d in (dq, dk, dv)]
        if ranks == 2:
            rows = part.reshape(groups, ranks, span, width)
            give = lax.dynamic_index_in_dim(rows, 1 - rank, 1, keepdims=False).astype(BF)
            part_own = own_tokens(part) + lax.ppermute(give, "r", swap).astype(F32)
        else:
            part_own = own_tokens(total(part))
        input_grad = spread((own_tokens(branch_grad) + part_own).astype(BF))

        if ranks == 2:
            low = out_w_grad.astype(BF)
            give = lax.dynamic_slice_in_dim(low, (1 - rank) * own_cols, own_cols, 1)
            keep = lax.dynamic_slice_in_dim(low, rank * own_cols, own_cols, 1)
            got = lax.ppermute(give, "r", swap)
            out_cols_grad = jnp.where(rank == 0, jnp.concatenate([keep, got], 0),
                                      jnp.concatenate([got, keep], 0))
        else:
            low = out_w_grad.astype(BF).reshape(own_cols, ranks, own_cols).transpose(1, 0, 2)
            out_cols_grad = lax.all_to_all(low, "r", 0, 0, tiled=True).reshape(width, own_cols)
        small_grad = jnp.concatenate([g.astype(BF) for g in qkv_w_grad] + [out_cols_grad], axis=1)

        def reduce(grad):
            owned = lax.psum_scatter(grad.astype(BF), F, scatter_dimension=0, tiled=True)
            return lax.psum(owned, "m")

        down_sum = reduce(down_w_grad)
        gu_sum = reduce(gu_w_grad)
        small_sum = reduce(small_grad)
        down_grad = jnp.moveaxis(share(down_sum), 1, 0).reshape(down_rows, width).astype(F32)
        gu_both = share(gu_sum.reshape(shard, 2 * fsdp, part_rows))
        gu_both = gu_both.reshape(shard, ranks, 2, fsdp, part_rows).astype(F32)
        gate_w, up_w = (
            gu_both[:, :, n].transpose(0, 2, 1, 3).reshape(shard, ff) for n in range(2))
        small_both = share(small_sum).reshape(shard, ranks, 4, own_cols).astype(F32)
        query_w, key_w, value_w, out_w = (
            small_both[:, :, n].reshape(shard, width) for n in range(4))
        gain_sums = lax.psum(jnp.stack([gain_attn_grad, gain_ffn_grad]), ("m",) + F)
        gain_own = lax.dynamic_slice_in_dim(gain_sums, lax.axis_index(F) * shard, shard, 1)
        return (output[:, None], input_grad[:, None], query_w, key_w, value_w, out_w,
                gate_w, up_w, down_grad, gain_own[0], gain_own[1])

    return body


def solution(mesh):
    def run(*args):
        groups = args[0].shape[0]
        seq, fsdp = mesh.shape["seq"], mesh.shape["fsdp"]
        ranks = seq // groups
        square = fsdp == 4
        names = ("m", "r") + (("y", "x") if square else ("f",))
        sizes = (groups, ranks) + ((2, 2) if square else (fsdp,))
        order = [mesh.axis_names.index(name) for name in ("seq", "fsdp")]
        inner = Mesh(mesh.devices.transpose(order).reshape(sizes), names)
        f = ("y", "x") if square else "f"
        s = ("m", "r")
        rows = P(f, None)
        data = P(None, f, s, None)
        in_specs = (data, P(None, f, s)) + (rows,) * 7 + (P(f), P(f), data)
        out_specs = (data, data) + (rows,) * 7 + (P(f), P(f))
        body = make_body(groups, ranks, fsdp, square)
        return jax.shard_map(
            body, mesh=inner, in_specs=in_specs, out_specs=out_specs, check_vma=False)(*args)

    return run
```

```python
import math

import jax
import jax.numpy as jnp
from jax import lax
from jax.experimental import pallas as pl
from jax.experimental.pallas import tpu as pltpu
from jax.sharding import Mesh, PartitionSpec as P

HEADS = 12
DOCS = 4
EPS = 1e-06
NEGATIVE = -1e30
BF = jnp.bfloat16
F32 = jnp.float32


def dot(left, right, dims=((1,), (0,))):
    return lax.dot_general(left, right, (dims, ((), ())), preferred_element_type=F32)


def rotary_tables(seq_tokens, head_size, copies):
    half = head_size // 2
    frequency = 10000.0 ** (-jnp.arange(half, dtype=F32) / half)
    angle = jnp.arange(seq_tokens, dtype=jnp.int32).astype(F32)[:, None] * frequency[None, :]
    cosine, sine = jnp.cos(angle), jnp.sin(angle)
    return (
        jnp.concatenate([cosine, cosine] * copies, axis=1),
        jnp.concatenate([-sine, sine] * copies, axis=1),
    )


def turn(rows, half):
    lanes = rows.shape[1]
    lane = lax.broadcasted_iota(jnp.int32, (1, lanes), 1)
    low = (lane // half) % 2 == 0
    return jnp.where(low, pltpu.roll(rows, lanes - half, 1), pltpu.roll(rows, half, 1))


def first_key(query_first, block, window):
    return max(0, (query_first - window + 1) // block * block)


def start_row(seg_ref):
    seg = seg_ref[...]
    starts = jnp.zeros_like(seg)
    for doc in range(1, DOCS):
        before = jnp.sum(jnp.where(seg < doc, 1.0, 0.0), axis=1, keepdims=True)
        starts = jnp.maximum(starts, jnp.where(seg >= doc, before, 0.0))
    return starts


def attend_kernel(seg_ref, x_ref, w_ref, cos_ref, sin_ref, q_ref, k_ref, v_ref, att_ref, lse_ref,
                  col_ref, *, block, window, scale, head_size):
    tokens = x_ref.shape[0]
    lane = lax.broadcasted_iota(jnp.int32, (1, 2 * head_size), 1)
    first = lane < head_size

    @pl.when(pl.program_id(0) == 0)
    def _():
        starts = start_row(seg_ref)
        col_ref[...] = jnp.broadcast_to(starts, (128, tokens)).T

    for low in range(0, tokens, block):
        rows = pl.ds(low, block)
        lin = [dot(x_ref[rows, :], w_ref[n]) for n in range(3)]
        cosine, sine = cos_ref[rows, :], sin_ref[rows, :]
        half = head_size // 2
        q_ref[rows, :] = (lin[0] * cosine + turn(lin[0], half) * sine).astype(BF)
        k_ref[rows, :] = (lin[1] * cosine + turn(lin[1], half) * sine).astype(BF)
        v_ref[rows, :] = lin[2].astype(BF)
    for low in range(0, tokens, block):
        begin = first_key(low, block, window)
        end = low + block
        q = q_ref[low:end, :] * jnp.asarray(scale, BF)
        zero = jnp.zeros_like(q)
        stacked = jnp.concatenate([jnp.where(first, q, zero), jnp.where(first, zero, q)], axis=0)
        scores = dot(stacked, k_ref[begin:end, :], ((1,), (1,)))
        key_index = lax.broadcasted_iota(jnp.int32, (block, end - begin), 1) + begin
        query_index = lax.broadcasted_iota(jnp.int32, (block, end - begin), 0) + low
        visible = (key_index.astype(F32) >= col_ref[low:end, 0:1]) & (key_index <= query_index)
        parts = []
        for head in range(2):
            own = jnp.where(visible, scores[head * block:(head + 1) * block], NEGATIVE)
            top = jnp.max(own, axis=1, keepdims=True)
            weights = jnp.exp(own - top)
            total = jnp.sum(weights, axis=1, keepdims=True)
            out = dot(weights.astype(BF), v_ref[begin:end, :]) / total
            parts.append(out)
            lse = jnp.broadcast_to(top + jnp.log(total), (block, 128))
            lse_ref[0, head:head + 1, low:end] = lse.T[0:1, :]
        att_ref[low:end, :] = jnp.where(first, parts[0], parts[1]).astype(BF)


def attend(seg, x, w, cosine, sine, window, head_size):
    tokens, width = x.shape
    pairs = w.shape[2] // (2 * head_size)
    lanes = 2 * head_size
    block = 256
    kernel = lambda *refs: attend_kernel(
        *refs, block=block, window=window, scale=1.0 / math.sqrt(head_size), head_size=head_size)
    whole = lambda p: (0, 0)
    column = pl.BlockSpec((tokens, lanes), lambda p: (0, p))
    flops = 2 * tokens * (width * 3 + 4 * window) * lanes * pairs
    return pl.pallas_call(
        kernel,
        grid=(pairs,),
        in_specs=[
            pl.BlockSpec((1, tokens), whole),
            pl.BlockSpec((tokens, width), whole),
            pl.BlockSpec((3, width, lanes), lambda p: (0, 0, p)),
            pl.BlockSpec((tokens, lanes), whole),
            pl.BlockSpec((tokens, lanes), whole),
        ],
        out_specs=[column, column, column, column, pl.BlockSpec((1, 8, tokens), lambda p: (p, 0, 0))],
        out_shape=[jax.ShapeDtypeStruct((tokens, lanes * pairs), BF)] * 4
        + [jax.ShapeDtypeStruct((pairs, 8, tokens), F32)],
        scratch_shapes=[pltpu.VMEM((tokens, 128), F32)],
        compiler_params=pltpu.CompilerParams(vmem_limit_bytes=40 << 20),
        cost_estimate=pl.CostEstimate(flops=flops, bytes_accessed=8 << 20, transcendentals=0),
        name="attend",
    )(seg, x, w, cosine, sine)


def attend_back_kernel(seg_ref, g_ref, w_ref, q_ref, k_ref, v_ref, att_ref, lse_ref, cos_ref, sin_ref,
                       dq_ref, dk_ref, dv_ref, grad_ref, k_sum, v_sum, *, block, window, scale, head_size):
    tokens = g_ref.shape[0]
    half = head_size // 2
    lane = lax.broadcasted_iota(jnp.int32, (1, 2 * head_size), 1)
    first = lane < head_size
    starts = start_row(seg_ref)
    k_sum[...] = jnp.zeros_like(k_sum)
    v_sum[...] = jnp.zeros_like(v_sum)
    for low in range(0, tokens, block):
        rows = pl.ds(low, block)
        grad_ref[rows, :] = dot(g_ref[rows, :], w_ref[...], ((1,), (1,))).astype(BF)
    for low in range(0, tokens, block):
        begin = first_key(low, block, window)
        end = low + block
        count = end - begin
        q = q_ref[low:end, :] * jnp.asarray(scale, BF)
        grad = grad_ref[low:end, :]
        product = (grad.astype(F32) * att_ref[low:end, :].astype(F32)).T
        k = k_ref[begin:end, :]
        v = v_ref[begin:end, :]
        zero = jnp.zeros_like(k)
        k_two = jnp.concatenate([jnp.where(first, k, zero), jnp.where(first, zero, k)], axis=0)
        v_two = jnp.concatenate([jnp.where(first, v, zero), jnp.where(first, zero, v)], axis=0)
        scores = dot(k_two, q, ((1,), (1,)))
        prob_grad = dot(v_two, grad, ((1,), (1,)))
        key_index = lax.broadcasted_iota(jnp.int32, (count, block), 0) + begin
        query_index = lax.broadcasted_iota(jnp.int32, (count, block), 1) + low
        visible = (key_index.astype(F32) >= starts[:, low:end]) & (key_index <= query_index)
        weights_low, score_low = [], []
        for head in range(2):
            part = slice(head * count, (head + 1) * count)
            weights = jnp.where(
                visible, jnp.exp(scores[part] - lse_ref[0, head:head + 1, low:end]), 0.0)
            row_dots = jnp.sum(
                product[head * head_size:(head + 1) * head_size], axis=0, keepdims=True)
            weights_low.append(weights.astype(BF))
            score_low.append((weights * (prob_grad[part] - row_dots)).astype(BF))
        weights_low = jnp.concatenate(weights_low, axis=0)
        score_low = jnp.concatenate(score_low, axis=0)
        v_part = dot(weights_low, grad)
        k_part = dot(score_low, q)
        v_sum[begin:end, :] += jnp.where(first, v_part[:count], v_part[count:])
        k_sum[begin:end, :] += jnp.where(first, k_part[:count], k_part[count:])
        dq = dot(score_low, k_two, ((0,), (0,))) * scale
        dq_ref[low:end, :] = (
            dq * cos_ref[low:end, :] - turn(dq, half) * sin_ref[low:end, :]).astype(BF)
    for low in range(0, tokens, block):
        rows = pl.ds(low, block)
        dk = k_sum[rows, :]
        dk_ref[rows, :] = (dk * cos_ref[rows, :] - turn(dk, half) * sin_ref[rows, :]).astype(BF)
        dv_ref[rows, :] = v_sum[rows, :].astype(BF)


def attend_back(seg, g, w_out, q, k, v, att, lse, cosine, sine, window, head_size):
    tokens, width = g.shape
    lanes = 2 * head_size
    pairs = q.shape[1] // lanes
    block = 256
    kernel = lambda *refs: attend_back_kernel(
        *refs, block=block, window=window, scale=1.0 / math.sqrt(head_size), head_size=head_size)
    whole = lambda p: (0, 0)
    column = pl.BlockSpec((tokens, lanes), lambda p: (0, p))
    flops = 2 * tokens * (width + 10 * window) * lanes * pairs
    return pl.pallas_call(
        kernel,
        grid=(pairs,),
        in_specs=[
            pl.BlockSpec((1, tokens), whole),
            pl.BlockSpec((tokens, width), whole),
            pl.BlockSpec((lanes, width), lambda p: (p, 0)),
            column, column, column, column,
            pl.BlockSpec((1, 8, tokens), lambda p: (p, 0, 0)),
            pl.BlockSpec((tokens, lanes), whole),
            pl.BlockSpec((tokens, lanes), whole),
        ],
        out_specs=[column, column, column],
        out_shape=[jax.ShapeDtypeStruct((tokens, lanes * pairs), BF)] * 3,
        scratch_shapes=[
            pltpu.VMEM((tokens, lanes), BF),
            pltpu.VMEM((tokens, lanes), F32),
            pltpu.VMEM((tokens, lanes), F32),
        ],
        compiler_params=pltpu.CompilerParams(vmem_limit_bytes=48 << 20),
        cost_estimate=pl.CostEstimate(flops=flops, bytes_accessed=8 << 20, transcendentals=0),
        name="attend_back",
    )(seg, g, w_out, q, k, v, att, lse, cosine, sine)


def normalize(rows, gain):
    factor = lax.rsqrt(jnp.mean(rows * rows, axis=-1, keepdims=True) + EPS)
    unit = rows * factor
    return unit * gain, unit, factor


def normalize_back(grad, unit, factor, gain):
    scaled = grad * gain
    inner = jnp.mean(scaled * unit, axis=-1, keepdims=True)
    return factor * (scaled - unit * inner), jnp.sum(grad * unit, axis=0)


def join_kernel(rank_ref, own_ref, other_ref, *out_refs, moves, plain):
    swapped = rank_ref[0] == 1
    own, other = own_ref[...], other_ref[...]
    halves = (jnp.where(swapped, other, own), jnp.where(swapped, own, other))
    for out, half, (rows, cols), (to_rows, to_cols) in moves:
        out_refs[out][to_rows, to_cols] = halves[half][rows, cols].astype(F32)
    for out, (rows, cols) in plain:
        out_refs[out][...] = own[rows, cols].astype(F32)


def join(rank, own, other, moves, plain, shapes):
    kernel = lambda *refs: join_kernel(*refs, moves=moves, plain=plain)
    return pl.pallas_call(
        kernel,
        in_specs=[
            pl.BlockSpec(memory_space=pltpu.SMEM),
            pl.BlockSpec(memory_space=pltpu.VMEM),
            pl.BlockSpec(memory_space=pltpu.VMEM),
        ],
        out_specs=[pl.BlockSpec(memory_space=pltpu.VMEM)] * len(shapes),
        out_shape=[jax.ShapeDtypeStruct(shape, F32) for shape in shapes],
        compiler_params=pltpu.CompilerParams(vmem_limit_bytes=32 << 20),
        name="join",
    )(rank.reshape(1), own, other)


def make_body(groups, ranks, fsdp, square):
    F = ("y", "x") if square else ("f",)
    swap = [(0, 1), (1, 0)]
    pairs = square and ranks == 2 and groups == 4

    def hop(value, k):
        return lax.ppermute(value, "m", [(i, i ^ k) for i in range(groups)])

    def after(value, *earlier):
        return lax.optimization_barrier((value,) + earlier)[0]

    def spread(slabs, wait=()):
        me = lax.axis_index("m")
        out = jnp.zeros_like(slabs)
        for k in range(groups):
            slab = lax.dynamic_index_in_dim(slabs, me ^ k, 0, keepdims=False)
            if k:
                slab = hop(after(slab, *wait) if wait else slab, k)
            out = lax.dynamic_update_index_in_dim(out, slab, me ^ k, 0)
        return out

    def share(part):
        if ranks == 2:
            other = lax.ppermute(part, "r", swap)
            mine_first = lax.axis_index("r") == 0
            return jnp.stack(
                [jnp.where(mine_first, part, other), jnp.where(mine_first, other, part)], axis=1)
        return lax.all_gather(part, "r", axis=1)

    def total(part):
        if ranks == 2:
            return part + lax.ppermute(part.astype(BF), "r", swap).astype(F32)
        return lax.psum(part.astype(BF), "r").astype(F32)

    def gather_rows(part, wait=()):
        if not square:
            return lax.all_gather(part, F, axis=0), ()
        rows = (part.shape[0] // 2) // 16 * 16
        me = lax.axis_index(F)
        send = after(part, *wait) if wait else part
        from_x = lax.ppermute(send, "x", swap)
        from_y = lax.ppermute(send, "y", swap)
        far_a = lax.ppermute(from_y[:rows], "x", swap)
        far_b = lax.ppermute(from_x[rows:], "y", swap)
        out = jnp.zeros((fsdp,) + part.shape, part.dtype)
        out = lax.dynamic_update_index_in_dim(out, part, me, 0)
        out = lax.dynamic_update_index_in_dim(out, from_x, me ^ 1, 0)
        out = lax.dynamic_update_index_in_dim(out, from_y, me ^ 2, 0)
        out = lax.dynamic_update_slice(out, far_a[None], (me ^ 3, 0, 0))
        return lax.dynamic_update_slice(out, far_b[None], (me ^ 3, rows, 0)), (from_x, from_y)

    def add(*parts):
        return sum(part.astype(F32) for part in parts).astype(BF)

    def reduce(grad, axis):
        if not pairs:
            owned = lax.psum_scatter(grad, F, scatter_dimension=0, tiled=False)
            return lax.psum(owned, "m")
        me = lax.axis_index(F)
        take = lambda k: lax.dynamic_index_in_dim(grad, me ^ k, 0, keepdims=False)
        rows = (grad.shape[1] // 2) // 16 * 16
        far = take(3)
        low = lax.ppermute(far[:rows], "x", swap)
        high = lax.ppermute(far[rows:], "y", swap)
        to_x, to_y = take(1), take(2)
        to_x = jnp.concatenate([to_x[:rows], add(to_x[rows:], high)], axis=0)
        to_y = jnp.concatenate([add(to_y[:rows], low), to_y[rows:]], axis=0)
        owned = add(take(0), lax.ppermute(to_x, "x", swap), lax.ppermute(to_y, "y", swap))
        m = lax.axis_index("m")
        stages = []
        for bit in (1, 2):
            half = owned.shape[axis] // 2
            side = (m // bit) % 2
            give = lax.dynamic_slice_in_dim(owned, (1 - side) * half, half, axis)
            keep = lax.dynamic_slice_in_dim(owned, side * half, half, axis)
            owned = add(keep, hop(give, bit))
            stages.append((bit, side))
        for bit, side in reversed(stages):
            other = hop(owned, bit)
            first = side == 0
            owned = jnp.concatenate(
                [jnp.where(first, owned, other), jnp.where(first, other, owned)], axis=axis)
        return owned

    def body(tokens, segments, w_query, w_key, w_value, w_out, w_gate, w_up, w_down,
             gain_attn, gain_ffn, cotangent):
        micro, _, span, width = tokens.shape
        head_size = width // HEADS
        seq_tokens = span * groups * ranks
        window = seq_tokens // 2
        rank = lax.axis_index("r")
        own_cols = width // ranks
        shard = w_query.shape[0]
        down_rows = w_down.shape[0]
        part_rows = down_rows // ranks
        ff = w_gate.shape[1]
        half_ff = ff // ranks

        def columns(w):
            return lax.dynamic_slice_in_dim(w, rank * own_cols, own_cols, 1)

        def ff_columns(w):
            blocks = [
                lax.dynamic_slice_in_dim(w, j * down_rows + rank * part_rows, part_rows, 1)
                for j in range(fsdp)]
            return jnp.concatenate(blocks, axis=1)

        gain_rows = jnp.pad(
            jnp.stack([gain_attn, gain_ffn]), ((0, 14), (0, 4 * own_cols - shard)))
        small = jnp.concatenate(
            [jnp.concatenate([columns(w) for w in (w_query, w_key, w_value, w_out)], axis=1),
             gain_rows], axis=0)
        seg_rows = jnp.pad(segments[:, 0, None, :].astype(BF), ((0, 0), (0, 15), (0, width - span)))
        token_slabs = jnp.concatenate([tokens[:, 0], seg_rows], axis=1)

        mine = spread(token_slabs)
        small_all, sent = gather_rows(small)
        gate_up = jnp.concatenate([ff_columns(w_gate), ff_columns(w_up)], axis=1)
        down = lax.dynamic_slice_in_dim(w_down, rank * part_rows, part_rows, 0)
        gu_all, sent = gather_rows(gate_up, sent)
        down_all, sent = gather_rows(down, sent)
        gu_all = gu_all.reshape(width, 2 * half_ff)
        down_all = down_all.reshape(half_ff, width)
        gains = small_all[:, shard:shard + 2, :shard].astype(F32).transpose(1, 0, 2)
        gains = gains.reshape(2, width)
        gain_one, gain_two = gains[0], gains[1]
        small_all = small_all[:, :shard].reshape(width, 4 * own_cols)
        cot_mine = spread(cotangent[:, 0], (mine,))

        both = share(mine)
        x = both[:, :, :span].reshape(seq_tokens, width)
        seg = both[:, :, span, :span].reshape(1, seq_tokens).astype(F32)
        cosine, sine = rotary_tables(seq_tokens, head_size, 2)
        w_qkv = jnp.stack([small_all[:, n * own_cols:(n + 1) * own_cols] for n in range(3)])
        spare = -own_cols % (2 * head_size)
        out_cols = small_all[:, 3 * own_cols:]
        if ranks == 2:
            give = lax.dynamic_slice_in_dim(out_cols, (1 - rank) * own_cols, own_cols, 0)
            keep = lax.dynamic_slice_in_dim(out_cols, rank * own_cols, own_cols, 0)
            got = lax.ppermute(give, "r", swap)
            w_out_own = jnp.where(rank == 0, jnp.concatenate([keep, got], 1),
                                  jnp.concatenate([got, keep], 1))
        else:
            pieces = lax.all_to_all(out_cols, "r", 0, 0, tiled=True)
            pieces = pieces.reshape(ranks, own_cols, own_cols)
            w_out_own = jnp.concatenate([pieces[i] for i in range(ranks)], axis=1)

        w_qkv_even = jnp.pad(w_qkv, ((0, 0), (0, 0), (0, spare)))
        w_out_even = jnp.pad(w_out_own, ((0, spare), (0, 0)))
        q, k, v, att_even, lse = attend(seg, x, w_qkv_even, cosine, sine, window, head_size)
        att = att_even[:, :own_cols]
        branch = total(dot(att, w_out_own))
        middle, unit_one, factor_one = normalize(x.astype(F32) + branch, gain_one)
        middle_low = middle.astype(BF)
        gate_up_pre = dot(middle_low, gu_all)
        gate_pre, up_pre = gate_up_pre[:, :half_ff], gate_up_pre[:, half_ff:]
        gate_sig = jax.nn.sigmoid(gate_pre)
        gate_silu = gate_pre * gate_sig
        hidden_low = (gate_silu * up_pre).astype(BF)
        ffn_out = total(dot(hidden_low, down_all))
        result, unit_two, factor_two = normalize(middle + ffn_out, gain_two)

        def own_tokens(rows):
            rows = rows.reshape(groups, ranks, span, width)
            return lax.dynamic_index_in_dim(rows, rank, 1, keepdims=False)

        output = spread(own_tokens(result.astype(BF)))
        cot = share(cot_mine).reshape(seq_tokens, width).astype(F32)
        ffn_grad, gain_ffn_grad = normalize_back(cot, unit_two, factor_two, gain_two)
        ffn_grad_low = ffn_grad.astype(BF)
        down_w_grad = dot(hidden_low, ffn_grad_low, ((0,), (0,))).astype(BF)
        hidden_grad = dot(ffn_grad_low, down_all, ((1,), (1,)))
        gate_grad = hidden_grad * up_pre * gate_sig * (1.0 + gate_pre * (1.0 - gate_sig))
        up_grad = hidden_grad * gate_silu
        gu_grad_low = jnp.concatenate([gate_grad.astype(BF), up_grad.astype(BF)], axis=1)
        gu_w_grad = dot(middle_low, gu_grad_low, ((0,), (0,))).astype(BF)
        middle_grad = ffn_grad + total(dot(gu_grad_low, gu_all, ((1,), (1,))))
        branch_grad, gain_attn_grad = normalize_back(middle_grad, unit_one, factor_one, gain_one)
        branch_grad_low = branch_grad.astype(BF)
        out_w_grad = dot(att, branch_grad_low, ((0,), (0,)))
        dq, dk, dv = (d[:, :own_cols] for d in attend_back(
            seg, branch_grad_low, w_out_even, q, k, v, att_even, lse, cosine, sine,
            window, head_size))
        part = sum(dot(d, w_qkv[n], ((1,), (1,))) for n, d in enumerate((dq, dk, dv)))
        qkv_w_grad = [dot(x, d, ((0,), (0,))) for d in (dq, dk, dv)]
        if ranks == 2:
            rows = part.reshape(groups, ranks, span, width)
            give = lax.dynamic_index_in_dim(rows, 1 - rank, 1, keepdims=False).astype(BF)
            part_own = own_tokens(part) + lax.ppermute(give, "r", swap).astype(F32)
        else:
            part_own = own_tokens(total(part))
        input_grad = spread((own_tokens(branch_grad) + part_own).astype(BF))

        if ranks == 2:
            low = out_w_grad.astype(BF)
            give = lax.dynamic_slice_in_dim(low, (1 - rank) * own_cols, own_cols, 1)
            keep = lax.dynamic_slice_in_dim(low, rank * own_cols, own_cols, 1)
            got = lax.ppermute(give, "r", swap)
            out_cols_grad = jnp.where(rank == 0, jnp.concatenate([keep, got], 0),
                                      jnp.concatenate([got, keep], 0))
        else:
            low = out_w_grad.astype(BF).reshape(own_cols, ranks, own_cols).transpose(1, 0, 2)
            out_cols_grad = lax.all_to_all(low, "r", 0, 0, tiled=True).reshape(width, own_cols)
        small_grad = jnp.concatenate([g.astype(BF) for g in qkv_w_grad] + [out_cols_grad], axis=1)
        gain_grads = jnp.stack([gain_attn_grad, gain_ffn_grad]).astype(BF)
        gain_grads = gain_grads.reshape(2, fsdp, shard).transpose(1, 0, 2)
        gain_grads = jnp.pad(gain_grads, ((0, 0), (0, 14), (0, 4 * own_cols - shard)))
        small_grad = jnp.concatenate(
            [small_grad.reshape(fsdp, shard, 4 * own_cols), gain_grads], axis=1)

        down_sum = reduce(down_w_grad.reshape(fsdp, part_rows, width), 0)
        gu_sum = reduce(gu_w_grad.reshape(fsdp, shard, 2 * half_ff), 0)
        small_sum = reduce(small_grad, 1)
        if ranks == 2:
            everything = slice(None)
            down_moves = [
                (0, h, (everything, everything), (slice(h * part_rows, (h + 1) * part_rows), everything))
                for h in range(2)]
            gu_moves = [
                (n, h,
                 (everything, slice(n * half_ff + j * part_rows, n * half_ff + (j + 1) * part_rows)),
                 (everything, slice(j * down_rows + h * part_rows, j * down_rows + (h + 1) * part_rows)))
                for n in range(2) for h in range(2) for j in range(fsdp)]
            small_moves = [
                (n, h, (slice(0, shard), slice(n * own_cols, (n + 1) * own_cols)),
                 (everything, slice(h * own_cols, (h + 1) * own_cols)))
                for n in range(4) for h in range(2)]
            small_plain = [
                (4 + n, (slice(shard + n, shard + n + 1), slice(0, shard))) for n in range(2)]
            down_grad, = join(rank, down_sum, lax.ppermute(down_sum, "r", swap),
                              down_moves, [], [(down_rows, width)])
            gate_w, up_w = join(rank, gu_sum, lax.ppermute(gu_sum, "r", swap),
                                gu_moves, [], [(shard, ff)] * 2)
            query_w, key_w, value_w, out_w, gain_a, gain_f = join(
                rank, small_sum, lax.ppermute(small_sum, "r", swap), small_moves, small_plain,
                [(shard, width)] * 4 + [(1, shard)] * 2)
        else:
            down_grad = jnp.moveaxis(share(down_sum), 1, 0).reshape(down_rows, width).astype(F32)
            gu_both = share(gu_sum.reshape(shard, 2 * fsdp, part_rows))
            gu_both = gu_both.reshape(shard, ranks, 2, fsdp, part_rows).astype(F32)
            gate_w, up_w = (
                gu_both[:, :, n].transpose(0, 2, 1, 3).reshape(shard, ff) for n in range(2))
            small_both = share(small_sum)[:shard].reshape(shard, ranks, 4, own_cols).astype(F32)
            query_w, key_w, value_w, out_w = (
                small_both[:, :, n].reshape(shard, width) for n in range(4))
            gain_a, gain_f = small_sum[shard, :shard].astype(F32), small_sum[shard + 1, :shard].astype(F32)
        return (output[:, None], input_grad[:, None], query_w, key_w, value_w, out_w,
                gate_w, up_w, down_grad, gain_a.reshape(shard), gain_f.reshape(shard))

    return body


def solution(mesh):
    def run(*args):
        groups = args[0].shape[0]
        seq, fsdp = mesh.shape["seq"], mesh.shape["fsdp"]
        ranks = seq // groups
        square = fsdp == 4
        names = ("m", "r") + (("y", "x") if square else ("f",))
        sizes = (groups, ranks) + ((2, 2) if square else (fsdp,))
        order = [mesh.axis_names.index(name) for name in ("seq", "fsdp")]
        inner = Mesh(mesh.devices.transpose(order).reshape(sizes), names)
        f = ("y", "x") if square else "f"
        s = ("m", "r")
        rows = P(f, None)
        data = P(None, f, s, None)
        in_specs = (data, P(None, f, s)) + (rows,) * 7 + (P(f), P(f), data)
        out_specs = (data, data) + (rows,) * 7 + (P(f), P(f))
        body = make_body(groups, ranks, fsdp, square)
        return jax.shard_map(
            body, mesh=inner, in_specs=in_specs, out_specs=out_specs, check_vma=False)(*args)

    return run
```

```python
import math

import jax
import jax.numpy as jnp
from jax import lax
from jax.experimental import pallas as pl
from jax.experimental.pallas import tpu as pltpu
from jax.sharding import Mesh, PartitionSpec as P

HEADS = 12
DOCS = 4
EPS = 1e-06
NEGATIVE = -1e30
BF = jnp.bfloat16
F32 = jnp.float32


def dot(left, right, dims=((1,), (0,))):
    return lax.dot_general(left, right, (dims, ((), ())), preferred_element_type=F32)


def rotary_tables(seq_tokens, head_size, copies):
    half = head_size // 2
    frequency = 10000.0 ** (-jnp.arange(half, dtype=F32) / half)
    angle = jnp.arange(seq_tokens, dtype=jnp.int32).astype(F32)[:, None] * frequency[None, :]
    cosine, sine = jnp.cos(angle), jnp.sin(angle)
    return (
        jnp.concatenate([cosine, cosine] * copies, axis=1),
        jnp.concatenate([-sine, sine] * copies, axis=1),
    )


def turn(rows, half):
    lanes = rows.shape[1]
    lane = lax.broadcasted_iota(jnp.int32, (1, lanes), 1)
    low = (lane // half) % 2 == 0
    return jnp.where(low, pltpu.roll(rows, lanes - half, 1), pltpu.roll(rows, half, 1))


def first_key(query_first, block, window):
    return max(0, (query_first - window + 1) // block * block)


def start_row(seg_ref):
    seg = seg_ref[...]
    starts = jnp.zeros_like(seg)
    for doc in range(1, DOCS):
        before = jnp.sum(jnp.where(seg < doc, 1.0, 0.0), axis=1, keepdims=True)
        starts = jnp.maximum(starts, jnp.where(seg >= doc, before, 0.0))
    return starts


def place(target, refs, pieces, me, shard):
    for ref, (offset, first, rows) in zip(refs, pieces):
        if offset is None:
            target[...] = ref[...]
        else:
            start = pl.multiple_of((me ^ offset) * shard + first, 16)
            target[pl.ds(start, rows), :] = ref[0:rows, 0:target.shape[1]]


def place_tokens(target, refs, where_ref, ranks):
    if len(refs) == 1:
        target[...] = refs[0][...]
        return
    groups = len(refs) // ranks
    span = target.shape[0] // (groups * ranks)
    for n, ref in enumerate(refs):
        rank = where_ref[2] if n < groups else 1 - where_ref[2]
        chunk = (where_ref[1] ^ (n % groups)) * ranks + rank
        target[pl.ds(pl.multiple_of(chunk * span, span), span), :] = ref[0:span, :]


def place_segments(target, refs, where_ref, ranks):
    groups = len(refs) // ranks
    span = target.shape[1] // (groups * ranks)
    for n, ref in enumerate(refs):
        rank = where_ref[2] if n < groups else 1 - where_ref[2]
        chunk = (where_ref[1] ^ (n % groups)) * ranks + rank
        row = ref[span:span + 16, 0:span].astype(F32)[0:1, :]
        target[:, pl.ds(pl.multiple_of(chunk * span, span), span)] = row


def place_stack(gu, down, stack_ref, shard, part_rows):
    chunks = gu.shape[1] // 256
    for j in range(stack_ref.shape[0]):
        for c in range(chunks):
            gu[j * shard:(j + 1) * shard, c * 256:(c + 1) * 256] = (
                stack_ref[j, c * shard:(c + 1) * shard, :])
        for c in range(down.shape[1] // 256):
            at = chunks * shard + c * part_rows
            down[j * part_rows:(j + 1) * part_rows, c * 256:(c + 1) * 256] = (
                stack_ref[j, at:at + part_rows, :])


def attend_kernel(where_ref, cos_ref, sin_ref, *refs, pieces, token_count, ranks, shard, block,
                  window, scale, head_size):
    inputs, refs = refs[:-9], refs[-9:]
    q_ref, k_ref, v_ref, att_ref, lse_ref, w_ref, x_ref, seg_ref, col_ref = refs
    token_refs, w_refs = inputs[:token_count], inputs[token_count:]
    tokens = x_ref.shape[0]
    lanes = 2 * head_size
    lane = lax.broadcasted_iota(jnp.int32, (1, lanes), 1)
    first = lane < head_size
    pair = pl.program_id(0)

    @pl.when(pair == 0)
    def _():
        place(w_ref, w_refs, pieces, where_ref[0], shard)
        place_tokens(x_ref, token_refs[:1] if token_count == 2 else token_refs, where_ref, ranks)
        if token_count == 2:
            seg_ref[...] = token_refs[1][...]
        else:
            place_segments(seg_ref, token_refs, where_ref, ranks)
        starts = start_row(seg_ref)
        col_ref[...] = jnp.broadcast_to(starts, (128, tokens)).T

    w = w_ref[:, pl.ds(pl.multiple_of(pair * 3 * lanes, lanes), 3 * lanes)]
    for low in range(0, tokens, block):
        rows = pl.ds(low, block)
        lin = dot(x_ref[rows, :], w)
        cosine, sine = cos_ref[rows, :], sin_ref[rows, :]
        half = head_size // 2
        q_lin, k_lin = lin[:, :lanes], lin[:, lanes:2 * lanes]
        q_ref[rows, :] = (q_lin * cosine + turn(q_lin, half) * sine).astype(BF)
        k_ref[rows, :] = (k_lin * cosine + turn(k_lin, half) * sine).astype(BF)
        v_ref[rows, :] = lin[:, 2 * lanes:].astype(BF)
    for low in range(0, tokens, block):
        begin = first_key(low, block, window)
        end = low + block
        q = q_ref[low:end, :] * jnp.asarray(scale, BF)
        zero = jnp.zeros_like(q)
        stacked = jnp.concatenate([jnp.where(first, q, zero), jnp.where(first, zero, q)], axis=0)
        scores = dot(stacked, k_ref[begin:end, :], ((1,), (1,)))
        key_index = lax.broadcasted_iota(jnp.int32, (block, end - begin), 1) + begin
        query_index = lax.broadcasted_iota(jnp.int32, (block, end - begin), 0) + low
        visible = (key_index.astype(F32) >= col_ref[low:end, 0:1]) & (key_index <= query_index)
        parts = []
        for head in range(2):
            own = jnp.where(visible, scores[head * block:(head + 1) * block], NEGATIVE)
            top = jnp.max(own, axis=1, keepdims=True)
            weights = jnp.exp(own - top)
            total = jnp.sum(weights, axis=1, keepdims=True)
            out = dot(weights.astype(BF), v_ref[begin:end, :]) / total
            parts.append(out)
            lse = jnp.broadcast_to(top + jnp.log(total), (block, 128))
            lse_ref[0, head:head + 1, low:end] = lse.T[0:1, :]
        att_ref[low:end, :] = jnp.where(first, parts[0], parts[1]).astype(BF)


SMALL_COST = pl.CostEstimate(flops=1, bytes_accessed=1, transcendentals=0)
VMEM_SPEC = pl.BlockSpec(memory_space=pltpu.VMEM)
SMEM_SPEC = pl.BlockSpec(memory_space=pltpu.SMEM)


def attend(where, cosine, sine, token_refs, ranks, weights, pieces, shard, lanes_all, window,
           head_size, width):
    tokens = cosine.shape[0]
    lanes = 2 * head_size
    pairs = lanes_all // lanes
    kernel = lambda *refs: attend_kernel(
        *refs, pieces=pieces, token_count=len(token_refs), ranks=ranks, shard=shard, block=256,
        window=window, scale=1.0 / math.sqrt(head_size), head_size=head_size)
    column = pl.BlockSpec((tokens, lanes), lambda p: (0, p))
    whole = lambda *shape: pl.BlockSpec(shape, lambda p: (0, 0))
    return pl.pallas_call(
        kernel,
        grid=(pairs,),
        in_specs=[SMEM_SPEC] + [VMEM_SPEC] * (2 + len(token_refs) + len(weights)),
        out_specs=[column, column, column, column,
                   pl.BlockSpec((1, 8, tokens), lambda p: (p, 0, 0)),
                   whole(width, 3 * lanes_all), whole(tokens, width), whole(1, tokens)],
        out_shape=[jax.ShapeDtypeStruct((tokens, lanes_all), BF)] * 4
        + [jax.ShapeDtypeStruct((pairs, 8, tokens), F32),
           jax.ShapeDtypeStruct((width, 3 * lanes_all), BF),
           jax.ShapeDtypeStruct((tokens, width), BF),
           jax.ShapeDtypeStruct((1, tokens), F32)],
        scratch_shapes=[pltpu.VMEM((tokens, 128), F32)],
        compiler_params=pltpu.CompilerParams(vmem_limit_bytes=40 << 20),
        cost_estimate=SMALL_COST,
        name="attend",
    )(where, cosine, sine, *token_refs, *weights)


def unit_of(rows):
    factor = lax.rsqrt(jnp.mean(rows * rows, axis=1, keepdims=True) + EPS)
    return rows * factor, factor


def forward_kernel(x_ref, own_ref, got_ref, gain_ref, stack_ref, sum_ref, low_ref, hidden_ref,
                   gate_ref, silu_ref, part_ref, gu, down, *, shard, part_rows):
    @pl.when(pl.program_id(0) == 0)
    def _():
        place_stack(gu, down, stack_ref, shard, part_rows)

    total = x_ref[...].astype(F32) + own_ref[...].astype(F32) + got_ref[...].astype(F32)
    sum_ref[...] = total
    middle_low = (unit_of(total)[0] * gain_ref[...]).astype(BF)
    low_ref[...] = middle_low
    ff = down.shape[0]
    for c in range(0, ff, 256):
        gate = dot(middle_low, gu[:, c:c + 256])
        up = dot(middle_low, gu[:, ff + c:ff + c + 256])
        sigmoid = jax.nn.sigmoid(gate)
        silu = gate * sigmoid
        hidden_ref[:, c:c + 256] = (silu * up).astype(BF)
        gate_ref[:, c:c + 256] = (up * sigmoid * (1.0 + gate * (1.0 - sigmoid))).astype(BF)
        silu_ref[:, c:c + 256] = silu.astype(BF)
    part_ref[...] = dot(hidden_ref[...], down[...]).astype(BF)


def forward(x, own, got, gain, stack, shard, part_rows, ff, block):
    tokens, width = x.shape
    row = lambda cols: pl.BlockSpec((block, cols), lambda i: (i, 0))
    return pl.pallas_call(
        lambda *refs: forward_kernel(*refs, shard=shard, part_rows=part_rows),
        grid=(tokens // block,),
        in_specs=[row(width), row(width), row(width), VMEM_SPEC, VMEM_SPEC],
        out_specs=[row(width), row(width), row(ff), row(ff), row(ff), row(width)],
        out_shape=[jax.ShapeDtypeStruct((tokens, width), F32),
                   jax.ShapeDtypeStruct((tokens, width), BF)]
        + [jax.ShapeDtypeStruct((tokens, ff), BF)] * 3
        + [jax.ShapeDtypeStruct((tokens, width), BF)],
        scratch_shapes=[pltpu.VMEM((width, 2 * ff), BF), pltpu.VMEM((ff, width), BF)],
        compiler_params=pltpu.CompilerParams(vmem_limit_bytes=40 << 20),
        cost_estimate=pl.CostEstimate(
            flops=6 * tokens * width * ff, bytes_accessed=24 << 20, transcendentals=0),
        name="ffn_forward",
    )(x, own, got, gain, stack)


def backward_kernel(where_ref, sum_ref, own_ref, got_ref, gate_ref, silu_ref, gains_ref, *refs,
                    cot_count, shard, part_rows, groups, ranks):
    cot_refs, stack_ref, refs = refs[:cot_count], refs[cot_count], refs[cot_count + 1:]
    out_refs, refs = refs[:groups], refs[groups:]
    grad_ref, low_ref, gu_grad_ref, part_ref, gain_ref, gu, down, cot_ref, rows_ref = refs
    step = pl.program_id(0)

    @pl.when(step == 0)
    def _():
        place_stack(gu, down, stack_ref, shard, part_rows)
        place_tokens(cot_ref, cot_refs, where_ref, ranks)
        gain_ref[...] = jnp.zeros_like(gain_ref)

    gain_two = gains_ref[1:2, :]
    middle = unit_of(sum_ref[...])[0] * gains_ref[0:1, :]
    unit, factor = unit_of(middle + own_ref[...].astype(F32) + got_ref[...].astype(F32))
    block, span = rows_ref.shape[0], out_refs[0].shape[0]
    rows_ref[...] = unit * gain_two
    kept = rows_ref[pl.ds(pl.multiple_of(where_ref[2] * span, span), span), :].astype(BF)
    for k, out_ref in enumerate(out_refs):
        @pl.when(step == (where_ref[1] ^ k))
        def _(out_ref=out_ref):
            out_ref[...] = kept
    cot = cot_ref[pl.ds(pl.multiple_of(step * block, block), block), :].astype(F32)
    gain_ref[...] += jnp.sum(cot * unit, axis=0, keepdims=True)
    scaled = cot * gain_two
    grad = factor * (scaled - unit * jnp.mean(scaled * unit, axis=1, keepdims=True))
    grad_ref[...] = grad
    grad_low = grad.astype(BF)
    low_ref[...] = grad_low
    ff = down.shape[0]
    for c in range(0, ff, 256):
        hidden_grad = dot(grad_low, down[c:c + 256, :], ((1,), (1,)))
        gu_grad_ref[:, c:c + 256] = (hidden_grad * gate_ref[:, c:c + 256].astype(F32)).astype(BF)
        gu_grad_ref[:, ff + c:ff + c + 256] = (
            hidden_grad * silu_ref[:, c:c + 256].astype(F32)).astype(BF)
    part_ref[...] = dot(gu_grad_ref[...], gu[...], ((1,), (1,))).astype(BF)


def backward(where, total, own, got, gate, silu, gains, cot, stack, shard, part_rows, block,
             groups, ranks):
    tokens, width = total.shape
    ff = gate.shape[1]
    kernel = lambda *refs: backward_kernel(
        *refs, cot_count=len(cot), shard=shard, part_rows=part_rows, groups=groups, ranks=ranks)
    row = lambda cols: pl.BlockSpec((block, cols), lambda i: (i, 0))
    slab = pl.BlockSpec((block // ranks, width), lambda i: (0, 0))
    return pl.pallas_call(
        kernel,
        grid=(tokens // block,),
        in_specs=[SMEM_SPEC] + [row(width)] * 3 + [row(ff)] * 2
        + [VMEM_SPEC] * (2 + len(cot)),
        out_specs=[slab] * groups + [row(width), row(width), row(2 * ff), row(width),
                                     pl.BlockSpec((1, width), lambda i: (0, 0))],
        out_shape=[jax.ShapeDtypeStruct((block // ranks, width), BF)] * groups
        + [jax.ShapeDtypeStruct((tokens, width), F32),
           jax.ShapeDtypeStruct((tokens, width), BF),
           jax.ShapeDtypeStruct((tokens, 2 * ff), BF),
           jax.ShapeDtypeStruct((tokens, width), BF),
           jax.ShapeDtypeStruct((1, width), F32)],
        scratch_shapes=[pltpu.VMEM((width, 2 * ff), BF), pltpu.VMEM((ff, width), BF),
                        pltpu.VMEM((tokens, width), BF), pltpu.VMEM((block, width), F32)],
        compiler_params=pltpu.CompilerParams(vmem_limit_bytes=44 << 20),
        cost_estimate=SMALL_COST,
        name="ffn_backward",
    )(where, total, own, got, gate, silu, gains, *cot, stack)


def norm_back_kernel(rank_ref, sum_ref, grad_ref, own_ref, got_ref, gain_ref,
                     low_ref, keep_ref, gain_grad_ref, rows_ref):
    @pl.when(pl.program_id(0) == 0)
    def _():
        gain_grad_ref[...] = jnp.zeros_like(gain_grad_ref)

    unit, factor = unit_of(sum_ref[...])
    grad = grad_ref[...] + own_ref[...].astype(F32) + got_ref[...].astype(F32)
    gain_grad_ref[...] += jnp.sum(grad * unit, axis=0, keepdims=True)
    scaled = grad * gain_ref[...]
    branch_grad = factor * (scaled - unit * jnp.mean(scaled * unit, axis=1, keepdims=True))
    low_ref[...] = branch_grad.astype(BF)
    rows_ref[...] = branch_grad
    span = keep_ref.shape[1]
    keep_ref[0] = rows_ref[pl.ds(pl.multiple_of(rank_ref[0] * span, span), span), :]


def norm_back(rank, total, grad, own, got, gain, block, span):
    tokens, width = total.shape
    row = pl.BlockSpec((block, width), lambda i: (i, 0))
    return pl.pallas_call(
        norm_back_kernel,
        grid=(tokens // block,),
        in_specs=[SMEM_SPEC, row, row, row, row, VMEM_SPEC],
        out_specs=[row, pl.BlockSpec((1, span, width), lambda i: (i, 0, 0)),
                   pl.BlockSpec((1, width), lambda i: (0, 0))],
        out_shape=[jax.ShapeDtypeStruct((tokens, width), BF),
                   jax.ShapeDtypeStruct((tokens // block, span, width), F32),
                   jax.ShapeDtypeStruct((1, width), F32)],
        scratch_shapes=[pltpu.VMEM((block, width), F32)],
        compiler_params=pltpu.CompilerParams(vmem_limit_bytes=24 << 20),
        cost_estimate=SMALL_COST,
        name="norm_back",
    )(rank, total, grad, own, got, gain)


def pick(rank, parts):
    value = parts[0]
    for r in range(1, len(parts)):
        value = jnp.where(rank == r, parts[r], value)
    return value


def pack_small_kernel(where_ref, query_ref, key_ref, value_ref, out_ref, gain_ref, tokens_ref,
                      seg_ref, cot_ref, small_ref, *slab_refs, ranks, lanes, lanes_all):
    slab_refs, cot_slabs = slab_refs[:len(slab_refs) // 2], slab_refs[len(slab_refs) // 2:]
    for k, ref in enumerate(cot_slabs):
        ref[...] = cot_ref[where_ref[1] ^ k, 0]
    rank, m = where_ref[2], where_ref[1]
    shard, width = query_ref.shape
    own_cols = width // ranks
    if lanes_all != own_cols:
        small_ref[...] = jnp.zeros_like(small_ref)
    for n, ref in enumerate((query_ref, key_ref, value_ref)):
        for low in range(0, own_cols, lanes):
            size = min(lanes, own_cols - low)
            at = (low // lanes * 3 + n) * lanes
            small_ref[0:shard, at:at + size] = pick(
                rank, [ref[:, r * own_cols + low:r * own_cols + low + size] for r in range(ranks)])
    small_ref[0:shard, 3 * lanes_all:] = pick(
        rank, [out_ref[:, r * own_cols:(r + 1) * own_cols] for r in range(ranks)])
    small_ref[shard:, :] = jnp.zeros_like(small_ref[shard:, :])
    small_ref[shard:, 0:shard] = gain_ref[...]
    span = tokens_ref.shape[2]
    for k, ref in enumerate(slab_refs):
        ref[0:span, :] = tokens_ref[m ^ k, 0]
        ref[span:, :] = jnp.zeros_like(ref[span:, :])
        row = seg_ref[pl.ds(m ^ k, 1), :].astype(F32)
        ref[span:, 0:span] = jnp.broadcast_to(row, (16, span)).astype(BF)


def pack_small(where, query, key, value, out, gains, tokens, segments, cot, ranks, lanes,
               lanes_all):
    shard, width = query.shape
    groups, _, span, _ = tokens.shape
    cols = 3 * lanes_all + width // ranks
    return pl.pallas_call(
        lambda *refs: pack_small_kernel(*refs, ranks=ranks, lanes=lanes, lanes_all=lanes_all),
        in_specs=[SMEM_SPEC] + [VMEM_SPEC] * 8,
        out_specs=[VMEM_SPEC] * (1 + 2 * groups),
        out_shape=[jax.ShapeDtypeStruct((shard + 16, cols), BF)]
        + [jax.ShapeDtypeStruct((span + 16, width), BF)] * groups
        + [jax.ShapeDtypeStruct((span, width), BF)] * groups,
        compiler_params=pltpu.CompilerParams(vmem_limit_bytes=24 << 20),
        cost_estimate=SMALL_COST,
        name="pack_small",
    )(where, query, key, value, out, gains, tokens, segments, cot)


def pack_kernel(where_ref, gate_ref, up_ref, down_ref, out_ref, gu, *, fsdp, ranks):
    rank = where_ref[2]
    shard, cols = gu.shape
    part = down_ref.shape[0] // ranks
    for n, ref in enumerate((gate_ref, up_ref)):
        for j in range(fsdp):
            low = (n * fsdp + j) * part
            gu[:, low:low + part] = pick(
                rank, [ref[:, (j * ranks + r) * part:(j * ranks + r + 1) * part]
                       for r in range(ranks)])
    chunks = cols // 256
    for c in range(chunks):
        out_ref[c * shard:(c + 1) * shard, :] = gu[:, c * 256:(c + 1) * 256]
    rows = pl.ds(pl.multiple_of(rank * part, 16), part)
    for c in range(down_ref.shape[1] // 256):
        at = chunks * shard + c * part
        out_ref[at:at + part, :] = down_ref[rows, c * 256:(c + 1) * 256]


def pack(where, gate, up, down, fsdp, ranks):
    shard, ff = gate.shape
    cols = 2 * ff // ranks
    rows = cols // 256 * shard + down.shape[1] // 256 * (down.shape[0] // ranks)
    return pl.pallas_call(
        lambda *refs: pack_kernel(*refs, fsdp=fsdp, ranks=ranks),
        in_specs=[SMEM_SPEC] + [VMEM_SPEC] * 3,
        out_specs=VMEM_SPEC,
        out_shape=jax.ShapeDtypeStruct((rows, 256), BF),
        scratch_shapes=[pltpu.VMEM((shard, cols), BF)],
        compiler_params=pltpu.CompilerParams(vmem_limit_bytes=24 << 20),
        cost_estimate=SMALL_COST,
        name="pack",
    )(where, gate, up, down)


def arrange_kernel(gu_ref, down_ref, out_ref):
    shard, part = gu_ref.shape[0], down_ref.shape[0]
    chunks = gu_ref.shape[1] // 256
    for c in range(chunks):
        out_ref[0, c * shard:(c + 1) * shard, :] = gu_ref[:, c * 256:(c + 1) * 256]
    for c in range(down_ref.shape[1] // 256):
        at = chunks * shard + c * part
        out_ref[0, at:at + part, :] = down_ref[:, c * 256:(c + 1) * 256]


def arrange(gu, down, fsdp):
    shard, part = gu.shape[0] // fsdp, down.shape[0] // fsdp
    rows = gu.shape[1] // 256 * shard + down.shape[1] // 256 * part
    return pl.pallas_call(
        arrange_kernel,
        grid=(fsdp,),
        in_specs=[pl.BlockSpec((shard, gu.shape[1]), lambda j: (j, 0)),
                  pl.BlockSpec((part, down.shape[1]), lambda j: (j, 0))],
        out_specs=pl.BlockSpec((1, rows, 256), lambda j: (j, 0, 0)),
        out_shape=jax.ShapeDtypeStruct((fsdp, rows, 256), BF),
        compiler_params=pltpu.CompilerParams(vmem_limit_bytes=24 << 20),
        cost_estimate=SMALL_COST,
        name="arrange",
    )(gu, down)


def finish_kernel(where_ref, keep_ref, part_ref, got_ref, *out_refs, ranks):
    groups, span, _ = keep_ref.shape
    for k, ref in enumerate(out_refs):
        group = where_ref[1] ^ k
        row = (group * ranks + where_ref[2]) * span
        own = part_ref[pl.ds(pl.multiple_of(row, span), span), :].astype(F32)
        ref[...] = (keep_ref[group] + own + got_ref[group].astype(F32)).astype(BF)


def finish(where, keep, part, got, ranks):
    groups, span, width = keep.shape
    return pl.pallas_call(
        lambda *refs: finish_kernel(*refs, ranks=ranks),
        in_specs=[SMEM_SPEC] + [VMEM_SPEC] * 3,
        out_specs=[VMEM_SPEC] * groups,
        out_shape=[jax.ShapeDtypeStruct((span, width), BF)] * groups,
        compiler_params=pltpu.CompilerParams(vmem_limit_bytes=24 << 20),
        cost_estimate=SMALL_COST,
        name="finish",
    )(where, keep, part, got)


def stack_kernel(where_ref, *refs):
    out_ref = refs[-1]
    for k, ref in enumerate(refs[:-1]):
        out_ref[where_ref[1] ^ k, 0] = ref[...]


def stack(where, slabs):
    span, width = slabs[0].shape
    return pl.pallas_call(
        stack_kernel,
        in_specs=[SMEM_SPEC] + [VMEM_SPEC] * len(slabs),
        out_specs=VMEM_SPEC,
        out_shape=jax.ShapeDtypeStruct((len(slabs), 1, span, width), BF),
        compiler_params=pltpu.CompilerParams(vmem_limit_bytes=16 << 20),
        cost_estimate=SMALL_COST,
        name="stack",
    )(where, *slabs)


def attend_back_kernel(seg_ref, g_ref, w_out_ref, q_ref, k_ref, v_ref, att_ref, lse_ref,
                       cos_ref, sin_ref, d_ref, grad_ref, k_sum, v_sum,
                       *, block, window, scale, head_size):
    tokens = g_ref.shape[0]
    half = head_size // 2
    lanes = 2 * head_size
    lane = lax.broadcasted_iota(jnp.int32, (1, lanes), 1)
    first = lane < head_size
    starts = start_row(seg_ref)
    k_sum[...] = jnp.zeros_like(k_sum)
    v_sum[...] = jnp.zeros_like(v_sum)
    for low in range(0, tokens, block):
        rows = pl.ds(low, block)
        grad_ref[rows, :] = dot(g_ref[rows, :], w_out_ref[...], ((1,), (1,))).astype(BF)
    for low in range(0, tokens, block):
        begin = first_key(low, block, window)
        end = low + block
        count = end - begin
        q = q_ref[low:end, :] * jnp.asarray(scale, BF)
        grad = grad_ref[low:end, :]
        product = (grad.astype(F32) * att_ref[low:end, :].astype(F32)).T
        k = k_ref[begin:end, :]
        v = v_ref[begin:end, :]
        zero = jnp.zeros_like(k)
        k_two = jnp.concatenate([jnp.where(first, k, zero), jnp.where(first, zero, k)], axis=0)
        v_two = jnp.concatenate([jnp.where(first, v, zero), jnp.where(first, zero, v)], axis=0)
        scores = dot(k_two, q, ((1,), (1,)))
        prob_grad = dot(v_two, grad, ((1,), (1,)))
        key_index = lax.broadcasted_iota(jnp.int32, (count, block), 0) + begin
        query_index = lax.broadcasted_iota(jnp.int32, (count, block), 1) + low
        visible = (key_index.astype(F32) >= starts[:, low:end]) & (key_index <= query_index)
        weights_low, score_low = [], []
        for head in range(2):
            part = slice(head * count, (head + 1) * count)
            weights = jnp.where(
                visible, jnp.exp(scores[part] - lse_ref[0, head:head + 1, low:end]), 0.0)
            row_dots = jnp.sum(
                product[head * head_size:(head + 1) * head_size], axis=0, keepdims=True)
            weights_low.append(weights.astype(BF))
            score_low.append((weights * (prob_grad[part] - row_dots)).astype(BF))
        weights_low = jnp.concatenate(weights_low, axis=0)
        score_low = jnp.concatenate(score_low, axis=0)
        v_part = dot(weights_low, grad)
        k_part = dot(score_low, q)
        v_sum[begin:end, :] += jnp.where(first, v_part[:count], v_part[count:])
        k_sum[begin:end, :] += jnp.where(first, k_part[:count], k_part[count:])
        dq = dot(score_low, k_two, ((0,), (0,))) * scale
        d_ref[low:end, :lanes] = (
            dq * cos_ref[low:end, :] - turn(dq, half) * sin_ref[low:end, :]).astype(BF)
    for low in range(0, tokens, block):
        rows = pl.ds(low, block)
        dk = k_sum[rows, :]
        d_ref[rows, lanes:2 * lanes] = (
            dk * cos_ref[rows, :] - turn(dk, half) * sin_ref[rows, :]).astype(BF)
        d_ref[rows, 2 * lanes:] = v_sum[rows, :].astype(BF)

def attend_back(seg, g, w_out, q, k, v, att, lse, cosine, sine, window, head_size):
    tokens, width = g.shape
    lanes = 2 * head_size
    pairs = q.shape[1] // lanes
    kernel = lambda *refs: attend_back_kernel(
        *refs, block=256, window=window, scale=1.0 / math.sqrt(head_size), head_size=head_size)
    column = pl.BlockSpec((tokens, lanes), lambda p: (0, p))
    return pl.pallas_call(
        kernel,
        grid=(pairs,),
        in_specs=[
            VMEM_SPEC, VMEM_SPEC,
            pl.BlockSpec((lanes, width), lambda p: (p, 0)),
            column, column, column, column,
            pl.BlockSpec((1, 8, tokens), lambda p: (p, 0, 0)),
            VMEM_SPEC, VMEM_SPEC,
        ],
        out_specs=pl.BlockSpec((tokens, 3 * lanes), lambda p: (0, p)),
        out_shape=jax.ShapeDtypeStruct((tokens, 3 * lanes * pairs), BF),
        scratch_shapes=[
            pltpu.VMEM((tokens, lanes), BF),
            pltpu.VMEM((tokens, lanes), F32),
            pltpu.VMEM((tokens, lanes), F32),
        ],
        compiler_params=pltpu.CompilerParams(vmem_limit_bytes=48 << 20),
        cost_estimate=SMALL_COST,
        name="attend_back",
    )(seg, g, w_out, q, k, v, att, lse, cosine, sine)


def join_kernel(rank_ref, own_ref, other_ref, *out_refs, moves, plain):
    swapped = rank_ref[0] == 1
    own, other = own_ref[...], other_ref[...]
    halves = (jnp.where(swapped, other, own), jnp.where(swapped, own, other))
    for out, half, (rows, cols), (to_rows, to_cols) in moves:
        out_refs[out][to_rows, to_cols] = halves[half][rows, cols].astype(F32)
    for out, (rows, cols) in plain:
        out_refs[out][...] = own[rows, cols].astype(F32)


def join(rank, own, other, moves, plain, shapes):
    kernel = lambda *refs: join_kernel(*refs, moves=moves, plain=plain)
    return pl.pallas_call(
        kernel,
        in_specs=[
            pl.BlockSpec(memory_space=pltpu.SMEM),
            pl.BlockSpec(memory_space=pltpu.VMEM),
            pl.BlockSpec(memory_space=pltpu.VMEM),
        ],
        out_specs=[pl.BlockSpec(memory_space=pltpu.VMEM)] * len(shapes),
        out_shape=[jax.ShapeDtypeStruct(shape, F32) for shape in shapes],
        compiler_params=pltpu.CompilerParams(vmem_limit_bytes=32 << 20),
        name="join",
    )(rank.reshape(1), own, other)


def join_all_kernel(all_ref, *refs, moves):
    out_refs, whole_ref = refs[:-1], refs[-1]
    groups, ranks, rows, _ = all_ref.shape
    for h in range(ranks):
        for m in range(groups):
            whole_ref[h, m * rows:(m + 1) * rows, :] = all_ref[m, h]
    for out, half, (rows, cols), (to_rows, to_cols) in moves:
        out_refs[out][to_rows, to_cols] = whole_ref[half, rows, cols].astype(F32)


def join_all(parts, moves, shapes):
    groups, ranks, rows, cols = parts.shape
    return pl.pallas_call(
        lambda *refs: join_all_kernel(*refs, moves=moves),
        in_specs=[VMEM_SPEC],
        out_specs=[VMEM_SPEC] * len(shapes),
        out_shape=[jax.ShapeDtypeStruct(shape, F32) for shape in shapes],
        scratch_shapes=[pltpu.VMEM((ranks, groups * rows, cols), BF)],
        compiler_params=pltpu.CompilerParams(vmem_limit_bytes=32 << 20),
        cost_estimate=SMALL_COST,
        name="join_all",
    )(parts)


def make_body(groups, ranks, fsdp, square):
    F = ("y", "x") if square else ("f",)
    swap = [(0, 1), (1, 0)]
    pairs = square and ranks == 2 and groups == 4

    def hop(value, k):
        return lax.ppermute(value, "m", [(i, i ^ k) for i in range(groups)])

    def after(value, *earlier):
        return lax.optimization_barrier((value,) + earlier)[0]

    def between(slabs, value):
        hops, value = lax.optimization_barrier((slabs[1:], value))
        return slabs[:1] + hops, value

    def spread(slabs):
        return [hop(slab, k) if k else slab for k, slab in enumerate(slabs)]

    def both_ranks(where, slabs, span):
        if ranks == 2:
            return slabs + [lax.ppermute(slab, "r", swap) for slab in slabs]
        rows = lax.all_gather(stack(where, slabs)[:, 0], "r", axis=1)
        return [rows[:, :, :span].reshape(-1, rows.shape[-1]), rows]

    def share(part):
        if ranks == 2:
            other = lax.ppermute(part, "r", swap)
            mine_first = lax.axis_index("r") == 0
            return jnp.stack(
                [jnp.where(mine_first, part, other), jnp.where(mine_first, other, part)], axis=1)
        return lax.all_gather(part, "r", axis=1)

    def exchange(part):
        if ranks == 2:
            return part, lax.ppermute(part, "r", swap)
        return lax.psum(part, "r"), jnp.zeros_like(part)

    def gather_rows(part, wait=()):
        if not square:
            whole = lax.all_gather(part, F, axis=0, tiled=True)
            return [whole], [(None, 0, 0)], (), ()
        count = part.shape[0]
        rows = (count // 2) // 16 * 16
        send = after(part, *wait) if wait else part
        from_x = lax.ppermute(send, "x", swap)
        from_y = lax.ppermute(send, "y", swap)
        far_a = lax.ppermute(from_y[:rows], "x", swap)
        far_b = lax.ppermute(from_x[rows:], "y", swap)
        pieces = [(0, 0, count), (1, 0, count), (2, 0, count), (3, 0, rows), (3, rows, count - rows)]
        return [part, from_x, from_y, far_a, far_b], pieces, (from_x, from_y), (far_a, far_b)

    def add(*parts):
        return sum(part.astype(F32) for part in parts).astype(BF)

    def take(grad, k):
        return lax.dynamic_index_in_dim(grad, lax.axis_index(F) ^ k, 0, keepdims=False)

    def half_rows(grad):
        return (grad.shape[1] // 2) // 16 * 16

    def round_one(grad):
        far, rows = take(grad, 3), half_rows(grad)
        return lax.ppermute(far[:rows], "x", swap), lax.ppermute(far[rows:], "y", swap)

    def second_terms(grad, low, high):
        to_x, to_y, rows = take(grad, 1), take(grad, 2), half_rows(grad)
        to_x = jnp.concatenate([to_x[:rows], add(to_x[rows:], high)], axis=0)
        to_y = jnp.concatenate([add(to_y[:rows], low), to_y[rows:]], axis=0)
        return to_x, to_y

    def round_two(to_x, to_y):
        return lax.ppermute(to_x, "x", swap), lax.ppermute(to_y, "y", swap)

    def halve(owned, bit, axis):
        half = owned.shape[axis] // 2
        side = (lax.axis_index("m") // bit) % 2
        return (lax.dynamic_slice_in_dim(owned, (1 - side) * half, half, axis),
                lax.dynamic_slice_in_dim(owned, side * half, half, axis))

    def join_halves(owned, other, bit, axis):
        first = (lax.axis_index("m") // bit) % 2 == 0
        return jnp.concatenate(
            [jnp.where(first, owned, other), jnp.where(first, other, owned)], axis=axis)

    def reduce(grad):
        return lax.psum(lax.psum_scatter(grad, F, scatter_dimension=0, tiled=False), "m")

    def body(tokens, segments, w_query, w_key, w_value, w_out, w_gate, w_up, w_down,
             gain_attn, gain_ffn, cotangent):
        micro, _, span, width = tokens.shape
        head_size = width // HEADS
        seq_tokens = span * groups * ranks
        window = seq_tokens // 2
        rank = lax.axis_index("r")
        own_cols = width // ranks
        shard = w_query.shape[0]
        down_rows = w_down.shape[0]
        part_rows = down_rows // ranks
        ff = w_gate.shape[1]
        half_ff = ff // ranks

        lanes = 2 * head_size
        lanes_all = -(-own_cols // lanes) * lanes
        spare = lanes_all - own_cols
        block = span * ranks
        f_index = lax.axis_index(F)
        where = jnp.stack([f_index, lax.axis_index("m"), rank])
        small_cols = 3 * lanes_all + own_cols
        gains_in = jnp.pad(jnp.stack([gain_attn, gain_ffn]), ((0, 14), (0, 0)))
        stack_own = pack(where, w_gate, w_up, w_down, fsdp, ranks)
        stack_all = lax.all_gather(stack_own, F, axis=0)
        cosine, sine = rotary_tables(seq_tokens, head_size, 2)
        small, *slabs = pack_small(
            after(where, stack_own), w_query, w_key, w_value, w_out, gains_in, tokens,
            segments[:, 0], cotangent, ranks, lanes, lanes_all)
        token_slabs, cot_slabs = slabs[:groups], slabs[groups:]
        token_slabs = spread(token_slabs)
        small_refs, small_pieces, near, far = gather_rows(small)
        if square:
            cot_slabs = cot_slabs[:1] + [after(slab, *token_slabs) for slab in cot_slabs[1:]]
        cot_slabs = spread(cot_slabs)
        if square:
            token_slabs = token_slabs[:1] + [
                after(slab, cosine, sine) for slab in token_slabs[1:]]
        token_refs = both_ranks(where, token_slabs, span)
        if ranks != 2:
            seg = token_refs[1][:, :, span, :span].reshape(1, seq_tokens).astype(F32)
            token_refs = [token_refs[0], seg]
        if square:
            own, from_x, from_y, far_a, far_b = small_refs
            at = far_a.shape[0]
            ends = [own, from_x, from_y, jnp.concatenate([far_a, far_b[:shard - at]], axis=0)]
            tails = [v[shard:shard + 2, :shard] for v in (own, from_x, from_y)]
            tails.append(far_b[shard - at:shard - at + 2, :shard])
            gains = jnp.zeros((fsdp, 2, shard), BF)
            out_cols = jnp.zeros((width, own_cols), BF)
            for offset in range(4):
                to = (f_index ^ offset) * shard
                gains = lax.dynamic_update_index_in_dim(gains, tails[offset], f_index ^ offset, 0)
                out_cols = lax.dynamic_update_slice_in_dim(
                    out_cols, ends[offset][:shard, 3 * lanes_all:], to, 0)
            gains = gains.transpose(1, 0, 2).reshape(2, width)
            small_pieces = [(o, f, min(n, shard - f)) for o, f, n in small_pieces]
            qkv_refs = small_refs
        else:
            whole = small_refs[0].reshape(fsdp, shard + 16, small_cols)
            gains = whole[:, shard:shard + 2, :shard].transpose(1, 0, 2).reshape(2, width)
            out_cols = whole[:, :shard, 3 * lanes_all:].reshape(width, own_cols)
            qkv_refs = [whole[:, :shard, :3 * lanes_all].reshape(width, 3 * lanes_all)]
        gains = gains.astype(F32)
        if ranks == 2:
            give = lax.dynamic_slice_in_dim(out_cols, (1 - rank) * own_cols, own_cols, 0)
            keep = lax.dynamic_slice_in_dim(out_cols, rank * own_cols, own_cols, 0)
            got = lax.ppermute(give, "r", swap)
            w_out_own = jnp.where(rank == 0, jnp.concatenate([keep, got], 1),
                                  jnp.concatenate([got, keep], 1))
        else:
            pieces = lax.all_to_all(out_cols, "r", 0, 0, tiled=True)
            pieces = pieces.reshape(ranks, own_cols, own_cols)
            w_out_own = jnp.concatenate([pieces[i] for i in range(ranks)], axis=1)
        w_out_even = jnp.pad(w_out_own, ((0, spare), (0, 0)))

        q, k, v, att, lse, w_qkv, x, seg = attend(
            where, cosine, sine, token_refs, ranks, qkv_refs, small_pieces, shard, lanes_all,
            window, head_size, width)
        if square:
            cot_slabs, att = between(cot_slabs, att)
        own, got = exchange(dot(att, w_out_even).astype(BF))
        cot_refs = both_ranks(where, cot_slabs, span)
        if ranks != 2:
            cot_refs = cot_refs[:1]
        total, middle_low, hidden_low, gate_back, silu, part = forward(
            x, own, got, gains[0:1], stack_all, shard, part_rows, half_ff, block)
        own, got = exchange(part)

        *out_slabs, ffn_grad, ffn_grad_low, gu_grad_low, part, gain_ffn_grad = backward(
            where, total, own, got, gate_back, silu, gains, cot_refs, stack_all, shard, part_rows,
            block, groups, ranks)
        own, got = exchange(part)
        down_w_grad = dot(hidden_low, ffn_grad_low, ((0,), (0,))).astype(BF)
        gu_w_grad = dot(middle_low, gu_grad_low, ((0,), (0,))).astype(BF)
        stack_grad = arrange(gu_w_grad, down_w_grad, fsdp)
        stack_owned = lax.psum_scatter(stack_grad, F, scatter_dimension=0, tiled=False)
        own = after(own, stack_grad)
        branch_grad_low, branch_keep, gain_attn_grad = norm_back(
            where[2:], total, ffn_grad, own, got, gains[0:1], block, span)
        out_w_grad = dot(att, branch_grad_low, ((0,), (0,)))[:own_cols].astype(BF)
        if ranks == 2:
            give = lax.dynamic_slice_in_dim(out_w_grad, (1 - rank) * own_cols, own_cols, 1)
            keep = lax.dynamic_slice_in_dim(out_w_grad, rank * own_cols, own_cols, 1)
            got = lax.ppermute(give, "r", swap)
            out_cols_grad = jnp.where(rank == 0, jnp.concatenate([keep, got], 0),
                                      jnp.concatenate([got, keep], 0))
        else:
            rows = out_w_grad.reshape(own_cols, ranks, own_cols).transpose(1, 0, 2)
            out_cols_grad = lax.all_to_all(rows, "r", 0, 0, tiled=True).reshape(width, own_cols)
        gain_grads = jnp.concatenate([gain_attn_grad, gain_ffn_grad], axis=0).astype(BF)
        gain_grads = gain_grads.reshape(2, fsdp, shard).transpose(1, 0, 2)
        gain_grads = jnp.pad(gain_grads, ((0, 0), (0, 14), (0, small_cols - shard)))
        branch_grad_low = after(branch_grad_low, out_cols_grad, gain_grads)
        d_qkv = attend_back(
            seg, branch_grad_low, w_out_even, q, k, v, att, lse, cosine, sine, window, head_size)
        if square:
            out_slabs, d_qkv = between(spread(out_slabs), d_qkv)
        else:
            out_slabs = spread(out_slabs)
        output = stack(where, out_slabs)
        qkv_w_grad = dot(x, d_qkv, ((0,), (0,))).astype(BF)
        small_grad = jnp.concatenate([qkv_w_grad, out_cols_grad], axis=1)
        small_grad = jnp.concatenate(
            [small_grad.reshape(fsdp, shard, small_cols), gain_grads], axis=1)
        if pairs:
            small_one = round_one(small_grad)
            d_qkv = after(d_qkv, small_grad)
        part = dot(d_qkv, w_qkv, ((1,), (1,))).astype(BF)
        if ranks == 2:
            rows = part.reshape(groups, ranks, span, width)
            give = lax.dynamic_index_in_dim(rows, 1 - rank, 1, keepdims=False)
            got = lax.ppermute(give, "r", swap)
        else:
            part = lax.psum(part, "r")
            got = jnp.zeros_like(branch_keep, BF)
        grad_slabs = list(finish(where, branch_keep, part, got, ranks))
        if pairs:
            grad_slabs, small_one = between(spread(grad_slabs), small_one)
        else:
            grad_slabs = spread(grad_slabs)
        if pairs:
            terms = second_terms(small_grad, *small_one)
            small_two = round_two(*terms)
            stack_owned = after(stack_owned, *terms)
            quarter = lax.psum_scatter(stack_owned, "m", scatter_dimension=0, tiled=True)
            give, keep = halve(add(take(small_grad, 0), *small_two), 1, 1)
            got, quarter = lax.optimization_barrier((hop(give, 1), quarter))
            stack_parts = lax.all_gather(quarter, ("m", "r"), axis=0)
            stack_parts = stack_parts.reshape((groups, ranks) + quarter.shape)
            give, keep = halve(add(keep, got), 2, 1)
            owned = add(keep, hop(give, 2))
            owned = join_halves(owned, hop(owned, 2), 2, 1)
            small_sum = join_halves(owned, hop(owned, 1), 1, 1)
        else:
            stack_sum = lax.psum(stack_owned, "m")
            small_sum = reduce(small_grad)
        input_grad = stack(where, grad_slabs)
        if pairs:
            everything = slice(None)
            chunks = 2 * half_ff // 256
            stack_moves = [
                (n, h, (slice((n * fsdp + j) * shard, (n * fsdp + j + 1) * shard), everything),
                 (everything, slice(j * down_rows + h * part_rows, j * down_rows + (h + 1) * part_rows)))
                for n in range(2) for h in range(2) for j in range(fsdp)]
            stack_moves += [
                (2, h, (slice(chunks * shard + c * part_rows, chunks * shard + (c + 1) * part_rows),
                        everything),
                 (slice(h * part_rows, (h + 1) * part_rows), slice(c * 256, (c + 1) * 256)))
                for h in range(2) for c in range(width // 256)]
            small_moves = [
                (n, h, (slice(0, shard), slice((3 * p + n) * lanes, (3 * p + n + 1) * lanes)),
                 (everything, slice(h * own_cols + p * lanes, h * own_cols + (p + 1) * lanes)))
                for n in range(3) for h in range(2) for p in range(own_cols // lanes)]
            small_moves += [
                (3, h, (slice(0, shard), slice(3 * lanes_all, small_cols)),
                 (everything, slice(h * own_cols, (h + 1) * own_cols))) for h in range(2)]
            small_plain = [
                (4 + n, (slice(shard + n, shard + n + 1), slice(0, shard))) for n in range(2)]
            gate_w, up_w, down_grad = join_all(
                stack_parts, stack_moves, [(shard, ff)] * 2 + [(down_rows, width)])
            query_w, key_w, value_w, out_w, gain_a, gain_f = join(
                rank, small_sum, lax.ppermute(small_sum, "r", swap), small_moves, small_plain,
                [(shard, width)] * 4 + [(1, shard)] * 2)
        else:
            at = 2 * half_ff // 256 * shard
            down_sum = jnp.moveaxis(stack_sum[at:].reshape(-1, part_rows, 256), 0, 1)
            down_grad = jnp.moveaxis(share(down_sum.reshape(part_rows, width)), 1, 0)
            down_grad = down_grad.reshape(down_rows, width).astype(F32)
            gu_sum = jnp.moveaxis(stack_sum[:at].reshape(-1, shard, 256), 0, 1)
            gu_both = share(gu_sum.reshape(shard, 2 * fsdp, part_rows))
            gu_both = gu_both.reshape(shard, ranks, 2, fsdp, part_rows).astype(F32)
            gate_w, up_w = (
                gu_both[:, :, n].transpose(0, 2, 1, 3).reshape(shard, ff) for n in range(2))
            small_both = share(small_sum)[:shard].astype(F32)
            three = small_both[:, :, :3 * lanes_all].reshape(shard, ranks, -1, 3, lanes)
            query_w, key_w, value_w = (
                three[:, :, :, n].reshape(shard, ranks, lanes_all)[:, :, :own_cols].reshape(shard, width)
                for n in range(3))
            out_w = small_both[:, :, 3 * lanes_all:].reshape(shard, width)
            gain_a, gain_f = small_sum[shard, :shard].astype(F32), small_sum[shard + 1, :shard].astype(F32)
        return (output, input_grad, query_w, key_w, value_w, out_w,
                gate_w, up_w, down_grad, gain_a.reshape(shard), gain_f.reshape(shard))

    return body


def solution(mesh):
    def run(*args):
        groups = args[0].shape[0]
        seq, fsdp = mesh.shape["seq"], mesh.shape["fsdp"]
        ranks = seq // groups
        square = fsdp == 4
        names = ("m", "r") + (("y", "x") if square else ("f",))
        sizes = (groups, ranks) + ((2, 2) if square else (fsdp,))
        order = [mesh.axis_names.index(name) for name in ("seq", "fsdp")]
        inner = Mesh(mesh.devices.transpose(order).reshape(sizes), names)
        f = ("y", "x") if square else "f"
        s = ("m", "r")
        rows = P(f, None)
        data = P(None, f, s, None)
        in_specs = (data, P(None, f, s)) + (rows,) * 7 + (P(f), P(f), data)
        out_specs = (data, data) + (rows,) * 7 + (P(f), P(f))
        body = make_body(groups, ranks, fsdp, square)
        return jax.shard_map(
            body, mesh=inner, in_specs=in_specs, out_specs=out_specs, check_vma=False)(*args)

    return run
```

```python
import math

import jax
import jax.numpy as jnp
from jax import lax
from jax.experimental import pallas as pl
from jax.experimental.pallas import tpu as pltpu
from jax.sharding import Mesh, PartitionSpec as P

HEADS = 12
DOCS = 4
EPS = 1e-06
NEGATIVE = -1e30
BF = jnp.bfloat16
F32 = jnp.float32


def dot(left, right, dims=((1,), (0,))):
    return lax.dot_general(left, right, (dims, ((), ())), preferred_element_type=F32)


def rotary_tables(seq_tokens, head_size, copies):
    half = head_size // 2
    frequency = 10000.0 ** (-jnp.arange(half, dtype=F32) / half)
    angle = jnp.arange(seq_tokens, dtype=jnp.int32).astype(F32)[:, None] * frequency[None, :]
    cosine, sine = jnp.cos(angle), jnp.sin(angle)
    return (
        jnp.concatenate([cosine, cosine] * copies, axis=1),
        jnp.concatenate([-sine, sine] * copies, axis=1),
    )


def turn(rows, half):
    lanes = rows.shape[1]
    lane = lax.broadcasted_iota(jnp.int32, (1, lanes), 1)
    low = (lane // half) % 2 == 0
    return jnp.where(low, pltpu.roll(rows, lanes - half, 1), pltpu.roll(rows, half, 1))


def first_key(query_first, block, window):
    return max(0, (query_first - window + 1) // block * block)


def start_row(seg_ref):
    seg = seg_ref[...]
    starts = jnp.zeros_like(seg)
    for doc in range(1, DOCS):
        before = jnp.sum(jnp.where(seg < doc, 1.0, 0.0), axis=1, keepdims=True)
        starts = jnp.maximum(starts, jnp.where(seg >= doc, before, 0.0))
    return starts


def place(target, refs, pieces, me, shard):
    for ref, (offset, first, rows) in zip(refs, pieces):
        if offset is None:
            target[...] = ref[...]
        else:
            start = pl.multiple_of((me ^ offset) * shard + first, 16)
            target[pl.ds(start, rows), :] = ref[0:rows, 0:target.shape[1]]


def place_tokens(target, refs, where_ref, ranks):
    if len(refs) == 1:
        target[...] = refs[0][...]
        return
    groups = len(refs) // ranks
    span = target.shape[0] // (groups * ranks)
    for n, ref in enumerate(refs):
        rank = where_ref[2] if n < groups else 1 - where_ref[2]
        chunk = (where_ref[1] ^ (n % groups)) * ranks + rank
        target[pl.ds(pl.multiple_of(chunk * span, span), span), :] = ref[0:span, :]


def place_segments(target, refs, where_ref, ranks):
    groups = len(refs) // ranks
    span = target.shape[1] // (groups * ranks)
    for n, ref in enumerate(refs):
        rank = where_ref[2] if n < groups else 1 - where_ref[2]
        chunk = (where_ref[1] ^ (n % groups)) * ranks + rank
        row = ref[span:span + 16, 0:span].astype(F32)[0:1, :]
        target[:, pl.ds(pl.multiple_of(chunk * span, span), span)] = row


def stack_copies(gu, down, stack_ref, sems, shard, part_rows):
    members, chunks, groups = stack_ref.shape[0], gu.shape[1] // 256, []
    for c in range(chunks):
        groups.append([
            pltpu.make_async_copy(
                stack_ref.at[j, c * shard:(c + 1) * shard, :],
                gu.at[j * shard:(j + 1) * shard, c * 256:(c + 1) * 256],
                sems.at[c, j]) for j in range(members)])
    for c in range(down.shape[1] // 256):
        at = chunks * shard + c * part_rows
        groups.append([
            pltpu.make_async_copy(
                stack_ref.at[j, at:at + part_rows, :],
                down.at[j * part_rows:(j + 1) * part_rows, c * 256:(c + 1) * 256],
                sems.at[chunks + c, j]) for j in range(members)])
    return groups


def place_tokens(target, refs, where_ref, ranks):
    if len(refs) == 1:
        target[...] = refs[0][...]
        return
    groups = len(refs) // ranks
    span = target.shape[0] // (groups * ranks)
    for n, ref in enumerate(refs):
        rank = where_ref[2] if n < groups else 1 - where_ref[2]
        chunk = (where_ref[1] ^ (n % groups)) * ranks + rank
        target[pl.ds(pl.multiple_of(chunk * span, span), span), :] = ref[0:span, :]


def place_segments(target, refs, where_ref, ranks):
    groups = len(refs) // ranks
    span = target.shape[1] // (groups * ranks)
    for n, ref in enumerate(refs):
        rank = where_ref[2] if n < groups else 1 - where_ref[2]
        chunk = (where_ref[1] ^ (n % groups)) * ranks + rank
        row = ref[span:span + 16, 0:span].astype(F32)[0:1, :]
        target[:, pl.ds(pl.multiple_of(chunk * span, span), span)] = row


def place_stack(gu, down, stack_ref, shard, part_rows):
    chunks = gu.shape[1] // 256
    for j in range(stack_ref.shape[0]):
        for c in range(chunks):
            gu[j * shard:(j + 1) * shard, c * 256:(c + 1) * 256] = (
                stack_ref[j, c * shard:(c + 1) * shard, :])
        for c in range(down.shape[1] // 256):
            at = chunks * shard + c * part_rows
            down[j * part_rows:(j + 1) * part_rows, c * 256:(c + 1) * 256] = (
                stack_ref[j, at:at + part_rows, :])


def attend_kernel(where_ref, cos_ref, sin_ref, *refs, pieces, token_count, ranks, shard, block,
                  window, scale, head_size):
    inputs, refs = refs[:-9], refs[-9:]
    q_ref, k_ref, v_ref, att_ref, lse_ref, w_ref, x_ref, seg_ref, col_ref = refs
    token_refs, w_refs = inputs[:token_count], inputs[token_count:]
    tokens = x_ref.shape[0]
    lanes = 2 * head_size
    lane = lax.broadcasted_iota(jnp.int32, (1, lanes), 1)
    first = lane < head_size
    pair = pl.program_id(0)

    @pl.when(pair == 0)
    def _():
        place(w_ref, w_refs, pieces, where_ref[0], shard)
        place_tokens(x_ref, token_refs[:1] if token_count == 2 else token_refs, where_ref, ranks)
        if token_count == 2:
            seg_ref[...] = token_refs[1][...]
        else:
            place_segments(seg_ref, token_refs, where_ref, ranks)
        starts = start_row(seg_ref)
        col_ref[...] = jnp.broadcast_to(starts, (128, tokens)).T

    w = w_ref[:, pl.ds(pl.multiple_of(pair * 3 * lanes, lanes), 3 * lanes)]
    for low in range(0, tokens, block):
        rows = pl.ds(low, block)
        lin = dot(x_ref[rows, :], w)
        cosine, sine = cos_ref[rows, :], sin_ref[rows, :]
        half = head_size // 2
        q_lin, k_lin = lin[:, :lanes], lin[:, lanes:2 * lanes]
        q_ref[rows, :] = (q_lin * cosine + turn(q_lin, half) * sine).astype(BF)
        k_ref[rows, :] = (k_lin * cosine + turn(k_lin, half) * sine).astype(BF)
        v_ref[rows, :] = lin[:, 2 * lanes:].astype(BF)
    for low in range(0, tokens, block):
        begin = first_key(low, block, window)
        end = low + block
        q = q_ref[low:end, :] * jnp.asarray(scale, BF)
        zero = jnp.zeros_like(q)
        stacked = jnp.concatenate([jnp.where(first, q, zero), jnp.where(first, zero, q)], axis=0)
        scores = dot(stacked, k_ref[begin:end, :], ((1,), (1,)))
        key_index = lax.broadcasted_iota(jnp.int32, (block, end - begin), 1) + begin
        query_index = lax.broadcasted_iota(jnp.int32, (block, end - begin), 0) + low
        visible = (key_index.astype(F32) >= col_ref[low:end, 0:1]) & (key_index <= query_index)
        parts = []
        for head in range(2):
            own = jnp.where(visible, scores[head * block:(head + 1) * block], NEGATIVE)
            top = jnp.max(own, axis=1, keepdims=True)
            weights = jnp.exp(own - top)
            total = jnp.sum(weights, axis=1, keepdims=True)
            out = dot(weights.astype(BF), v_ref[begin:end, :]) / total
            parts.append(out)
            lse = jnp.broadcast_to(top + jnp.log(total), (block, 128))
            lse_ref[0, head:head + 1, low:end] = lse.T[0:1, :]
        att_ref[low:end, :] = jnp.where(first, parts[0], parts[1]).astype(BF)


def hbm(*arrays):
    return [pltpu.with_memory_space_constraint(a, pltpu.HBM) for a in arrays]


def whole_specs(*arrays):
    return [pl.BlockSpec(a.shape, lambda *_, n=a.ndim: (0,) * n, pipeline_mode=pl.Buffered(1))
            for a in arrays]


SMALL_COST = pl.CostEstimate(flops=1, bytes_accessed=1, transcendentals=0)
VMEM_SPEC = pl.BlockSpec(memory_space=pltpu.VMEM)
SMEM_SPEC = pl.BlockSpec(memory_space=pltpu.SMEM)


def attend(where, cosine, sine, token_refs, ranks, weights, pieces, shard, lanes_all, window,
           head_size, width):
    tokens = cosine.shape[0]
    lanes = 2 * head_size
    pairs = lanes_all // lanes
    kernel = lambda *refs: attend_kernel(
        *refs, pieces=pieces, token_count=len(token_refs), ranks=ranks, shard=shard, block=256,
        window=window, scale=1.0 / math.sqrt(head_size), head_size=head_size)
    column = pl.BlockSpec((tokens, lanes), lambda p: (0, p))
    whole = lambda *shape: pl.BlockSpec(shape, lambda p: (0, 0))
    inputs = hbm(cosine, sine, *token_refs, *weights)
    return pl.pallas_call(
        kernel,
        grid=(pairs,),
        in_specs=[SMEM_SPEC] + whole_specs(*inputs),
        out_specs=[column, column, column, column,
                   pl.BlockSpec((1, 8, tokens), lambda p: (p, 0, 0)),
                   whole(width, 3 * lanes_all), whole(tokens, width), whole(1, tokens)],
        out_shape=[pltpu.HBM((tokens, lanes_all), BF)] * 4
        + [pltpu.HBM((pairs, 8, tokens), F32), pltpu.HBM((width, 3 * lanes_all), BF),
           pltpu.HBM((tokens, width), BF), pltpu.HBM((1, tokens), F32)],
        scratch_shapes=[pltpu.VMEM((tokens, 128), F32)],
        compiler_params=pltpu.CompilerParams(vmem_limit_bytes=28 << 20),
        cost_estimate=SMALL_COST,
        name="attend",
    )(where, *inputs)


def unit_of(rows):
    factor = lax.rsqrt(jnp.mean(rows * rows, axis=1, keepdims=True) + EPS)
    return rows * factor, factor


def forward_kernel(x_ref, own_ref, got_ref, gain_ref, stack_ref, sum_ref, low_ref, hidden_ref,
                   gate_ref, silu_ref, part_ref, gu, down, sems, *, shard, part_rows):
    step = pl.program_id(0)
    ff = down.shape[0]
    chunks = ff // 256
    copies = stack_copies(gu, down, stack_ref, sems, shard, part_rows)
    order = [n * chunks + c for c in range(chunks) for n in range(2)]
    order += list(range(2 * chunks, len(copies)))

    def wait_for(numbers):
        @pl.when(step == 0)
        def _():
            for number in numbers:
                for copy in copies[number]:
                    copy.wait()

    @pl.when(step == 0)
    def _():
        for number in order:
            for copy in copies[number]:
                copy.start()

    total = x_ref[...].astype(F32) + own_ref[...].astype(F32) + got_ref[...].astype(F32)
    sum_ref[...] = total
    middle_low = (unit_of(total)[0] * gain_ref[...]).astype(BF)
    low_ref[...] = middle_low
    for c in range(chunks):
        wait_for([c, chunks + c])
        cols = slice(c * 256, (c + 1) * 256)
        gate = dot(middle_low, gu[:, cols])
        up = dot(middle_low, gu[:, ff + c * 256:ff + (c + 1) * 256])
        sigmoid = jax.nn.sigmoid(gate)
        silu = gate * sigmoid
        hidden_ref[:, cols] = (silu * up).astype(BF)
        gate_ref[:, cols] = (up * sigmoid * (1.0 + gate * (1.0 - sigmoid))).astype(BF)
        silu_ref[:, cols] = silu.astype(BF)
    wait_for(range(2 * chunks, len(copies)))
    part_ref[...] = dot(hidden_ref[...], down[...]).astype(BF)


HBM_SPEC = pl.BlockSpec(memory_space=pltpu.HBM)


def forward(x, own, got, gain, stack, shard, part_rows, ff, block):
    tokens, width = x.shape
    row = lambda cols: pl.BlockSpec((block, cols), lambda i: (i, 0))
    x, stack = hbm(x, stack)
    return pl.pallas_call(
        lambda *refs: forward_kernel(*refs, shard=shard, part_rows=part_rows),
        grid=(tokens // block,),
        in_specs=[row(width), row(width), row(width)] + whole_specs(gain) + [HBM_SPEC],
        out_specs=[row(width), row(width), row(ff), row(ff), row(ff), row(width)],
        out_shape=[pltpu.HBM((tokens, width), F32), pltpu.HBM((tokens, width), BF)]
        + [pltpu.HBM((tokens, ff), BF)] * 3 + [pltpu.HBM((tokens, width), BF)],
        scratch_shapes=[pltpu.VMEM((width, 2 * ff), BF), pltpu.VMEM((ff, width), BF),
                        pltpu.SemaphoreType.DMA(((2 * ff + width) // 256, stack.shape[0]))],
        compiler_params=pltpu.CompilerParams(vmem_limit_bytes=28 << 20),
        cost_estimate=SMALL_COST,
        name="ffn_forward",
    )(x, own, got, gain, stack)


def backward_kernel(where_ref, sum_ref, own_ref, got_ref, gate_ref, silu_ref, gains_ref, *refs,
                    cot_count, shard, part_rows, groups, ranks):
    cot_refs, stack_ref, refs = refs[:cot_count], refs[cot_count], refs[cot_count + 1:]
    out_refs, refs = refs[:groups], refs[groups:]
    grad_ref, low_ref, gu_grad_ref, part_ref, gain_ref, gu, down, cot_ref, rows_ref, sems = refs
    step = pl.program_id(0)
    copies = stack_copies(gu, down, stack_ref, sems, shard, part_rows)
    chunks = gu.shape[1] // 256

    def wait_for(numbers):
        @pl.when(step == 0)
        def _():
            for number in numbers:
                for copy in copies[number]:
                    copy.wait()

    @pl.when(step == 0)
    def _():
        for group in copies[chunks:] + copies[:chunks]:
            for copy in group:
                copy.start()
        place_tokens(cot_ref, cot_refs, where_ref, ranks)
        gain_ref[...] = jnp.zeros_like(gain_ref)

    gain_two = gains_ref[1:2, :]
    middle = unit_of(sum_ref[...])[0] * gains_ref[0:1, :]
    unit, factor = unit_of(middle + own_ref[...].astype(F32) + got_ref[...].astype(F32))
    block, span = rows_ref.shape[0], out_refs[0].shape[0]
    rows_ref[...] = unit * gain_two
    kept = rows_ref[pl.ds(pl.multiple_of(where_ref[2] * span, span), span), :].astype(BF)
    for k, out_ref in enumerate(out_refs):
        @pl.when(step == (where_ref[1] ^ k))
        def _(out_ref=out_ref):
            out_ref[...] = kept
    cot = cot_ref[pl.ds(pl.multiple_of(step * block, block), block), :].astype(F32)
    gain_ref[...] += jnp.sum(cot * unit, axis=0, keepdims=True)
    scaled = cot * gain_two
    grad = factor * (scaled - unit * jnp.mean(scaled * unit, axis=1, keepdims=True))
    grad_ref[...] = grad
    grad_low = grad.astype(BF)
    low_ref[...] = grad_low
    ff = down.shape[0]
    wait_for(range(chunks, len(copies)))
    for c in range(0, ff, 256):
        hidden_grad = dot(grad_low, down[c:c + 256, :], ((1,), (1,)))
        gu_grad_ref[:, c:c + 256] = (hidden_grad * gate_ref[:, c:c + 256].astype(F32)).astype(BF)
        gu_grad_ref[:, ff + c:ff + c + 256] = (
            hidden_grad * silu_ref[:, c:c + 256].astype(F32)).astype(BF)
    wait_for(range(chunks))
    part_ref[...] = dot(gu_grad_ref[...], gu[...], ((1,), (1,))).astype(BF)


def backward(where, total, own, got, gate, silu, gains, cot, stack, shard, part_rows, block,
             groups, ranks):
    tokens, width = total.shape
    ff = gate.shape[1]
    kernel = lambda *refs: backward_kernel(
        *refs, cot_count=len(cot), shard=shard, part_rows=part_rows, groups=groups, ranks=ranks)
    row = lambda cols: pl.BlockSpec((block, cols), lambda i: (i, 0))
    slab = pl.BlockSpec((block // ranks, width), lambda i: (0, 0))
    total, gate, silu, stack = hbm(total, gate, silu, stack)
    return pl.pallas_call(
        kernel,
        grid=(tokens // block,),
        in_specs=[SMEM_SPEC] + [row(width)] * 3 + [row(ff)] * 2
        + whole_specs(gains, *cot) + [HBM_SPEC],
        out_specs=[slab] * groups + [row(width), row(width), row(2 * ff), row(width),
                                     pl.BlockSpec((1, width), lambda i: (0, 0))],
        out_shape=[pltpu.HBM((block // ranks, width), BF)] * groups
        + [pltpu.HBM((tokens, width), F32), pltpu.HBM((tokens, width), BF),
           pltpu.HBM((tokens, 2 * ff), BF), pltpu.HBM((tokens, width), BF),
           pltpu.HBM((1, width), F32)],
        scratch_shapes=[pltpu.VMEM((width, 2 * ff), BF), pltpu.VMEM((ff, width), BF),
                        pltpu.VMEM((tokens, width), BF), pltpu.VMEM((block, width), F32),
                        pltpu.SemaphoreType.DMA(((2 * ff + width) // 256, stack.shape[0]))],
        compiler_params=pltpu.CompilerParams(vmem_limit_bytes=32 << 20),
        cost_estimate=SMALL_COST,
        name="ffn_backward",
    )(where, total, own, got, gate, silu, gains, *cot, stack)


def norm_back_kernel(rank_ref, sum_ref, grad_ref, own_ref, got_ref, gain_ref,
                     low_ref, keep_ref, gain_grad_ref, rows_ref):
    @pl.when(pl.program_id(0) == 0)
    def _():
        gain_grad_ref[...] = jnp.zeros_like(gain_grad_ref)

    unit, factor = unit_of(sum_ref[...])
    grad = grad_ref[...] + own_ref[...].astype(F32) + got_ref[...].astype(F32)
    gain_grad_ref[...] += jnp.sum(grad * unit, axis=0, keepdims=True)
    scaled = grad * gain_ref[...]
    branch_grad = factor * (scaled - unit * jnp.mean(scaled * unit, axis=1, keepdims=True))
    low_ref[...] = branch_grad.astype(BF)
    rows_ref[...] = branch_grad
    span = keep_ref.shape[1]
    keep_ref[0] = rows_ref[pl.ds(pl.multiple_of(rank_ref[0] * span, span), span), :]


def norm_back(rank, total, grad, own, got, gain, block, span):
    tokens, width = total.shape
    row = pl.BlockSpec((block, width), lambda i: (i, 0))
    total, grad = hbm(total, grad)
    return pl.pallas_call(
        norm_back_kernel,
        grid=(tokens // block,),
        in_specs=[SMEM_SPEC, row, row, row, row] + whole_specs(gain),
        out_specs=[row, pl.BlockSpec((1, span, width), lambda i: (i, 0, 0)),
                   pl.BlockSpec((1, width), lambda i: (0, 0))],
        out_shape=[pltpu.HBM((tokens, width), BF),
                   pltpu.HBM((tokens // block, span, width), F32),
                   pltpu.HBM((1, width), F32)],
        scratch_shapes=[pltpu.VMEM((block, width), F32)],
        compiler_params=pltpu.CompilerParams(vmem_limit_bytes=16 << 20),
        cost_estimate=SMALL_COST,
        name="norm_back",
    )(rank, total, grad, own, got, gain)


def pick(rank, parts):
    value = parts[0]
    for r in range(1, len(parts)):
        value = jnp.where(rank == r, parts[r], value)
    return value


def pack_small_kernel(where_ref, query_ref, key_ref, value_ref, out_ref, gain_ref, tokens_ref,
                      seg_ref, cot_ref, small_ref, *slab_refs, ranks, lanes, lanes_all):
    slab_refs, cot_slabs = slab_refs[:len(slab_refs) // 2], slab_refs[len(slab_refs) // 2:]
    for k, ref in enumerate(cot_slabs):
        ref[...] = cot_ref[where_ref[1] ^ k, 0]
    rank, m = where_ref[2], where_ref[1]
    shard, width = query_ref.shape
    own_cols = width // ranks
    if lanes_all != own_cols:
        small_ref[...] = jnp.zeros_like(small_ref)
    for n, ref in enumerate((query_ref, key_ref, value_ref)):
        for low in range(0, own_cols, lanes):
            size = min(lanes, own_cols - low)
            at = (low // lanes * 3 + n) * lanes
            small_ref[0:shard, at:at + size] = pick(
                rank, [ref[:, r * own_cols + low:r * own_cols + low + size] for r in range(ranks)])
    small_ref[0:shard, 3 * lanes_all:] = pick(
        rank, [out_ref[:, r * own_cols:(r + 1) * own_cols] for r in range(ranks)])
    small_ref[shard:, :] = jnp.zeros_like(small_ref[shard:, :])
    small_ref[shard:, 0:shard] = gain_ref[...]
    span = tokens_ref.shape[2]
    for k, ref in enumerate(slab_refs):
        ref[0:span, :] = tokens_ref[m ^ k, 0]
        ref[span:, :] = jnp.zeros_like(ref[span:, :])
        row = seg_ref[pl.ds(m ^ k, 1), :].astype(F32)
        ref[span:, 0:span] = jnp.broadcast_to(row, (16, span)).astype(BF)


def pack_small(where, query, key, value, out, gains, tokens, segments, cot, ranks, lanes,
               lanes_all):
    shard, width = query.shape
    groups, _, span, _ = tokens.shape
    cols = 3 * lanes_all + width // ranks
    inputs = hbm(query, key, value, out, gains, tokens, segments, cot)
    shapes = [(shard + 16, cols)] + [(span + 16, width)] * groups + [(span, width)] * groups
    return pl.pallas_call(
        lambda *refs: pack_small_kernel(*refs, ranks=ranks, lanes=lanes, lanes_all=lanes_all),
        grid=(1,),
        in_specs=[SMEM_SPEC] + whole_specs(*inputs),
        out_specs=[pl.BlockSpec(shape, lambda i: (0, 0)) for shape in shapes],
        out_shape=[pltpu.HBM(shape, BF) for shape in shapes],
        compiler_params=pltpu.CompilerParams(vmem_limit_bytes=24 << 20),
        cost_estimate=SMALL_COST,
        name="pack_small",
    )(where, *inputs)


def pack_kernel(where_ref, gate_ref, up_ref, down_ref, out_ref, gu, *, fsdp, ranks):
    rank = where_ref[2]
    shard, cols = gu.shape
    part = down_ref.shape[0] // ranks
    for n, ref in enumerate((gate_ref, up_ref)):
        for j in range(fsdp):
            low = (n * fsdp + j) * part
            gu[:, low:low + part] = pick(
                rank, [ref[:, (j * ranks + r) * part:(j * ranks + r + 1) * part]
                       for r in range(ranks)])
    chunks = cols // 256
    for c in range(chunks):
        out_ref[c * shard:(c + 1) * shard, :] = gu[:, c * 256:(c + 1) * 256]
    rows = pl.ds(pl.multiple_of(rank * part, 16), part)
    for c in range(down_ref.shape[1] // 256):
        at = chunks * shard + c * part
        out_ref[at:at + part, :] = down_ref[rows, c * 256:(c + 1) * 256]


def pack(where, gate, up, down, fsdp, ranks):
    shard, ff = gate.shape
    cols = 2 * ff // ranks
    rows = cols // 256 * shard + down.shape[1] // 256 * (down.shape[0] // ranks)
    inputs = hbm(gate, up, down)
    return pl.pallas_call(
        lambda *refs: pack_kernel(*refs, fsdp=fsdp, ranks=ranks),
        grid=(1,),
        in_specs=[SMEM_SPEC] + whole_specs(*inputs),
        out_specs=pl.BlockSpec((rows, 256), lambda i: (0, 0)),
        out_shape=pltpu.HBM((rows, 256), BF),
        scratch_shapes=[pltpu.VMEM((shard, cols), BF)],
        compiler_params=pltpu.CompilerParams(vmem_limit_bytes=24 << 20),
        cost_estimate=SMALL_COST,
        name="pack",
    )(where, *inputs)


def arrange_kernel(gu_ref, down_ref, out_ref):
    shard, part = gu_ref.shape[0], down_ref.shape[0]
    chunks = gu_ref.shape[1] // 256
    for c in range(chunks):
        out_ref[0, c * shard:(c + 1) * shard, :] = gu_ref[:, c * 256:(c + 1) * 256]
    for c in range(down_ref.shape[1] // 256):
        at = chunks * shard + c * part
        out_ref[0, at:at + part, :] = down_ref[:, c * 256:(c + 1) * 256]


def arrange(gu, down, fsdp):
    shard, part = gu.shape[0] // fsdp, down.shape[0] // fsdp
    rows = gu.shape[1] // 256 * shard + down.shape[1] // 256 * part
    return pl.pallas_call(
        arrange_kernel,
        grid=(fsdp,),
        in_specs=[pl.BlockSpec((shard, gu.shape[1]), lambda j: (j, 0)),
                  pl.BlockSpec((part, down.shape[1]), lambda j: (j, 0))],
        out_specs=pl.BlockSpec((1, rows, 256), lambda j: (j, 0, 0)),
        out_shape=pltpu.HBM((fsdp, rows, 256), BF),
        compiler_params=pltpu.CompilerParams(vmem_limit_bytes=24 << 20),
        cost_estimate=SMALL_COST,
        name="arrange",
    )(gu, down)


def finish_kernel(where_ref, keep_ref, part_ref, got_ref, *out_refs, ranks):
    groups, span, _ = keep_ref.shape
    for k, ref in enumerate(out_refs):
        group = where_ref[1] ^ k
        row = (group * ranks + where_ref[2]) * span
        own = part_ref[pl.ds(pl.multiple_of(row, span), span), :].astype(F32)
        ref[...] = (keep_ref[group] + own + got_ref[group].astype(F32)).astype(BF)


def finish(where, keep, part, got, ranks):
    groups, span, width = keep.shape
    return pl.pallas_call(
        lambda *refs: finish_kernel(*refs, ranks=ranks),
        in_specs=[SMEM_SPEC] + [VMEM_SPEC] * 3,
        out_specs=[VMEM_SPEC] * groups,
        out_shape=[jax.ShapeDtypeStruct((span, width), BF)] * groups,
        compiler_params=pltpu.CompilerParams(vmem_limit_bytes=24 << 20),
        cost_estimate=SMALL_COST,
        name="finish",
    )(where, keep, part, got)


def stack_kernel(where_ref, *refs):
    out_ref = refs[-1]
    for k, ref in enumerate(refs[:-1]):
        out_ref[where_ref[1] ^ k, 0] = ref[...]


def stack(where, slabs):
    span, width = slabs[0].shape
    return pl.pallas_call(
        stack_kernel,
        in_specs=[SMEM_SPEC] + [VMEM_SPEC] * len(slabs),
        out_specs=VMEM_SPEC,
        out_shape=jax.ShapeDtypeStruct((len(slabs), 1, span, width), BF),
        compiler_params=pltpu.CompilerParams(vmem_limit_bytes=16 << 20),
        cost_estimate=SMALL_COST,
        name="stack",
    )(where, *slabs)


def attend_back_kernel(seg_ref, g_ref, w_out_ref, q_ref, k_ref, v_ref, att_ref, lse_ref,
                       cos_ref, sin_ref, d_ref, grad_ref, k_sum, v_sum,
                       *, block, window, scale, head_size):
    tokens = g_ref.shape[0]
    half = head_size // 2
    lanes = 2 * head_size
    lane = lax.broadcasted_iota(jnp.int32, (1, lanes), 1)
    first = lane < head_size
    starts = start_row(seg_ref)
    k_sum[...] = jnp.zeros_like(k_sum)
    v_sum[...] = jnp.zeros_like(v_sum)
    for low in range(0, tokens, block):
        rows = pl.ds(low, block)
        grad_ref[rows, :] = dot(g_ref[rows, :], w_out_ref[...], ((1,), (1,))).astype(BF)
    for low in range(0, tokens, block):
        begin = first_key(low, block, window)
        end = low + block
        count = end - begin
        q = q_ref[low:end, :] * jnp.asarray(scale, BF)
        grad = grad_ref[low:end, :]
        product = (grad.astype(F32) * att_ref[low:end, :].astype(F32)).T
        k = k_ref[begin:end, :]
        v = v_ref[begin:end, :]
        zero = jnp.zeros_like(k)
        k_two = jnp.concatenate([jnp.where(first, k, zero), jnp.where(first, zero, k)], axis=0)
        v_two = jnp.concatenate([jnp.where(first, v, zero), jnp.where(first, zero, v)], axis=0)
        scores = dot(k_two, q, ((1,), (1,)))
        prob_grad = dot(v_two, grad, ((1,), (1,)))
        key_index = lax.broadcasted_iota(jnp.int32, (count, block), 0) + begin
        query_index = lax.broadcasted_iota(jnp.int32, (count, block), 1) + low
        visible = (key_index.astype(F32) >= starts[:, low:end]) & (key_index <= query_index)
        weights_low, score_low = [], []
        for head in range(2):
            part = slice(head * count, (head + 1) * count)
            weights = jnp.where(
                visible, jnp.exp(scores[part] - lse_ref[0, head:head + 1, low:end]), 0.0)
            row_dots = jnp.sum(
                product[head * head_size:(head + 1) * head_size], axis=0, keepdims=True)
            weights_low.append(weights.astype(BF))
            score_low.append((weights * (prob_grad[part] - row_dots)).astype(BF))
        weights_low = jnp.concatenate(weights_low, axis=0)
        score_low = jnp.concatenate(score_low, axis=0)
        v_part = dot(weights_low, grad)
        k_part = dot(score_low, q)
        v_sum[begin:end, :] += jnp.where(first, v_part[:count], v_part[count:])
        k_sum[begin:end, :] += jnp.where(first, k_part[:count], k_part[count:])
        dq = dot(score_low, k_two, ((0,), (0,))) * scale
        d_ref[low:end, :lanes] = (
            dq * cos_ref[low:end, :] - turn(dq, half) * sin_ref[low:end, :]).astype(BF)
    for low in range(0, tokens, block):
        rows = pl.ds(low, block)
        dk = k_sum[rows, :]
        d_ref[rows, lanes:2 * lanes] = (
            dk * cos_ref[rows, :] - turn(dk, half) * sin_ref[rows, :]).astype(BF)
        d_ref[rows, 2 * lanes:] = v_sum[rows, :].astype(BF)

def attend_back(seg, g, w_out, q, k, v, att, lse, cosine, sine, window, head_size):
    tokens, width = g.shape
    lanes = 2 * head_size
    pairs = q.shape[1] // lanes
    kernel = lambda *refs: attend_back_kernel(
        *refs, block=256, window=window, scale=1.0 / math.sqrt(head_size), head_size=head_size)
    column = pl.BlockSpec((tokens, lanes), lambda p: (0, p))
    inputs = hbm(seg, g, w_out, q, k, v, att, lse, cosine, sine)
    return pl.pallas_call(
        kernel,
        grid=(pairs,),
        in_specs=whole_specs(seg, g) + [
            pl.BlockSpec((lanes, width), lambda p: (p, 0)),
            column, column, column, column,
            pl.BlockSpec((1, 8, tokens), lambda p: (p, 0, 0)),
        ] + whole_specs(cosine, sine),
        out_specs=pl.BlockSpec((tokens, 3 * lanes), lambda p: (0, p)),
        out_shape=pltpu.HBM((tokens, 3 * lanes * pairs), BF),
        scratch_shapes=[
            pltpu.VMEM((tokens, lanes), BF),
            pltpu.VMEM((tokens, lanes), F32),
            pltpu.VMEM((tokens, lanes), F32),
        ],
        compiler_params=pltpu.CompilerParams(vmem_limit_bytes=28 << 20),
        cost_estimate=SMALL_COST,
        name="attend_back",
    )(*inputs)


def join_kernel(rank_ref, own_ref, other_ref, *out_refs, moves, plain):
    swapped = rank_ref[0] == 1
    own, other = own_ref[...], other_ref[...]
    halves = (jnp.where(swapped, other, own), jnp.where(swapped, own, other))
    for out, half, (rows, cols), (to_rows, to_cols) in moves:
        out_refs[out][to_rows, to_cols] = halves[half][rows, cols].astype(F32)
    for out, (rows, cols) in plain:
        out_refs[out][...] = own[rows, cols].astype(F32)


def join(rank, own, other, moves, plain, shapes):
    kernel = lambda *refs: join_kernel(*refs, moves=moves, plain=plain)
    return pl.pallas_call(
        kernel,
        in_specs=[
            pl.BlockSpec(memory_space=pltpu.SMEM),
            pl.BlockSpec(memory_space=pltpu.VMEM),
            pl.BlockSpec(memory_space=pltpu.VMEM),
        ],
        out_specs=[pl.BlockSpec(memory_space=pltpu.VMEM)] * len(shapes),
        out_shape=[jax.ShapeDtypeStruct(shape, F32) for shape in shapes],
        compiler_params=pltpu.CompilerParams(vmem_limit_bytes=32 << 20),
        name="join",
    )(rank.reshape(1), own, other)


def join_all_kernel(all_ref, *refs, moves):
    out_refs, whole_ref = refs[:-1], refs[-1]
    groups, ranks, rows, _ = all_ref.shape
    for h in range(ranks):
        for m in range(groups):
            whole_ref[h, m * rows:(m + 1) * rows, :] = all_ref[m, h]
    for out, half, (rows, cols), (to_rows, to_cols) in moves:
        out_refs[out][to_rows, to_cols] = whole_ref[half, rows, cols].astype(F32)


def join_all(parts, moves, shapes):
    groups, ranks, rows, cols = parts.shape
    return pl.pallas_call(
        lambda *refs: join_all_kernel(*refs, moves=moves),
        in_specs=[VMEM_SPEC],
        out_specs=[VMEM_SPEC] * len(shapes),
        out_shape=[jax.ShapeDtypeStruct(shape, F32) for shape in shapes],
        scratch_shapes=[pltpu.VMEM((ranks, groups * rows, cols), BF)],
        compiler_params=pltpu.CompilerParams(vmem_limit_bytes=32 << 20),
        cost_estimate=SMALL_COST,
        name="join_all",
    )(parts)


def make_body(groups, ranks, fsdp, square):
    F = ("y", "x") if square else ("f",)
    swap = [(0, 1), (1, 0)]
    pairs = square and ranks == 2 and groups == 4

    def hop(value, k):
        return lax.ppermute(value, "m", [(i, i ^ k) for i in range(groups)])

    def after(value, *earlier):
        return lax.optimization_barrier((value,) + earlier)[0]

    def between(slabs, value):
        hops, value = lax.optimization_barrier((slabs[1:], value))
        return slabs[:1] + hops, value

    def spread(slabs):
        return [hop(slab, k) if k else slab for k, slab in enumerate(slabs)]

    def both_ranks(where, slabs, span):
        if ranks == 2:
            return slabs + [lax.ppermute(slab, "r", swap) for slab in slabs]
        rows = lax.all_gather(stack(where, slabs)[:, 0], "r", axis=1)
        return [rows[:, :, :span].reshape(-1, rows.shape[-1]), rows]

    def share(part):
        if ranks == 2:
            other = lax.ppermute(part, "r", swap)
            mine_first = lax.axis_index("r") == 0
            return jnp.stack(
                [jnp.where(mine_first, part, other), jnp.where(mine_first, other, part)], axis=1)
        return lax.all_gather(part, "r", axis=1)

    def exchange(part):
        if ranks == 2:
            return part, lax.ppermute(part, "r", swap)
        return lax.psum(part, "r"), jnp.zeros_like(part)

    def gather_rows(part, wait=()):
        if not square:
            whole = lax.all_gather(part, F, axis=0, tiled=True)
            return [whole], [(None, 0, 0)], (), ()
        count = part.shape[0]
        rows = (count // 2) // 16 * 16
        send = after(part, *wait) if wait else part
        from_x = lax.ppermute(send, "x", swap)
        from_y = lax.ppermute(send, "y", swap)
        far_a = lax.ppermute(from_y[:rows], "x", swap)
        far_b = lax.ppermute(from_x[rows:], "y", swap)
        pieces = [(0, 0, count), (1, 0, count), (2, 0, count), (3, 0, rows), (3, rows, count - rows)]
        return [part, from_x, from_y, far_a, far_b], pieces, (from_x, from_y), (far_a, far_b)

    def add(*parts):
        return sum(part.astype(F32) for part in parts).astype(BF)

    def take(grad, k):
        return lax.dynamic_index_in_dim(grad, lax.axis_index(F) ^ k, 0, keepdims=False)

    def half_rows(grad):
        return (grad.shape[1] // 2) // 16 * 16

    def round_one(grad):
        far, rows = take(grad, 3), half_rows(grad)
        return lax.ppermute(far[:rows], "x", swap), lax.ppermute(far[rows:], "y", swap)

    def second_terms(grad, low, high):
        to_x, to_y, rows = take(grad, 1), take(grad, 2), half_rows(grad)
        to_x = jnp.concatenate([to_x[:rows], add(to_x[rows:], high)], axis=0)
        to_y = jnp.concatenate([add(to_y[:rows], low), to_y[rows:]], axis=0)
        return to_x, to_y

    def round_two(to_x, to_y):
        return lax.ppermute(to_x, "x", swap), lax.ppermute(to_y, "y", swap)

    def halve(owned, bit, axis):
        half = owned.shape[axis] // 2
        side = (lax.axis_index("m") // bit) % 2
        return (lax.dynamic_slice_in_dim(owned, (1 - side) * half, half, axis),
                lax.dynamic_slice_in_dim(owned, side * half, half, axis))

    def join_halves(owned, other, bit, axis):
        first = (lax.axis_index("m") // bit) % 2 == 0
        return jnp.concatenate(
            [jnp.where(first, owned, other), jnp.where(first, other, owned)], axis=axis)

    def reduce(grad):
        return lax.psum(lax.psum_scatter(grad, F, scatter_dimension=0, tiled=False), "m")

    def body(tokens, segments, w_query, w_key, w_value, w_out, w_gate, w_up, w_down,
             gain_attn, gain_ffn, cotangent):
        micro, _, span, width = tokens.shape
        head_size = width // HEADS
        seq_tokens = span * groups * ranks
        window = seq_tokens // 2
        rank = lax.axis_index("r")
        own_cols = width // ranks
        shard = w_query.shape[0]
        down_rows = w_down.shape[0]
        part_rows = down_rows // ranks
        ff = w_gate.shape[1]
        half_ff = ff // ranks

        lanes = 2 * head_size
        lanes_all = -(-own_cols // lanes) * lanes
        spare = lanes_all - own_cols
        block = span * ranks
        f_index = lax.axis_index(F)
        where = jnp.stack([f_index, lax.axis_index("m"), rank])
        small_cols = 3 * lanes_all + own_cols
        gains_in = jnp.pad(jnp.stack([gain_attn, gain_ffn]), ((0, 14), (0, 0)))
        stack_own = pack(where, w_gate, w_up, w_down, fsdp, ranks)
        stack_all = lax.all_gather(stack_own, F, axis=0)
        cosine, sine = rotary_tables(seq_tokens, head_size, 2)
        small, *slabs = pack_small(
            after(where, stack_own), w_query, w_key, w_value, w_out, gains_in, tokens,
            segments[:, 0], cotangent, ranks, lanes, lanes_all)
        token_slabs, cot_slabs = slabs[:groups], slabs[groups:]
        token_slabs = spread(token_slabs)
        small_refs, small_pieces, near, far = gather_rows(small)
        if square:
            cot_slabs = cot_slabs[:1] + [after(slab, *token_slabs) for slab in cot_slabs[1:]]
        cot_slabs = spread(cot_slabs)
        if square:
            token_slabs = token_slabs[:1] + [
                after(slab, cosine, sine) for slab in token_slabs[1:]]
        token_refs = both_ranks(where, token_slabs, span)
        if ranks != 2:
            seg = token_refs[1][:, :, span, :span].reshape(1, seq_tokens).astype(F32)
            token_refs = [token_refs[0], seg]
        if square:
            own, from_x, from_y, far_a, far_b = small_refs
            at = far_a.shape[0]
            ends = [own, from_x, from_y, jnp.concatenate([far_a, far_b[:shard - at]], axis=0)]
            tails = [v[shard:shard + 2, :shard] for v in (own, from_x, from_y)]
            tails.append(far_b[shard - at:shard - at + 2, :shard])
            gains = jnp.zeros((fsdp, 2, shard), BF)
            out_cols = jnp.zeros((width, own_cols), BF)
            for offset in range(4):
                to = (f_index ^ offset) * shard
                gains = lax.dynamic_update_index_in_dim(gains, tails[offset], f_index ^ offset, 0)
                out_cols = lax.dynamic_update_slice_in_dim(
                    out_cols, ends[offset][:shard, 3 * lanes_all:], to, 0)
            gains = gains.transpose(1, 0, 2).reshape(2, width)
            small_pieces = [(o, f, min(n, shard - f)) for o, f, n in small_pieces]
            qkv_refs = small_refs
        else:
            whole = small_refs[0].reshape(fsdp, shard + 16, small_cols)
            gains = whole[:, shard:shard + 2, :shard].transpose(1, 0, 2).reshape(2, width)
            out_cols = whole[:, :shard, 3 * lanes_all:].reshape(width, own_cols)
            qkv_refs = [whole[:, :shard, :3 * lanes_all].reshape(width, 3 * lanes_all)]
        gains = gains.astype(F32)
        if ranks == 2:
            give = lax.dynamic_slice_in_dim(out_cols, (1 - rank) * own_cols, own_cols, 0)
            keep = lax.dynamic_slice_in_dim(out_cols, rank * own_cols, own_cols, 0)
            got = lax.ppermute(give, "r", swap)
            w_out_own = jnp.where(rank == 0, jnp.concatenate([keep, got], 1),
                                  jnp.concatenate([got, keep], 1))
        else:
            pieces = lax.all_to_all(out_cols, "r", 0, 0, tiled=True)
            pieces = pieces.reshape(ranks, own_cols, own_cols)
            w_out_own = jnp.concatenate([pieces[i] for i in range(ranks)], axis=1)
        w_out_even = jnp.pad(w_out_own, ((0, spare), (0, 0)))

        q, k, v, att, lse, w_qkv, x, seg = attend(
            where, cosine, sine, token_refs, ranks, qkv_refs, small_pieces, shard, lanes_all,
            window, head_size, width)
        if square:
            cot_slabs, att = between(cot_slabs, att)
        own, got = exchange(dot(att, w_out_even).astype(BF))
        cot_refs = both_ranks(where, cot_slabs, span)
        if ranks != 2:
            cot_refs = cot_refs[:1]
        total, middle_low, hidden_low, gate_back, silu, part = forward(
            x, own, got, gains[0:1], stack_all, shard, part_rows, half_ff, block)
        own, got = exchange(part)

        *out_slabs, ffn_grad, ffn_grad_low, gu_grad_low, part, gain_ffn_grad = backward(
            where, total, own, got, gate_back, silu, gains, cot_refs, stack_all, shard, part_rows,
            block, groups, ranks)
        own, got = exchange(part)
        gu_w_grad = dot(middle_low, gu_grad_low, ((0,), (0,))).astype(BF)
        if ranks == 2:
            got, gu_w_grad = lax.optimization_barrier((got, gu_w_grad))
        down_w_grad = dot(hidden_low, ffn_grad_low, ((0,), (0,))).astype(BF)
        stack_grad = arrange(gu_w_grad, down_w_grad, fsdp)
        stack_owned = lax.psum_scatter(stack_grad, F, scatter_dimension=0, tiled=False)
        own = after(own, stack_grad)
        branch_grad_low, branch_keep, gain_attn_grad = norm_back(
            where[2:], total, ffn_grad, own, got, gains[0:1], block, span)
        out_w_grad = dot(att, branch_grad_low, ((0,), (0,)))[:own_cols].astype(BF)
        if ranks == 2:
            give = lax.dynamic_slice_in_dim(out_w_grad, (1 - rank) * own_cols, own_cols, 1)
            keep = lax.dynamic_slice_in_dim(out_w_grad, rank * own_cols, own_cols, 1)
            got = lax.ppermute(give, "r", swap)
            out_cols_grad = jnp.where(rank == 0, jnp.concatenate([keep, got], 0),
                                      jnp.concatenate([got, keep], 0))
        else:
            rows = out_w_grad.reshape(own_cols, ranks, own_cols).transpose(1, 0, 2)
            out_cols_grad = lax.all_to_all(rows, "r", 0, 0, tiled=True).reshape(width, own_cols)
        gain_grads = jnp.concatenate([gain_attn_grad, gain_ffn_grad], axis=0).astype(BF)
        gain_grads = gain_grads.reshape(2, fsdp, shard).transpose(1, 0, 2)
        gain_grads = jnp.pad(gain_grads, ((0, 0), (0, 14), (0, small_cols - shard)))
        branch_grad_low = after(branch_grad_low, out_cols_grad, gain_grads)
        d_qkv = attend_back(
            seg, branch_grad_low, w_out_even, q, k, v, att, lse, cosine, sine, window, head_size)
        if square:
            out_slabs, d_qkv = between(spread(out_slabs), d_qkv)
        else:
            out_slabs = spread(out_slabs)
        output = stack(where, out_slabs)
        qkv_w_grad = dot(x, d_qkv, ((0,), (0,))).astype(BF)
        small_grad = jnp.concatenate([qkv_w_grad, out_cols_grad], axis=1)
        small_grad = jnp.concatenate(
            [small_grad.reshape(fsdp, shard, small_cols), gain_grads], axis=1)
        if pairs:
            small_one = round_one(small_grad)
            d_qkv = after(d_qkv, small_grad)
        part = dot(d_qkv, w_qkv, ((1,), (1,))).astype(BF)
        if ranks == 2:
            rows = part.reshape(groups, ranks, span, width)
            give = lax.dynamic_index_in_dim(rows, 1 - rank, 1, keepdims=False)
            got = lax.ppermute(give, "r", swap)
        else:
            part = lax.psum(part, "r")
            got = jnp.zeros_like(branch_keep, BF)
        grad_slabs = list(finish(where, branch_keep, part, got, ranks))
        if pairs:
            grad_slabs, small_one = between(spread(grad_slabs), small_one)
        else:
            grad_slabs = spread(grad_slabs)
        if pairs:
            terms = second_terms(small_grad, *small_one)
            small_two = round_two(*terms)
            stack_owned = after(stack_owned, *terms)
            quarter = lax.psum_scatter(stack_owned, "m", scatter_dimension=0, tiled=True)
            give, keep = halve(add(take(small_grad, 0), *small_two), 1, 1)
            got, quarter = lax.optimization_barrier((hop(give, 1), quarter))
            stack_parts = lax.all_gather(quarter, ("m", "r"), axis=0)
            stack_parts = stack_parts.reshape((groups, ranks) + quarter.shape)
            give, keep = halve(add(keep, got), 2, 1)
            owned = add(keep, hop(give, 2))
            owned = join_halves(owned, hop(owned, 2), 2, 1)
            small_sum = join_halves(owned, hop(owned, 1), 1, 1)
        else:
            stack_sum = lax.psum(stack_owned, "m")
            small_sum = reduce(small_grad)
        input_grad = stack(where, grad_slabs)
        if pairs:
            everything = slice(None)
            chunks = 2 * half_ff // 256
            stack_moves = [
                (n, h, (slice((n * fsdp + j) * shard, (n * fsdp + j + 1) * shard), everything),
                 (everything, slice(j * down_rows + h * part_rows, j * down_rows + (h + 1) * part_rows)))
                for n in range(2) for h in range(2) for j in range(fsdp)]
            stack_moves += [
                (2, h, (slice(chunks * shard + c * part_rows, chunks * shard + (c + 1) * part_rows),
                        everything),
                 (slice(h * part_rows, (h + 1) * part_rows), slice(c * 256, (c + 1) * 256)))
                for h in range(2) for c in range(width // 256)]
            small_moves = [
                (n, h, (slice(0, shard), slice((3 * p + n) * lanes, (3 * p + n + 1) * lanes)),
                 (everything, slice(h * own_cols + p * lanes, h * own_cols + (p + 1) * lanes)))
                for n in range(3) for h in range(2) for p in range(own_cols // lanes)]
            small_moves += [
                (3, h, (slice(0, shard), slice(3 * lanes_all, small_cols)),
                 (everything, slice(h * own_cols, (h + 1) * own_cols))) for h in range(2)]
            small_plain = [
                (4 + n, (slice(shard + n, shard + n + 1), slice(0, shard))) for n in range(2)]
            gate_w, up_w, down_grad = join_all(
                stack_parts, stack_moves, [(shard, ff)] * 2 + [(down_rows, width)])
            query_w, key_w, value_w, out_w, gain_a, gain_f = join(
                rank, small_sum, lax.ppermute(small_sum, "r", swap), small_moves, small_plain,
                [(shard, width)] * 4 + [(1, shard)] * 2)
        else:
            at = 2 * half_ff // 256 * shard
            down_sum = jnp.moveaxis(stack_sum[at:].reshape(-1, part_rows, 256), 0, 1)
            down_grad = jnp.moveaxis(share(down_sum.reshape(part_rows, width)), 1, 0)
            down_grad = down_grad.reshape(down_rows, width).astype(F32)
            gu_sum = jnp.moveaxis(stack_sum[:at].reshape(-1, shard, 256), 0, 1)
            gu_both = share(gu_sum.reshape(shard, 2 * fsdp, part_rows))
            gu_both = gu_both.reshape(shard, ranks, 2, fsdp, part_rows).astype(F32)
            gate_w, up_w = (
                gu_both[:, :, n].transpose(0, 2, 1, 3).reshape(shard, ff) for n in range(2))
            small_both = share(small_sum)[:shard].astype(F32)
            three = small_both[:, :, :3 * lanes_all].reshape(shard, ranks, -1, 3, lanes)
            query_w, key_w, value_w = (
                three[:, :, :, n].reshape(shard, ranks, lanes_all)[:, :, :own_cols].reshape(shard, width)
                for n in range(3))
            out_w = small_both[:, :, 3 * lanes_all:].reshape(shard, width)
            gain_a, gain_f = small_sum[shard, :shard].astype(F32), small_sum[shard + 1, :shard].astype(F32)
        return (output, input_grad, query_w, key_w, value_w, out_w,
                gate_w, up_w, down_grad, gain_a.reshape(shard), gain_f.reshape(shard))

    return body


def solution(mesh):
    def run(*args):
        groups = args[0].shape[0]
        seq, fsdp = mesh.shape["seq"], mesh.shape["fsdp"]
        ranks = seq // groups
        square = fsdp == 4
        names = ("m", "r") + (("y", "x") if square else ("f",))
        sizes = (groups, ranks) + ((2, 2) if square else (fsdp,))
        order = [mesh.axis_names.index(name) for name in ("seq", "fsdp")]
        inner = Mesh(mesh.devices.transpose(order).reshape(sizes), names)
        f = ("y", "x") if square else "f"
        s = ("m", "r")
        rows = P(f, None)
        data = P(None, f, s, None)
        in_specs = (data, P(None, f, s)) + (rows,) * 7 + (P(f), P(f), data)
        out_specs = (data, data) + (rows,) * 7 + (P(f), P(f))
        body = make_body(groups, ranks, fsdp, square)
        return jax.shard_map(
            body, mesh=inner, in_specs=in_specs, out_specs=out_specs, check_vma=False)(*args)

    return run
```

```python
import math

import jax
import jax.numpy as jnp
from jax import lax
from jax.experimental import pallas as pl
from jax.experimental.pallas import tpu as pltpu
from jax.sharding import Mesh, PartitionSpec as P

HEADS = 12
DOCS = 4
EPS = 1e-06
NEGATIVE = -1e30
BF = jnp.bfloat16
F32 = jnp.float32


def dot(left, right, dims=((1,), (0,))):
    return lax.dot_general(left, right, (dims, ((), ())), preferred_element_type=F32)


def rotary_tables(seq_tokens, head_size, copies):
    half = head_size // 2
    frequency = 10000.0 ** (-jnp.arange(half, dtype=F32) / half)
    angle = jnp.arange(seq_tokens, dtype=jnp.int32).astype(F32)[:, None] * frequency[None, :]
    cosine, sine = jnp.cos(angle), jnp.sin(angle)
    return (
        jnp.concatenate([cosine, cosine] * copies, axis=1),
        jnp.concatenate([-sine, sine] * copies, axis=1),
    )


def turn(rows, half):
    lanes = rows.shape[1]
    lane = lax.broadcasted_iota(jnp.int32, (1, lanes), 1)
    low = (lane // half) % 2 == 0
    return jnp.where(low, pltpu.roll(rows, lanes - half, 1), pltpu.roll(rows, half, 1))


def first_key(query_first, block, window):
    return max(0, (query_first - window + 1) // block * block)


def start_row(seg_ref):
    seg = seg_ref[...]
    starts = jnp.zeros_like(seg)
    for doc in range(1, DOCS):
        before = jnp.sum(jnp.where(seg < doc, 1.0, 0.0), axis=1, keepdims=True)
        starts = jnp.maximum(starts, jnp.where(seg >= doc, before, 0.0))
    return starts


def place(target, refs, pieces, me, shard):
    for ref, (offset, first, rows) in zip(refs, pieces):
        if offset is None:
            target[...] = ref[...]
        else:
            start = pl.multiple_of((me ^ offset) * shard + first, 16)
            target[pl.ds(start, rows), :] = ref[0:rows, 0:target.shape[1]]


def place_tokens(target, refs, where_ref, ranks):
    if len(refs) == 1:
        target[...] = refs[0][...]
        return
    groups = len(refs) // ranks
    span = target.shape[0] // (groups * ranks)
    for n, ref in enumerate(refs):
        rank = where_ref[2] if n < groups else 1 - where_ref[2]
        chunk = (where_ref[1] ^ (n % groups)) * ranks + rank
        target[pl.ds(pl.multiple_of(chunk * span, span), span), :] = ref[0:span, :]


def place_segments(target, refs, where_ref, ranks):
    groups = len(refs) // ranks
    span = target.shape[1] // (groups * ranks)
    for n, ref in enumerate(refs):
        rank = where_ref[2] if n < groups else 1 - where_ref[2]
        chunk = (where_ref[1] ^ (n % groups)) * ranks + rank
        row = ref[span:span + 16, 0:span].astype(F32)[0:1, :]
        target[:, pl.ds(pl.multiple_of(chunk * span, span), span)] = row


def stack_copies(gu, down, stack_ref, sems, shard, part_rows):
    members, chunks, groups = stack_ref.shape[0], gu.shape[1] // 256, []
    for c in range(chunks):
        groups.append([
            pltpu.make_async_copy(
                stack_ref.at[j, c * shard:(c + 1) * shard, :],
                gu.at[j * shard:(j + 1) * shard, c * 256:(c + 1) * 256],
                sems.at[c, j]) for j in range(members)])
    for c in range(down.shape[1] // 256):
        at = chunks * shard + c * part_rows
        groups.append([
            pltpu.make_async_copy(
                stack_ref.at[j, at:at + part_rows, :],
                down.at[j * part_rows:(j + 1) * part_rows, c * 256:(c + 1) * 256],
                sems.at[chunks + c, j]) for j in range(members)])
    return groups


def place_tokens(target, refs, where_ref, ranks):
    if len(refs) == 1:
        target[...] = refs[0][...]
        return
    groups = len(refs) // ranks
    span = target.shape[0] // (groups * ranks)
    for n, ref in enumerate(refs):
        rank = where_ref[2] if n < groups else 1 - where_ref[2]
        chunk = (where_ref[1] ^ (n % groups)) * ranks + rank
        target[pl.ds(pl.multiple_of(chunk * span, span), span), :] = ref[0:span, :]


def place_segments(target, refs, where_ref, ranks):
    groups = len(refs) // ranks
    span = target.shape[1] // (groups * ranks)
    for n, ref in enumerate(refs):
        rank = where_ref[2] if n < groups else 1 - where_ref[2]
        chunk = (where_ref[1] ^ (n % groups)) * ranks + rank
        row = ref[span:span + 16, 0:span].astype(F32)[0:1, :]
        target[:, pl.ds(pl.multiple_of(chunk * span, span), span)] = row


def place_stack(gu, down, stack_ref, shard, part_rows):
    chunks = gu.shape[1] // 256
    for j in range(stack_ref.shape[0]):
        for c in range(chunks):
            gu[j * shard:(j + 1) * shard, c * 256:(c + 1) * 256] = (
                stack_ref[j, c * shard:(c + 1) * shard, :])
        for c in range(down.shape[1] // 256):
            at = chunks * shard + c * part_rows
            down[j * part_rows:(j + 1) * part_rows, c * 256:(c + 1) * 256] = (
                stack_ref[j, at:at + part_rows, :])


def attend_kernel(where_ref, cos_ref, sin_ref, *refs, pieces, token_count, ranks, shard, block,
                  window, scale, head_size):
    inputs, refs = refs[:-9], refs[-9:]
    q_ref, k_ref, v_ref, att_ref, lse_ref, w_ref, x_ref, seg_ref, col_ref = refs
    token_refs, w_refs = inputs[:token_count], inputs[token_count:]
    tokens = x_ref.shape[0]
    lanes = 2 * head_size
    lane = lax.broadcasted_iota(jnp.int32, (1, lanes), 1)
    first = lane < head_size
    pair = pl.program_id(0)

    @pl.when(pair == 0)
    def _():
        place(w_ref, w_refs, pieces, where_ref[0], shard)
        place_tokens(x_ref, token_refs[:1] if token_count == 2 else token_refs, where_ref, ranks)
        if token_count == 2:
            seg_ref[...] = token_refs[1][...]
        else:
            place_segments(seg_ref, token_refs, where_ref, ranks)
        starts = start_row(seg_ref)
        col_ref[...] = jnp.broadcast_to(starts, (128, tokens)).T

    w = w_ref[:, pl.ds(pl.multiple_of(pair * 3 * lanes, lanes), 3 * lanes)]
    for low in range(0, tokens, block):
        rows = pl.ds(low, block)
        lin = dot(x_ref[rows, :], w)
        cosine, sine = cos_ref[rows, :], sin_ref[rows, :]
        half = head_size // 2
        q_lin, k_lin = lin[:, :lanes], lin[:, lanes:2 * lanes]
        q_ref[rows, :] = (q_lin * cosine + turn(q_lin, half) * sine).astype(BF)
        k_ref[rows, :] = (k_lin * cosine + turn(k_lin, half) * sine).astype(BF)
        v_ref[rows, :] = lin[:, 2 * lanes:].astype(BF)
    for low in range(0, tokens, block):
        begin = first_key(low, block, window)
        end = low + block
        q = q_ref[low:end, :] * jnp.asarray(scale, BF)
        zero = jnp.zeros_like(q)
        stacked = jnp.concatenate([jnp.where(first, q, zero), jnp.where(first, zero, q)], axis=0)
        scores = dot(stacked, k_ref[begin:end, :], ((1,), (1,)))
        key_index = lax.broadcasted_iota(jnp.int32, (block, end - begin), 1) + begin
        query_index = lax.broadcasted_iota(jnp.int32, (block, end - begin), 0) + low
        visible = (key_index.astype(F32) >= col_ref[low:end, 0:1]) & (key_index <= query_index)
        parts = []
        for head in range(2):
            own = jnp.where(visible, scores[head * block:(head + 1) * block], NEGATIVE)
            top = jnp.max(own, axis=1, keepdims=True)
            weights = jnp.exp(own - top)
            total = jnp.sum(weights, axis=1, keepdims=True)
            out = dot(weights.astype(BF), v_ref[begin:end, :]) / total
            parts.append(out)
            lse = jnp.broadcast_to(top + jnp.log(total), (block, 128))
            lse_ref[0, head:head + 1, low:end] = lse.T[0:1, :]
        att_ref[low:end, :] = jnp.where(first, parts[0], parts[1]).astype(BF)


def hbm(*arrays):
    return [pltpu.with_memory_space_constraint(a, pltpu.HBM) for a in arrays]


def vmem(*arrays):
    return [pltpu.with_memory_space_constraint(a, pltpu.VMEM) for a in arrays]


def whole_specs(*arrays):
    return [pl.BlockSpec(a.shape, lambda *_, n=a.ndim: (0,) * n, pipeline_mode=pl.Buffered(1))
            for a in arrays]


SMALL_COST = pl.CostEstimate(flops=1, bytes_accessed=1, transcendentals=0)
VMEM_SPEC = pl.BlockSpec(memory_space=pltpu.VMEM)
SMEM_SPEC = pl.BlockSpec(memory_space=pltpu.SMEM)


def attend(where, cosine, sine, token_refs, ranks, weights, pieces, shard, lanes_all, window,
           head_size, width):
    tokens = cosine.shape[0]
    lanes = 2 * head_size
    pairs = lanes_all // lanes
    kernel = lambda *refs: attend_kernel(
        *refs, pieces=pieces, token_count=len(token_refs), ranks=ranks, shard=shard, block=256,
        window=window, scale=1.0 / math.sqrt(head_size), head_size=head_size)
    column = pl.BlockSpec((tokens, lanes), lambda p: (0, p))
    whole = lambda *shape: pl.BlockSpec(shape, lambda p: (0, 0))
    inputs = hbm(cosine, sine, *token_refs, *weights)
    return pl.pallas_call(
        kernel,
        grid=(pairs,),
        in_specs=[SMEM_SPEC] + whole_specs(*inputs),
        out_specs=[column, column, column, column,
                   pl.BlockSpec((1, 8, tokens), lambda p: (p, 0, 0)),
                   whole(width, 3 * lanes_all), whole(tokens, width), whole(1, tokens)],
        out_shape=[pltpu.HBM((tokens, lanes_all), BF)] * 4
        + [pltpu.HBM((pairs, 8, tokens), F32), pltpu.HBM((width, 3 * lanes_all), BF),
           pltpu.HBM((tokens, width), BF), pltpu.HBM((1, tokens), F32)],
        scratch_shapes=[pltpu.VMEM((tokens, 128), F32)],
        compiler_params=pltpu.CompilerParams(vmem_limit_bytes=28 << 20),
        cost_estimate=SMALL_COST,
        name="attend",
    )(where, *inputs)


def unit_of(rows):
    factor = lax.rsqrt(jnp.mean(rows * rows, axis=1, keepdims=True) + EPS)
    return rows * factor, factor


def forward_kernel(x_ref, own_ref, got_ref, gain_ref, stack_ref, sum_ref, low_ref, hidden_ref,
                   gate_ref, silu_ref, part_ref, gu, down, sems, *, shard, part_rows):
    step, block = pl.program_id(0), x_ref.shape[0]
    ff = down.shape[0]

    @pl.when(step == 0)
    def _():
        copies = stack_copies(gu, down, stack_ref, sems, shard, part_rows)
        for group in copies:
            for copy in group:
                copy.start()
        for group in copies:
            for copy in group:
                copy.wait()

    rows = pl.ds(pl.multiple_of(step * block, block), block)
    total = x_ref[...].astype(F32) + own_ref[...].astype(F32) + got_ref[...].astype(F32)
    sum_ref[rows, :] = total
    middle_low = (unit_of(total)[0] * gain_ref[...]).astype(BF)
    low_ref[rows, :] = middle_low
    for c in range(0, ff, 256):
        cols = slice(c, c + 256)
        gate = dot(middle_low, gu[:, cols])
        up = dot(middle_low, gu[:, ff + c:ff + c + 256])
        sigmoid = jax.nn.sigmoid(gate)
        silu = gate * sigmoid
        hidden_ref[rows, cols] = (silu * up).astype(BF)
        gate_ref[rows, cols] = (up * sigmoid * (1.0 + gate * (1.0 - sigmoid))).astype(BF)
        silu_ref[rows, cols] = silu.astype(BF)
    part_ref[...] = dot(hidden_ref[rows, :], down[...]).astype(BF)


HBM_SPEC = pl.BlockSpec(memory_space=pltpu.HBM)


def forward(x, own, got, gain, stack, shard, part_rows, ff, block):
    tokens, width = x.shape
    row = lambda cols: pl.BlockSpec((block, cols), lambda i: (i, 0))
    x, own, got, stack = hbm(x, own, got, stack)
    return pl.pallas_call(
        lambda *refs: forward_kernel(*refs, shard=shard, part_rows=part_rows),
        grid=(tokens // block,),
        in_specs=[row(width), row(width), row(width)] + whole_specs(gain) + [HBM_SPEC],
        out_specs=[VMEM_SPEC] * 5 + [row(width)] + [VMEM_SPEC] * 2,
        out_shape=[pltpu.VMEM((tokens, width), F32), pltpu.VMEM((tokens, width), BF)]
        + [pltpu.VMEM((tokens, ff), BF)] * 3 + [jax.ShapeDtypeStruct((tokens, width), BF)]
        + [pltpu.VMEM((width, 2 * ff), BF), pltpu.VMEM((ff, width), BF)],
        scratch_shapes=[pltpu.SemaphoreType.DMA(((2 * ff + width) // 256, stack.shape[0]))],
        compiler_params=pltpu.CompilerParams(vmem_limit_bytes=16 << 20),
        cost_estimate=SMALL_COST,
        name="ffn_forward",
    )(x, own, got, gain, stack)


def backward_kernel(where_ref, sum_ref, own_ref, got_ref, gate_ref, silu_ref, gains_ref, gu, down,
                    *refs, cot_count, groups, ranks):
    cot_refs, refs = refs[:cot_count], refs[cot_count:]
    out_refs, refs = refs[:groups], refs[groups:]
    low_ref, gu_grad_ref, part_ref, gain_ref, cot_ref, rows_ref = refs
    step = pl.program_id(0)
    block, span = rows_ref.shape[0], out_refs[0].shape[0]

    @pl.when(step == 0)
    def _():
        place_tokens(cot_ref, cot_refs, where_ref, ranks)
        gain_ref[...] = jnp.zeros_like(gain_ref)

    rows = pl.ds(pl.multiple_of(step * block, block), block)
    gain_two = gains_ref[1:2, :]
    middle = unit_of(sum_ref[rows, :])[0] * gains_ref[0:1, :]
    unit, factor = unit_of(middle + own_ref[...].astype(F32) + got_ref[...].astype(F32))
    rows_ref[...] = unit * gain_two
    cot = cot_ref[rows, :].astype(F32)
    gain_ref[...] += jnp.sum(cot * unit, axis=0, keepdims=True)
    scaled = cot * gain_two
    grad_low = (factor * (scaled - unit * jnp.mean(scaled * unit, axis=1, keepdims=True))).astype(BF)
    low_ref[rows, :] = grad_low
    ff = down.shape[0]
    for c in range(0, ff, 256):
        cols = slice(c, c + 256)
        hidden_grad = dot(grad_low, down[cols, :], ((1,), (1,)))
        gu_grad_ref[rows, cols] = (hidden_grad * gate_ref[rows, cols].astype(F32)).astype(BF)
        gu_grad_ref[rows, ff + c:ff + c + 256] = (
            hidden_grad * silu_ref[rows, cols].astype(F32)).astype(BF)
    part_ref[...] = dot(gu_grad_ref[rows, :], gu[...], ((1,), (1,))).astype(BF)
    kept = rows_ref[pl.ds(pl.multiple_of(where_ref[2] * span, span), span), :].astype(BF)
    for k, out_ref in enumerate(out_refs):
        @pl.when(step == (where_ref[1] ^ k))
        def _(out_ref=out_ref):
            out_ref[...] = kept


def backward(where, total, own, got, gate, silu, gains, gu, down, cot, block, groups, ranks):
    tokens, width = total.shape
    ff = gate.shape[1]
    kernel = lambda *refs: backward_kernel(
        *refs, cot_count=len(cot), groups=groups, ranks=ranks)
    row = pl.BlockSpec((block, width), lambda i: (i, 0))
    slab = pl.BlockSpec((block // ranks, width), lambda i: (0, 0))
    total, gate, silu, gu, down = vmem(total, gate, silu, gu, down)
    cot = hbm(*cot)
    return pl.pallas_call(
        kernel,
        grid=(tokens // block,),
        in_specs=[SMEM_SPEC, VMEM_SPEC, row, row, VMEM_SPEC, VMEM_SPEC] + whole_specs(gains)
        + [VMEM_SPEC] * 2 + whole_specs(*cot),
        out_specs=[slab] * groups + [VMEM_SPEC, VMEM_SPEC, row,
                                     pl.BlockSpec((1, width), lambda i: (0, 0))],
        out_shape=[pltpu.HBM((block // ranks, width), BF)] * groups
        + [pltpu.VMEM((tokens, width), BF), pltpu.VMEM((tokens, 2 * ff), BF),
           jax.ShapeDtypeStruct((tokens, width), BF), pltpu.HBM((1, width), F32)],
        scratch_shapes=[pltpu.VMEM((tokens, width), BF), pltpu.VMEM((block, width), F32)],
        compiler_params=pltpu.CompilerParams(vmem_limit_bytes=20 << 20),
        cost_estimate=SMALL_COST,
        name="ffn_backward",
    )(where, total, own, got, gate, silu, gains, gu, down, *cot)


def norm_back_kernel(rank_ref, sum_ref, grad_ref, own_ref, got_ref, gain_ref, other_ref,
                     low_ref, keep_ref, out_ref, rows_ref, gain_grad_ref):
    step, block = pl.program_id(0), rows_ref.shape[0]

    @pl.when(step == 0)
    def _():
        gain_grad_ref[...] = jnp.zeros_like(gain_grad_ref)

    rows = pl.ds(pl.multiple_of(step * block, block), block)
    unit, factor = unit_of(sum_ref[rows, :])
    grad = (grad_ref[...].astype(F32) + own_ref[...].astype(F32)) + got_ref[...].astype(F32)
    gain_grad_ref[...] += jnp.sum(grad * unit, axis=0, keepdims=True)
    scaled = grad * gain_ref[...]
    branch_grad = factor * (scaled - unit * jnp.mean(scaled * unit, axis=1, keepdims=True))
    low_ref[rows, :] = branch_grad.astype(BF)
    rows_ref[...] = branch_grad
    span = keep_ref.shape[1]
    keep_ref[0] = rows_ref[pl.ds(pl.multiple_of(rank_ref[0] * span, span), span), :]

    @pl.when(step == pl.num_programs(0) - 1)
    def _():
        out_ref[...] = jnp.zeros_like(out_ref)
        shard = gain_ref.shape[1] // out_ref.shape[0]
        first = lax.broadcasted_iota(jnp.int32, (16, shard), 0)
        for j in range(out_ref.shape[0]):
            lanes = slice(j * shard, (j + 1) * shard)
            one = jnp.broadcast_to(gain_grad_ref[:, lanes], (16, shard))
            two = jnp.broadcast_to(other_ref[:, lanes], (16, shard))
            out_ref[j, :, 0:shard] = jnp.where(
                first == 0, one, jnp.where(first == 1, two, 0.0)).astype(BF)


def norm_back(rank, total, grad, own, got, gain, other_grad, fsdp, cols, block, span):
    tokens, width = total.shape
    row = pl.BlockSpec((block, width), lambda i: (i, 0))
    inputs = vmem(total) + hbm(grad, own, got)
    return pl.pallas_call(
        norm_back_kernel,
        grid=(tokens // block,),
        in_specs=[SMEM_SPEC, VMEM_SPEC, row, row, row] + whole_specs(gain, other_grad),
        out_specs=[VMEM_SPEC, pl.BlockSpec((1, span, width), lambda i: (i, 0, 0)),
                   pl.BlockSpec((fsdp, 16, cols), lambda i: (0, 0, 0))],
        out_shape=[pltpu.VMEM((tokens, width), BF),
                   pltpu.HBM((tokens // block, span, width), F32),
                   pltpu.HBM((fsdp, 16, cols), BF)],
        scratch_shapes=[pltpu.VMEM((block, width), F32), pltpu.VMEM((1, width), F32)],
        compiler_params=pltpu.CompilerParams(vmem_limit_bytes=16 << 20),
        cost_estimate=SMALL_COST,
        name="norm_back",
    )(rank, *inputs, gain, other_grad)


def pick(rank, parts):
    value = parts[0]
    for r in range(1, len(parts)):
        value = jnp.where(rank == r, parts[r], value)
    return value


def pack_small_kernel(where_ref, query_ref, key_ref, value_ref, out_ref, gain_ref, tokens_ref,
                      seg_ref, cot_ref, small_ref, *slab_refs, ranks, lanes, lanes_all):
    slab_refs, cot_slabs = slab_refs[:len(slab_refs) // 2], slab_refs[len(slab_refs) // 2:]
    for k, ref in enumerate(cot_slabs):
        ref[...] = cot_ref[where_ref[1] ^ k, 0]
    rank, m = where_ref[2], where_ref[1]
    shard, width = query_ref.shape
    own_cols = width // ranks
    if lanes_all != own_cols:
        small_ref[...] = jnp.zeros_like(small_ref)
    for n, ref in enumerate((query_ref, key_ref, value_ref)):
        for low in range(0, own_cols, lanes):
            size = min(lanes, own_cols - low)
            at = (low // lanes * 3 + n) * lanes
            small_ref[0:shard, at:at + size] = pick(
                rank, [ref[:, r * own_cols + low:r * own_cols + low + size] for r in range(ranks)])
    small_ref[0:shard, 3 * lanes_all:] = pick(
        rank, [out_ref[:, r * own_cols:(r + 1) * own_cols] for r in range(ranks)])
    small_ref[shard:, :] = jnp.zeros_like(small_ref[shard:, :])
    small_ref[shard:, 0:shard] = gain_ref[...]
    span = tokens_ref.shape[2]
    for k, ref in enumerate(slab_refs):
        ref[0:span, :] = tokens_ref[m ^ k, 0]
        ref[span:, :] = jnp.zeros_like(ref[span:, :])
        row = seg_ref[pl.ds(m ^ k, 1), :].astype(F32)
        ref[span:, 0:span] = jnp.broadcast_to(row, (16, span)).astype(BF)


def pack_small(where, query, key, value, out, gains, tokens, segments, cot, ranks, lanes,
               lanes_all):
    shard, width = query.shape
    groups, _, span, _ = tokens.shape
    cols = 3 * lanes_all + width // ranks
    inputs = hbm(query, key, value, out, gains, tokens, segments, cot)
    shapes = [(shard + 16, cols)] + [(span + 16, width)] * groups + [(span, width)] * groups
    return pl.pallas_call(
        lambda *refs: pack_small_kernel(*refs, ranks=ranks, lanes=lanes, lanes_all=lanes_all),
        grid=(1,),
        in_specs=[SMEM_SPEC] + whole_specs(*inputs),
        out_specs=[pl.BlockSpec(shape, lambda i: (0, 0)) for shape in shapes],
        out_shape=[pltpu.HBM(shape, BF) for shape in shapes],
        compiler_params=pltpu.CompilerParams(vmem_limit_bytes=24 << 20),
        cost_estimate=SMALL_COST,
        name="pack_small",
    )(where, *inputs)


def pack_kernel(where_ref, gate_ref, up_ref, down_ref, out_ref, gu, *, fsdp, ranks):
    rank = where_ref[2]
    shard, cols = gu.shape
    part = down_ref.shape[0] // ranks
    for n, ref in enumerate((gate_ref, up_ref)):
        for j in range(fsdp):
            low = (n * fsdp + j) * part
            gu[:, low:low + part] = pick(
                rank, [ref[:, (j * ranks + r) * part:(j * ranks + r + 1) * part]
                       for r in range(ranks)])
    chunks = cols // 256
    for c in range(chunks):
        out_ref[c * shard:(c + 1) * shard, :] = gu[:, c * 256:(c + 1) * 256]
    rows = pl.ds(pl.multiple_of(rank * part, 16), part)
    for c in range(down_ref.shape[1] // 256):
        at = chunks * shard + c * part
        out_ref[at:at + part, :] = down_ref[rows, c * 256:(c + 1) * 256]


def pack(where, gate, up, down, fsdp, ranks):
    shard, ff = gate.shape
    cols = 2 * ff // ranks
    rows = cols // 256 * shard + down.shape[1] // 256 * (down.shape[0] // ranks)
    inputs = hbm(gate, up, down)
    return pl.pallas_call(
        lambda *refs: pack_kernel(*refs, fsdp=fsdp, ranks=ranks),
        grid=(1,),
        in_specs=[SMEM_SPEC] + whole_specs(*inputs),
        out_specs=pl.BlockSpec((rows, 256), lambda i: (0, 0)),
        out_shape=pltpu.HBM((rows, 256), BF),
        scratch_shapes=[pltpu.VMEM((shard, cols), BF)],
        compiler_params=pltpu.CompilerParams(vmem_limit_bytes=24 << 20),
        cost_estimate=SMALL_COST,
        name="pack",
    )(where, *inputs)


def arrange_kernel(gu_ref, down_ref, out_ref):
    shard, part = gu_ref.shape[0], down_ref.shape[0]
    chunks = gu_ref.shape[1] // 256
    for c in range(chunks):
        out_ref[0, c * shard:(c + 1) * shard, :] = gu_ref[:, c * 256:(c + 1) * 256]
    for c in range(down_ref.shape[1] // 256):
        at = chunks * shard + c * part
        out_ref[0, at:at + part, :] = down_ref[:, c * 256:(c + 1) * 256]


def arrange(gu, down, fsdp):
    shard, part = gu.shape[0] // fsdp, down.shape[0] // fsdp
    rows = gu.shape[1] // 256 * shard + down.shape[1] // 256 * part
    return pl.pallas_call(
        arrange_kernel,
        grid=(fsdp,),
        in_specs=[pl.BlockSpec((shard, gu.shape[1]), lambda j: (j, 0)),
                  pl.BlockSpec((part, down.shape[1]), lambda j: (j, 0))],
        out_specs=pl.BlockSpec((1, rows, 256), lambda j: (j, 0, 0)),
        out_shape=pltpu.HBM((fsdp, rows, 256), BF),
        compiler_params=pltpu.CompilerParams(vmem_limit_bytes=24 << 20),
        cost_estimate=SMALL_COST,
        name="arrange",
    )(gu, down)


def finish_kernel(where_ref, keep_ref, part_ref, got_ref, *out_refs, ranks):
    groups, span, _ = keep_ref.shape
    for k, ref in enumerate(out_refs):
        group = where_ref[1] ^ k
        row = (group * ranks + where_ref[2]) * span
        own = part_ref[pl.ds(pl.multiple_of(row, span), span), :].astype(F32)
        ref[...] = (keep_ref[group] + own + got_ref[group].astype(F32)).astype(BF)


def finish(where, keep, part, got, ranks):
    groups, span, width = keep.shape
    return pl.pallas_call(
        lambda *refs: finish_kernel(*refs, ranks=ranks),
        in_specs=[SMEM_SPEC] + [VMEM_SPEC] * 3,
        out_specs=[VMEM_SPEC] * groups,
        out_shape=[jax.ShapeDtypeStruct((span, width), BF)] * groups,
        compiler_params=pltpu.CompilerParams(vmem_limit_bytes=24 << 20),
        cost_estimate=SMALL_COST,
        name="finish",
    )(where, keep, part, got)


def stack_kernel(where_ref, *refs):
    out_ref = refs[-1]
    for k, ref in enumerate(refs[:-1]):
        out_ref[where_ref[1] ^ k, 0] = ref[...]


def stack(where, slabs):
    span, width = slabs[0].shape
    return pl.pallas_call(
        stack_kernel,
        in_specs=[SMEM_SPEC] + [VMEM_SPEC] * len(slabs),
        out_specs=VMEM_SPEC,
        out_shape=jax.ShapeDtypeStruct((len(slabs), 1, span, width), BF),
        compiler_params=pltpu.CompilerParams(vmem_limit_bytes=16 << 20),
        cost_estimate=SMALL_COST,
        name="stack",
    )(where, *slabs)


def attend_back_kernel(seg_ref, g_ref, w_out_ref, q_ref, k_ref, v_ref, att_ref, lse_ref,
                       cos_ref, sin_ref, d_ref, grad_ref, k_sum, v_sum,
                       *, block, window, scale, head_size):
    tokens = g_ref.shape[0]
    half = head_size // 2
    lanes = 2 * head_size
    lane = lax.broadcasted_iota(jnp.int32, (1, lanes), 1)
    first = lane < head_size
    starts = start_row(seg_ref)
    k_sum[...] = jnp.zeros_like(k_sum)
    v_sum[...] = jnp.zeros_like(v_sum)
    for low in range(0, tokens, block):
        rows = pl.ds(low, block)
        grad_ref[rows, :] = dot(g_ref[rows, :], w_out_ref[...], ((1,), (1,))).astype(BF)
    small = block // 2
    for low in range(0, tokens, small):
        begin = first_key(low, small, window)
        end = low + small
        count = end - begin
        q = q_ref[low:end, :] * jnp.asarray(scale, BF)
        grad = grad_ref[low:end, :]
        product = (grad.astype(F32) * att_ref[low:end, :].astype(F32)).T
        zero = jnp.zeros_like(q)
        q_two = jnp.concatenate([jnp.where(first, q, zero), jnp.where(first, zero, q)], axis=0)
        grad_two = jnp.concatenate(
            [jnp.where(first, grad, zero), jnp.where(first, zero, grad)], axis=0)
        k = k_ref[begin:end, :]
        scores = dot(k, q_two, ((1,), (1,)))
        prob_grad = dot(v_ref[begin:end, :], grad_two, ((1,), (1,)))
        key_index = lax.broadcasted_iota(jnp.int32, (count, small), 0) + begin
        query_index = lax.broadcasted_iota(jnp.int32, (count, small), 1) + low
        visible = (key_index.astype(F32) >= starts[:, low:end]) & (key_index <= query_index)
        visible = jnp.concatenate([visible, visible], axis=1)
        lse = jnp.concatenate([lse_ref[0, h:h + 1, low:end] for h in range(2)], axis=1)
        row_dots = jnp.concatenate(
            [jnp.sum(product[h * head_size:(h + 1) * head_size], axis=0, keepdims=True)
             for h in range(2)], axis=1)
        weights = jnp.where(visible, jnp.exp(scores - lse), 0.0)
        score_low = (weights * (prob_grad - row_dots)).astype(BF)
        v_sum[begin:end, :] += dot(weights.astype(BF), grad_two)
        k_sum[begin:end, :] += dot(score_low, q_two)
        dq = dot(score_low, k, ((0,), (0,))) * scale
        dq = jnp.where(first, dq[:small], dq[small:])
        d_ref[low:end, :lanes] = (
            dq * cos_ref[low:end, :] - turn(dq, half) * sin_ref[low:end, :]).astype(BF)
    for low in range(0, tokens, block):
        rows = pl.ds(low, block)
        dk = k_sum[rows, :]
        d_ref[rows, lanes:2 * lanes] = (
            dk * cos_ref[rows, :] - turn(dk, half) * sin_ref[rows, :]).astype(BF)
        d_ref[rows, 2 * lanes:] = v_sum[rows, :].astype(BF)

def attend_back(seg, g, w_out, q, k, v, att, lse, cosine, sine, window, head_size):
    tokens, width = g.shape
    lanes = 2 * head_size
    pairs = q.shape[1] // lanes
    kernel = lambda *refs: attend_back_kernel(
        *refs, block=256, window=window, scale=1.0 / math.sqrt(head_size), head_size=head_size)
    column = pl.BlockSpec((tokens, lanes), lambda p: (0, p))
    inputs = hbm(seg) + vmem(g) + hbm(w_out, q, k, v, att, lse, cosine, sine)
    return pl.pallas_call(
        kernel,
        grid=(pairs,),
        in_specs=whole_specs(seg) + [
            VMEM_SPEC,
            pl.BlockSpec((lanes, width), lambda p: (p, 0)),
            column, column, column, column,
            pl.BlockSpec((1, 8, tokens), lambda p: (p, 0, 0)),
        ] + whole_specs(cosine, sine),
        out_specs=pl.BlockSpec((tokens, 3 * lanes), lambda p: (0, p)),
        out_shape=jax.ShapeDtypeStruct((tokens, 3 * lanes * pairs), BF),
        scratch_shapes=[
            pltpu.VMEM((tokens, lanes), BF),
            pltpu.VMEM((tokens, lanes), F32),
            pltpu.VMEM((tokens, lanes), F32),
        ],
        compiler_params=pltpu.CompilerParams(vmem_limit_bytes=28 << 20),
        cost_estimate=SMALL_COST,
        name="attend_back",
    )(*inputs)


def join_kernel(rank_ref, own_ref, other_ref, *out_refs, moves, plain):
    swapped = rank_ref[0] == 1
    own, other = own_ref[...], other_ref[...]
    halves = (jnp.where(swapped, other, own), jnp.where(swapped, own, other))
    for out, half, (rows, cols), (to_rows, to_cols) in moves:
        out_refs[out][to_rows, to_cols] = halves[half][rows, cols].astype(F32)
    for out, (rows, cols) in plain:
        out_refs[out][...] = own[rows, cols].astype(F32)


def join(rank, own, other, moves, plain, shapes):
    kernel = lambda *refs: join_kernel(*refs, moves=moves, plain=plain)
    return pl.pallas_call(
        kernel,
        in_specs=[
            pl.BlockSpec(memory_space=pltpu.SMEM),
            pl.BlockSpec(memory_space=pltpu.VMEM),
            pl.BlockSpec(memory_space=pltpu.VMEM),
        ],
        out_specs=[pl.BlockSpec(memory_space=pltpu.VMEM)] * len(shapes),
        out_shape=[jax.ShapeDtypeStruct(shape, F32) for shape in shapes],
        compiler_params=pltpu.CompilerParams(vmem_limit_bytes=32 << 20),
        name="join",
    )(rank.reshape(1), own, other)


def join_all_kernel(all_ref, *refs, moves):
    out_refs, whole_ref = refs[:-1], refs[-1]
    groups, ranks, rows, _ = all_ref.shape
    for h in range(ranks):
        for m in range(groups):
            whole_ref[h, m * rows:(m + 1) * rows, :] = all_ref[m, h]
    for out, half, (rows, cols), (to_rows, to_cols) in moves:
        out_refs[out][to_rows, to_cols] = whole_ref[half, rows, cols].astype(F32)


def join_all(parts, moves, shapes):
    groups, ranks, rows, cols = parts.shape
    parts, = hbm(parts)
    return pl.pallas_call(
        lambda *refs: join_all_kernel(*refs, moves=moves),
        grid=(1,),
        in_specs=whole_specs(parts),
        out_specs=[pl.BlockSpec(shape, lambda i: (0, 0)) for shape in shapes],
        out_shape=[jax.ShapeDtypeStruct(shape, F32) for shape in shapes],
        scratch_shapes=[pltpu.VMEM((ranks, groups * rows, cols), BF)],
        compiler_params=pltpu.CompilerParams(vmem_limit_bytes=32 << 20),
        cost_estimate=SMALL_COST,
        name="join_all",
    )(parts)


def make_body(groups, ranks, fsdp, square):
    F = ("y", "x") if square else ("f",)
    swap = [(0, 1), (1, 0)]
    pairs = square and ranks == 2 and groups == 4

    def hop(value, k):
        return lax.ppermute(value, "m", [(i, i ^ k) for i in range(groups)])

    def after(value, *earlier):
        return lax.optimization_barrier((value,) + earlier)[0]

    def between(slabs, value):
        hops, value = lax.optimization_barrier((slabs[1:], value))
        return slabs[:1] + hops, value

    def spread(slabs):
        return [hop(slab, k) if k else slab for k, slab in enumerate(slabs)]

    def both_ranks(where, slabs, span):
        if ranks == 2:
            return slabs + [lax.ppermute(slab, "r", swap) for slab in slabs]
        rows = lax.all_gather(stack(where, slabs)[:, 0], "r", axis=1)
        return [rows[:, :, :span].reshape(-1, rows.shape[-1]), rows]

    def share(part):
        if ranks == 2:
            other = lax.ppermute(part, "r", swap)
            mine_first = lax.axis_index("r") == 0
            return jnp.stack(
                [jnp.where(mine_first, part, other), jnp.where(mine_first, other, part)], axis=1)
        return lax.all_gather(part, "r", axis=1)

    def exchange(part):
        if ranks == 2:
            return part, lax.ppermute(part, "r", swap)
        return lax.psum(part, "r"), jnp.zeros_like(part)

    def gather_rows(part, wait=()):
        if not square:
            whole = lax.all_gather(part, F, axis=0, tiled=True)
            return [whole], [(None, 0, 0)], (), ()
        count = part.shape[0]
        rows = (count // 2) // 16 * 16
        send = after(part, *wait) if wait else part
        from_x = lax.ppermute(send, "x", swap)
        from_y = lax.ppermute(send, "y", swap)
        far_a = lax.ppermute(from_y[:rows], "x", swap)
        far_b = lax.ppermute(from_x[rows:], "y", swap)
        pieces = [(0, 0, count), (1, 0, count), (2, 0, count), (3, 0, rows), (3, rows, count - rows)]
        return [part, from_x, from_y, far_a, far_b], pieces, (from_x, from_y), (far_a, far_b)

    def add(*parts):
        return sum(part.astype(F32) for part in parts).astype(BF)

    def take(grad, k):
        return lax.dynamic_index_in_dim(grad, lax.axis_index(F) ^ k, 0, keepdims=False)

    def half_rows(grad):
        return (grad.shape[1] // 2) // 16 * 16

    def round_one(grad):
        far, rows = take(grad, 3), half_rows(grad)
        return lax.ppermute(far[:rows], "x", swap), lax.ppermute(far[rows:], "y", swap)

    def second_terms(grad, low, high):
        to_x, to_y, rows = take(grad, 1), take(grad, 2), half_rows(grad)
        to_x = jnp.concatenate([to_x[:rows], add(to_x[rows:], high)], axis=0)
        to_y = jnp.concatenate([add(to_y[:rows], low), to_y[rows:]], axis=0)
        return to_x, to_y

    def round_two(to_x, to_y):
        return lax.ppermute(to_x, "x", swap), lax.ppermute(to_y, "y", swap)

    def halve(owned, bit, axis):
        half = owned.shape[axis] // 2
        side = (lax.axis_index("m") // bit) % 2
        return (lax.dynamic_slice_in_dim(owned, (1 - side) * half, half, axis),
                lax.dynamic_slice_in_dim(owned, side * half, half, axis))

    def join_halves(owned, other, bit, axis):
        first = (lax.axis_index("m") // bit) % 2 == 0
        return jnp.concatenate(
            [jnp.where(first, owned, other), jnp.where(first, other, owned)], axis=axis)

    def reduce(grad):
        return lax.psum(lax.psum_scatter(grad, F, scatter_dimension=0, tiled=False), "m")

    def body(tokens, segments, w_query, w_key, w_value, w_out, w_gate, w_up, w_down,
             gain_attn, gain_ffn, cotangent):
        micro, _, span, width = tokens.shape
        head_size = width // HEADS
        seq_tokens = span * groups * ranks
        window = seq_tokens // 2
        rank = lax.axis_index("r")
        own_cols = width // ranks
        shard = w_query.shape[0]
        down_rows = w_down.shape[0]
        part_rows = down_rows // ranks
        ff = w_gate.shape[1]
        half_ff = ff // ranks

        lanes = 2 * head_size
        lanes_all = -(-own_cols // lanes) * lanes
        spare = lanes_all - own_cols
        block = span * ranks
        f_index = lax.axis_index(F)
        where = jnp.stack([f_index, lax.axis_index("m"), rank])
        small_cols = 3 * lanes_all + own_cols
        gains_in = jnp.pad(jnp.stack([gain_attn, gain_ffn]), ((0, 14), (0, 0)))
        stack_own = pack(where, w_gate, w_up, w_down, fsdp, ranks)
        stack_all = lax.all_gather(stack_own, F, axis=0)
        cosine, sine = rotary_tables(seq_tokens, head_size, 2)
        small, *slabs = pack_small(
            after(where, stack_own), w_query, w_key, w_value, w_out, gains_in, tokens,
            segments[:, 0], cotangent, ranks, lanes, lanes_all)
        token_slabs, cot_slabs = slabs[:groups], slabs[groups:]
        token_slabs = spread(token_slabs)
        small_refs, small_pieces, near, far = gather_rows(small)
        if square:
            cot_slabs = cot_slabs[:1] + [after(slab, *token_slabs) for slab in cot_slabs[1:]]
        cot_slabs = spread(cot_slabs)
        if square:
            token_slabs = token_slabs[:1] + [
                after(slab, cosine, sine) for slab in token_slabs[1:]]
        token_refs = both_ranks(where, token_slabs, span)
        if ranks != 2:
            seg = token_refs[1][:, :, span, :span].reshape(1, seq_tokens).astype(F32)
            token_refs = [token_refs[0], seg]
        if square:
            own, from_x, from_y, far_a, far_b = small_refs
            at = far_a.shape[0]
            ends = [own, from_x, from_y, jnp.concatenate([far_a, far_b[:shard - at]], axis=0)]
            tails = [v[shard:shard + 2, :shard] for v in (own, from_x, from_y)]
            tails.append(far_b[shard - at:shard - at + 2, :shard])
            gains = jnp.zeros((fsdp, 2, shard), BF)
            out_cols = jnp.zeros((width, own_cols), BF)
            for offset in range(4):
                to = (f_index ^ offset) * shard
                gains = lax.dynamic_update_index_in_dim(gains, tails[offset], f_index ^ offset, 0)
                out_cols = lax.dynamic_update_slice_in_dim(
                    out_cols, ends[offset][:shard, 3 * lanes_all:], to, 0)
            gains = gains.transpose(1, 0, 2).reshape(2, width)
            small_pieces = [(o, f, min(n, shard - f)) for o, f, n in small_pieces]
            qkv_refs = small_refs
        else:
            whole = small_refs[0].reshape(fsdp, shard + 16, small_cols)
            gains = whole[:, shard:shard + 2, :shard].transpose(1, 0, 2).reshape(2, width)
            out_cols = whole[:, :shard, 3 * lanes_all:].reshape(width, own_cols)
            qkv_refs = [whole[:, :shard, :3 * lanes_all].reshape(width, 3 * lanes_all)]
        gains = gains.astype(F32)
        gain_one = gains[0:1]
        if ranks == 2:
            give = lax.dynamic_slice_in_dim(out_cols, (1 - rank) * own_cols, own_cols, 0)
            keep = lax.dynamic_slice_in_dim(out_cols, rank * own_cols, own_cols, 0)
            got = lax.ppermute(give, "r", swap)
            w_out_own = jnp.where(rank == 0, jnp.concatenate([keep, got], 1),
                                  jnp.concatenate([got, keep], 1))
        else:
            pieces = lax.all_to_all(out_cols, "r", 0, 0, tiled=True)
            pieces = pieces.reshape(ranks, own_cols, own_cols)
            w_out_own = jnp.concatenate([pieces[i] for i in range(ranks)], axis=1)
        w_out_even = jnp.pad(w_out_own, ((0, spare), (0, 0)))

        q, k, v, att, lse, w_qkv, x, seg = attend(
            where, after(cosine, gains, gain_one), sine, token_refs, ranks, qkv_refs, small_pieces, shard, lanes_all,
            window, head_size, width)
        if square:
            cot_slabs, att = between(cot_slabs, att)
        own, got = exchange(dot(att, w_out_even).astype(BF))
        cot_refs = both_ranks(where, cot_slabs, span)
        if ranks != 2:
            cot_refs = cot_refs[:1]
        total, middle_low, hidden_low, gate_back, silu, part, gu, down = forward(
            x, own, got, gain_one, stack_all, shard, part_rows, half_ff, block)
        own, got = exchange(part)

        *out_slabs, ffn_grad_low, gu_grad_low, part, gain_ffn_grad = backward(
            where, total, own, got, gate_back, silu, gains, gu, down, cot_refs, block, groups, ranks)
        own, got = exchange(part)
        gu_w_grad = dot(middle_low, gu_grad_low, ((0,), (0,))).astype(BF)
        if ranks == 2:
            got, gu_w_grad = lax.optimization_barrier((got, gu_w_grad))
        down_w_grad = dot(hidden_low, ffn_grad_low, ((0,), (0,))).astype(BF)
        stack_grad = arrange(gu_w_grad, down_w_grad, fsdp)
        stack_owned = lax.psum_scatter(stack_grad, F, scatter_dimension=0, tiled=False)
        own = after(own, stack_grad)
        branch_grad_low, branch_keep, gain_grads = norm_back(
            where[2:], total, ffn_grad_low, own, got, gain_one, gain_ffn_grad,
            fsdp, small_cols, block, span)
        out_w_grad = dot(att, branch_grad_low, ((0,), (0,)))[:own_cols].astype(BF)
        if ranks == 2:
            give = lax.dynamic_slice_in_dim(out_w_grad, (1 - rank) * own_cols, own_cols, 1)
            keep = lax.dynamic_slice_in_dim(out_w_grad, rank * own_cols, own_cols, 1)
            got = lax.ppermute(give, "r", swap)
            out_cols_grad = jnp.where(rank == 0, jnp.concatenate([keep, got], 0),
                                      jnp.concatenate([got, keep], 0))
        else:
            rows = out_w_grad.reshape(own_cols, ranks, own_cols).transpose(1, 0, 2)
            out_cols_grad = lax.all_to_all(rows, "r", 0, 0, tiled=True).reshape(width, own_cols)
        branch_grad_low = after(branch_grad_low, out_cols_grad)
        d_qkv = attend_back(
            seg, branch_grad_low, w_out_even, q, k, v, att, lse, cosine, sine, window, head_size)
        if square:
            out_slabs, d_qkv = between(spread(out_slabs), d_qkv)
        else:
            out_slabs = spread(out_slabs)
        output = stack(where, out_slabs)
        qkv_w_grad = dot(x, d_qkv, ((0,), (0,))).astype(BF)
        small_grad = jnp.concatenate([qkv_w_grad, out_cols_grad], axis=1)
        small_grad = jnp.concatenate(
            [small_grad.reshape(fsdp, shard, small_cols), gain_grads], axis=1)
        if pairs:
            small_one = round_one(small_grad)
            d_qkv = after(d_qkv, small_grad)
        part = dot(d_qkv, w_qkv, ((1,), (1,))).astype(BF)
        if ranks == 2:
            rows = part.reshape(groups, ranks, span, width)
            give = lax.dynamic_index_in_dim(rows, 1 - rank, 1, keepdims=False)
            got = lax.ppermute(give, "r", swap)
        else:
            part = lax.psum(part, "r")
            got = jnp.zeros_like(branch_keep, BF)
        grad_slabs = list(finish(where, branch_keep, part, got, ranks))
        grad_slabs = spread(grad_slabs)
        if pairs:
            grad_slabs[:3], small_one = between(grad_slabs[:3], small_one)
            terms = second_terms(small_grad, *small_one)
            small_two, output, grad_slabs[3] = lax.optimization_barrier(
                (round_two(*terms), output, grad_slabs[3]))
            input_grad = stack(where, grad_slabs)
            stack_owned = after(stack_owned, *terms)
            quarter = lax.psum_scatter(stack_owned, "m", scatter_dimension=0, tiled=True)
            give, keep = halve(add(take(small_grad, 0), *small_two), 1, 1)
            got, quarter, input_grad = lax.optimization_barrier((hop(give, 1), quarter, input_grad))
            stack_parts = lax.all_gather(quarter, ("m", "r"), axis=0)
            stack_parts = stack_parts.reshape((groups, ranks) + quarter.shape)
            give, keep = halve(add(keep, got), 2, 1)
            owned = add(keep, hop(give, 2))
            owned = join_halves(owned, hop(owned, 2), 2, 1)
            small_sum = join_halves(owned, hop(owned, 1), 1, 1)
        else:
            stack_sum = lax.psum(stack_owned, "m")
            small_sum = reduce(small_grad)
            input_grad = stack(where, grad_slabs)
        if pairs:
            everything = slice(None)
            chunks = 2 * half_ff // 256
            stack_moves = [
                (n, h, (slice((n * fsdp + j) * shard, (n * fsdp + j + 1) * shard), everything),
                 (everything, slice(j * down_rows + h * part_rows, j * down_rows + (h + 1) * part_rows)))
                for n in range(2) for h in range(2) for j in range(fsdp)]
            stack_moves += [
                (2, h, (slice(chunks * shard + c * part_rows, chunks * shard + (c + 1) * part_rows),
                        everything),
                 (slice(h * part_rows, (h + 1) * part_rows), slice(c * 256, (c + 1) * 256)))
                for h in range(2) for c in range(width // 256)]
            small_moves = [
                (n, h, (slice(0, shard), slice((3 * p + n) * lanes, (3 * p + n + 1) * lanes)),
                 (everything, slice(h * own_cols + p * lanes, h * own_cols + (p + 1) * lanes)))
                for n in range(3) for h in range(2) for p in range(own_cols // lanes)]
            small_moves += [
                (3, h, (slice(0, shard), slice(3 * lanes_all, small_cols)),
                 (everything, slice(h * own_cols, (h + 1) * own_cols))) for h in range(2)]
            small_plain = [
                (4 + n, (slice(shard + n, shard + n + 1), slice(0, shard))) for n in range(2)]
            gate_w, up_w, down_grad = join_all(
                stack_parts, stack_moves, [(shard, ff)] * 2 + [(down_rows, width)])
            query_w, key_w, value_w, out_w, gain_a, gain_f = join(
                rank, small_sum, lax.ppermute(small_sum, "r", swap), small_moves, small_plain,
                [(shard, width)] * 4 + [(1, shard)] * 2)
        else:
            at = 2 * half_ff // 256 * shard
            down_sum = jnp.moveaxis(stack_sum[at:].reshape(-1, part_rows, 256), 0, 1)
            down_grad = jnp.moveaxis(share(down_sum.reshape(part_rows, width)), 1, 0)
            down_grad = down_grad.reshape(down_rows, width).astype(F32)
            gu_sum = jnp.moveaxis(stack_sum[:at].reshape(-1, shard, 256), 0, 1)
            gu_both = share(gu_sum.reshape(shard, 2 * fsdp, part_rows))
            gu_both = gu_both.reshape(shard, ranks, 2, fsdp, part_rows).astype(F32)
            gate_w, up_w = (
                gu_both[:, :, n].transpose(0, 2, 1, 3).reshape(shard, ff) for n in range(2))
            small_both = share(small_sum)[:shard].astype(F32)
            three = small_both[:, :, :3 * lanes_all].reshape(shard, ranks, -1, 3, lanes)
            query_w, key_w, value_w = (
                three[:, :, :, n].reshape(shard, ranks, lanes_all)[:, :, :own_cols].reshape(shard, width)
                for n in range(3))
            out_w = small_both[:, :, 3 * lanes_all:].reshape(shard, width)
            gain_a, gain_f = small_sum[shard, :shard].astype(F32), small_sum[shard + 1, :shard].astype(F32)
        return (output, input_grad, query_w, key_w, value_w, out_w,
                gate_w, up_w, down_grad, gain_a.reshape(shard), gain_f.reshape(shard))

    return body


def solution(mesh):
    def run(*args):
        groups = args[0].shape[0]
        seq, fsdp = mesh.shape["seq"], mesh.shape["fsdp"]
        ranks = seq // groups
        square = fsdp == 4
        names = ("m", "r") + (("y", "x") if square else ("f",))
        sizes = (groups, ranks) + ((2, 2) if square else (fsdp,))
        order = [mesh.axis_names.index(name) for name in ("seq", "fsdp")]
        inner = Mesh(mesh.devices.transpose(order).reshape(sizes), names)
        f = ("y", "x") if square else "f"
        s = ("m", "r")
        rows = P(f, None)
        data = P(None, f, s, None)
        in_specs = (data, P(None, f, s)) + (rows,) * 7 + (P(f), P(f), data)
        out_specs = (data, data) + (rows,) * 7 + (P(f), P(f))
        body = make_body(groups, ranks, fsdp, square)
        return jax.shard_map(
            body, mesh=inner, in_specs=in_specs, out_specs=out_specs, check_vma=False)(*args)

    return run
```

```python
import math

import jax
import jax.numpy as jnp
from jax import lax
from jax.experimental import pallas as pl
from jax.experimental.pallas import tpu as pltpu
from jax.sharding import Mesh, PartitionSpec as P

HEADS = 12
DOCS = 4
EPS = 1e-06
NEGATIVE = -1e30
BF = jnp.bfloat16
F32 = jnp.float32


def dot(left, right, dims=((1,), (0,))):
    return lax.dot_general(left, right, (dims, ((), ())), preferred_element_type=F32)


def rotary_tables(seq_tokens, head_size, copies):
    half = head_size // 2
    frequency = 10000.0 ** (-jnp.arange(half, dtype=F32) / half)
    angle = jnp.arange(seq_tokens, dtype=jnp.int32).astype(F32)[:, None] * frequency[None, :]
    cosine, sine = jnp.cos(angle), jnp.sin(angle)
    return (
        jnp.concatenate([cosine, cosine] * copies, axis=1),
        jnp.concatenate([-sine, sine] * copies, axis=1),
    )


def turn(rows, half):
    lanes = rows.shape[1]
    lane = lax.broadcasted_iota(jnp.int32, (1, lanes), 1)
    low = (lane // half) % 2 == 0
    return jnp.where(low, pltpu.roll(rows, lanes - half, 1), pltpu.roll(rows, half, 1))


def first_key(query_first, block, window):
    return max(0, (query_first - window + 1) // block * block)


def start_row(seg_ref):
    seg = seg_ref[...]
    starts = jnp.zeros_like(seg)
    for doc in range(1, DOCS):
        before = jnp.sum(jnp.where(seg < doc, 1.0, 0.0), axis=1, keepdims=True)
        starts = jnp.maximum(starts, jnp.where(seg >= doc, before, 0.0))
    return starts


def place(target, refs, pieces, me, shard):
    for ref, (offset, first, rows) in zip(refs, pieces):
        if offset is None:
            target[...] = ref[...]
        else:
            start = pl.multiple_of((me ^ offset) * shard + first, 16)
            target[pl.ds(start, rows), :] = ref[0:rows, 0:target.shape[1]]


def place_tokens(target, refs, where_ref, ranks):
    if len(refs) == 1:
        target[...] = refs[0][...]
        return
    groups = len(refs) // ranks
    span = target.shape[0] // (groups * ranks)
    for n, ref in enumerate(refs):
        rank = where_ref[2] if n < groups else 1 - where_ref[2]
        chunk = (where_ref[1] ^ (n % groups)) * ranks + rank
        target[pl.ds(pl.multiple_of(chunk * span, span), span), :] = ref[0:span, :]


def place_segments(target, refs, where_ref, ranks):
    groups = len(refs) // ranks
    span = target.shape[1] // (groups * ranks)
    for n, ref in enumerate(refs):
        rank = where_ref[2] if n < groups else 1 - where_ref[2]
        chunk = (where_ref[1] ^ (n % groups)) * ranks + rank
        row = ref[span:span + 16, 0:span].astype(F32)[0:1, :]
        target[:, pl.ds(pl.multiple_of(chunk * span, span), span)] = row


def stack_copies(gu, down, stack_ref, sems, shard, part_rows):
    members, chunks, groups = stack_ref.shape[0], gu.shape[1] // 256, []
    for c in range(chunks):
        groups.append([
            pltpu.make_async_copy(
                stack_ref.at[j, c * shard:(c + 1) * shard, :],
                gu.at[j * shard:(j + 1) * shard, c * 256:(c + 1) * 256],
                sems.at[c, j]) for j in range(members)])
    for c in range(down.shape[1] // 256):
        at = chunks * shard + c * part_rows
        groups.append([
            pltpu.make_async_copy(
                stack_ref.at[j, at:at + part_rows, :],
                down.at[j * part_rows:(j + 1) * part_rows, c * 256:(c + 1) * 256],
                sems.at[chunks + c, j]) for j in range(members)])
    return groups


def attend_kernel(where_ref, cos_ref, sin_ref, *refs, pieces, token_count, ranks, shard, block,
                  window, scale, head_size):
    inputs, refs = refs[:-9], refs[-9:]
    q_ref, k_ref, v_ref, att_ref, lse_ref, w_ref, x_ref, seg_ref, col_ref = refs
    token_refs, w_refs = inputs[:token_count], inputs[token_count:]
    tokens = x_ref.shape[0]
    lanes = 2 * head_size
    lane = lax.broadcasted_iota(jnp.int32, (1, lanes), 1)
    first = lane < head_size
    pair = pl.program_id(0)

    @pl.when(pair == 0)
    def _():
        place(w_ref, w_refs, pieces, where_ref[0], shard)
        place_tokens(x_ref, token_refs[:1] if token_count == 2 else token_refs, where_ref, ranks)
        if token_count == 2:
            seg_ref[...] = token_refs[1][...]
        else:
            place_segments(seg_ref, token_refs, where_ref, ranks)
        starts = start_row(seg_ref)
        col_ref[...] = jnp.broadcast_to(starts, (128, tokens)).T

    w = w_ref[:, pl.ds(pl.multiple_of(pair * 3 * lanes, lanes), 3 * lanes)]
    for low in range(0, tokens, block):
        rows = pl.ds(low, block)
        lin = dot(x_ref[rows, :], w)
        cosine, sine = cos_ref[rows, :], sin_ref[rows, :]
        half = head_size // 2
        q_lin, k_lin = lin[:, :lanes], lin[:, lanes:2 * lanes]
        q_ref[rows, :] = (q_lin * cosine + turn(q_lin, half) * sine).astype(BF)
        k_ref[rows, :] = (k_lin * cosine + turn(k_lin, half) * sine).astype(BF)
        v_ref[rows, :] = lin[:, 2 * lanes:].astype(BF)
    for low in range(0, tokens, block):
        begin = first_key(low, block, window)
        end = low + block
        q = q_ref[low:end, :] * jnp.asarray(scale, BF)
        zero = jnp.zeros_like(q)
        stacked = jnp.concatenate([jnp.where(first, q, zero), jnp.where(first, zero, q)], axis=0)
        scores = dot(stacked, k_ref[begin:end, :], ((1,), (1,)))
        key_index = lax.broadcasted_iota(jnp.int32, (block, end - begin), 1) + begin
        query_index = lax.broadcasted_iota(jnp.int32, (block, end - begin), 0) + low
        visible = (key_index.astype(F32) >= col_ref[low:end, 0:1]) & (key_index <= query_index)
        parts = []
        for head in range(2):
            own = jnp.where(visible, scores[head * block:(head + 1) * block], NEGATIVE)
            top = jnp.max(own, axis=1, keepdims=True)
            weights = jnp.exp(own - top)
            total = jnp.sum(weights, axis=1, keepdims=True)
            out = dot(weights.astype(BF), v_ref[begin:end, :]) / total
            parts.append(out)
            lse = jnp.broadcast_to(top + jnp.log(total), (block, 128))
            lse_ref[0, head:head + 1, low:end] = lse.T[0:1, :]
        att_ref[low:end, :] = jnp.where(first, parts[0], parts[1]).astype(BF)


def hbm(*arrays):
    return [pltpu.with_memory_space_constraint(a, pltpu.HBM) for a in arrays]


def vmem(*arrays):
    return [pltpu.with_memory_space_constraint(a, pltpu.VMEM) for a in arrays]


def whole_specs(*arrays):
    return [pl.BlockSpec(a.shape, lambda *_, n=a.ndim: (0,) * n, pipeline_mode=pl.Buffered(1))
            for a in arrays]


SMALL_COST = pl.CostEstimate(flops=1, bytes_accessed=1, transcendentals=0)
VMEM_SPEC = pl.BlockSpec(memory_space=pltpu.VMEM)
SMEM_SPEC = pl.BlockSpec(memory_space=pltpu.SMEM)


def attend(where, cosine, sine, token_refs, ranks, weights, pieces, shard, lanes_all, window,
           head_size, width):
    tokens = cosine.shape[0]
    lanes = 2 * head_size
    pairs = lanes_all // lanes
    kernel = lambda *refs: attend_kernel(
        *refs, pieces=pieces, token_count=len(token_refs), ranks=ranks, shard=shard, block=256,
        window=window, scale=1.0 / math.sqrt(head_size), head_size=head_size)
    column = pl.BlockSpec((tokens, lanes), lambda p: (0, p))
    whole = lambda *shape: pl.BlockSpec(shape, lambda p: (0, 0))
    inputs = hbm(cosine, sine, *token_refs, *weights)
    return pl.pallas_call(
        kernel,
        grid=(pairs,),
        in_specs=[SMEM_SPEC] + whole_specs(*inputs),
        out_specs=[column, column, column, column,
                   pl.BlockSpec((1, 8, tokens), lambda p: (p, 0, 0)),
                   whole(width, 3 * lanes_all), whole(tokens, width), whole(1, tokens)],
        out_shape=[pltpu.HBM((tokens, lanes_all), BF)] * 4
        + [pltpu.HBM((pairs, 8, tokens), F32), pltpu.HBM((width, 3 * lanes_all), BF),
           pltpu.HBM((tokens, width), BF), pltpu.HBM((1, tokens), F32)],
        scratch_shapes=[pltpu.VMEM((tokens, 128), F32)],
        compiler_params=pltpu.CompilerParams(vmem_limit_bytes=28 << 20),
        cost_estimate=SMALL_COST,
        name="attend",
    )(where, *inputs)


def unit_of(rows):
    factor = lax.rsqrt(jnp.mean(rows * rows, axis=1, keepdims=True) + EPS)
    return rows * factor, factor


def forward_kernel(x_ref, own_ref, got_ref, gain_ref, stack_ref, sum_ref, low_ref, hidden_ref,
                   gate_ref, silu_ref, part_ref, gu, down, sems, *, shard, part_rows):
    step, block = pl.program_id(0), x_ref.shape[0]
    ff = down.shape[0]

    @pl.when(step == 0)
    def _():
        copies = stack_copies(gu, down, stack_ref, sems, shard, part_rows)
        for group in copies:
            for copy in group:
                copy.start()
        for group in copies:
            for copy in group:
                copy.wait()

    rows = pl.ds(pl.multiple_of(step * block, block), block)
    total = x_ref[...].astype(F32) + own_ref[...].astype(F32) + got_ref[...].astype(F32)
    sum_ref[rows, :] = total
    middle_low = (unit_of(total)[0] * gain_ref[...]).astype(BF)
    low_ref[rows, :] = middle_low
    for c in range(0, ff, 256):
        cols = slice(c, c + 256)
        gate = dot(middle_low, gu[:, cols])
        up = dot(middle_low, gu[:, ff + c:ff + c + 256])
        sigmoid = jax.nn.sigmoid(gate)
        silu = gate * sigmoid
        hidden_ref[rows, cols] = (silu * up).astype(BF)
        gate_ref[rows, cols] = (up * sigmoid * (1.0 + gate * (1.0 - sigmoid))).astype(BF)
        silu_ref[rows, cols] = silu.astype(BF)
    part_ref[...] = dot(hidden_ref[rows, :], down[...]).astype(BF)


HBM_SPEC = pl.BlockSpec(memory_space=pltpu.HBM)


def forward(x, own, got, gain, stack, shard, part_rows, ff, block):
    tokens, width = x.shape
    row = lambda cols: pl.BlockSpec((block, cols), lambda i: (i, 0))
    x, own, got, stack = hbm(x, own, got, stack)
    return pl.pallas_call(
        lambda *refs: forward_kernel(*refs, shard=shard, part_rows=part_rows),
        grid=(tokens // block,),
        in_specs=[row(width), row(width), row(width)] + whole_specs(gain) + [HBM_SPEC],
        out_specs=[VMEM_SPEC] * 5 + [row(width)] + [VMEM_SPEC] * 2,
        out_shape=[pltpu.VMEM((tokens, width), F32), pltpu.VMEM((tokens, width), BF)]
        + [pltpu.VMEM((tokens, ff), BF)] * 3 + [jax.ShapeDtypeStruct((tokens, width), BF)]
        + [pltpu.VMEM((width, 2 * ff), BF), pltpu.VMEM((ff, width), BF)],
        scratch_shapes=[pltpu.SemaphoreType.DMA(((2 * ff + width) // 256, stack.shape[0]))],
        compiler_params=pltpu.CompilerParams(vmem_limit_bytes=16 << 20),
        cost_estimate=SMALL_COST,
        name="ffn_forward",
    )(x, own, got, gain, stack)


def backward_kernel(where_ref, sum_ref, own_ref, got_ref, gate_ref, silu_ref, gains_ref, gu, down,
                    *refs, cot_count, groups, ranks):
    cot_refs, refs = refs[:cot_count], refs[cot_count:]
    out_refs, refs = refs[:groups], refs[groups:]
    low_ref, gu_grad_ref, part_ref, gain_ref, cot_ref, rows_ref = refs
    step = pl.program_id(0)
    block, span = rows_ref.shape[0], out_refs[0].shape[0]

    @pl.when(step == 0)
    def _():
        place_tokens(cot_ref, cot_refs, where_ref, ranks)
        gain_ref[...] = jnp.zeros_like(gain_ref)

    rows = pl.ds(pl.multiple_of(step * block, block), block)
    gain_two = gains_ref[1:2, :]
    middle = unit_of(sum_ref[rows, :])[0] * gains_ref[0:1, :]
    unit, factor = unit_of(middle + own_ref[...].astype(F32) + got_ref[...].astype(F32))
    rows_ref[...] = unit * gain_two
    cot = cot_ref[rows, :].astype(F32)
    gain_ref[...] += jnp.sum(cot * unit, axis=0, keepdims=True)
    scaled = cot * gain_two
    grad_low = (factor * (scaled - unit * jnp.mean(scaled * unit, axis=1, keepdims=True))).astype(BF)
    low_ref[rows, :] = grad_low
    ff = down.shape[0]
    for c in range(0, ff, 256):
        cols = slice(c, c + 256)
        hidden_grad = dot(grad_low, down[cols, :], ((1,), (1,)))
        gu_grad_ref[rows, cols] = (hidden_grad * gate_ref[rows, cols].astype(F32)).astype(BF)
        gu_grad_ref[rows, ff + c:ff + c + 256] = (
            hidden_grad * silu_ref[rows, cols].astype(F32)).astype(BF)
    part_ref[...] = dot(gu_grad_ref[rows, :], gu[...], ((1,), (1,))).astype(BF)
    kept = rows_ref[pl.ds(pl.multiple_of(where_ref[2] * span, span), span), :].astype(BF)
    for k, out_ref in enumerate(out_refs):
        @pl.when(step == (where_ref[1] ^ k))
        def _(out_ref=out_ref):
            out_ref[...] = kept


def backward(where, total, own, got, gate, silu, gains, gu, down, cot, block, groups, ranks):
    tokens, width = total.shape
    ff = gate.shape[1]
    kernel = lambda *refs: backward_kernel(
        *refs, cot_count=len(cot), groups=groups, ranks=ranks)
    row = pl.BlockSpec((block, width), lambda i: (i, 0))
    slab = pl.BlockSpec((block // ranks, width), lambda i: (0, 0))
    total, gate, silu, gu, down = vmem(total, gate, silu, gu, down)
    return pl.pallas_call(
        kernel,
        grid=(tokens // block,),
        in_specs=[SMEM_SPEC, VMEM_SPEC, row, row, VMEM_SPEC, VMEM_SPEC] + whole_specs(gains)
        + [VMEM_SPEC] * 2 + whole_specs(*cot),
        out_specs=[slab] * groups + [VMEM_SPEC, VMEM_SPEC, row,
                                     pl.BlockSpec((1, width), lambda i: (0, 0))],
        out_shape=[pltpu.HBM((block // ranks, width), BF)] * groups
        + [pltpu.VMEM((tokens, width), BF), pltpu.VMEM((tokens, 2 * ff), BF),
           pltpu.HBM((tokens, width), BF), pltpu.HBM((1, width), F32)],
        scratch_shapes=[pltpu.VMEM((tokens, width), BF), pltpu.VMEM((block, width), F32)],
        compiler_params=pltpu.CompilerParams(vmem_limit_bytes=20 << 20),
        cost_estimate=SMALL_COST,
        name="ffn_backward",
    )(where, total, own, got, gate, silu, gains, gu, down, *cot)


def norm_back_kernel(rank_ref, sum_ref, grad_ref, own_ref, got_ref, gain_ref, other_ref,
                     low_ref, keep_ref, out_ref, rows_ref, gain_grad_ref):
    step, block = pl.program_id(0), rows_ref.shape[0]

    @pl.when(step == 0)
    def _():
        gain_grad_ref[...] = jnp.zeros_like(gain_grad_ref)

    rows = pl.ds(pl.multiple_of(step * block, block), block)
    unit, factor = unit_of(sum_ref[rows, :])
    grad = (grad_ref[...].astype(F32) + own_ref[...].astype(F32)) + got_ref[...].astype(F32)
    gain_grad_ref[...] += jnp.sum(grad * unit, axis=0, keepdims=True)
    scaled = grad * gain_ref[...]
    branch_grad = factor * (scaled - unit * jnp.mean(scaled * unit, axis=1, keepdims=True))
    low_ref[rows, :] = branch_grad.astype(BF)
    rows_ref[...] = branch_grad
    span = keep_ref.shape[1]
    keep_ref[0] = rows_ref[pl.ds(pl.multiple_of(rank_ref[0] * span, span), span), :]

    @pl.when(step == pl.num_programs(0) - 1)
    def _():
        out_ref[...] = jnp.zeros_like(out_ref)
        shard = gain_ref.shape[1] // out_ref.shape[0]
        first = lax.broadcasted_iota(jnp.int32, (16, shard), 0)
        for j in range(out_ref.shape[0]):
            lanes = slice(j * shard, (j + 1) * shard)
            one = jnp.broadcast_to(gain_grad_ref[:, lanes], (16, shard))
            two = jnp.broadcast_to(other_ref[:, lanes], (16, shard))
            out_ref[j, :, 0:shard] = jnp.where(
                first == 0, one, jnp.where(first == 1, two, 0.0)).astype(BF)


def norm_back(rank, total, grad, own, got, gain, other_grad, fsdp, cols, block, span):
    tokens, width = total.shape
    row = pl.BlockSpec((block, width), lambda i: (i, 0))
    inputs = vmem(total) + hbm(grad, own, got)
    return pl.pallas_call(
        norm_back_kernel,
        grid=(tokens // block,),
        in_specs=[SMEM_SPEC, VMEM_SPEC, row, row, row] + whole_specs(gain, other_grad),
        out_specs=[VMEM_SPEC, pl.BlockSpec((1, span, width), lambda i: (i, 0, 0)),
                   pl.BlockSpec((fsdp, 16, cols), lambda i: (0, 0, 0))],
        out_shape=[pltpu.VMEM((tokens, width), BF),
                   pltpu.HBM((tokens // block, span, width), F32),
                   pltpu.HBM((fsdp, 16, cols), BF)],
        scratch_shapes=[pltpu.VMEM((block, width), F32), pltpu.VMEM((1, width), F32)],
        compiler_params=pltpu.CompilerParams(vmem_limit_bytes=16 << 20),
        cost_estimate=SMALL_COST,
        name="norm_back",
    )(rank, *inputs, gain, other_grad)


def pick(rank, parts):
    value = parts[0]
    for r in range(1, len(parts)):
        value = jnp.where(rank == r, parts[r], value)
    return value


def pack_small_kernel(where_ref, query_ref, key_ref, value_ref, out_ref, gain_ref, tokens_ref,
                      seg_ref, cot_ref, small_ref, *slab_refs, ranks, lanes, lanes_all):
    slab_refs, cot_slabs = slab_refs[:len(slab_refs) // 2], slab_refs[len(slab_refs) // 2:]
    for k, ref in enumerate(cot_slabs):
        ref[...] = cot_ref[where_ref[1] ^ k, 0]
    rank, m = where_ref[2], where_ref[1]
    shard, width = query_ref.shape
    own_cols = width // ranks
    if lanes_all != own_cols:
        small_ref[...] = jnp.zeros_like(small_ref)
    for n, ref in enumerate((query_ref, key_ref, value_ref)):
        for low in range(0, own_cols, lanes):
            size = min(lanes, own_cols - low)
            at = (low // lanes * 3 + n) * lanes
            small_ref[0:shard, at:at + size] = pick(
                rank, [ref[:, r * own_cols + low:r * own_cols + low + size] for r in range(ranks)])
    small_ref[0:shard, 3 * lanes_all:] = pick(
        rank, [out_ref[:, r * own_cols:(r + 1) * own_cols] for r in range(ranks)])
    small_ref[shard:, :] = jnp.zeros_like(small_ref[shard:, :])
    small_ref[shard:, 0:shard] = gain_ref[...]
    span = tokens_ref.shape[2]
    for k, ref in enumerate(slab_refs):
        ref[0:span, :] = tokens_ref[m ^ k, 0]
        ref[span:, :] = jnp.zeros_like(ref[span:, :])
        row = seg_ref[pl.ds(m ^ k, 1), :].astype(F32)
        ref[span:, 0:span] = jnp.broadcast_to(row, (16, span)).astype(BF)


def pack_small(where, query, key, value, out, gains, tokens, segments, cot, ranks, lanes,
               lanes_all):
    shard, width = query.shape
    groups, _, span, _ = tokens.shape
    cols = 3 * lanes_all + width // ranks
    inputs = hbm(query, key, value, out, gains, tokens, segments, cot)
    shapes = [(shard + 16, cols)] + [(span + 16, width)] * groups + [(span, width)] * groups
    return pl.pallas_call(
        lambda *refs: pack_small_kernel(*refs, ranks=ranks, lanes=lanes, lanes_all=lanes_all),
        grid=(1,),
        in_specs=[SMEM_SPEC] + whole_specs(*inputs),
        out_specs=[pl.BlockSpec(shape, lambda i: (0, 0)) for shape in shapes],
        out_shape=[pltpu.HBM(shape, BF) for shape in shapes],
        compiler_params=pltpu.CompilerParams(vmem_limit_bytes=24 << 20),
        cost_estimate=SMALL_COST,
        name="pack_small",
    )(where, *inputs)


def pack_kernel(where_ref, gate_ref, up_ref, down_ref, out_ref, gu, *, fsdp, ranks):
    rank = where_ref[2]
    shard, cols = gu.shape
    part = down_ref.shape[0] // ranks
    for n, ref in enumerate((gate_ref, up_ref)):
        for j in range(fsdp):
            low = (n * fsdp + j) * part
            gu[:, low:low + part] = pick(
                rank, [ref[:, (j * ranks + r) * part:(j * ranks + r + 1) * part]
                       for r in range(ranks)])
    chunks = cols // 256
    for c in range(chunks):
        out_ref[c * shard:(c + 1) * shard, :] = gu[:, c * 256:(c + 1) * 256]
    rows = pl.ds(pl.multiple_of(rank * part, 16), part)
    for c in range(down_ref.shape[1] // 256):
        at = chunks * shard + c * part
        out_ref[at:at + part, :] = down_ref[rows, c * 256:(c + 1) * 256]


def pack(where, gate, up, down, fsdp, ranks):
    shard, ff = gate.shape
    cols = 2 * ff // ranks
    rows = cols // 256 * shard + down.shape[1] // 256 * (down.shape[0] // ranks)
    inputs = hbm(gate, up, down)
    return pl.pallas_call(
        lambda *refs: pack_kernel(*refs, fsdp=fsdp, ranks=ranks),
        grid=(1,),
        in_specs=[SMEM_SPEC] + whole_specs(*inputs),
        out_specs=pl.BlockSpec((rows, 256), lambda i: (0, 0)),
        out_shape=pltpu.HBM((rows, 256), BF),
        scratch_shapes=[pltpu.VMEM((shard, cols), BF)],
        compiler_params=pltpu.CompilerParams(vmem_limit_bytes=24 << 20),
        cost_estimate=SMALL_COST,
        name="pack",
    )(where, *inputs)


def arrange_kernel(gu_ref, down_ref, out_ref):
    shard, part = gu_ref.shape[0], down_ref.shape[0]
    chunks = gu_ref.shape[1] // 256
    for c in range(chunks):
        out_ref[0, c * shard:(c + 1) * shard, :] = gu_ref[:, c * 256:(c + 1) * 256]
    for c in range(down_ref.shape[1] // 256):
        at = chunks * shard + c * part
        out_ref[0, at:at + part, :] = down_ref[:, c * 256:(c + 1) * 256]


def arrange(gu, down, fsdp):
    shard, part = gu.shape[0] // fsdp, down.shape[0] // fsdp
    rows = gu.shape[1] // 256 * shard + down.shape[1] // 256 * part
    return pl.pallas_call(
        arrange_kernel,
        grid=(fsdp,),
        in_specs=[pl.BlockSpec((shard, gu.shape[1]), lambda j: (j, 0)),
                  pl.BlockSpec((part, down.shape[1]), lambda j: (j, 0))],
        out_specs=pl.BlockSpec((1, rows, 256), lambda j: (j, 0, 0)),
        out_shape=pltpu.HBM((fsdp, rows, 256), BF),
        compiler_params=pltpu.CompilerParams(vmem_limit_bytes=24 << 20),
        cost_estimate=SMALL_COST,
        name="arrange",
    )(gu, down)


def finish_kernel(where_ref, keep_ref, part_ref, got_ref, *out_refs, ranks):
    groups, span, _ = keep_ref.shape
    for k, ref in enumerate(out_refs):
        group = where_ref[1] ^ k
        row = (group * ranks + where_ref[2]) * span
        own = part_ref[pl.ds(pl.multiple_of(row, span), span), :].astype(F32)
        ref[...] = (keep_ref[group] + own + got_ref[group].astype(F32)).astype(BF)


def finish(where, keep, part, got, ranks):
    groups, span, width = keep.shape
    return pl.pallas_call(
        lambda *refs: finish_kernel(*refs, ranks=ranks),
        in_specs=[SMEM_SPEC] + [VMEM_SPEC] * 3,
        out_specs=[VMEM_SPEC] * groups,
        out_shape=[jax.ShapeDtypeStruct((span, width), BF)] * groups,
        compiler_params=pltpu.CompilerParams(vmem_limit_bytes=24 << 20),
        cost_estimate=SMALL_COST,
        name="finish",
    )(where, keep, part, got)


def stack_kernel(where_ref, *refs):
    out_ref = refs[-1]
    for k, ref in enumerate(refs[:-1]):
        out_ref[where_ref[1] ^ k, 0] = ref[...]


def stack(where, slabs):
    span, width = slabs[0].shape
    return pl.pallas_call(
        stack_kernel,
        in_specs=[SMEM_SPEC] + [VMEM_SPEC] * len(slabs),
        out_specs=VMEM_SPEC,
        out_shape=jax.ShapeDtypeStruct((len(slabs), 1, span, width), BF),
        compiler_params=pltpu.CompilerParams(vmem_limit_bytes=16 << 20),
        cost_estimate=SMALL_COST,
        name="stack",
    )(where, *slabs)


def attend_back_kernel(seg_ref, g_ref, w_out_ref, q_ref, k_ref, v_ref, att_ref, lse_ref,
                       cos_ref, sin_ref, d_ref, grad_ref, k_sum, v_sum,
                       *, block, window, scale, head_size):
    tokens = g_ref.shape[0]
    half = head_size // 2
    lanes = 2 * head_size
    lane = lax.broadcasted_iota(jnp.int32, (1, lanes), 1)
    first = lane < head_size
    starts = start_row(seg_ref)
    k_sum[...] = jnp.zeros_like(k_sum)
    v_sum[...] = jnp.zeros_like(v_sum)
    for low in range(0, tokens, block):
        rows = pl.ds(low, block)
        grad_ref[rows, :] = dot(g_ref[rows, :], w_out_ref[...], ((1,), (1,))).astype(BF)
    small = block // 2
    for low in range(0, tokens, small):
        begin = first_key(low, small, window)
        end = low + small
        count = end - begin
        q = q_ref[low:end, :] * jnp.asarray(scale, BF)
        grad = grad_ref[low:end, :]
        product = (grad.astype(F32) * att_ref[low:end, :].astype(F32)).T
        zero = jnp.zeros_like(q)
        q_two = jnp.concatenate([jnp.where(first, q, zero), jnp.where(first, zero, q)], axis=0)
        grad_two = jnp.concatenate(
            [jnp.where(first, grad, zero), jnp.where(first, zero, grad)], axis=0)
        k = k_ref[begin:end, :]
        scores = dot(k, q_two, ((1,), (1,)))
        prob_grad = dot(v_ref[begin:end, :], grad_two, ((1,), (1,)))
        key_index = lax.broadcasted_iota(jnp.int32, (count, small), 0) + begin
        query_index = lax.broadcasted_iota(jnp.int32, (count, small), 1) + low
        visible = (key_index.astype(F32) >= starts[:, low:end]) & (key_index <= query_index)
        visible = jnp.concatenate([visible, visible], axis=1)
        lse = jnp.concatenate([lse_ref[0, h:h + 1, low:end] for h in range(2)], axis=1)
        row_dots = jnp.concatenate(
            [jnp.sum(product[h * head_size:(h + 1) * head_size], axis=0, keepdims=True)
             for h in range(2)], axis=1)
        weights = jnp.where(visible, jnp.exp(scores - lse), 0.0)
        score_low = (weights * (prob_grad - row_dots)).astype(BF)
        v_sum[begin:end, :] += dot(weights.astype(BF), grad_two)
        k_sum[begin:end, :] += dot(score_low, q_two)
        dq = dot(score_low, k, ((0,), (0,))) * scale
        dq = jnp.where(first, dq[:small], dq[small:])
        d_ref[low:end, :lanes] = (
            dq * cos_ref[low:end, :] - turn(dq, half) * sin_ref[low:end, :]).astype(BF)
    for low in range(0, tokens, block):
        rows = pl.ds(low, block)
        dk = k_sum[rows, :]
        d_ref[rows, lanes:2 * lanes] = (
            dk * cos_ref[rows, :] - turn(dk, half) * sin_ref[rows, :]).astype(BF)
        d_ref[rows, 2 * lanes:] = v_sum[rows, :].astype(BF)

def attend_back(seg, g, w_out, q, k, v, att, lse, cosine, sine, window, head_size):
    tokens, width = g.shape
    lanes = 2 * head_size
    pairs = q.shape[1] // lanes
    kernel = lambda *refs: attend_back_kernel(
        *refs, block=256, window=window, scale=1.0 / math.sqrt(head_size), head_size=head_size)
    column = pl.BlockSpec((tokens, lanes), lambda p: (0, p))
    inputs = hbm(seg) + vmem(g) + hbm(w_out, q, k, v, att, lse, cosine, sine)
    return pl.pallas_call(
        kernel,
        grid=(pairs,),
        in_specs=whole_specs(seg) + [
            VMEM_SPEC,
            pl.BlockSpec((lanes, width), lambda p: (p, 0)),
            column, column, column, column,
            pl.BlockSpec((1, 8, tokens), lambda p: (p, 0, 0)),
        ] + whole_specs(cosine, sine),
        out_specs=pl.BlockSpec((tokens, 3 * lanes), lambda p: (0, p)),
        out_shape=jax.ShapeDtypeStruct((tokens, 3 * lanes * pairs), BF),
        scratch_shapes=[
            pltpu.VMEM((tokens, lanes), BF),
            pltpu.VMEM((tokens, lanes), F32),
            pltpu.VMEM((tokens, lanes), F32),
        ],
        compiler_params=pltpu.CompilerParams(vmem_limit_bytes=28 << 20),
        cost_estimate=SMALL_COST,
        name="attend_back",
    )(*inputs)


def join_kernel(rank_ref, own_ref, other_ref, *out_refs, moves, plain):
    swapped = rank_ref[0] == 1
    own, other = own_ref[...], other_ref[...]
    halves = (jnp.where(swapped, other, own), jnp.where(swapped, own, other))
    for out, half, (rows, cols), (to_rows, to_cols) in moves:
        out_refs[out][to_rows, to_cols] = halves[half][rows, cols].astype(F32)
    for out, (rows, cols) in plain:
        out_refs[out][...] = own[rows, cols].astype(F32)


def join(rank, own, other, moves, plain, shapes):
    kernel = lambda *refs: join_kernel(*refs, moves=moves, plain=plain)
    return pl.pallas_call(
        kernel,
        in_specs=[
            pl.BlockSpec(memory_space=pltpu.SMEM),
            pl.BlockSpec(memory_space=pltpu.VMEM),
            pl.BlockSpec(memory_space=pltpu.VMEM),
        ],
        out_specs=[pl.BlockSpec(memory_space=pltpu.VMEM)] * len(shapes),
        out_shape=[jax.ShapeDtypeStruct(shape, F32) for shape in shapes],
        compiler_params=pltpu.CompilerParams(vmem_limit_bytes=32 << 20),
        name="join",
    )(rank.reshape(1), own, other)


def join_all_kernel(all_ref, *refs, moves):
    outs = (len(refs) - 2) // 2
    out_refs, whole_ref, blocks, sems = refs[:outs], refs[outs], refs[outs + 1:-1], refs[-1]
    groups, ranks, rows, _ = all_ref.shape
    for h in range(ranks):
        for m in range(groups):
            whole_ref[h, m * rows:(m + 1) * rows, :] = all_ref[m, h]
    copies = []
    for n in range(outs):
        for out, half, (rows, cols), (to_rows, to_cols) in moves:
            if out == n:
                blocks[out][to_rows, to_cols] = whole_ref[half, rows, cols].astype(F32)
        copies.append(pltpu.make_async_copy(blocks[n], out_refs[n], sems.at[n]))
        copies[-1].start()
    for copy in copies:
        copy.wait()


def join_all(parts, moves, shapes):
    groups, ranks, rows, cols = parts.shape
    parts, = hbm(parts)
    return pl.pallas_call(
        lambda *refs: join_all_kernel(*refs, moves=moves),
        grid=(1,),
        in_specs=whole_specs(parts),
        out_specs=[HBM_SPEC] * len(shapes),
        out_shape=[pltpu.HBM(shape, F32) for shape in shapes],
        scratch_shapes=[pltpu.VMEM((ranks, groups * rows, cols), BF)]
        + [pltpu.VMEM(shape, F32) for shape in shapes]
        + [pltpu.SemaphoreType.DMA((len(shapes),))],
        compiler_params=pltpu.CompilerParams(vmem_limit_bytes=24 << 20),
        cost_estimate=SMALL_COST,
        name="join_all",
    )(parts)


def make_body(groups, ranks, fsdp, square):
    F = ("y", "x") if square else ("f",)
    swap = [(0, 1), (1, 0)]
    pairs = square and ranks == 2 and groups == 4

    def hop(value, k):
        return lax.ppermute(value, "m", [(i, i ^ k) for i in range(groups)])

    def after(value, *earlier):
        return lax.optimization_barrier((value,) + earlier)[0]

    def between(slabs, value):
        hops, value = lax.optimization_barrier((slabs[1:], value))
        return slabs[:1] + hops, value

    def spread(slabs):
        return [hop(slab, k) if k else slab for k, slab in enumerate(slabs)]

    def both_ranks(where, slabs, span):
        if ranks == 2:
            return slabs + [lax.ppermute(slab, "r", swap) for slab in slabs]
        rows = lax.all_gather(stack(where, slabs)[:, 0], "r", axis=1)
        return [rows[:, :, :span].reshape(-1, rows.shape[-1]), rows]

    def share(part):
        if ranks == 2:
            other = lax.ppermute(part, "r", swap)
            mine_first = lax.axis_index("r") == 0
            return jnp.stack(
                [jnp.where(mine_first, part, other), jnp.where(mine_first, other, part)], axis=1)
        return lax.all_gather(part, "r", axis=1)

    def exchange(part):
        if ranks == 2:
            return part, lax.ppermute(part, "r", swap)
        return lax.psum(part, "r"), jnp.zeros_like(part)

    def gather_rows(part, wait=()):
        if not square:
            whole = lax.all_gather(part, F, axis=0, tiled=True)
            return [whole], [(None, 0, 0)], (), ()
        count = part.shape[0]
        rows = (count // 2) // 16 * 16
        send = after(part, *wait) if wait else part
        from_x = lax.ppermute(send, "x", swap)
        from_y = lax.ppermute(send, "y", swap)
        far_a = lax.ppermute(from_y[:rows], "x", swap)
        far_b = lax.ppermute(from_x[rows:], "y", swap)
        pieces = [(0, 0, count), (1, 0, count), (2, 0, count), (3, 0, rows), (3, rows, count - rows)]
        return [part, from_x, from_y, far_a, far_b], pieces, (from_x, from_y), (far_a, far_b)

    def add(*parts):
        return sum(part.astype(F32) for part in parts).astype(BF)

    def take(grad, k):
        return lax.dynamic_index_in_dim(grad, lax.axis_index(F) ^ k, 0, keepdims=False)

    def half_rows(grad):
        return (grad.shape[1] // 2) // 16 * 16

    def round_one(grad):
        far, rows = take(grad, 3), half_rows(grad)
        return lax.ppermute(far[:rows], "x", swap), lax.ppermute(far[rows:], "y", swap)

    def second_terms(grad, low, high):
        to_x, to_y, rows = take(grad, 1), take(grad, 2), half_rows(grad)
        to_x = jnp.concatenate([to_x[:rows], add(to_x[rows:], high)], axis=0)
        to_y = jnp.concatenate([add(to_y[:rows], low), to_y[rows:]], axis=0)
        return to_x, to_y

    def round_two(to_x, to_y):
        return lax.ppermute(to_x, "x", swap), lax.ppermute(to_y, "y", swap)

    def halve(owned, bit, axis):
        half = owned.shape[axis] // 2
        side = (lax.axis_index("m") // bit) % 2
        return (lax.dynamic_slice_in_dim(owned, (1 - side) * half, half, axis),
                lax.dynamic_slice_in_dim(owned, side * half, half, axis))

    def join_halves(owned, other, bit, axis):
        first = (lax.axis_index("m") // bit) % 2 == 0
        return jnp.concatenate(
            [jnp.where(first, owned, other), jnp.where(first, other, owned)], axis=axis)

    def reduce(grad):
        return lax.psum(lax.psum_scatter(grad, F, scatter_dimension=0, tiled=False), "m")

    def body(tokens, segments, w_query, w_key, w_value, w_out, w_gate, w_up, w_down,
             gain_attn, gain_ffn, cotangent):
        micro, _, span, width = tokens.shape
        head_size = width // HEADS
        seq_tokens = span * groups * ranks
        window = seq_tokens // 2
        rank = lax.axis_index("r")
        own_cols = width // ranks
        shard = w_query.shape[0]
        down_rows = w_down.shape[0]
        part_rows = down_rows // ranks
        ff = w_gate.shape[1]
        half_ff = ff // ranks

        lanes = 2 * head_size
        lanes_all = -(-own_cols // lanes) * lanes
        spare = lanes_all - own_cols
        block = span * ranks
        f_index = lax.axis_index(F)
        own_at, other_at, other_rank = (
            at.astype(jnp.uint32) for at in (rank * own_cols, (1 - rank) * own_cols, 1 - rank))
        where = jnp.stack([f_index, lax.axis_index("m"), rank])
        small_cols = 3 * lanes_all + own_cols
        gains_in = jnp.pad(jnp.stack([gain_attn, gain_ffn]), ((0, 14), (0, 0)))
        stack_own = pack(where, w_gate, w_up, w_down, fsdp, ranks)
        stack_all = lax.all_gather(stack_own, F, axis=0)
        cosine, sine = rotary_tables(seq_tokens, head_size, 2)
        small, *slabs = pack_small(
            after(where, stack_own), w_query, w_key, w_value, w_out, gains_in, tokens,
            segments[:, 0], cotangent, ranks, lanes, lanes_all)
        token_slabs, cot_slabs = slabs[:groups], slabs[groups:]
        token_slabs = spread(token_slabs)
        small_refs, small_pieces, near, far = gather_rows(small)
        if square:
            cot_slabs = cot_slabs[:1] + [after(slab, *token_slabs) for slab in cot_slabs[1:]]
        cot_slabs = spread(cot_slabs)
        if square:
            token_slabs = token_slabs[:1] + [
                after(slab, cosine, sine) for slab in token_slabs[1:]]
        token_refs = both_ranks(where, token_slabs, span)
        if ranks != 2:
            seg = token_refs[1][:, :, span, :span].reshape(1, seq_tokens).astype(F32)
            token_refs = [token_refs[0], seg]
        if square:
            own, from_x, from_y, far_a, far_b = small_refs
            at = far_a.shape[0]
            ends = [own, from_x, from_y, jnp.concatenate([far_a, far_b[:shard - at]], axis=0)]
            tails = [v[shard:shard + 2, :shard] for v in (own, from_x, from_y)]
            tails.append(far_b[shard - at:shard - at + 2, :shard])
            gains = jnp.zeros((fsdp, 2, shard), BF)
            out_cols = jnp.zeros((width, own_cols), BF)
            for offset in range(4):
                to = (f_index ^ offset) * shard
                gains = lax.dynamic_update_index_in_dim(gains, tails[offset], f_index ^ offset, 0)
                out_cols = lax.dynamic_update_slice_in_dim(
                    out_cols, ends[offset][:shard, 3 * lanes_all:], to, 0)
            gains = gains.transpose(1, 0, 2).reshape(2, width)
            small_pieces = [(o, f, min(n, shard - f)) for o, f, n in small_pieces]
            qkv_refs = small_refs
        else:
            whole = small_refs[0].reshape(fsdp, shard + 16, small_cols)
            gains = whole[:, shard:shard + 2, :shard].transpose(1, 0, 2).reshape(2, width)
            out_cols = whole[:, :shard, 3 * lanes_all:].reshape(width, own_cols)
            qkv_refs = [whole[:, :shard, :3 * lanes_all].reshape(width, 3 * lanes_all)]
        gains = gains.astype(F32)
        gain_one = gains[0:1]
        if ranks == 2:
            give = lax.dynamic_slice_in_dim(out_cols, (1 - rank) * own_cols, own_cols, 0)
            keep = lax.dynamic_slice_in_dim(out_cols, rank * own_cols, own_cols, 0)
            got = lax.ppermute(give, "r", swap)
            w_out_own = jnp.where(rank == 0, jnp.concatenate([keep, got], 1),
                                  jnp.concatenate([got, keep], 1))
        else:
            pieces = lax.all_to_all(out_cols, "r", 0, 0, tiled=True)
            pieces = pieces.reshape(ranks, own_cols, own_cols)
            w_out_own = jnp.concatenate([pieces[i] for i in range(ranks)], axis=1)
        w_out_even = jnp.pad(w_out_own, ((0, spare), (0, 0)))

        cosine, gains, gain_one, own_at, other_at, other_rank = lax.optimization_barrier(
            (cosine, gains, gain_one, own_at, other_at, other_rank))
        q, k, v, att, lse, w_qkv, x, seg = attend(
            where, cosine, sine, token_refs, ranks, qkv_refs, small_pieces, shard, lanes_all,
            window, head_size, width)
        if square:
            cot_slabs, att = between(cot_slabs, att)
        own, got = exchange(dot(att, w_out_even).astype(BF))
        cot_refs = both_ranks(where, cot_slabs, span)
        if ranks != 2:
            cot_refs = cot_refs[:1]
        total, middle_low, hidden_low, gate_back, silu, part, gu, down = forward(
            x, own, got, gain_one, stack_all, shard, part_rows, half_ff, block)
        own, got = exchange(part)

        *out_slabs, ffn_grad_low, gu_grad_low, part, gain_ffn_grad = backward(
            where, total, own, got, gate_back, silu, gains, gu, down, cot_refs, block, groups, ranks)
        own, got = exchange(part)
        gu_w_grad = dot(middle_low, gu_grad_low, ((0,), (0,))).astype(BF)
        if ranks == 2:
            got, gu_w_grad = lax.optimization_barrier((got, gu_w_grad))
        down_w_grad = dot(hidden_low, ffn_grad_low, ((0,), (0,))).astype(BF)
        stack_grad = arrange(gu_w_grad, down_w_grad, fsdp)
        stack_owned = lax.psum_scatter(stack_grad, F, scatter_dimension=0, tiled=False)
        own, got = after(own, stack_grad), after(got, stack_grad)
        branch_grad_low, branch_keep, gain_grads = norm_back(
            where[2:], total, ffn_grad_low, own, got, gain_one, gain_ffn_grad,
            fsdp, small_cols, block, span)
        out_w_grad = dot(att, branch_grad_low, ((0,), (0,)))[:own_cols].astype(BF)
        if ranks == 2:
            give = lax.dynamic_slice_in_dim(out_w_grad, other_at, own_cols, 1)
            keep = lax.dynamic_slice_in_dim(out_w_grad, own_at, own_cols, 1)
            got = lax.ppermute(give, "r", swap)
            out_cols_grad = jnp.where(rank == 0, jnp.concatenate([keep, got], 0),
                                      jnp.concatenate([got, keep], 0))
        else:
            rows = out_w_grad.reshape(own_cols, ranks, own_cols).transpose(1, 0, 2)
            out_cols_grad = lax.all_to_all(rows, "r", 0, 0, tiled=True).reshape(width, own_cols)
        branch_grad_low = after(branch_grad_low, out_cols_grad)
        d_qkv = attend_back(
            seg, branch_grad_low, w_out_even, q, k, v, att, lse, cosine, sine, window, head_size)
        if square:
            out_slabs, d_qkv = between(spread(out_slabs), d_qkv)
        else:
            out_slabs = spread(out_slabs)
        output = stack(where, out_slabs)
        qkv_w_grad = dot(x, d_qkv, ((0,), (0,))).astype(BF)
        small_grad = jnp.concatenate([qkv_w_grad, out_cols_grad], axis=1)
        small_grad = jnp.concatenate(
            [small_grad.reshape(fsdp, shard, small_cols), gain_grads], axis=1)
        if pairs:
            small_one = round_one(small_grad)
            d_qkv = after(d_qkv, small_grad)
        part = dot(d_qkv, w_qkv, ((1,), (1,))).astype(BF)
        if ranks == 2:
            rows = part.reshape(groups, ranks, span, width)
            give = lax.dynamic_index_in_dim(rows, other_rank, 1, keepdims=False)
            got = lax.ppermute(give, "r", swap)
        else:
            part = lax.psum(part, "r")
            got = jnp.zeros_like(branch_keep, BF)
        grad_slabs = list(finish(where, branch_keep, part, got, ranks))
        grad_slabs = spread(grad_slabs)
        if pairs:
            grad_slabs[:3], small_one = between(grad_slabs[:3], small_one)
            terms = second_terms(small_grad, *small_one)
            small_two, output, grad_slabs[3] = lax.optimization_barrier(
                (round_two(*terms), output, grad_slabs[3]))
            input_grad = stack(where, grad_slabs)
            stack_owned = after(stack_owned, *terms)
            quarter = lax.psum_scatter(stack_owned, "m", scatter_dimension=0, tiled=True)
            give, keep = halve(add(take(small_grad, 0), *small_two), 1, 1)
            got, quarter, input_grad = lax.optimization_barrier((hop(give, 1), quarter, input_grad))
            stack_parts = lax.all_gather(quarter, ("m", "r"), axis=0)
            stack_parts = stack_parts.reshape((groups, ranks) + quarter.shape)
            give, keep = halve(add(keep, got), 2, 1)
            owned = add(keep, hop(give, 2))
            owned = join_halves(owned, hop(owned, 2), 2, 1)
            small_sum = join_halves(owned, hop(owned, 1), 1, 1)
        else:
            stack_sum = lax.psum(stack_owned, "m")
            small_sum = reduce(small_grad)
            input_grad = stack(where, grad_slabs)
        if pairs:
            everything = slice(None)
            chunks = 2 * half_ff // 256
            stack_moves = [
                (n, h, (slice((n * fsdp + j) * shard, (n * fsdp + j + 1) * shard), everything),
                 (everything, slice(j * down_rows + h * part_rows, j * down_rows + (h + 1) * part_rows)))
                for n in range(2) for h in range(2) for j in range(fsdp)]
            stack_moves += [
                (2, h, (slice(chunks * shard + c * part_rows, chunks * shard + (c + 1) * part_rows),
                        everything),
                 (slice(h * part_rows, (h + 1) * part_rows), slice(c * 256, (c + 1) * 256)))
                for h in range(2) for c in range(width // 256)]
            small_moves = [
                (n, h, (slice(0, shard), slice((3 * p + n) * lanes, (3 * p + n + 1) * lanes)),
                 (everything, slice(h * own_cols + p * lanes, h * own_cols + (p + 1) * lanes)))
                for n in range(3) for h in range(2) for p in range(own_cols // lanes)]
            small_moves += [
                (3, h, (slice(0, shard), slice(3 * lanes_all, small_cols)),
                 (everything, slice(h * own_cols, (h + 1) * own_cols))) for h in range(2)]
            small_plain = [
                (4 + n, (slice(shard + n, shard + n + 1), slice(0, shard))) for n in range(2)]
            gate_w, up_w, down_grad = join_all(
                stack_parts, stack_moves, [(shard, ff)] * 2 + [(down_rows, width)])
            small_got, gate_w, up_w, down_grad = lax.optimization_barrier(
                (lax.ppermute(small_sum, "r", swap), gate_w, up_w, down_grad))
            query_w, key_w, value_w, out_w, gain_a, gain_f = join(
                rank, small_sum, small_got, small_moves, small_plain,
                [(shard, width)] * 4 + [(1, shard)] * 2)
        else:
            at = 2 * half_ff // 256 * shard
            down_sum = jnp.moveaxis(stack_sum[at:].reshape(-1, part_rows, 256), 0, 1)
            down_grad = jnp.moveaxis(share(down_sum.reshape(part_rows, width)), 1, 0)
            down_grad = down_grad.reshape(down_rows, width).astype(F32)
            gu_sum = jnp.moveaxis(stack_sum[:at].reshape(-1, shard, 256), 0, 1)
            gu_both = share(gu_sum.reshape(shard, 2 * fsdp, part_rows))
            gu_both = gu_both.reshape(shard, ranks, 2, fsdp, part_rows).astype(F32)
            gate_w, up_w = (
                gu_both[:, :, n].transpose(0, 2, 1, 3).reshape(shard, ff) for n in range(2))
            small_both = share(small_sum)[:shard].astype(F32)
            three = small_both[:, :, :3 * lanes_all].reshape(shard, ranks, -1, 3, lanes)
            query_w, key_w, value_w = (
                three[:, :, :, n].reshape(shard, ranks, lanes_all)[:, :, :own_cols].reshape(shard, width)
                for n in range(3))
            out_w = small_both[:, :, 3 * lanes_all:].reshape(shard, width)
            gain_a, gain_f = small_sum[shard, :shard].astype(F32), small_sum[shard + 1, :shard].astype(F32)
        return (output, input_grad, query_w, key_w, value_w, out_w,
                gate_w, up_w, down_grad, gain_a.reshape(shard), gain_f.reshape(shard))

    return body


def solution(mesh):
    def run(*args):
        groups = args[0].shape[0]
        seq, fsdp = mesh.shape["seq"], mesh.shape["fsdp"]
        ranks = seq // groups
        square = fsdp == 4
        names = ("m", "r") + (("y", "x") if square else ("f",))
        sizes = (groups, ranks) + ((2, 2) if square else (fsdp,))
        order = [mesh.axis_names.index(name) for name in ("seq", "fsdp")]
        inner = Mesh(mesh.devices.transpose(order).reshape(sizes), names)
        f = ("y", "x") if square else "f"
        s = ("m", "r")
        rows = P(f, None)
        data = P(None, f, s, None)
        in_specs = (data, P(None, f, s)) + (rows,) * 7 + (P(f), P(f), data)
        out_specs = (data, data) + (rows,) * 7 + (P(f), P(f))
        body = make_body(groups, ranks, fsdp, square)
        return jax.shard_map(
            body, mesh=inner, in_specs=in_specs, out_specs=out_specs, check_vma=False)(*args)

    return run
```

```python
import math

import jax
import jax.numpy as jnp
from jax import lax
from jax.experimental import pallas as pl
from jax.experimental.pallas import tpu as pltpu
from jax.sharding import Mesh, PartitionSpec as P

HEADS = 12
DOCS = 4
EPS = 1e-06
NEGATIVE = -1e30
BF = jnp.bfloat16
F32 = jnp.float32


def dot(left, right, dims=((1,), (0,))):
    return lax.dot_general(left, right, (dims, ((), ())), preferred_element_type=F32)


def rotary_tables(seq_tokens, head_size, copies):
    half = head_size // 2
    frequency = 10000.0 ** (-jnp.arange(half, dtype=F32) / half)
    angle = jnp.arange(seq_tokens, dtype=jnp.int32).astype(F32)[:, None] * frequency[None, :]
    cosine, sine = jnp.cos(angle), jnp.sin(angle)
    return (
        jnp.concatenate([cosine, cosine] * copies, axis=1),
        jnp.concatenate([-sine, sine] * copies, axis=1),
    )


def turn(rows, half):
    lanes = rows.shape[1]
    lane = lax.broadcasted_iota(jnp.int32, (1, lanes), 1)
    low = (lane // half) % 2 == 0
    return jnp.where(low, pltpu.roll(rows, lanes - half, 1), pltpu.roll(rows, half, 1))


def first_key(query_first, block, window):
    return max(0, (query_first - window + 1) // block * block)


def start_row(seg_ref):
    seg = seg_ref[...]
    starts = jnp.zeros_like(seg)
    for doc in range(1, DOCS):
        before = jnp.sum(jnp.where(seg < doc, 1.0, 0.0), axis=1, keepdims=True)
        starts = jnp.maximum(starts, jnp.where(seg >= doc, before, 0.0))
    return starts


def place(target, refs, pieces, me, shard):
    for ref, (offset, first, rows) in zip(refs, pieces):
        if offset is None:
            target[...] = ref[...]
        else:
            start = pl.multiple_of((me ^ offset) * shard + first, 16)
            target[pl.ds(start, rows), :] = ref[0:rows, 0:target.shape[1]]


def place_tokens(target, refs, where_ref, ranks):
    if len(refs) == 1:
        target[...] = refs[0][...]
        return
    groups = len(refs) // ranks
    span = target.shape[0] // (groups * ranks)
    for n, ref in enumerate(refs):
        rank = where_ref[2] if n < groups else 1 - where_ref[2]
        chunk = (where_ref[1] ^ (n % groups)) * ranks + rank
        target[pl.ds(pl.multiple_of(chunk * span, span), span), :] = ref[0:span, :]


def place_segments(target, refs, where_ref, ranks):
    groups = len(refs) // ranks
    span = target.shape[1] // (groups * ranks)
    for n, ref in enumerate(refs):
        rank = where_ref[2] if n < groups else 1 - where_ref[2]
        chunk = (where_ref[1] ^ (n % groups)) * ranks + rank
        row = ref[span:span + 8, 0:span].astype(F32)[0:1, :]
        target[:, pl.ds(pl.multiple_of(chunk * span, span), span)] = row


def stack_copies(gu, down, stack_ref, sems, shard, part_rows):
    members, chunks, groups = stack_ref.shape[0], gu.shape[1] // 256, []
    for c in range(chunks):
        groups.append([
            pltpu.make_async_copy(
                stack_ref.at[j, c * shard:(c + 1) * shard, :],
                gu.at[j * shard:(j + 1) * shard, c * 256:(c + 1) * 256],
                sems.at[c, j]) for j in range(members)])
    for c in range(down.shape[1] // 256):
        at = chunks * shard + c * part_rows
        groups.append([
            pltpu.make_async_copy(
                stack_ref.at[j, at:at + part_rows, :],
                down.at[j * part_rows:(j + 1) * part_rows, c * 256:(c + 1) * 256],
                sems.at[chunks + c, j]) for j in range(members)])
    return groups


def attend_kernel(where_ref, cos_ref, sin_ref, *refs, pieces, token_count, ranks, shard, block,
                  window, scale, head_size):
    inputs, refs = refs[:-9], refs[-9:]
    q_ref, k_ref, v_ref, att_ref, lse_ref, w_ref, x_ref, seg_ref, col_ref = refs
    token_refs, w_refs = inputs[:token_count], inputs[token_count:]
    tokens = x_ref.shape[0]
    lanes = 2 * head_size
    lane = lax.broadcasted_iota(jnp.int32, (1, lanes), 1)
    first = lane < head_size
    pair = pl.program_id(0)

    @pl.when(pair == 0)
    def _():
        place(w_ref, w_refs, pieces, where_ref[0], shard)
        place_tokens(x_ref, token_refs[:1] if token_count == 2 else token_refs, where_ref, ranks)
        if token_count == 2:
            seg_ref[...] = token_refs[1][...]
        else:
            place_segments(seg_ref, token_refs, where_ref, ranks)
        starts = start_row(seg_ref)
        col_ref[...] = jnp.broadcast_to(starts, (128, tokens)).T

    w = w_ref[:, pl.ds(pl.multiple_of(pair * 3 * lanes, lanes), 3 * lanes)]
    for low in range(0, tokens, block):
        rows = pl.ds(low, block)
        lin = dot(x_ref[rows, :], w)
        cosine, sine = cos_ref[rows, :], sin_ref[rows, :]
        half = head_size // 2
        q_lin, k_lin = lin[:, :lanes], lin[:, lanes:2 * lanes]
        q_ref[rows, :] = (q_lin * cosine + turn(q_lin, half) * sine).astype(BF)
        k_ref[rows, :] = (k_lin * cosine + turn(k_lin, half) * sine).astype(BF)
        v_ref[rows, :] = lin[:, 2 * lanes:].astype(BF)
    for low in range(0, tokens, block):
        begin = first_key(low, block, window)
        end = low + block
        q = q_ref[low:end, :] * jnp.asarray(scale, BF)
        zero = jnp.zeros_like(q)
        stacked = jnp.concatenate([jnp.where(first, q, zero), jnp.where(first, zero, q)], axis=0)
        scores = dot(stacked, k_ref[begin:end, :], ((1,), (1,)))
        key_index = lax.broadcasted_iota(jnp.int32, (block, end - begin), 1) + begin
        query_index = lax.broadcasted_iota(jnp.int32, (block, end - begin), 0) + low
        visible = (key_index.astype(F32) >= col_ref[low:end, 0:1]) & (key_index <= query_index)
        parts = []
        for head in range(2):
            own = jnp.where(visible, scores[head * block:(head + 1) * block], NEGATIVE)
            top = jnp.max(own, axis=1, keepdims=True)
            weights = jnp.exp(own - top)
            total = jnp.sum(weights, axis=1, keepdims=True)
            out = dot(weights.astype(BF), v_ref[begin:end, :]) / total
            parts.append(out)
            lse = jnp.broadcast_to(top + jnp.log(total), (block, 128))
            lse_ref[0, head:head + 1, low:end] = lse.T[0:1, :]
        att_ref[low:end, :] = jnp.where(first, parts[0], parts[1]).astype(BF)


def hbm(*arrays):
    return [pltpu.with_memory_space_constraint(a, pltpu.HBM) for a in arrays]


def vmem(*arrays):
    return [pltpu.with_memory_space_constraint(a, pltpu.VMEM) for a in arrays]


def whole_specs(*arrays):
    return [pl.BlockSpec(a.shape, lambda *_, n=a.ndim: (0,) * n, pipeline_mode=pl.Buffered(1))
            for a in arrays]


SMALL_COST = pl.CostEstimate(flops=1, bytes_accessed=1, transcendentals=0)
VMEM_SPEC = pl.BlockSpec(memory_space=pltpu.VMEM)
SMEM_SPEC = pl.BlockSpec(memory_space=pltpu.SMEM)


def attend(where, cosine, sine, token_refs, ranks, weights, pieces, shard, lanes_all, window,
           head_size, width):
    tokens = cosine.shape[0]
    lanes = 2 * head_size
    pairs = lanes_all // lanes
    kernel = lambda *refs: attend_kernel(
        *refs, pieces=pieces, token_count=len(token_refs), ranks=ranks, shard=shard, block=256,
        window=window, scale=1.0 / math.sqrt(head_size), head_size=head_size)
    column = pl.BlockSpec((tokens, lanes), lambda p: (0, p))
    whole = lambda *shape: pl.BlockSpec(shape, lambda p: (0, 0))
    inputs = hbm(cosine, sine, *token_refs, *weights)
    return pl.pallas_call(
        kernel,
        grid=(pairs,),
        in_specs=[SMEM_SPEC] + whole_specs(*inputs),
        out_specs=[column, column, column, column,
                   pl.BlockSpec((1, 8, tokens), lambda p: (p, 0, 0)),
                   whole(width, 3 * lanes_all), whole(tokens, width), whole(1, tokens)],
        out_shape=[pltpu.HBM((tokens, lanes_all), BF)] * 4
        + [pltpu.HBM((pairs, 8, tokens), F32), pltpu.HBM((width, 3 * lanes_all), BF),
           pltpu.HBM((tokens, width), BF), pltpu.HBM((1, tokens), F32)],
        scratch_shapes=[pltpu.VMEM((tokens, 128), F32)],
        compiler_params=pltpu.CompilerParams(vmem_limit_bytes=28 << 20),
        cost_estimate=SMALL_COST,
        name="attend",
    )(where, *inputs)


def unit_of(rows):
    factor = lax.rsqrt(jnp.mean(rows * rows, axis=1, keepdims=True) + EPS)
    return rows * factor, factor


def forward_kernel(x_ref, own_ref, got_ref, gain_ref, stack_ref, sum_ref, low_ref, hidden_ref,
                   gate_ref, silu_ref, part_ref, gu, down, sems, *, shard, part_rows):
    step, block = pl.program_id(0), x_ref.shape[0]
    ff = down.shape[0]

    @pl.when(step == 0)
    def _():
        copies = stack_copies(gu, down, stack_ref, sems, shard, part_rows)
        for group in copies:
            for copy in group:
                copy.start()
        for group in copies:
            for copy in group:
                copy.wait()

    rows = pl.ds(pl.multiple_of(step * block, block), block)
    total = x_ref[...].astype(F32) + own_ref[...].astype(F32) + got_ref[...].astype(F32)
    sum_ref[rows, :] = total
    middle_low = (unit_of(total)[0] * gain_ref[...]).astype(BF)
    low_ref[rows, :] = middle_low
    for c in range(0, ff, 256):
        cols = slice(c, c + 256)
        gate = dot(middle_low, gu[:, cols])
        up = dot(middle_low, gu[:, ff + c:ff + c + 256])
        sigmoid = jax.nn.sigmoid(gate)
        silu = gate * sigmoid
        hidden_ref[rows, cols] = (silu * up).astype(BF)
        gate_ref[rows, cols] = (up * sigmoid * (1.0 + gate * (1.0 - sigmoid))).astype(BF)
        silu_ref[rows, cols] = silu.astype(BF)
    part_ref[...] = dot(hidden_ref[rows, :], down[...]).astype(BF)


HBM_SPEC = pl.BlockSpec(memory_space=pltpu.HBM)


def forward(x, own, got, gain, stack, shard, part_rows, ff, block):
    tokens, width = x.shape
    row = lambda cols: pl.BlockSpec((block, cols), lambda i: (i, 0))
    x, own, got, stack = hbm(x, own, got, stack)
    return pl.pallas_call(
        lambda *refs: forward_kernel(*refs, shard=shard, part_rows=part_rows),
        grid=(tokens // block,),
        in_specs=[row(width), row(width), row(width)] + whole_specs(gain) + [HBM_SPEC],
        out_specs=[VMEM_SPEC] * 5 + [row(width)] + [VMEM_SPEC] * 2,
        out_shape=[pltpu.VMEM((tokens, width), F32), pltpu.VMEM((tokens, width), BF)]
        + [pltpu.VMEM((tokens, ff), BF)] * 3 + [jax.ShapeDtypeStruct((tokens, width), BF)]
        + [pltpu.VMEM((width, 2 * ff), BF), pltpu.VMEM((ff, width), BF)],
        scratch_shapes=[pltpu.SemaphoreType.DMA(((2 * ff + width) // 256, stack.shape[0]))],
        compiler_params=pltpu.CompilerParams(vmem_limit_bytes=16 << 20),
        cost_estimate=SMALL_COST,
        name="ffn_forward",
    )(x, own, got, gain, stack)


def backward_kernel(where_ref, sum_ref, own_ref, got_ref, gate_ref, silu_ref, gains_ref, gu, down,
                    *refs, cot_count, groups, ranks):
    cot_refs, refs = refs[:cot_count], refs[cot_count:]
    out_refs, refs = refs[:groups], refs[groups:]
    low_ref, gu_grad_ref, part_ref, gain_ref, cot_ref, rows_ref = refs
    step = pl.program_id(0)
    block, span = rows_ref.shape[0], out_refs[0].shape[0]

    @pl.when(step == 0)
    def _():
        place_tokens(cot_ref, cot_refs, where_ref, ranks)
        gain_ref[...] = jnp.zeros_like(gain_ref)

    rows = pl.ds(pl.multiple_of(step * block, block), block)
    gain_two = gains_ref[1:2, :]
    middle = unit_of(sum_ref[rows, :])[0] * gains_ref[0:1, :]
    unit, factor = unit_of(middle + own_ref[...].astype(F32) + got_ref[...].astype(F32))
    rows_ref[...] = unit * gain_two
    cot = cot_ref[rows, :].astype(F32)
    gain_ref[...] += jnp.sum(cot * unit, axis=0, keepdims=True)
    scaled = cot * gain_two
    grad_low = (factor * (scaled - unit * jnp.mean(scaled * unit, axis=1, keepdims=True))).astype(BF)
    low_ref[rows, :] = grad_low
    ff = down.shape[0]
    for c in range(0, ff, 256):
        cols = slice(c, c + 256)
        hidden_grad = dot(grad_low, down[cols, :], ((1,), (1,)))
        gu_grad_ref[rows, cols] = (hidden_grad * gate_ref[rows, cols].astype(F32)).astype(BF)
        gu_grad_ref[rows, ff + c:ff + c + 256] = (
            hidden_grad * silu_ref[rows, cols].astype(F32)).astype(BF)
    part_ref[...] = dot(gu_grad_ref[rows, :], gu[...], ((1,), (1,))).astype(BF)
    kept = rows_ref[pl.ds(pl.multiple_of(where_ref[2] * span, span), span), :].astype(BF)
    for k, out_ref in enumerate(out_refs):
        @pl.when(step == (where_ref[1] ^ k))
        def _(out_ref=out_ref):
            out_ref[...] = kept


def backward(where, total, own, got, gate, silu, gains, gu, down, cot, block, groups, ranks):
    tokens, width = total.shape
    ff = gate.shape[1]
    kernel = lambda *refs: backward_kernel(
        *refs, cot_count=len(cot), groups=groups, ranks=ranks)
    row = pl.BlockSpec((block, width), lambda i: (i, 0))
    slab = pl.BlockSpec((block // ranks, width), lambda i: (0, 0))
    total, gate, silu, gu, down = vmem(total, gate, silu, gu, down)
    return pl.pallas_call(
        kernel,
        grid=(tokens // block,),
        in_specs=[SMEM_SPEC, VMEM_SPEC, row, row, VMEM_SPEC, VMEM_SPEC] + whole_specs(gains)
        + [VMEM_SPEC] * 2 + whole_specs(*cot),
        out_specs=[slab] * groups + [VMEM_SPEC, VMEM_SPEC, row,
                                     pl.BlockSpec((1, width), lambda i: (0, 0))],
        out_shape=[pltpu.HBM((block // ranks, width), BF)] * groups
        + [pltpu.VMEM((tokens, width), BF), pltpu.VMEM((tokens, 2 * ff), BF),
           pltpu.HBM((tokens, width), BF), pltpu.HBM((1, width), F32)],
        scratch_shapes=[pltpu.VMEM((tokens, width), BF), pltpu.VMEM((block, width), F32)],
        compiler_params=pltpu.CompilerParams(vmem_limit_bytes=20 << 20),
        cost_estimate=SMALL_COST,
        name="ffn_backward",
    )(where, total, own, got, gate, silu, gains, gu, down, *cot)


def norm_back_kernel(rank_ref, sum_ref, grad_ref, own_ref, got_ref, gain_ref, other_ref,
                     low_ref, keep_ref, out_ref, rows_ref, gain_grad_ref):
    step, block = pl.program_id(0), rows_ref.shape[0]

    @pl.when(step == 0)
    def _():
        gain_grad_ref[...] = jnp.zeros_like(gain_grad_ref)

    rows = pl.ds(pl.multiple_of(step * block, block), block)
    unit, factor = unit_of(sum_ref[rows, :])
    grad = (grad_ref[...].astype(F32) + own_ref[...].astype(F32)) + got_ref[...].astype(F32)
    gain_grad_ref[...] += jnp.sum(grad * unit, axis=0, keepdims=True)
    scaled = grad * gain_ref[...]
    branch_grad = factor * (scaled - unit * jnp.mean(scaled * unit, axis=1, keepdims=True))
    low_ref[rows, :] = branch_grad.astype(BF)
    rows_ref[...] = branch_grad
    span = keep_ref.shape[1]
    keep_ref[0] = rows_ref[pl.ds(pl.multiple_of(rank_ref[0] * span, span), span), :]

    @pl.when(step == pl.num_programs(0) - 1)
    def _():
        out_ref[...] = jnp.zeros_like(out_ref)
        shard = gain_ref.shape[1] // out_ref.shape[0]
        first = lax.broadcasted_iota(jnp.int32, (8, shard), 0)
        for j in range(out_ref.shape[0]):
            lanes = slice(j * shard, (j + 1) * shard)
            one = jnp.broadcast_to(gain_grad_ref[:, lanes], (8, shard))
            two = jnp.broadcast_to(other_ref[:, lanes], (8, shard))
            out_ref[j, :, 0:shard] = jnp.where(
                first == 0, one, jnp.where(first == 1, two, 0.0)).astype(BF)


def norm_back(rank, total, grad, own, got, gain, other_grad, fsdp, cols, block, span):
    tokens, width = total.shape
    row = pl.BlockSpec((block, width), lambda i: (i, 0))
    inputs = vmem(total) + hbm(grad, own, got)
    return pl.pallas_call(
        norm_back_kernel,
        grid=(tokens // block,),
        in_specs=[SMEM_SPEC, VMEM_SPEC, row, row, row] + whole_specs(gain, other_grad),
        out_specs=[VMEM_SPEC, pl.BlockSpec((1, span, width), lambda i: (i, 0, 0)),
                   pl.BlockSpec((fsdp, 8, cols), lambda i: (0, 0, 0))],
        out_shape=[pltpu.VMEM((tokens, width), BF),
                   pltpu.HBM((tokens // block, span, width), F32),
                   pltpu.HBM((fsdp, 8, cols), BF)],
        scratch_shapes=[pltpu.VMEM((block, width), F32), pltpu.VMEM((1, width), F32)],
        compiler_params=pltpu.CompilerParams(vmem_limit_bytes=16 << 20),
        cost_estimate=SMALL_COST,
        name="norm_back",
    )(rank, *inputs, gain, other_grad)


def pick(rank, parts):
    value = parts[0]
    for r in range(1, len(parts)):
        value = jnp.where(rank == r, parts[r], value)
    return value


def pack_small_kernel(where_ref, query_ref, key_ref, value_ref, out_ref, gain_ref, tokens_ref,
                      seg_ref, cot_ref, small_ref, *slab_refs, ranks, lanes, lanes_all):
    slab_refs, cot_slabs = slab_refs[:len(slab_refs) // 2], slab_refs[len(slab_refs) // 2:]
    for k, ref in enumerate(cot_slabs):
        ref[...] = cot_ref[where_ref[1] ^ k, 0]
    rank, m = where_ref[2], where_ref[1]
    shard, width = query_ref.shape
    own_cols = width // ranks
    if lanes_all != own_cols:
        small_ref[...] = jnp.zeros_like(small_ref)
    for n, ref in enumerate((query_ref, key_ref, value_ref)):
        for low in range(0, own_cols, lanes):
            size = min(lanes, own_cols - low)
            at = (low // lanes * 3 + n) * lanes
            small_ref[0:shard, at:at + size] = pick(
                rank, [ref[:, r * own_cols + low:r * own_cols + low + size] for r in range(ranks)])
    small_ref[0:shard, 3 * lanes_all:] = pick(
        rank, [out_ref[:, r * own_cols:(r + 1) * own_cols] for r in range(ranks)])
    small_ref[shard:, :] = jnp.zeros_like(small_ref[shard:, :])
    small_ref[shard:, 0:shard] = gain_ref[...]
    span = tokens_ref.shape[2]
    for k, ref in enumerate(slab_refs):
        ref[0:span, :] = tokens_ref[m ^ k, 0]
        ref[span:, :] = jnp.zeros_like(ref[span:, :])
        row = seg_ref[pl.ds(m ^ k, 1), :].astype(F32)
        ref[span:, 0:span] = jnp.broadcast_to(row, (8, span)).astype(BF)


def pack_small(where, query, key, value, out, gains, tokens, segments, cot, ranks, lanes,
               lanes_all):
    shard, width = query.shape
    groups, _, span, _ = tokens.shape
    cols = 3 * lanes_all + width // ranks
    inputs = hbm(query, key, value, out, gains, tokens, segments, cot)
    shapes = [(shard + 8, cols)] + [(span + 8, width)] * groups + [(span, width)] * groups
    return pl.pallas_call(
        lambda *refs: pack_small_kernel(*refs, ranks=ranks, lanes=lanes, lanes_all=lanes_all),
        grid=(1,),
        in_specs=[SMEM_SPEC] + whole_specs(*inputs),
        out_specs=[pl.BlockSpec(shape, lambda i: (0, 0)) for shape in shapes],
        out_shape=[pltpu.HBM(shape, BF) for shape in shapes],
        compiler_params=pltpu.CompilerParams(vmem_limit_bytes=24 << 20),
        cost_estimate=SMALL_COST,
        name="pack_small",
    )(where, *inputs)


def pack_kernel(where_ref, gate_ref, up_ref, down_ref, out_ref, gu, *, fsdp, ranks):
    rank = where_ref[2]
    shard, cols = gu.shape
    part = down_ref.shape[0] // ranks
    for n, ref in enumerate((gate_ref, up_ref)):
        for j in range(fsdp):
            low = (n * fsdp + j) * part
            gu[:, low:low + part] = pick(
                rank, [ref[:, (j * ranks + r) * part:(j * ranks + r + 1) * part]
                       for r in range(ranks)])
    chunks = cols // 256
    for c in range(chunks):
        out_ref[c * shard:(c + 1) * shard, :] = gu[:, c * 256:(c + 1) * 256]
    rows = pl.ds(pl.multiple_of(rank * part, 16), part)
    for c in range(down_ref.shape[1] // 256):
        at = chunks * shard + c * part
        out_ref[at:at + part, :] = down_ref[rows, c * 256:(c + 1) * 256]


def pack(where, gate, up, down, fsdp, ranks):
    shard, ff = gate.shape
    cols = 2 * ff // ranks
    rows = cols // 256 * shard + down.shape[1] // 256 * (down.shape[0] // ranks)
    inputs = hbm(gate, up, down)
    return pl.pallas_call(
        lambda *refs: pack_kernel(*refs, fsdp=fsdp, ranks=ranks),
        grid=(1,),
        in_specs=[SMEM_SPEC] + whole_specs(*inputs),
        out_specs=pl.BlockSpec((rows, 256), lambda i: (0, 0)),
        out_shape=pltpu.HBM((rows, 256), BF),
        scratch_shapes=[pltpu.VMEM((shard, cols), BF)],
        compiler_params=pltpu.CompilerParams(vmem_limit_bytes=24 << 20),
        cost_estimate=SMALL_COST,
        name="pack",
    )(where, *inputs)


def arrange_kernel(gu_ref, hidden_ref, grad_ref, out_ref, down, sems):
    fsdp = out_ref.shape[0]
    shard, part = gu_ref.shape[0] // fsdp, hidden_ref.shape[1] // fsdp
    chunks = gu_ref.shape[1] // 256
    copies = []

    def send(source, j, low, rows):
        copies.append(pltpu.make_async_copy(
            source, out_ref.at[j, low:low + rows, :], sems.at[len(copies)]))
        copies[-1].start()

    for c in range(chunks):
        for j in range(fsdp):
            send(gu_ref.at[j * shard:(j + 1) * shard, c * 256:(c + 1) * 256], j, c * shard, shard)
    for c in range(grad_ref.shape[1] // 256):
        down[c] = dot(hidden_ref[...], grad_ref[:, c * 256:(c + 1) * 256], ((0,), (0,))).astype(BF)
        for j in range(fsdp):
            send(down.at[c, j * part:(j + 1) * part, :], j, chunks * shard + c * part, part)
    for copy in copies:
        copy.wait()


def arrange(gu, hidden, grad, fsdp):
    shard, ff, width = gu.shape[0] // fsdp, hidden.shape[1], grad.shape[1]
    rows = gu.shape[1] // 256 * shard + width // 256 * (ff // fsdp)
    return pl.pallas_call(
        arrange_kernel,
        in_specs=[VMEM_SPEC] * 3,
        out_specs=HBM_SPEC,
        out_shape=pltpu.HBM((fsdp, rows, 256), BF),
        scratch_shapes=[pltpu.VMEM((width // 256, ff, 256), BF),
                        pltpu.SemaphoreType.DMA(((gu.shape[1] + width) // 256 * fsdp,))],
        compiler_params=pltpu.CompilerParams(vmem_limit_bytes=16 << 20),
        cost_estimate=SMALL_COST,
        name="arrange",
    )(*vmem(gu, hidden, grad))


def finish_kernel(where_ref, keep_ref, part_ref, got_ref, *out_refs, ranks):
    groups, span, _ = keep_ref.shape
    for k, ref in enumerate(out_refs):
        group = where_ref[1] ^ k
        row = (group * ranks + where_ref[2]) * span
        own = part_ref[pl.ds(pl.multiple_of(row, span), span), :].astype(F32)
        ref[...] = (keep_ref[group] + own + got_ref[group].astype(F32)).astype(BF)


def finish(where, keep, part, got, ranks):
    groups, span, width = keep.shape
    return pl.pallas_call(
        lambda *refs: finish_kernel(*refs, ranks=ranks),
        in_specs=[SMEM_SPEC] + [VMEM_SPEC] * 3,
        out_specs=[VMEM_SPEC] * groups,
        out_shape=[jax.ShapeDtypeStruct((span, width), BF)] * groups,
        compiler_params=pltpu.CompilerParams(vmem_limit_bytes=24 << 20),
        cost_estimate=SMALL_COST,
        name="finish",
    )(where, keep, part, got)


def stack_kernel(where_ref, *refs):
    out_ref = refs[-1]
    for k, ref in enumerate(refs[:-1]):
        out_ref[where_ref[1] ^ k, 0] = ref[...]


def stack(where, slabs):
    span, width = slabs[0].shape
    return pl.pallas_call(
        stack_kernel,
        in_specs=[SMEM_SPEC] + [VMEM_SPEC] * len(slabs),
        out_specs=VMEM_SPEC,
        out_shape=jax.ShapeDtypeStruct((len(slabs), 1, span, width), BF),
        compiler_params=pltpu.CompilerParams(vmem_limit_bytes=16 << 20),
        cost_estimate=SMALL_COST,
        name="stack",
    )(where, *slabs)


def attend_back_kernel(seg_ref, g_ref, w_out_ref, q_ref, k_ref, v_ref, att_ref, lse_ref,
                       cos_ref, sin_ref, d_ref, grad_ref, k_sum, v_sum,
                       *, block, window, scale, head_size):
    tokens = g_ref.shape[0]
    half = head_size // 2
    lanes = 2 * head_size
    lane = lax.broadcasted_iota(jnp.int32, (1, lanes), 1)
    first = lane < head_size
    starts = start_row(seg_ref)
    k_sum[...] = jnp.zeros_like(k_sum)
    v_sum[...] = jnp.zeros_like(v_sum)
    for low in range(0, tokens, block):
        rows = pl.ds(low, block)
        grad_ref[rows, :] = dot(g_ref[rows, :], w_out_ref[...], ((1,), (1,))).astype(BF)
    small = block // 2
    for low in range(0, tokens, small):
        begin = first_key(low, small, window)
        end = low + small
        count = end - begin
        q = q_ref[low:end, :] * jnp.asarray(scale, BF)
        grad = grad_ref[low:end, :]
        product = (grad.astype(F32) * att_ref[low:end, :].astype(F32)).T
        zero = jnp.zeros_like(q)
        q_two = jnp.concatenate([jnp.where(first, q, zero), jnp.where(first, zero, q)], axis=0)
        grad_two = jnp.concatenate(
            [jnp.where(first, grad, zero), jnp.where(first, zero, grad)], axis=0)
        k = k_ref[begin:end, :]
        scores = dot(k, q_two, ((1,), (1,)))
        prob_grad = dot(v_ref[begin:end, :], grad_two, ((1,), (1,)))
        key_index = lax.broadcasted_iota(jnp.int32, (count, small), 0) + begin
        query_index = lax.broadcasted_iota(jnp.int32, (count, small), 1) + low
        visible = (key_index.astype(F32) >= starts[:, low:end]) & (key_index <= query_index)
        visible = jnp.concatenate([visible, visible], axis=1)
        lse = jnp.concatenate([lse_ref[0, h:h + 1, low:end] for h in range(2)], axis=1)
        row_dots = jnp.concatenate(
            [jnp.sum(product[h * head_size:(h + 1) * head_size], axis=0, keepdims=True)
             for h in range(2)], axis=1)
        weights = jnp.where(visible, jnp.exp(scores - lse), 0.0)
        score_low = (weights * (prob_grad - row_dots)).astype(BF)
        v_sum[begin:end, :] += dot(weights.astype(BF), grad_two)
        k_sum[begin:end, :] += dot(score_low, q_two)
        dq = dot(score_low, k, ((0,), (0,))) * scale
        dq = jnp.where(first, dq[:small], dq[small:])
        d_ref[low:end, :lanes] = (
            dq * cos_ref[low:end, :] - turn(dq, half) * sin_ref[low:end, :]).astype(BF)
    for low in range(0, tokens, block):
        rows = pl.ds(low, block)
        dk = k_sum[rows, :]
        d_ref[rows, lanes:2 * lanes] = (
            dk * cos_ref[rows, :] - turn(dk, half) * sin_ref[rows, :]).astype(BF)
        d_ref[rows, 2 * lanes:] = v_sum[rows, :].astype(BF)

def attend_back(seg, g, w_out, q, k, v, att, lse, cosine, sine, window, head_size):
    tokens, width = g.shape
    lanes = 2 * head_size
    pairs = q.shape[1] // lanes
    kernel = lambda *refs: attend_back_kernel(
        *refs, block=256, window=window, scale=1.0 / math.sqrt(head_size), head_size=head_size)
    column = pl.BlockSpec((tokens, lanes), lambda p: (0, p))
    inputs = hbm(seg) + vmem(g) + hbm(w_out, q, k, v, att, lse, cosine, sine)
    return pl.pallas_call(
        kernel,
        grid=(pairs,),
        in_specs=whole_specs(seg) + [
            VMEM_SPEC,
            pl.BlockSpec((lanes, width), lambda p: (p, 0)),
            column, column, column, column,
            pl.BlockSpec((1, 8, tokens), lambda p: (p, 0, 0)),
        ] + whole_specs(cosine, sine),
        out_specs=pl.BlockSpec((tokens, 3 * lanes), lambda p: (0, p)),
        out_shape=jax.ShapeDtypeStruct((tokens, 3 * lanes * pairs), BF),
        scratch_shapes=[
            pltpu.VMEM((tokens, lanes), BF),
            pltpu.VMEM((tokens, lanes), F32),
            pltpu.VMEM((tokens, lanes), F32),
        ],
        compiler_params=pltpu.CompilerParams(vmem_limit_bytes=28 << 20),
        cost_estimate=SMALL_COST,
        name="attend_back",
    )(*inputs)


def join_kernel(rank_ref, own_ref, other_ref, *out_refs, moves, plain):
    swapped = rank_ref[0] == 1
    own, other = own_ref[...], other_ref[...]
    halves = (jnp.where(swapped, other, own), jnp.where(swapped, own, other))
    for out, half, (rows, cols), (to_rows, to_cols) in moves:
        out_refs[out][to_rows, to_cols] = halves[half][rows, cols].astype(F32)
    for out, (rows, cols) in plain:
        out_refs[out][...] = own[rows, cols].astype(F32)


def join(rank, own, other, moves, plain, shapes):
    kernel = lambda *refs: join_kernel(*refs, moves=moves, plain=plain)
    return pl.pallas_call(
        kernel,
        in_specs=[
            pl.BlockSpec(memory_space=pltpu.SMEM),
            pl.BlockSpec(memory_space=pltpu.VMEM),
            pl.BlockSpec(memory_space=pltpu.VMEM),
        ],
        out_specs=[pl.BlockSpec(memory_space=pltpu.VMEM)] * len(shapes),
        out_shape=[jax.ShapeDtypeStruct(shape, F32) for shape in shapes],
        compiler_params=pltpu.CompilerParams(vmem_limit_bytes=32 << 20),
        name="join",
    )(rank.reshape(1), own, other)


def join_all_kernel(all_ref, *refs, moves):
    outs = (len(refs) - 2) // 2
    out_refs, whole_ref, blocks, sems = refs[:outs], refs[outs], refs[outs + 1:-1], refs[-1]
    groups, ranks, rows, _ = all_ref.shape
    for h in range(ranks):
        for m in range(groups):
            whole_ref[h, m * rows:(m + 1) * rows, :] = all_ref[m, h]
    copies = []
    for n in range(outs):
        for out, half, (rows, cols), (to_rows, to_cols) in moves:
            if out == n:
                blocks[out][to_rows, to_cols] = whole_ref[half, rows, cols].astype(F32)
        copies.append(pltpu.make_async_copy(blocks[n], out_refs[n], sems.at[n]))
        copies[-1].start()
    for copy in copies:
        copy.wait()


def join_all(parts, moves, shapes):
    groups, ranks, rows, cols = parts.shape
    parts, = hbm(parts)
    return pl.pallas_call(
        lambda *refs: join_all_kernel(*refs, moves=moves),
        grid=(1,),
        in_specs=whole_specs(parts),
        out_specs=[HBM_SPEC] * len(shapes),
        out_shape=[pltpu.HBM(shape, F32) for shape in shapes],
        scratch_shapes=[pltpu.VMEM((ranks, groups * rows, cols), BF)]
        + [pltpu.VMEM(shape, F32) for shape in shapes]
        + [pltpu.SemaphoreType.DMA((len(shapes),))],
        compiler_params=pltpu.CompilerParams(vmem_limit_bytes=24 << 20),
        cost_estimate=SMALL_COST,
        name="join_all",
    )(parts)


def make_body(groups, ranks, fsdp, square):
    F = ("y", "x") if square else ("f",)
    swap = [(0, 1), (1, 0)]
    pairs = square and ranks == 2 and groups == 4

    def hop(value, k):
        return lax.ppermute(value, "m", [(i, i ^ k) for i in range(groups)])

    def after(value, *earlier):
        return lax.optimization_barrier((value,) + earlier)[0]

    def between(slabs, value):
        hops, value = lax.optimization_barrier((slabs[1:], value))
        return slabs[:1] + hops, value

    def spread(slabs):
        return [hop(slab, k) if k else slab for k, slab in enumerate(slabs)]

    def both_ranks(where, slabs, span):
        if ranks == 2:
            return slabs + [lax.ppermute(slab, "r", swap) for slab in slabs]
        rows = lax.all_gather(stack(where, slabs)[:, 0], "r", axis=1)
        return [rows[:, :, :span].reshape(-1, rows.shape[-1]), rows]

    def share(part):
        if ranks == 2:
            other = lax.ppermute(part, "r", swap)
            mine_first = lax.axis_index("r") == 0
            return jnp.stack(
                [jnp.where(mine_first, part, other), jnp.where(mine_first, other, part)], axis=1)
        return lax.all_gather(part, "r", axis=1)

    def exchange(part):
        if ranks == 2:
            return part, lax.ppermute(part, "r", swap)
        return lax.psum(part, "r"), jnp.zeros_like(part)

    def gather_rows(part, wait=()):
        if not square:
            whole = lax.all_gather(part, F, axis=0, tiled=True)
            return [whole], [(None, 0, 0)], (), ()
        count = part.shape[0]
        rows = (count // 2) // 16 * 16
        send = after(part, *wait) if wait else part
        from_x = lax.ppermute(send, "x", swap)
        from_y = lax.ppermute(send, "y", swap)
        far_a = lax.ppermute(from_y[:rows], "x", swap)
        far_b = lax.ppermute(from_x[rows:], "y", swap)
        pieces = [(0, 0, count), (1, 0, count), (2, 0, count), (3, 0, rows), (3, rows, count - rows)]
        return [part, from_x, from_y, far_a, far_b], pieces, (from_x, from_y), (far_a, far_b)

    def add(*parts):
        return sum(part.astype(F32) for part in parts).astype(BF)

    def take(grad, k):
        return lax.dynamic_index_in_dim(grad, lax.axis_index(F) ^ k, 0, keepdims=False)

    def half_rows(grad):
        return (grad.shape[1] // 2) // 16 * 16

    def round_one(grad):
        far, rows = take(grad, 3), half_rows(grad)
        return lax.ppermute(far[:rows], "x", swap), lax.ppermute(far[rows:], "y", swap)

    def second_terms(grad, low, high):
        to_x, to_y, rows = take(grad, 1), take(grad, 2), half_rows(grad)
        to_x = jnp.concatenate([to_x[:rows], add(to_x[rows:], high)], axis=0)
        to_y = jnp.concatenate([add(to_y[:rows], low), to_y[rows:]], axis=0)
        return to_x, to_y

    def round_two(to_x, to_y):
        return lax.ppermute(to_x, "x", swap), lax.ppermute(to_y, "y", swap)

    def halve(owned, bit, axis):
        half = owned.shape[axis] // 2
        side = (lax.axis_index("m") // bit) % 2
        return (lax.dynamic_slice_in_dim(owned, (1 - side) * half, half, axis),
                lax.dynamic_slice_in_dim(owned, side * half, half, axis))

    def join_halves(owned, other, bit, axis):
        first = (lax.axis_index("m") // bit) % 2 == 0
        return jnp.concatenate(
            [jnp.where(first, owned, other), jnp.where(first, other, owned)], axis=axis)

    def reduce(grad):
        return lax.psum(lax.psum_scatter(grad, F, scatter_dimension=0, tiled=False), "m")

    def body(tokens, segments, w_query, w_key, w_value, w_out, w_gate, w_up, w_down,
             gain_attn, gain_ffn, cotangent):
        micro, _, span, width = tokens.shape
        head_size = width // HEADS
        seq_tokens = span * groups * ranks
        window = seq_tokens // 2
        rank = lax.axis_index("r")
        own_cols = width // ranks
        shard = w_query.shape[0]
        down_rows = w_down.shape[0]
        part_rows = down_rows // ranks
        ff = w_gate.shape[1]
        half_ff = ff // ranks

        lanes = 2 * head_size
        lanes_all = -(-own_cols // lanes) * lanes
        spare = lanes_all - own_cols
        block = span * ranks
        f_index = lax.axis_index(F)
        own_at, other_at, other_rank = (
            at.astype(jnp.uint32) for at in (rank * own_cols, (1 - rank) * own_cols, 1 - rank))
        where = jnp.stack([f_index, lax.axis_index("m"), rank])
        small_cols = 3 * lanes_all + own_cols
        gains_in = jnp.pad(jnp.stack([gain_attn, gain_ffn]), ((0, 6), (0, 0)))
        stack_own = pack(where, w_gate, w_up, w_down, fsdp, ranks)
        stack_all = lax.all_gather(stack_own, F, axis=0)
        cosine, sine = rotary_tables(seq_tokens, head_size, 2)
        small, *slabs = pack_small(
            after(where, stack_own), w_query, w_key, w_value, w_out, gains_in, tokens,
            segments[:, 0], cotangent, ranks, lanes, lanes_all)
        token_slabs, cot_slabs = slabs[:groups], slabs[groups:]
        token_slabs = spread(token_slabs)
        small_refs, small_pieces, near, far = gather_rows(small)
        if square:
            cot_slabs = cot_slabs[:1] + [after(slab, *token_slabs) for slab in cot_slabs[1:]]
        cot_slabs = spread(cot_slabs)
        if square:
            token_slabs = token_slabs[:1] + [
                after(slab, cosine, sine) for slab in token_slabs[1:]]
        token_refs = both_ranks(where, token_slabs, span)
        if ranks != 2:
            seg = token_refs[1][:, :, span, :span].reshape(1, seq_tokens).astype(F32)
            token_refs = [token_refs[0], seg]
        if square:
            own, from_x, from_y, far_a, far_b = small_refs
            at = far_a.shape[0]
            ends = [own, from_x, from_y, jnp.concatenate([far_a, far_b[:shard - at]], axis=0)]
            tails = [v[shard:shard + 2, :shard] for v in (own, from_x, from_y)]
            tails.append(far_b[shard - at:shard - at + 2, :shard])
            gains = jnp.zeros((fsdp, 2, shard), BF)
            out_cols = jnp.zeros((width, own_cols), BF)
            for offset in range(4):
                to = (f_index ^ offset) * shard
                gains = lax.dynamic_update_index_in_dim(gains, tails[offset], f_index ^ offset, 0)
                out_cols = lax.dynamic_update_slice_in_dim(
                    out_cols, ends[offset][:shard, 3 * lanes_all:], to, 0)
            gains = gains.transpose(1, 0, 2).reshape(2, width)
            small_pieces = [(o, f, min(n, shard - f)) for o, f, n in small_pieces]
            qkv_refs = small_refs
        else:
            whole = small_refs[0].reshape(fsdp, shard + 8, small_cols)
            gains = whole[:, shard:shard + 2, :shard].transpose(1, 0, 2).reshape(2, width)
            out_cols = whole[:, :shard, 3 * lanes_all:].reshape(width, own_cols)
            qkv_refs = [whole[:, :shard, :3 * lanes_all].reshape(width, 3 * lanes_all)]
        gains = gains.astype(F32)
        gain_one = gains[0:1]
        if ranks == 2:
            give = lax.dynamic_slice_in_dim(out_cols, (1 - rank) * own_cols, own_cols, 0)
            keep = lax.dynamic_slice_in_dim(out_cols, rank * own_cols, own_cols, 0)
            got = lax.ppermute(give, "r", swap)
            w_out_own = jnp.where(rank == 0, jnp.concatenate([keep, got], 1),
                                  jnp.concatenate([got, keep], 1))
        else:
            pieces = lax.all_to_all(out_cols, "r", 0, 0, tiled=True)
            pieces = pieces.reshape(ranks, own_cols, own_cols)
            w_out_own = jnp.concatenate([pieces[i] for i in range(ranks)], axis=1)
        w_out_even = jnp.pad(w_out_own, ((0, spare), (0, 0)))

        cosine, gains, gain_one, own_at, other_at, other_rank = lax.optimization_barrier(
            (cosine, gains, gain_one, own_at, other_at, other_rank))
        q, k, v, att, lse, w_qkv, x, seg = attend(
            where, cosine, sine, token_refs, ranks, qkv_refs, small_pieces, shard, lanes_all,
            window, head_size, width)
        if square:
            cot_slabs, att = between(cot_slabs, att)
        own, got = exchange(dot(att, w_out_even).astype(BF))
        cot_refs = both_ranks(where, cot_slabs, span)
        if ranks != 2:
            cot_refs = cot_refs[:1]
        total, middle_low, hidden_low, gate_back, silu, part, gu, down = forward(
            x, own, got, gain_one, stack_all, shard, part_rows, half_ff, block)
        own, got = exchange(part)

        *out_slabs, ffn_grad_low, gu_grad_low, part, gain_ffn_grad = backward(
            where, total, own, got, gate_back, silu, gains, gu, down, cot_refs, block, groups, ranks)
        own, got = exchange(part)
        gu_w_grad = dot(middle_low, gu_grad_low, ((0,), (0,))).astype(BF)
        if ranks == 2:
            got, gu_w_grad = lax.optimization_barrier((got, gu_w_grad))
        stack_grad = arrange(gu_w_grad, hidden_low, ffn_grad_low, fsdp)
        stack_owned = lax.psum_scatter(stack_grad, F, scatter_dimension=0, tiled=False)
        own, got = after(own, stack_grad), after(got, stack_grad)
        branch_grad_low, branch_keep, gain_grads = norm_back(
            where[2:], total, ffn_grad_low, own, got, gain_one, gain_ffn_grad,
            fsdp, small_cols, block, span)
        out_w_grad = dot(att, branch_grad_low, ((0,), (0,)))[:own_cols].astype(BF)
        if ranks == 2:
            give = lax.dynamic_slice_in_dim(out_w_grad, other_at, own_cols, 1)
            keep = lax.dynamic_slice_in_dim(out_w_grad, own_at, own_cols, 1)
            got = lax.ppermute(give, "r", swap)
            out_cols_grad = jnp.where(rank == 0, jnp.concatenate([keep, got], 0),
                                      jnp.concatenate([got, keep], 0))
        else:
            rows = out_w_grad.reshape(own_cols, ranks, own_cols).transpose(1, 0, 2)
            out_cols_grad = lax.all_to_all(rows, "r", 0, 0, tiled=True).reshape(width, own_cols)
        branch_grad_low = after(branch_grad_low, out_cols_grad)
        d_qkv = attend_back(
            seg, branch_grad_low, w_out_even, q, k, v, att, lse, cosine, sine, window, head_size)
        if square:
            out_slabs, d_qkv = between(spread(out_slabs), d_qkv)
        else:
            out_slabs = spread(out_slabs)
        output = stack(where, out_slabs)
        qkv_w_grad = dot(x, d_qkv, ((0,), (0,))).astype(BF)
        small_grad = jnp.concatenate([qkv_w_grad, out_cols_grad], axis=1)
        small_grad = jnp.concatenate(
            [small_grad.reshape(fsdp, shard, small_cols), gain_grads], axis=1)
        if pairs:
            small_one = round_one(small_grad)
            d_qkv = after(d_qkv, small_grad)
        part = dot(d_qkv, w_qkv, ((1,), (1,))).astype(BF)
        if ranks == 2:
            rows = part.reshape(groups, ranks, span, width)
            give = lax.dynamic_index_in_dim(rows, other_rank, 1, keepdims=False)
            got = lax.ppermute(give, "r", swap)
        else:
            part = lax.psum(part, "r")
            got = jnp.zeros_like(branch_keep, BF)
        grad_slabs = list(finish(where, branch_keep, part, got, ranks))
        grad_slabs = spread(grad_slabs)
        if pairs:
            grad_slabs[:3], small_one = between(grad_slabs[:3], small_one)
            terms = second_terms(small_grad, *small_one)
            small_two, output, grad_slabs[3] = lax.optimization_barrier(
                (round_two(*terms), output, grad_slabs[3]))
            input_grad = stack(where, grad_slabs)
            stack_owned = after(stack_owned, *terms)
            quarter = lax.psum_scatter(stack_owned, "m", scatter_dimension=0, tiled=True)
            give, keep = halve(add(take(small_grad, 0), *small_two), 1, 1)
            got, quarter, input_grad = lax.optimization_barrier((hop(give, 1), quarter, input_grad))
            stack_parts = lax.all_gather(quarter, ("m", "r"), axis=0)
            stack_parts = stack_parts.reshape((groups, ranks) + quarter.shape)
            give, keep = halve(add(keep, got), 2, 1)
            owned = add(keep, hop(give, 2))
            owned = join_halves(owned, hop(owned, 2), 2, 1)
            small_sum = join_halves(owned, hop(owned, 1), 1, 1)
        else:
            stack_sum = lax.psum(stack_owned, "m")
            small_sum = reduce(small_grad)
            input_grad = stack(where, grad_slabs)
        if pairs:
            everything = slice(None)
            chunks = 2 * half_ff // 256
            stack_moves = [
                (n, h, (slice((n * fsdp + j) * shard, (n * fsdp + j + 1) * shard), everything),
                 (everything, slice(j * down_rows + h * part_rows, j * down_rows + (h + 1) * part_rows)))
                for n in range(2) for h in range(2) for j in range(fsdp)]
            stack_moves += [
                (2, h, (slice(chunks * shard + c * part_rows, chunks * shard + (c + 1) * part_rows),
                        everything),
                 (slice(h * part_rows, (h + 1) * part_rows), slice(c * 256, (c + 1) * 256)))
                for h in range(2) for c in range(width // 256)]
            small_moves = [
                (n, h, (slice(0, shard), slice((3 * p + n) * lanes, (3 * p + n + 1) * lanes)),
                 (everything, slice(h * own_cols + p * lanes, h * own_cols + (p + 1) * lanes)))
                for n in range(3) for h in range(2) for p in range(own_cols // lanes)]
            small_moves += [
                (3, h, (slice(0, shard), slice(3 * lanes_all, small_cols)),
                 (everything, slice(h * own_cols, (h + 1) * own_cols))) for h in range(2)]
            small_plain = [
                (4 + n, (slice(shard + n, shard + n + 1), slice(0, shard))) for n in range(2)]
            gate_w, up_w, down_grad = join_all(
                stack_parts, stack_moves, [(shard, ff)] * 2 + [(down_rows, width)])
            small_got, gate_w, up_w, down_grad = lax.optimization_barrier(
                (lax.ppermute(small_sum, "r", swap), gate_w, up_w, down_grad))
            query_w, key_w, value_w, out_w, gain_a, gain_f = join(
                rank, small_sum, small_got, small_moves, small_plain,
                [(shard, width)] * 4 + [(1, shard)] * 2)
        else:
            at = 2 * half_ff // 256 * shard
            down_sum = jnp.moveaxis(stack_sum[at:].reshape(-1, part_rows, 256), 0, 1)
            down_grad = jnp.moveaxis(share(down_sum.reshape(part_rows, width)), 1, 0)
            down_grad = down_grad.reshape(down_rows, width).astype(F32)
            gu_sum = jnp.moveaxis(stack_sum[:at].reshape(-1, shard, 256), 0, 1)
            gu_both = share(gu_sum.reshape(shard, 2 * fsdp, part_rows))
            gu_both = gu_both.reshape(shard, ranks, 2, fsdp, part_rows).astype(F32)
            gate_w, up_w = (
                gu_both[:, :, n].transpose(0, 2, 1, 3).reshape(shard, ff) for n in range(2))
            small_both = share(small_sum)[:shard].astype(F32)
            three = small_both[:, :, :3 * lanes_all].reshape(shard, ranks, -1, 3, lanes)
            query_w, key_w, value_w = (
                three[:, :, :, n].reshape(shard, ranks, lanes_all)[:, :, :own_cols].reshape(shard, width)
                for n in range(3))
            out_w = small_both[:, :, 3 * lanes_all:].reshape(shard, width)
            gain_a, gain_f = small_sum[shard, :shard].astype(F32), small_sum[shard + 1, :shard].astype(F32)
        return (output, input_grad, query_w, key_w, value_w, out_w,
                gate_w, up_w, down_grad, gain_a.reshape(shard), gain_f.reshape(shard))

    return body


def solution(mesh):
    def run(*args):
        groups = args[0].shape[0]
        seq, fsdp = mesh.shape["seq"], mesh.shape["fsdp"]
        ranks = seq // groups
        square = fsdp == 4
        names = ("m", "r") + (("y", "x") if square else ("f",))
        sizes = (groups, ranks) + ((2, 2) if square else (fsdp,))
        order = [mesh.axis_names.index(name) for name in ("seq", "fsdp")]
        inner = Mesh(mesh.devices.transpose(order).reshape(sizes), names)
        f = ("y", "x") if square else "f"
        s = ("m", "r")
        rows = P(f, None)
        data = P(None, f, s, None)
        in_specs = (data, P(None, f, s)) + (rows,) * 7 + (P(f), P(f), data)
        out_specs = (data, data) + (rows,) * 7 + (P(f), P(f))
        body = make_body(groups, ranks, fsdp, square)
        return jax.shard_map(
            body, mesh=inner, in_specs=in_specs, out_specs=out_specs, check_vma=False)(*args)

    return run
```

```python
import math

import jax
import jax.numpy as jnp
from jax import lax
from jax.experimental import pallas as pl
from jax.experimental.pallas import tpu as pltpu
from jax.sharding import Mesh, PartitionSpec as P

HEADS = 12
DOCS = 4
EPS = 1e-06
NEGATIVE = -1e30
BF = jnp.bfloat16
F32 = jnp.float32


def dot(left, right, dims=((1,), (0,))):
    return lax.dot_general(left, right, (dims, ((), ())), preferred_element_type=F32)


def rotary_tables(seq_tokens, head_size, copies):
    half = head_size // 2
    frequency = 10000.0 ** (-jnp.arange(half, dtype=F32) / half)
    angle = jnp.arange(seq_tokens, dtype=jnp.int32).astype(F32)[:, None] * frequency[None, :]
    cosine, sine = jnp.cos(angle), jnp.sin(angle)
    return (
        jnp.concatenate([cosine, cosine] * copies, axis=1),
        jnp.concatenate([-sine, sine] * copies, axis=1),
    )


def turn(rows, half):
    lanes = rows.shape[1]
    lane = lax.broadcasted_iota(jnp.int32, (1, lanes), 1)
    low = (lane // half) % 2 == 0
    return jnp.where(low, pltpu.roll(rows, lanes - half, 1), pltpu.roll(rows, half, 1))


def first_key(query_first, block, window):
    return max(0, (query_first - window + 1) // block * block)


def start_row(seg_ref):
    seg = seg_ref[...]
    starts = jnp.zeros_like(seg)
    for doc in range(1, DOCS):
        before = jnp.sum(jnp.where(seg < doc, 1.0, 0.0), axis=1, keepdims=True)
        starts = jnp.maximum(starts, jnp.where(seg >= doc, before, 0.0))
    return starts


def place(target, refs, pieces, me, shard):
    for ref, (offset, first, rows) in zip(refs, pieces):
        if offset is None:
            target[...] = ref[...]
        else:
            start = pl.multiple_of((me ^ offset) * shard + first, 16)
            target[pl.ds(start, rows), :] = ref[0:rows, 0:target.shape[1]]


def place_tokens(target, refs, where_ref, ranks):
    if len(refs) == 1:
        target[...] = refs[0][...]
        return
    groups = len(refs) // ranks
    span = target.shape[0] // (groups * ranks)
    for n, ref in enumerate(refs):
        rank = where_ref[2] if n < groups else 1 - where_ref[2]
        chunk = (where_ref[1] ^ (n % groups)) * ranks + rank
        target[pl.ds(pl.multiple_of(chunk * span, span), span), :] = ref[0:span, :]


def place_segments(target, refs, where_ref, ranks):
    groups = len(refs) // ranks
    span = target.shape[1] // (groups * ranks)
    for n, ref in enumerate(refs):
        rank = where_ref[2] if n < groups else 1 - where_ref[2]
        chunk = (where_ref[1] ^ (n % groups)) * ranks + rank
        row = ref[span:span + 16, 0:span].astype(F32)[0:1, :]
        target[:, pl.ds(pl.multiple_of(chunk * span, span), span)] = row


def stack_copies(gu, down, stack_ref, sems, shard, part_rows):
    members, chunks, groups = stack_ref.shape[0], gu.shape[1] // 256, []
    for c in range(chunks):
        groups.append([
            pltpu.make_async_copy(
                stack_ref.at[j, c * shard:(c + 1) * shard, :],
                gu.at[j * shard:(j + 1) * shard, c * 256:(c + 1) * 256],
                sems.at[c, j]) for j in range(members)])
    for c in range(down.shape[1] // 256):
        at = chunks * shard + c * part_rows
        groups.append([
            pltpu.make_async_copy(
                stack_ref.at[j, at:at + part_rows, :],
                down.at[j * part_rows:(j + 1) * part_rows, c * 256:(c + 1) * 256],
                sems.at[chunks + c, j]) for j in range(members)])
    return groups


def attend_kernel(where_ref, cos_ref, sin_ref, *refs, pieces, token_count, ranks, shard, block,
                  window, scale, head_size):
    inputs, refs = refs[:-9], refs[-9:]
    q_ref, k_ref, v_ref, att_ref, lse_ref, w_ref, x_ref, seg_ref, col_ref = refs
    token_refs, w_refs = inputs[:token_count], inputs[token_count:]
    tokens = x_ref.shape[0]
    lanes = 2 * head_size
    lane = lax.broadcasted_iota(jnp.int32, (1, lanes), 1)
    first = lane < head_size
    pair = pl.program_id(0)

    @pl.when(pair == 0)
    def _():
        place(w_ref, w_refs, pieces, where_ref[0], shard)
        place_tokens(x_ref, token_refs[:1] if token_count == 2 else token_refs, where_ref, ranks)
        if token_count == 2:
            seg_ref[...] = token_refs[1][...]
        else:
            place_segments(seg_ref, token_refs, where_ref, ranks)
        starts = start_row(seg_ref)
        col_ref[...] = jnp.broadcast_to(starts, (128, tokens)).T

    w = w_ref[:, pl.ds(pl.multiple_of(pair * 3 * lanes, lanes), 3 * lanes)]
    for low in range(0, tokens, block):
        rows = pl.ds(low, block)
        lin = dot(x_ref[rows, :], w)
        cosine, sine = cos_ref[rows, :], sin_ref[rows, :]
        half = head_size // 2
        q_lin, k_lin = lin[:, :lanes], lin[:, lanes:2 * lanes]
        q_ref[rows, :] = (q_lin * cosine + turn(q_lin, half) * sine).astype(BF)
        k_ref[rows, :] = (k_lin * cosine + turn(k_lin, half) * sine).astype(BF)
        v_ref[rows, :] = lin[:, 2 * lanes:].astype(BF)
    for low in range(0, tokens, block):
        begin = first_key(low, block, window)
        end = low + block
        q = q_ref[low:end, :] * jnp.asarray(scale, BF)
        zero = jnp.zeros_like(q)
        stacked = jnp.concatenate([jnp.where(first, q, zero), jnp.where(first, zero, q)], axis=0)
        scores = dot(stacked, k_ref[begin:end, :], ((1,), (1,)))
        key_index = lax.broadcasted_iota(jnp.int32, (block, end - begin), 1) + begin
        query_index = lax.broadcasted_iota(jnp.int32, (block, end - begin), 0) + low
        visible = (key_index.astype(F32) >= col_ref[low:end, 0:1]) & (key_index <= query_index)
        parts = []
        for head in range(2):
            own = jnp.where(visible, scores[head * block:(head + 1) * block], NEGATIVE)
            top = jnp.max(own, axis=1, keepdims=True)
            weights = jnp.exp(own - top)
            total = jnp.sum(weights, axis=1, keepdims=True)
            out = dot(weights.astype(BF), v_ref[begin:end, :]) / total
            parts.append(out)
            lse = jnp.broadcast_to(top + jnp.log(total), (block, 128))
            lse_ref[0, head:head + 1, low:end] = lse.T[0:1, :]
        att_ref[low:end, :] = jnp.where(first, parts[0], parts[1]).astype(BF)


def hbm(*arrays):
    return [pltpu.with_memory_space_constraint(a, pltpu.HBM) for a in arrays]


def vmem(*arrays):
    return [pltpu.with_memory_space_constraint(a, pltpu.VMEM) for a in arrays]


def whole_specs(*arrays):
    return [pl.BlockSpec(a.shape, lambda *_, n=a.ndim: (0,) * n, pipeline_mode=pl.Buffered(1))
            for a in arrays]


SMALL_COST = pl.CostEstimate(flops=1, bytes_accessed=1, transcendentals=0)
VMEM_SPEC = pl.BlockSpec(memory_space=pltpu.VMEM)
SMEM_SPEC = pl.BlockSpec(memory_space=pltpu.SMEM)


def attend(where, cosine, sine, token_refs, ranks, weights, pieces, shard, lanes_all, window,
           head_size, width):
    tokens = cosine.shape[0]
    lanes = 2 * head_size
    pairs = lanes_all // lanes
    kernel = lambda *refs: attend_kernel(
        *refs, pieces=pieces, token_count=len(token_refs), ranks=ranks, shard=shard, block=256,
        window=window, scale=1.0 / math.sqrt(head_size), head_size=head_size)
    column = pl.BlockSpec((tokens, lanes), lambda p: (0, p))
    whole = lambda *shape: pl.BlockSpec(shape, lambda p: (0, 0))
    inputs = hbm(cosine, sine, *token_refs, *weights)
    return pl.pallas_call(
        kernel,
        grid=(pairs,),
        in_specs=[SMEM_SPEC] + whole_specs(*inputs),
        out_specs=[column, column, column, column,
                   pl.BlockSpec((1, 8, tokens), lambda p: (p, 0, 0)),
                   whole(width, 3 * lanes_all), whole(tokens, width), whole(1, tokens)],
        out_shape=[pltpu.HBM((tokens, lanes_all), BF)] * 4
        + [pltpu.HBM((pairs, 8, tokens), F32), pltpu.HBM((width, 3 * lanes_all), BF),
           pltpu.HBM((tokens, width), BF), pltpu.HBM((1, tokens), F32)],
        scratch_shapes=[pltpu.VMEM((tokens, 128), F32)],
        compiler_params=pltpu.CompilerParams(vmem_limit_bytes=28 << 20),
        cost_estimate=SMALL_COST,
        name="attend",
    )(where, *inputs)


def unit_of(rows):
    factor = lax.rsqrt(jnp.mean(rows * rows, axis=1, keepdims=True) + EPS)
    return rows * factor, factor


def forward_kernel(x_ref, own_ref, got_ref, gain_ref, stack_ref, sum_ref, low_ref, hidden_ref,
                   gate_ref, silu_ref, part_ref, gu, down, sems, *, shard, part_rows):
    step, block = pl.program_id(0), x_ref.shape[0]
    ff = down.shape[0]

    @pl.when(step == 0)
    def _():
        copies = stack_copies(gu, down, stack_ref, sems, shard, part_rows)
        for group in copies:
            for copy in group:
                copy.start()
        for group in copies:
            for copy in group:
                copy.wait()

    rows = pl.ds(pl.multiple_of(step * block, block), block)
    total = x_ref[...].astype(F32) + own_ref[...].astype(F32) + got_ref[...].astype(F32)
    sum_ref[rows, :] = total
    middle_low = (unit_of(total)[0] * gain_ref[...]).astype(BF)
    low_ref[rows, :] = middle_low
    for c in range(0, ff, 256):
        cols = slice(c, c + 256)
        gate = dot(middle_low, gu[:, cols])
        up = dot(middle_low, gu[:, ff + c:ff + c + 256])
        sigmoid = jax.nn.sigmoid(gate)
        silu = gate * sigmoid
        hidden_ref[rows, cols] = (silu * up).astype(BF)
        gate_ref[rows, cols] = (up * sigmoid * (1.0 + gate * (1.0 - sigmoid))).astype(BF)
        silu_ref[rows, cols] = silu.astype(BF)
    part_ref[...] = dot(hidden_ref[rows, :], down[...]).astype(BF)


HBM_SPEC = pl.BlockSpec(memory_space=pltpu.HBM)


def forward(x, own, got, gain, stack, shard, part_rows, ff, block):
    tokens, width = x.shape
    row = lambda cols: pl.BlockSpec((block, cols), lambda i: (i, 0))
    x, own, got, stack = hbm(x, own, got, stack)
    return pl.pallas_call(
        lambda *refs: forward_kernel(*refs, shard=shard, part_rows=part_rows),
        grid=(tokens // block,),
        in_specs=[row(width), row(width), row(width)] + whole_specs(gain) + [HBM_SPEC],
        out_specs=[VMEM_SPEC] * 5 + [row(width)] + [VMEM_SPEC] * 2,
        out_shape=[pltpu.VMEM((tokens, width), F32), pltpu.VMEM((tokens, width), BF)]
        + [pltpu.VMEM((tokens, ff), BF)] * 3 + [jax.ShapeDtypeStruct((tokens, width), BF)]
        + [pltpu.VMEM((width, 2 * ff), BF), pltpu.VMEM((ff, width), BF)],
        scratch_shapes=[pltpu.SemaphoreType.DMA(((2 * ff + width) // 256, stack.shape[0]))],
        compiler_params=pltpu.CompilerParams(vmem_limit_bytes=16 << 20),
        cost_estimate=SMALL_COST,
        name="ffn_forward",
    )(x, own, got, gain, stack)


def backward_kernel(where_ref, sum_ref, own_ref, got_ref, gate_ref, silu_ref, gains_ref, gu, down,
                    *refs, cot_count, groups, ranks):
    cot_refs, refs = refs[:cot_count], refs[cot_count:]
    out_refs, refs = refs[:groups], refs[groups:]
    low_ref, gu_grad_ref, part_ref, gain_ref, cot_ref, rows_ref = refs
    step = pl.program_id(0)
    block, span = rows_ref.shape[0], out_refs[0].shape[0]

    @pl.when(step == 0)
    def _():
        place_tokens(cot_ref, cot_refs, where_ref, ranks)
        gain_ref[...] = jnp.zeros_like(gain_ref)

    rows = pl.ds(pl.multiple_of(step * block, block), block)
    gain_two = gains_ref[1:2, :]
    middle = unit_of(sum_ref[rows, :])[0] * gains_ref[0:1, :]
    unit, factor = unit_of(middle + own_ref[...].astype(F32) + got_ref[...].astype(F32))
    rows_ref[...] = unit * gain_two
    cot = cot_ref[rows, :].astype(F32)
    gain_ref[...] += jnp.sum(cot * unit, axis=0, keepdims=True)
    scaled = cot * gain_two
    grad_low = (factor * (scaled - unit * jnp.mean(scaled * unit, axis=1, keepdims=True))).astype(BF)
    low_ref[rows, :] = grad_low
    ff = down.shape[0]
    for c in range(0, ff, 256):
        cols = slice(c, c + 256)
        hidden_grad = dot(grad_low, down[cols, :], ((1,), (1,)))
        gu_grad_ref[rows, cols] = (hidden_grad * gate_ref[rows, cols].astype(F32)).astype(BF)
        gu_grad_ref[rows, ff + c:ff + c + 256] = (
            hidden_grad * silu_ref[rows, cols].astype(F32)).astype(BF)
    part_ref[...] = dot(gu_grad_ref[rows, :], gu[...], ((1,), (1,))).astype(BF)
    kept = rows_ref[pl.ds(pl.multiple_of(where_ref[2] * span, span), span), :].astype(BF)
    for k, out_ref in enumerate(out_refs):
        @pl.when(step == (where_ref[1] ^ k))
        def _(out_ref=out_ref):
            out_ref[...] = kept


def backward(where, total, own, got, gate, silu, gains, gu, down, cot, block, groups, ranks):
    tokens, width = total.shape
    ff = gate.shape[1]
    kernel = lambda *refs: backward_kernel(
        *refs, cot_count=len(cot), groups=groups, ranks=ranks)
    row = pl.BlockSpec((block, width), lambda i: (i, 0))
    slab = pl.BlockSpec((block // ranks, width), lambda i: (0, 0))
    total, gate, silu, gu, down = vmem(total, gate, silu, gu, down)
    return pl.pallas_call(
        kernel,
        grid=(tokens // block,),
        in_specs=[SMEM_SPEC, VMEM_SPEC, row, row, VMEM_SPEC, VMEM_SPEC] + whole_specs(gains)
        + [VMEM_SPEC] * 2 + whole_specs(*cot),
        out_specs=[slab] * groups + [VMEM_SPEC, VMEM_SPEC, row,
                                     pl.BlockSpec((1, width), lambda i: (0, 0))],
        out_shape=[pltpu.HBM((block // ranks, width), BF)] * groups
        + [pltpu.VMEM((tokens, width), BF), pltpu.VMEM((tokens, 2 * ff), BF),
           pltpu.HBM((tokens, width), BF), pltpu.HBM((1, width), F32)],
        scratch_shapes=[pltpu.VMEM((tokens, width), BF), pltpu.VMEM((block, width), F32)],
        compiler_params=pltpu.CompilerParams(vmem_limit_bytes=20 << 20),
        cost_estimate=SMALL_COST,
        name="ffn_backward",
    )(where, total, own, got, gate, silu, gains, gu, down, *cot)


def norm_back_kernel(rank_ref, sum_ref, grad_ref, own_ref, got_ref, gain_ref, other_ref,
                     low_ref, keep_ref, out_ref, rows_ref, gain_grad_ref):
    step, block = pl.program_id(0), rows_ref.shape[0]

    @pl.when(step == 0)
    def _():
        gain_grad_ref[...] = jnp.zeros_like(gain_grad_ref)

    rows = pl.ds(pl.multiple_of(step * block, block), block)
    unit, factor = unit_of(sum_ref[rows, :])
    grad = (grad_ref[...].astype(F32) + own_ref[...].astype(F32)) + got_ref[...].astype(F32)
    gain_grad_ref[...] += jnp.sum(grad * unit, axis=0, keepdims=True)
    scaled = grad * gain_ref[...]
    branch_grad = factor * (scaled - unit * jnp.mean(scaled * unit, axis=1, keepdims=True))
    low_ref[rows, :] = branch_grad.astype(BF)
    rows_ref[...] = branch_grad
    span = keep_ref.shape[1]
    keep_ref[0] = rows_ref[pl.ds(pl.multiple_of(rank_ref[0] * span, span), span), :]

    @pl.when(step == pl.num_programs(0) - 1)
    def _():
        out_ref[...] = jnp.zeros_like(out_ref)
        shard = gain_ref.shape[1] // out_ref.shape[0]
        first = lax.broadcasted_iota(jnp.int32, (16, shard), 0)
        for j in range(out_ref.shape[0]):
            lanes = slice(j * shard, (j + 1) * shard)
            one = jnp.broadcast_to(gain_grad_ref[:, lanes], (16, shard))
            two = jnp.broadcast_to(other_ref[:, lanes], (16, shard))
            out_ref[j, :, 0:shard] = jnp.where(
                first == 0, one, jnp.where(first == 1, two, 0.0)).astype(BF)


def norm_back(rank, total, grad, own, got, gain, other_grad, fsdp, cols, block, span):
    tokens, width = total.shape
    row = pl.BlockSpec((block, width), lambda i: (i, 0))
    inputs = vmem(total) + hbm(grad, own, got)
    return pl.pallas_call(
        norm_back_kernel,
        grid=(tokens // block,),
        in_specs=[SMEM_SPEC, VMEM_SPEC, row, row, row] + whole_specs(gain, other_grad),
        out_specs=[VMEM_SPEC, pl.BlockSpec((1, span, width), lambda i: (i, 0, 0)),
                   pl.BlockSpec((fsdp, 16, cols), lambda i: (0, 0, 0))],
        out_shape=[pltpu.VMEM((tokens, width), BF),
                   pltpu.HBM((tokens // block, span, width), F32),
                   pltpu.HBM((fsdp, 16, cols), BF)],
        scratch_shapes=[pltpu.VMEM((block, width), F32), pltpu.VMEM((1, width), F32)],
        compiler_params=pltpu.CompilerParams(vmem_limit_bytes=16 << 20),
        cost_estimate=SMALL_COST,
        name="norm_back",
    )(rank, *inputs, gain, other_grad)


def pick(rank, parts):
    value = parts[0]
    for r in range(1, len(parts)):
        value = jnp.where(rank == r, parts[r], value)
    return value


def pack_small_kernel(where_ref, query_ref, key_ref, value_ref, out_ref, gain_ref, tokens_ref,
                      seg_ref, cot_ref, small_ref, *slab_refs, ranks, lanes, lanes_all):
    slab_refs, cot_slabs = slab_refs[:len(slab_refs) // 2], slab_refs[len(slab_refs) // 2:]
    for k, ref in enumerate(cot_slabs):
        ref[...] = cot_ref[where_ref[1] ^ k, 0]
    rank, m = where_ref[2], where_ref[1]
    shard, width = query_ref.shape
    own_cols = width // ranks
    if lanes_all != own_cols:
        small_ref[...] = jnp.zeros_like(small_ref)
    for n, ref in enumerate((query_ref, key_ref, value_ref)):
        for low in range(0, own_cols, lanes):
            size = min(lanes, own_cols - low)
            at = (low // lanes * 3 + n) * lanes
            small_ref[0:shard, at:at + size] = pick(
                rank, [ref[:, r * own_cols + low:r * own_cols + low + size] for r in range(ranks)])
    small_ref[0:shard, 3 * lanes_all:] = pick(
        rank, [out_ref[:, r * own_cols:(r + 1) * own_cols] for r in range(ranks)])
    small_ref[shard:, :] = jnp.zeros_like(small_ref[shard:, :])
    small_ref[shard:, 0:shard] = gain_ref[...]
    span = tokens_ref.shape[2]
    for k, ref in enumerate(slab_refs):
        ref[0:span, :] = tokens_ref[m ^ k, 0]
        ref[span:, :] = jnp.zeros_like(ref[span:, :])
        row = seg_ref[pl.ds(m ^ k, 1), :].astype(F32)
        ref[span:, 0:span] = jnp.broadcast_to(row, (16, span)).astype(BF)


def pack_small(where, query, key, value, out, gains, tokens, segments, cot, ranks, lanes,
               lanes_all):
    shard, width = query.shape
    groups, _, span, _ = tokens.shape
    cols = 3 * lanes_all + width // ranks
    inputs = hbm(query, key, value, out, gains, tokens, segments, cot)
    shapes = [(shard + 16, cols)] + [(span + 16, width)] * groups + [(span, width)] * groups
    return pl.pallas_call(
        lambda *refs: pack_small_kernel(*refs, ranks=ranks, lanes=lanes, lanes_all=lanes_all),
        grid=(1,),
        in_specs=[SMEM_SPEC] + whole_specs(*inputs),
        out_specs=[pl.BlockSpec(shape, lambda i: (0, 0)) for shape in shapes],
        out_shape=[pltpu.HBM(shape, BF) for shape in shapes],
        compiler_params=pltpu.CompilerParams(vmem_limit_bytes=24 << 20),
        cost_estimate=SMALL_COST,
        name="pack_small",
    )(where, *inputs)


def pack_kernel(where_ref, gate_ref, up_ref, down_ref, out_ref, gu, *, fsdp, ranks):
    rank = where_ref[2]
    shard, cols = gu.shape
    part = down_ref.shape[0] // ranks
    for n, ref in enumerate((gate_ref, up_ref)):
        for j in range(fsdp):
            low = (n * fsdp + j) * part
            gu[:, low:low + part] = pick(
                rank, [ref[:, (j * ranks + r) * part:(j * ranks + r + 1) * part]
                       for r in range(ranks)])
    chunks = cols // 256
    for c in range(chunks):
        out_ref[c * shard:(c + 1) * shard, :] = gu[:, c * 256:(c + 1) * 256]
    rows = pl.ds(pl.multiple_of(rank * part, 16), part)
    for c in range(down_ref.shape[1] // 256):
        at = chunks * shard + c * part
        out_ref[at:at + part, :] = down_ref[rows, c * 256:(c + 1) * 256]


def pack(where, gate, up, down, fsdp, ranks):
    shard, ff = gate.shape
    cols = 2 * ff // ranks
    rows = cols // 256 * shard + down.shape[1] // 256 * (down.shape[0] // ranks)
    inputs = hbm(gate, up, down)
    return pl.pallas_call(
        lambda *refs: pack_kernel(*refs, fsdp=fsdp, ranks=ranks),
        grid=(1,),
        in_specs=[SMEM_SPEC] + whole_specs(*inputs),
        out_specs=pl.BlockSpec((rows, 256), lambda i: (0, 0)),
        out_shape=pltpu.HBM((rows, 256), BF),
        scratch_shapes=[pltpu.VMEM((shard, cols), BF)],
        compiler_params=pltpu.CompilerParams(vmem_limit_bytes=24 << 20),
        cost_estimate=SMALL_COST,
        name="pack",
    )(where, *inputs)


def arrange_kernel(gu_ref, hidden_ref, grad_ref, out_ref, down, sems):
    fsdp = out_ref.shape[0]
    shard, part = gu_ref.shape[0] // fsdp, hidden_ref.shape[1] // fsdp
    chunks = gu_ref.shape[1] // 256
    copies = []

    def send(source, j, low, rows):
        copies.append(pltpu.make_async_copy(
            source, out_ref.at[j, low:low + rows, :], sems.at[len(copies)]))
        copies[-1].start()

    for c in range(chunks):
        for j in range(fsdp):
            send(gu_ref.at[j * shard:(j + 1) * shard, c * 256:(c + 1) * 256], j, c * shard, shard)
    for c in range(grad_ref.shape[1] // 256):
        down[c] = dot(hidden_ref[...], grad_ref[:, c * 256:(c + 1) * 256], ((0,), (0,))).astype(BF)
        for j in range(fsdp):
            send(down.at[c, j * part:(j + 1) * part, :], j, chunks * shard + c * part, part)
    for copy in copies:
        copy.wait()


def arrange(gu, hidden, grad, fsdp):
    shard, ff, width = gu.shape[0] // fsdp, hidden.shape[1], grad.shape[1]
    rows = gu.shape[1] // 256 * shard + width // 256 * (ff // fsdp)
    return pl.pallas_call(
        arrange_kernel,
        in_specs=[VMEM_SPEC] * 3,
        out_specs=HBM_SPEC,
        out_shape=pltpu.HBM((fsdp, rows, 256), BF),
        scratch_shapes=[pltpu.VMEM((width // 256, ff, 256), BF),
                        pltpu.SemaphoreType.DMA(((gu.shape[1] + width) // 256 * fsdp,))],
        compiler_params=pltpu.CompilerParams(vmem_limit_bytes=16 << 20),
        cost_estimate=SMALL_COST,
        name="arrange",
    )(*vmem(gu, hidden, grad))


def finish_kernel(where_ref, keep_ref, part_ref, got_ref, *out_refs, ranks):
    groups, span, _ = keep_ref.shape
    for k, ref in enumerate(out_refs):
        group = where_ref[1] ^ k
        row = (group * ranks + where_ref[2]) * span
        own = part_ref[pl.ds(pl.multiple_of(row, span), span), :].astype(F32)
        ref[...] = (keep_ref[group] + own + got_ref[group].astype(F32)).astype(BF)


def finish(where, keep, part, got, ranks):
    groups, span, width = keep.shape
    return pl.pallas_call(
        lambda *refs: finish_kernel(*refs, ranks=ranks),
        in_specs=[SMEM_SPEC] + [VMEM_SPEC] * 3,
        out_specs=[VMEM_SPEC] * groups,
        out_shape=[jax.ShapeDtypeStruct((span, width), BF)] * groups,
        compiler_params=pltpu.CompilerParams(vmem_limit_bytes=24 << 20),
        cost_estimate=SMALL_COST,
        name="finish",
    )(where, keep, part, got)


def stack_kernel(where_ref, *refs):
    out_ref = refs[-1]
    for k, ref in enumerate(refs[:-1]):
        out_ref[where_ref[1] ^ k, 0] = ref[...]


def stack(where, slabs):
    span, width = slabs[0].shape
    return pl.pallas_call(
        stack_kernel,
        in_specs=[SMEM_SPEC] + [VMEM_SPEC] * len(slabs),
        out_specs=VMEM_SPEC,
        out_shape=jax.ShapeDtypeStruct((len(slabs), 1, span, width), BF),
        compiler_params=pltpu.CompilerParams(vmem_limit_bytes=16 << 20),
        cost_estimate=SMALL_COST,
        name="stack",
    )(where, *slabs)


def attend_back_kernel(seg_ref, g_ref, w_out_ref, q_ref, k_ref, v_ref, att_ref, lse_ref,
                       cos_ref, sin_ref, d_ref, grad_ref, k_sum, v_sum,
                       *, block, window, scale, head_size):
    tokens = g_ref.shape[0]
    half = head_size // 2
    lanes = 2 * head_size
    lane = lax.broadcasted_iota(jnp.int32, (1, lanes), 1)
    first = lane < head_size
    starts = start_row(seg_ref)
    k_sum[...] = jnp.zeros_like(k_sum)
    v_sum[...] = jnp.zeros_like(v_sum)
    for low in range(0, tokens, block):
        rows = pl.ds(low, block)
        grad_ref[rows, :] = dot(g_ref[rows, :], w_out_ref[...], ((1,), (1,))).astype(BF)
    small = block // 2
    for low in range(0, tokens, small):
        begin = first_key(low, small, window)
        end = low + small
        count = end - begin
        q = q_ref[low:end, :] * jnp.asarray(scale, BF)
        grad = grad_ref[low:end, :]
        product = (grad.astype(F32) * att_ref[low:end, :].astype(F32)).T
        zero = jnp.zeros_like(q)
        q_two = jnp.concatenate([jnp.where(first, q, zero), jnp.where(first, zero, q)], axis=0)
        grad_two = jnp.concatenate(
            [jnp.where(first, grad, zero), jnp.where(first, zero, grad)], axis=0)
        k = k_ref[begin:end, :]
        scores = dot(k, q_two, ((1,), (1,)))
        prob_grad = dot(v_ref[begin:end, :], grad_two, ((1,), (1,)))
        key_index = lax.broadcasted_iota(jnp.int32, (count, small), 0) + begin
        query_index = lax.broadcasted_iota(jnp.int32, (count, small), 1) + low
        visible = (key_index.astype(F32) >= starts[:, low:end]) & (key_index <= query_index)
        visible = jnp.concatenate([visible, visible], axis=1)
        lse = jnp.concatenate([lse_ref[0, h:h + 1, low:end] for h in range(2)], axis=1)
        row_dots = jnp.concatenate(
            [jnp.sum(product[h * head_size:(h + 1) * head_size], axis=0, keepdims=True)
             for h in range(2)], axis=1)
        weights = jnp.where(visible, jnp.exp(scores - lse), 0.0)
        score_low = (weights * (prob_grad - row_dots)).astype(BF)
        v_sum[begin:end, :] += dot(weights.astype(BF), grad_two)
        k_sum[begin:end, :] += dot(score_low, q_two)
        dq = dot(score_low, k, ((0,), (0,))) * scale
        dq = jnp.where(first, dq[:small], dq[small:])
        d_ref[low:end, :lanes] = (
            dq * cos_ref[low:end, :] - turn(dq, half) * sin_ref[low:end, :]).astype(BF)
    for low in range(0, tokens, block):
        rows = pl.ds(low, block)
        dk = k_sum[rows, :]
        d_ref[rows, lanes:2 * lanes] = (
            dk * cos_ref[rows, :] - turn(dk, half) * sin_ref[rows, :]).astype(BF)
        d_ref[rows, 2 * lanes:] = v_sum[rows, :].astype(BF)

def attend_back(seg, g, w_out, q, k, v, att, lse, cosine, sine, window, head_size):
    tokens, width = g.shape
    lanes = 2 * head_size
    pairs = q.shape[1] // lanes
    kernel = lambda *refs: attend_back_kernel(
        *refs, block=256, window=window, scale=1.0 / math.sqrt(head_size), head_size=head_size)
    column = pl.BlockSpec((tokens, lanes), lambda p: (0, p))
    inputs = hbm(seg) + vmem(g) + hbm(w_out, q, k, v, att, lse, cosine, sine)
    return pl.pallas_call(
        kernel,
        grid=(pairs,),
        in_specs=whole_specs(seg) + [
            VMEM_SPEC,
            pl.BlockSpec((lanes, width), lambda p: (p, 0)),
            column, column, column, column,
            pl.BlockSpec((1, 8, tokens), lambda p: (p, 0, 0)),
        ] + whole_specs(cosine, sine),
        out_specs=pl.BlockSpec((tokens, 3 * lanes), lambda p: (0, p)),
        out_shape=jax.ShapeDtypeStruct((tokens, 3 * lanes * pairs), BF),
        scratch_shapes=[
            pltpu.VMEM((tokens, lanes), BF),
            pltpu.VMEM((tokens, lanes), F32),
            pltpu.VMEM((tokens, lanes), F32),
        ],
        compiler_params=pltpu.CompilerParams(vmem_limit_bytes=28 << 20),
        cost_estimate=SMALL_COST,
        name="attend_back",
    )(*inputs)


def join_kernel(rank_ref, own_ref, other_ref, *out_refs, moves, plain):
    swapped = rank_ref[0] == 1
    own, other = own_ref[...], other_ref[...]
    halves = (jnp.where(swapped, other, own), jnp.where(swapped, own, other))
    for out, half, (rows, cols), (to_rows, to_cols) in moves:
        out_refs[out][to_rows, to_cols] = halves[half][rows, cols].astype(F32)
    for out, (rows, cols) in plain:
        out_refs[out][...] = own[rows, cols].astype(F32)


def join(rank, own, other, moves, plain, shapes):
    kernel = lambda *refs: join_kernel(*refs, moves=moves, plain=plain)
    return pl.pallas_call(
        kernel,
        in_specs=[
            pl.BlockSpec(memory_space=pltpu.SMEM),
            pl.BlockSpec(memory_space=pltpu.VMEM),
            pl.BlockSpec(memory_space=pltpu.VMEM),
        ],
        out_specs=[pl.BlockSpec(memory_space=pltpu.VMEM)] * len(shapes),
        out_shape=[jax.ShapeDtypeStruct(shape, F32) for shape in shapes],
        compiler_params=pltpu.CompilerParams(vmem_limit_bytes=32 << 20),
        name="join",
    )(rank.reshape(1), own, other)


def join_all_kernel(all_ref, *refs, moves):
    outs = (len(refs) - 2) // 2
    out_refs, whole_ref, blocks, sems = refs[:outs], refs[outs], refs[outs + 1:-1], refs[-1]
    groups, ranks, rows, _ = all_ref.shape
    for h in range(ranks):
        for m in range(groups):
            whole_ref[h, m * rows:(m + 1) * rows, :] = all_ref[m, h]
    copies = []
    for n in range(outs):
        for out, half, (rows, cols), (to_rows, to_cols) in moves:
            if out == n:
                blocks[out][to_rows, to_cols] = whole_ref[half, rows, cols].astype(F32)
        copies.append(pltpu.make_async_copy(blocks[n], out_refs[n], sems.at[n]))
        copies[-1].start()
    for copy in copies:
        copy.wait()


def join_all(parts, moves, shapes):
    groups, ranks, rows, cols = parts.shape
    parts, = hbm(parts)
    return pl.pallas_call(
        lambda *refs: join_all_kernel(*refs, moves=moves),
        grid=(1,),
        in_specs=whole_specs(parts),
        out_specs=[HBM_SPEC] * len(shapes),
        out_shape=[pltpu.HBM(shape, F32) for shape in shapes],
        scratch_shapes=[pltpu.VMEM((ranks, groups * rows, cols), BF)]
        + [pltpu.VMEM(shape, F32) for shape in shapes]
        + [pltpu.SemaphoreType.DMA((len(shapes),))],
        compiler_params=pltpu.CompilerParams(vmem_limit_bytes=24 << 20),
        cost_estimate=SMALL_COST,
        name="join_all",
    )(parts)


def make_body(groups, ranks, fsdp, square):
    F = ("y", "x") if square else ("f",)
    swap = [(0, 1), (1, 0)]
    pairs = square and ranks == 2 and groups == 4

    def hop(value, k):
        return lax.ppermute(value, "m", [(i, i ^ k) for i in range(groups)])

    def after(value, *earlier):
        return lax.optimization_barrier((value,) + earlier)[0]

    def between(slabs, value):
        hops, value = lax.optimization_barrier((slabs[1:], value))
        return slabs[:1] + hops, value

    def spread(slabs):
        return [hop(slab, k) if k else slab for k, slab in enumerate(slabs)]

    def both_ranks(where, slabs, span):
        if ranks == 2:
            return slabs + [lax.ppermute(slab, "r", swap) for slab in slabs]
        rows = lax.all_gather(stack(where, slabs)[:, 0], "r", axis=1)
        return [rows[:, :, :span].reshape(-1, rows.shape[-1]), rows]

    def share(part):
        if ranks == 2:
            other = lax.ppermute(part, "r", swap)
            mine_first = lax.axis_index("r") == 0
            return jnp.stack(
                [jnp.where(mine_first, part, other), jnp.where(mine_first, other, part)], axis=1)
        return lax.all_gather(part, "r", axis=1)

    def exchange(part):
        if ranks == 2:
            return part, lax.ppermute(part, "r", swap)
        return lax.psum(part, "r"), jnp.zeros_like(part)

    def gather_rows(part, wait=()):
        if not square:
            whole = lax.all_gather(part, F, axis=0, tiled=True)
            return [whole], [(None, 0, 0)], (), ()
        count = part.shape[0]
        rows = (count // 2) // 16 * 16
        send = after(part, *wait) if wait else part
        from_x = lax.ppermute(send, "x", swap)
        from_y = lax.ppermute(send, "y", swap)
        far_a = lax.ppermute(from_y[:rows], "x", swap)
        far_b = lax.ppermute(from_x[rows:], "y", swap)
        pieces = [(0, 0, count), (1, 0, count), (2, 0, count), (3, 0, rows), (3, rows, count - rows)]
        return [part, from_x, from_y, far_a, far_b], pieces, (from_x, from_y), (far_a, far_b)

    def add(*parts):
        return sum(part.astype(F32) for part in parts).astype(BF)

    def take(grad, k):
        return lax.dynamic_index_in_dim(grad, lax.axis_index(F) ^ k, 0, keepdims=False)

    def half_rows(grad):
        return (grad.shape[1] // 2) // 16 * 16

    def round_one(grad):
        far, rows = take(grad, 3), half_rows(grad)
        return lax.ppermute(far[:rows], "x", swap), lax.ppermute(far[rows:], "y", swap)

    def second_terms(grad, low, high):
        to_x, to_y, rows = take(grad, 1), take(grad, 2), half_rows(grad)
        to_x = jnp.concatenate([to_x[:rows], add(to_x[rows:], high)], axis=0)
        to_y = jnp.concatenate([add(to_y[:rows], low), to_y[rows:]], axis=0)
        return to_x, to_y

    def round_two(to_x, to_y):
        return lax.ppermute(to_x, "x", swap), lax.ppermute(to_y, "y", swap)

    def halve(owned, bit, axis):
        half = owned.shape[axis] // 2
        side = (lax.axis_index("m") // bit) % 2
        return (lax.dynamic_slice_in_dim(owned, (1 - side) * half, half, axis),
                lax.dynamic_slice_in_dim(owned, side * half, half, axis))

    def join_halves(owned, other, bit, axis):
        first = (lax.axis_index("m") // bit) % 2 == 0
        return jnp.concatenate(
            [jnp.where(first, owned, other), jnp.where(first, other, owned)], axis=axis)

    def reduce(grad):
        return lax.psum(lax.psum_scatter(grad, F, scatter_dimension=0, tiled=False), "m")

    def body(tokens, segments, w_query, w_key, w_value, w_out, w_gate, w_up, w_down,
             gain_attn, gain_ffn, cotangent):
        micro, _, span, width = tokens.shape
        head_size = width // HEADS
        seq_tokens = span * groups * ranks
        window = seq_tokens // 2
        rank = lax.axis_index("r")
        own_cols = width // ranks
        shard = w_query.shape[0]
        down_rows = w_down.shape[0]
        part_rows = down_rows // ranks
        ff = w_gate.shape[1]
        half_ff = ff // ranks

        lanes = 2 * head_size
        lanes_all = -(-own_cols // lanes) * lanes
        spare = lanes_all - own_cols
        block = span * ranks
        f_index = lax.axis_index(F)
        own_at, other_at, other_rank = (
            at.astype(jnp.uint32) for at in (rank * own_cols, (1 - rank) * own_cols, 1 - rank))
        where = jnp.stack([f_index, lax.axis_index("m"), rank])
        small_cols = 3 * lanes_all + own_cols
        gains_in = jnp.pad(jnp.stack([gain_attn, gain_ffn]), ((0, 14), (0, 0)))
        stack_own = pack(where, w_gate, w_up, w_down, fsdp, ranks)
        stack_all = lax.all_gather(stack_own, F, axis=0)
        cosine, sine = rotary_tables(seq_tokens, head_size, 2)
        small, *slabs = pack_small(
            after(where, stack_own), w_query, w_key, w_value, w_out, gains_in, tokens,
            segments[:, 0], cotangent, ranks, lanes, lanes_all)
        token_slabs, cot_slabs = slabs[:groups], slabs[groups:]
        token_slabs = spread(token_slabs)
        small_refs, small_pieces, near, far = gather_rows(small)
        if square:
            cot_slabs = cot_slabs[:1] + [after(slab, *token_slabs) for slab in cot_slabs[1:]]
        cot_slabs = spread(cot_slabs)
        if square:
            token_slabs = token_slabs[:1] + [
                after(slab, cosine, sine) for slab in token_slabs[1:]]
        token_refs = both_ranks(where, token_slabs, span)
        if ranks != 2:
            seg = token_refs[1][:, :, span, :span].reshape(1, seq_tokens).astype(F32)
            token_refs = [token_refs[0], seg]
        if square:
            own, from_x, from_y, far_a, far_b = small_refs
            at = far_a.shape[0]
            ends = [own, from_x, from_y, jnp.concatenate([far_a, far_b[:shard - at]], axis=0)]
            tails = [v[shard:shard + 2, :shard] for v in (own, from_x, from_y)]
            tails.append(far_b[shard - at:shard - at + 2, :shard])
            gains = jnp.zeros((fsdp, 2, shard), BF)
            out_cols = jnp.zeros((width, own_cols), BF)
            for offset in range(4):
                to = (f_index ^ offset) * shard
                gains = lax.dynamic_update_index_in_dim(gains, tails[offset], f_index ^ offset, 0)
                out_cols = lax.dynamic_update_slice_in_dim(
                    out_cols, ends[offset][:shard, 3 * lanes_all:], to, 0)
            gains = gains.transpose(1, 0, 2).reshape(2, width)
            small_pieces = [(o, f, min(n, shard - f)) for o, f, n in small_pieces]
            qkv_refs = small_refs
        else:
            whole = small_refs[0].reshape(fsdp, shard + 16, small_cols)
            gains = whole[:, shard:shard + 2, :shard].transpose(1, 0, 2).reshape(2, width)
            out_cols = whole[:, :shard, 3 * lanes_all:].reshape(width, own_cols)
            qkv_refs = [whole[:, :shard, :3 * lanes_all].reshape(width, 3 * lanes_all)]
        gains = gains.astype(F32)
        gain_one = gains[0:1]
        if ranks == 2:
            give = lax.dynamic_slice_in_dim(out_cols, (1 - rank) * own_cols, own_cols, 0)
            keep = lax.dynamic_slice_in_dim(out_cols, rank * own_cols, own_cols, 0)
            got = lax.ppermute(give, "r", swap)
            w_out_own = jnp.where(rank == 0, jnp.concatenate([keep, got], 1),
                                  jnp.concatenate([got, keep], 1))
        else:
            pieces = lax.all_to_all(out_cols, "r", 0, 0, tiled=True)
            pieces = pieces.reshape(ranks, own_cols, own_cols)
            w_out_own = jnp.concatenate([pieces[i] for i in range(ranks)], axis=1)
        w_out_even = jnp.pad(w_out_own, ((0, spare), (0, 0)))

        cosine, gains, gain_one, own_at, other_at, other_rank = lax.optimization_barrier(
            (cosine, gains, gain_one, own_at, other_at, other_rank))
        q, k, v, att, lse, w_qkv, x, seg = attend(
            where, cosine, sine, token_refs, ranks, qkv_refs, small_pieces, shard, lanes_all,
            window, head_size, width)
        if square:
            cot_slabs, att = between(cot_slabs, att)
        own, got = exchange(dot(att, w_out_even).astype(BF))
        cot_refs = both_ranks(where, cot_slabs, span)
        if ranks != 2:
            cot_refs = cot_refs[:1]
        total, middle_low, hidden_low, gate_back, silu, part, gu, down = forward(
            x, own, got, gain_one, stack_all, shard, part_rows, half_ff, block)
        own, got = exchange(part)

        *out_slabs, ffn_grad_low, gu_grad_low, part, gain_ffn_grad = backward(
            where, total, own, got, gate_back, silu, gains, gu, down, cot_refs, block, groups, ranks)
        own, got = exchange(part)
        gu_w_grad = dot(middle_low, gu_grad_low, ((0,), (0,))).astype(BF)
        if ranks == 2:
            got, gu_w_grad = lax.optimization_barrier((got, gu_w_grad))
        stack_grad = arrange(gu_w_grad, hidden_low, ffn_grad_low, fsdp)
        stack_owned = lax.psum_scatter(stack_grad, F, scatter_dimension=0, tiled=False)
        own, got = after(own, stack_grad), after(got, stack_grad)
        branch_grad_low, branch_keep, gain_grads = norm_back(
            where[2:], total, ffn_grad_low, own, got, gain_one, gain_ffn_grad,
            fsdp, small_cols, block, span)
        out_w_grad = dot(att, branch_grad_low, ((0,), (0,)))[:own_cols].astype(BF)
        if ranks == 2:
            give = lax.dynamic_slice_in_dim(out_w_grad, other_at, own_cols, 1)
            keep = lax.dynamic_slice_in_dim(out_w_grad, own_at, own_cols, 1)
            got = lax.ppermute(give, "r", swap)
            out_cols_grad = jnp.where(rank == 0, jnp.concatenate([keep, got], 0),
                                      jnp.concatenate([got, keep], 0))
        else:
            rows = out_w_grad.reshape(own_cols, ranks, own_cols).transpose(1, 0, 2)
            out_cols_grad = lax.all_to_all(rows, "r", 0, 0, tiled=True).reshape(width, own_cols)
        branch_grad_low = after(branch_grad_low, out_cols_grad)
        d_qkv = attend_back(
            seg, branch_grad_low, w_out_even, q, k, v, att, lse, cosine, sine, window, head_size)
        if square:
            out_slabs, d_qkv = between(spread(out_slabs), d_qkv)
        else:
            out_slabs = spread(out_slabs)
        output = stack(where, out_slabs)
        qkv_w_grad = dot(x, d_qkv, ((0,), (0,))).astype(BF)
        small_grad = jnp.concatenate([qkv_w_grad, out_cols_grad], axis=1)
        small_grad = jnp.concatenate(
            [small_grad.reshape(fsdp, shard, small_cols), gain_grads], axis=1)
        if pairs:
            small_one = round_one(small_grad)
            d_qkv = after(d_qkv, small_grad)
        part = dot(d_qkv, w_qkv, ((1,), (1,))).astype(BF)
        if ranks == 2:
            rows = part.reshape(groups, ranks, span, width)
            give = lax.dynamic_index_in_dim(rows, other_rank, 1, keepdims=False)
            got = lax.ppermute(give, "r", swap)
        else:
            part = lax.psum(part, "r")
            got = jnp.zeros_like(branch_keep, BF)
        grad_slabs = list(finish(where, branch_keep, part, got, ranks))
        grad_slabs = spread(grad_slabs)
        if pairs:
            grad_slabs[:3], small_one = between(grad_slabs[:3], small_one)
            terms = second_terms(small_grad, *small_one)
            small_two, output, grad_slabs[3] = lax.optimization_barrier(
                (round_two(*terms), output, grad_slabs[3]))
            input_grad = stack(where, grad_slabs)
            stack_owned = after(stack_owned, *terms)
            quarter = lax.psum_scatter(stack_owned, "m", scatter_dimension=0, tiled=True)
            give, keep = halve(add(take(small_grad, 0), *small_two), 1, 1)
            got, quarter, input_grad = lax.optimization_barrier((hop(give, 1), quarter, input_grad))
            stack_parts = lax.all_gather(quarter, ("m", "r"), axis=0)
            stack_parts = stack_parts.reshape((groups, ranks) + quarter.shape)
            give, keep = halve(add(keep, got), 2, 1)
            owned = add(keep, hop(give, 2))
            owned = join_halves(owned, hop(owned, 2), 2, 1)
            small_sum = join_halves(owned, hop(owned, 1), 1, 1)
        else:
            stack_sum = lax.psum(stack_owned, "m")
            small_sum = reduce(small_grad)
            input_grad = stack(where, grad_slabs)
        if pairs:
            everything = slice(None)
            chunks = 2 * half_ff // 256
            stack_moves = [
                (n, h, (slice((n * fsdp + j) * shard, (n * fsdp + j + 1) * shard), everything),
                 (everything, slice(j * down_rows + h * part_rows, j * down_rows + (h + 1) * part_rows)))
                for n in range(2) for h in range(2) for j in range(fsdp)]
            stack_moves += [
                (2, h, (slice(chunks * shard + c * part_rows, chunks * shard + (c + 1) * part_rows),
                        everything),
                 (slice(h * part_rows, (h + 1) * part_rows), slice(c * 256, (c + 1) * 256)))
                for h in range(2) for c in range(width // 256)]
            small_moves = [
                (n, h, (slice(0, shard), slice((3 * p + n) * lanes, (3 * p + n + 1) * lanes)),
                 (everything, slice(h * own_cols + p * lanes, h * own_cols + (p + 1) * lanes)))
                for n in range(3) for h in range(2) for p in range(own_cols // lanes)]
            small_moves += [
                (3, h, (slice(0, shard), slice(3 * lanes_all, small_cols)),
                 (everything, slice(h * own_cols, (h + 1) * own_cols))) for h in range(2)]
            small_plain = [
                (4 + n, (slice(shard + n, shard + n + 1), slice(0, shard))) for n in range(2)]
            gate_w, up_w, down_grad = join_all(
                stack_parts, stack_moves, [(shard, ff)] * 2 + [(down_rows, width)])
            small_got, gate_w, up_w, down_grad = lax.optimization_barrier(
                (lax.ppermute(small_sum, "r", swap), gate_w, up_w, down_grad))
            query_w, key_w, value_w, out_w, gain_a, gain_f = join(
                rank, small_sum, small_got, small_moves, small_plain,
                [(shard, width)] * 4 + [(1, shard)] * 2)
        else:
            at = 2 * half_ff // 256 * shard
            down_sum = jnp.moveaxis(stack_sum[at:].reshape(-1, part_rows, 256), 0, 1)
            down_grad = jnp.moveaxis(share(down_sum.reshape(part_rows, width)), 1, 0)
            down_grad = down_grad.reshape(down_rows, width).astype(F32)
            gu_sum = jnp.moveaxis(stack_sum[:at].reshape(-1, shard, 256), 0, 1)
            gu_both = share(gu_sum.reshape(shard, 2 * fsdp, part_rows))
            gu_both = gu_both.reshape(shard, ranks, 2, fsdp, part_rows).astype(F32)
            gate_w, up_w = (
                gu_both[:, :, n].transpose(0, 2, 1, 3).reshape(shard, ff) for n in range(2))
            small_both = share(small_sum)[:shard].astype(F32)
            three = small_both[:, :, :3 * lanes_all].reshape(shard, ranks, -1, 3, lanes)
            query_w, key_w, value_w = (
                three[:, :, :, n].reshape(shard, ranks, lanes_all)[:, :, :own_cols].reshape(shard, width)
                for n in range(3))
            out_w = small_both[:, :, 3 * lanes_all:].reshape(shard, width)
            gain_a, gain_f = small_sum[shard, :shard].astype(F32), small_sum[shard + 1, :shard].astype(F32)
        return (output, input_grad, query_w, key_w, value_w, out_w,
                gate_w, up_w, down_grad, gain_a.reshape(shard), gain_f.reshape(shard))

    return body


def solution(mesh):
    def run(*args):
        groups = args[0].shape[0]
        seq, fsdp = mesh.shape["seq"], mesh.shape["fsdp"]
        ranks = seq // groups
        square = fsdp == 4
        names = ("m", "r") + (("y", "x") if square else ("f",))
        sizes = (groups, ranks) + ((2, 2) if square else (fsdp,))
        order = [mesh.axis_names.index(name) for name in ("seq", "fsdp")]
        inner = Mesh(mesh.devices.transpose(order).reshape(sizes), names)
        f = ("y", "x") if square else "f"
        s = ("m", "r")
        rows = P(f, None)
        data = P(None, f, s, None)
        in_specs = (data, P(None, f, s)) + (rows,) * 7 + (P(f), P(f), data)
        out_specs = (data, data) + (rows,) * 7 + (P(f), P(f))
        body = make_body(groups, ranks, fsdp, square)
        return jax.shard_map(
            body, mesh=inner, in_specs=in_specs, out_specs=out_specs, check_vma=False)(*args)

    return run
```

```python
import math

import jax
import jax.numpy as jnp
from jax import lax
from jax.experimental import pallas as pl
from jax.experimental.pallas import tpu as pltpu
from jax.sharding import Mesh, PartitionSpec as P

HEADS = 12
DOCS = 4
EPS = 1e-06
NEGATIVE = -1e30
BF = jnp.bfloat16
F32 = jnp.float32


def dot(left, right, dims=((1,), (0,))):
    return lax.dot_general(left, right, (dims, ((), ())), preferred_element_type=F32)


def rotary_tables(seq_tokens, head_size, copies):
    half = head_size // 2
    frequency = 10000.0 ** (-jnp.arange(half, dtype=F32) / half)
    angle = jnp.arange(seq_tokens, dtype=jnp.int32).astype(F32)[:, None] * frequency[None, :]
    cosine, sine = jnp.cos(angle), jnp.sin(angle)
    return (
        jnp.concatenate([cosine, cosine] * copies, axis=1),
        jnp.concatenate([-sine, sine] * copies, axis=1),
    )


def turn(rows, half):
    lanes = rows.shape[1]
    lane = lax.broadcasted_iota(jnp.int32, (1, lanes), 1)
    low = (lane // half) % 2 == 0
    return jnp.where(low, pltpu.roll(rows, lanes - half, 1), pltpu.roll(rows, half, 1))


def first_key(query_first, block, window):
    return max(0, (query_first - window + 1) // block * block)


def start_row(seg_ref):
    seg = seg_ref[...]
    starts = jnp.zeros_like(seg)
    for doc in range(1, DOCS):
        before = jnp.sum(jnp.where(seg < doc, 1.0, 0.0), axis=1, keepdims=True)
        starts = jnp.maximum(starts, jnp.where(seg >= doc, before, 0.0))
    return starts


def place(target, refs, pieces, me, shard):
    for ref, (offset, first, rows) in zip(refs, pieces):
        if offset is None:
            target[...] = ref[...]
        else:
            start = pl.multiple_of((me ^ offset) * shard + first, 16)
            target[pl.ds(start, rows), :] = ref[0:rows, 0:target.shape[1]]


def place_tokens(target, refs, where_ref, ranks):
    if len(refs) == 1:
        target[...] = refs[0][...]
        return
    groups = len(refs) // ranks
    span = target.shape[0] // (groups * ranks)
    for n, ref in enumerate(refs):
        rank = where_ref[2] if n < groups else 1 - where_ref[2]
        chunk = (where_ref[1] ^ (n % groups)) * ranks + rank
        target[pl.ds(pl.multiple_of(chunk * span, span), span), :] = ref[0:span, :]


def place_segments(target, refs, where_ref, ranks):
    groups = len(refs) // ranks
    span = target.shape[1] // (groups * ranks)
    for n, ref in enumerate(refs):
        rank = where_ref[2] if n < groups else 1 - where_ref[2]
        chunk = (where_ref[1] ^ (n % groups)) * ranks + rank
        row = ref[span:span + 16, 0:span].astype(F32)[0:1, :]
        target[:, pl.ds(pl.multiple_of(chunk * span, span), span)] = row


def stack_copies(gu, down, stack_ref, sems, shard, part_rows):
    members, chunks, groups = stack_ref.shape[0], gu.shape[1] // 256, []
    for c in range(chunks):
        groups.append([
            pltpu.make_async_copy(
                stack_ref.at[j, c * shard:(c + 1) * shard, :],
                gu.at[j * shard:(j + 1) * shard, c * 256:(c + 1) * 256],
                sems.at[c, j]) for j in range(members)])
    for c in range(down.shape[1] // 256):
        at = chunks * shard + c * part_rows
        groups.append([
            pltpu.make_async_copy(
                stack_ref.at[j, at:at + part_rows, :],
                down.at[j * part_rows:(j + 1) * part_rows, c * 256:(c + 1) * 256],
                sems.at[chunks + c, j]) for j in range(members)])
    return groups


def attend_kernel(where_ref, cos_ref, sin_ref, *refs, pieces, token_count, ranks, shard, block,
                  window, scale, head_size):
    inputs, refs = refs[:-9], refs[-9:]
    q_ref, k_ref, v_ref, att_ref, lse_ref, w_ref, x_ref, seg_ref, col_ref = refs
    token_refs, w_refs = inputs[:token_count], inputs[token_count:]
    tokens = x_ref.shape[0]
    lanes = 2 * head_size
    lane = lax.broadcasted_iota(jnp.int32, (1, lanes), 1)
    first = lane < head_size
    pair = pl.program_id(0)

    @pl.when(pair == 0)
    def _():
        place(w_ref, w_refs, pieces, where_ref[0], shard)
        place_tokens(x_ref, token_refs[:1] if token_count == 2 else token_refs, where_ref, ranks)
        if token_count == 2:
            seg_ref[...] = token_refs[1][...]
        else:
            place_segments(seg_ref, token_refs, where_ref, ranks)
        starts = start_row(seg_ref)
        col_ref[...] = jnp.broadcast_to(starts, (128, tokens)).T

    w = w_ref[:, pl.ds(pl.multiple_of(pair * 3 * lanes, lanes), 3 * lanes)]
    for low in range(0, tokens, block):
        rows = pl.ds(low, block)
        lin = dot(x_ref[rows, :], w)
        cosine, sine = cos_ref[rows, :], sin_ref[rows, :]
        half = head_size // 2
        q_lin, k_lin = lin[:, :lanes], lin[:, lanes:2 * lanes]
        q_ref[rows, :] = (q_lin * cosine + turn(q_lin, half) * sine).astype(BF)
        k_ref[rows, :] = (k_lin * cosine + turn(k_lin, half) * sine).astype(BF)
        v_ref[rows, :] = lin[:, 2 * lanes:].astype(BF)
    for low in range(0, tokens, block):
        begin = first_key(low, block, window)
        end = low + block
        q = q_ref[low:end, :] * jnp.asarray(scale, BF)
        zero = jnp.zeros_like(q)
        stacked = jnp.concatenate([jnp.where(first, q, zero), jnp.where(first, zero, q)], axis=0)
        scores = dot(stacked, k_ref[begin:end, :], ((1,), (1,)))
        key_index = lax.broadcasted_iota(jnp.int32, (block, end - begin), 1) + begin
        query_index = lax.broadcasted_iota(jnp.int32, (block, end - begin), 0) + low
        visible = (key_index.astype(F32) >= col_ref[low:end, 0:1]) & (key_index <= query_index)
        parts = []
        for head in range(2):
            own = jnp.where(visible, scores[head * block:(head + 1) * block], NEGATIVE)
            top = jnp.max(own, axis=1, keepdims=True)
            weights = jnp.exp(own - top)
            total = jnp.sum(weights, axis=1, keepdims=True)
            out = dot(weights.astype(BF), v_ref[begin:end, :]) / total
            parts.append(out)
            lse = jnp.broadcast_to(top + jnp.log(total), (block, 128))
            lse_ref[0, head:head + 1, low:end] = lse.T[0:1, :]
        att_ref[low:end, :] = jnp.where(first, parts[0], parts[1]).astype(BF)


def hbm(*arrays):
    return [pltpu.with_memory_space_constraint(a, pltpu.HBM) for a in arrays]


def vmem(*arrays):
    return [pltpu.with_memory_space_constraint(a, pltpu.VMEM) for a in arrays]


def whole_specs(*arrays):
    return [pl.BlockSpec(a.shape, lambda *_, n=a.ndim: (0,) * n, pipeline_mode=pl.Buffered(1))
            for a in arrays]


SMALL_COST = pl.CostEstimate(flops=1, bytes_accessed=1, transcendentals=0)
VMEM_SPEC = pl.BlockSpec(memory_space=pltpu.VMEM)
SMEM_SPEC = pl.BlockSpec(memory_space=pltpu.SMEM)


def attend(where, cosine, sine, token_refs, ranks, weights, pieces, shard, lanes_all, window,
           head_size, width):
    tokens = cosine.shape[0]
    lanes = 2 * head_size
    pairs = lanes_all // lanes
    kernel = lambda *refs: attend_kernel(
        *refs, pieces=pieces, token_count=len(token_refs), ranks=ranks, shard=shard, block=256,
        window=window, scale=1.0 / math.sqrt(head_size), head_size=head_size)
    column = pl.BlockSpec((tokens, lanes), lambda p: (0, p))
    whole = lambda *shape: pl.BlockSpec(shape, lambda p: (0, 0))
    inputs = hbm(cosine, sine, *token_refs, *weights)
    return pl.pallas_call(
        kernel,
        grid=(pairs,),
        in_specs=[SMEM_SPEC] + whole_specs(*inputs),
        out_specs=[column, column, column, column,
                   pl.BlockSpec((1, 8, tokens), lambda p: (p, 0, 0)),
                   whole(width, 3 * lanes_all), whole(tokens, width), whole(1, tokens)],
        out_shape=[pltpu.HBM((tokens, lanes_all), BF)] * 4
        + [pltpu.HBM((pairs, 8, tokens), F32), pltpu.HBM((width, 3 * lanes_all), BF),
           pltpu.HBM((tokens, width), BF), pltpu.HBM((1, tokens), F32)],
        scratch_shapes=[pltpu.VMEM((tokens, 128), F32)],
        compiler_params=pltpu.CompilerParams(vmem_limit_bytes=28 << 20),
        cost_estimate=SMALL_COST,
        name="attend",
    )(where, *inputs)


def unit_of(rows):
    factor = lax.rsqrt(jnp.mean(rows * rows, axis=1, keepdims=True) + EPS)
    return rows * factor, factor


def forward_kernel(x_ref, own_ref, got_ref, gain_ref, stack_ref, sum_ref, low_ref, hidden_ref,
                   gate_ref, silu_ref, part_ref, gu, down, sems, *, shard, part_rows):
    step, block = pl.program_id(0), x_ref.shape[0]
    ff = down.shape[0]

    @pl.when(step == 0)
    def _():
        copies = stack_copies(gu, down, stack_ref, sems, shard, part_rows)
        for group in copies:
            for copy in group:
                copy.start()
        for group in copies:
            for copy in group:
                copy.wait()

    rows = pl.ds(pl.multiple_of(step * block, block), block)
    total = x_ref[...].astype(F32) + own_ref[...].astype(F32) + got_ref[...].astype(F32)
    sum_ref[rows, :] = total
    middle_low = (unit_of(total)[0] * gain_ref[...]).astype(BF)
    low_ref[rows, :] = middle_low
    for c in range(0, ff, 256):
        cols = slice(c, c + 256)
        gate = dot(middle_low, gu[:, cols])
        up = dot(middle_low, gu[:, ff + c:ff + c + 256])
        sigmoid = jax.nn.sigmoid(gate)
        silu = gate * sigmoid
        hidden_ref[rows, cols] = (silu * up).astype(BF)
        gate_ref[rows, cols] = (up * sigmoid * (1.0 + gate * (1.0 - sigmoid))).astype(BF)
        silu_ref[rows, cols] = silu.astype(BF)
    part_ref[...] = dot(hidden_ref[rows, :], down[...]).astype(BF)


HBM_SPEC = pl.BlockSpec(memory_space=pltpu.HBM)


def forward(x, own, got, gain, stack, shard, part_rows, ff, block):
    tokens, width = x.shape
    row = lambda cols: pl.BlockSpec((block, cols), lambda i: (i, 0))
    x, own, got, stack = hbm(x, own, got, stack)
    return pl.pallas_call(
        lambda *refs: forward_kernel(*refs, shard=shard, part_rows=part_rows),
        grid=(tokens // block,),
        in_specs=[row(width), row(width), row(width)] + whole_specs(gain) + [HBM_SPEC],
        out_specs=[VMEM_SPEC] * 5 + [row(width)] + [VMEM_SPEC] * 2,
        out_shape=[pltpu.VMEM((tokens, width), F32), pltpu.VMEM((tokens, width), BF)]
        + [pltpu.VMEM((tokens, ff), BF)] * 3 + [jax.ShapeDtypeStruct((tokens, width), BF)]
        + [pltpu.VMEM((width, 2 * ff), BF), pltpu.VMEM((ff, width), BF)],
        scratch_shapes=[pltpu.SemaphoreType.DMA(((2 * ff + width) // 256, stack.shape[0]))],
        compiler_params=pltpu.CompilerParams(vmem_limit_bytes=16 << 20),
        cost_estimate=SMALL_COST,
        name="ffn_forward",
    )(x, own, got, gain, stack)


def backward_kernel(where_ref, sum_ref, own_ref, got_ref, gate_ref, silu_ref, gains_ref, gu, down,
                    *refs, cot_count, groups, ranks):
    cot_refs, refs = refs[:cot_count], refs[cot_count:]
    out_refs, refs = refs[:groups], refs[groups:]
    low_ref, gu_grad_ref, part_ref, gain_ref, cot_ref, rows_ref = refs
    step = pl.program_id(0)
    block, span = rows_ref.shape[0], out_refs[0].shape[0]

    @pl.when(step == 0)
    def _():
        place_tokens(cot_ref, cot_refs, where_ref, ranks)
        gain_ref[...] = jnp.zeros_like(gain_ref)

    rows = pl.ds(pl.multiple_of(step * block, block), block)
    gain_two = gains_ref[1:2, :]
    middle = unit_of(sum_ref[rows, :])[0] * gains_ref[0:1, :]
    unit, factor = unit_of(middle + own_ref[...].astype(F32) + got_ref[...].astype(F32))
    rows_ref[...] = unit * gain_two
    cot = cot_ref[rows, :].astype(F32)
    gain_ref[...] += jnp.sum(cot * unit, axis=0, keepdims=True)
    scaled = cot * gain_two
    grad_low = (factor * (scaled - unit * jnp.mean(scaled * unit, axis=1, keepdims=True))).astype(BF)
    low_ref[rows, :] = grad_low
    ff = down.shape[0]
    for c in range(0, ff, 256):
        cols = slice(c, c + 256)
        hidden_grad = dot(grad_low, down[cols, :], ((1,), (1,)))
        gu_grad_ref[rows, cols] = (hidden_grad * gate_ref[rows, cols].astype(F32)).astype(BF)
        gu_grad_ref[rows, ff + c:ff + c + 256] = (
            hidden_grad * silu_ref[rows, cols].astype(F32)).astype(BF)
    part_ref[...] = dot(gu_grad_ref[rows, :], gu[...], ((1,), (1,))).astype(BF)
    kept = rows_ref[pl.ds(pl.multiple_of(where_ref[2] * span, span), span), :].astype(BF)
    for k, out_ref in enumerate(out_refs):
        @pl.when(step == (where_ref[1] ^ k))
        def _(out_ref=out_ref):
            out_ref[...] = kept


def backward(where, total, own, got, gate, silu, gains, gu, down, cot, block, groups, ranks):
    tokens, width = total.shape
    ff = gate.shape[1]
    kernel = lambda *refs: backward_kernel(
        *refs, cot_count=len(cot), groups=groups, ranks=ranks)
    row = pl.BlockSpec((block, width), lambda i: (i, 0))
    slab = pl.BlockSpec((block // ranks, width), lambda i: (0, 0))
    total, gate, silu, gu, down = vmem(total, gate, silu, gu, down)
    return pl.pallas_call(
        kernel,
        grid=(tokens // block,),
        in_specs=[SMEM_SPEC, VMEM_SPEC, row, row, VMEM_SPEC, VMEM_SPEC] + whole_specs(gains)
        + [VMEM_SPEC] * 2 + whole_specs(*cot),
        out_specs=[slab] * groups + [VMEM_SPEC, VMEM_SPEC, row,
                                     pl.BlockSpec((1, width), lambda i: (0, 0))],
        out_shape=[pltpu.HBM((block // ranks, width), BF)] * groups
        + [pltpu.VMEM((tokens, width), BF), pltpu.VMEM((tokens, 2 * ff), BF),
           pltpu.HBM((tokens, width), BF), pltpu.HBM((1, width), F32)],
        scratch_shapes=[pltpu.VMEM((tokens, width), BF), pltpu.VMEM((block, width), F32)],
        compiler_params=pltpu.CompilerParams(vmem_limit_bytes=20 << 20),
        cost_estimate=SMALL_COST,
        name="ffn_backward",
    )(where, total, own, got, gate, silu, gains, gu, down, *cot)


def norm_back_kernel(rank_ref, sum_ref, grad_ref, own_ref, got_ref, gain_ref, other_ref,
                     low_ref, keep_ref, out_ref, rows_ref, gain_grad_ref):
    step, block = pl.program_id(0), rows_ref.shape[0]

    @pl.when(step == 0)
    def _():
        gain_grad_ref[...] = jnp.zeros_like(gain_grad_ref)

    rows = pl.ds(pl.multiple_of(step * block, block), block)
    unit, factor = unit_of(sum_ref[rows, :])
    grad = (grad_ref[...].astype(F32) + own_ref[...].astype(F32)) + got_ref[...].astype(F32)
    gain_grad_ref[...] += jnp.sum(grad * unit, axis=0, keepdims=True)
    scaled = grad * gain_ref[...]
    branch_grad = factor * (scaled - unit * jnp.mean(scaled * unit, axis=1, keepdims=True))
    low_ref[rows, :] = branch_grad.astype(BF)
    rows_ref[...] = branch_grad
    span = keep_ref.shape[1]
    keep_ref[0] = rows_ref[pl.ds(pl.multiple_of(rank_ref[0] * span, span), span), :]

    @pl.when(step == pl.num_programs(0) - 1)
    def _():
        out_ref[...] = jnp.zeros_like(out_ref)
        shard = gain_ref.shape[1] // out_ref.shape[0]
        first = lax.broadcasted_iota(jnp.int32, (16, shard), 0)
        for j in range(out_ref.shape[0]):
            lanes = slice(j * shard, (j + 1) * shard)
            one = jnp.broadcast_to(gain_grad_ref[:, lanes], (16, shard))
            two = jnp.broadcast_to(other_ref[:, lanes], (16, shard))
            out_ref[j, :, 0:shard] = jnp.where(
                first == 0, one, jnp.where(first == 1, two, 0.0)).astype(BF)


def norm_back(rank, total, grad, own, got, gain, other_grad, fsdp, cols, block, span):
    tokens, width = total.shape
    row = pl.BlockSpec((block, width), lambda i: (i, 0))
    inputs = vmem(total) + hbm(grad, own, got)
    return pl.pallas_call(
        norm_back_kernel,
        grid=(tokens // block,),
        in_specs=[SMEM_SPEC, VMEM_SPEC, row, row, row] + whole_specs(gain, other_grad),
        out_specs=[VMEM_SPEC, pl.BlockSpec((1, span, width), lambda i: (i, 0, 0)),
                   pl.BlockSpec((fsdp, 16, cols), lambda i: (0, 0, 0))],
        out_shape=[pltpu.VMEM((tokens, width), BF),
                   pltpu.HBM((tokens // block, span, width), F32),
                   pltpu.HBM((fsdp, 16, cols), BF)],
        scratch_shapes=[pltpu.VMEM((block, width), F32), pltpu.VMEM((1, width), F32)],
        compiler_params=pltpu.CompilerParams(vmem_limit_bytes=16 << 20),
        cost_estimate=SMALL_COST,
        name="norm_back",
    )(rank, *inputs, gain, other_grad)


def pick(rank, parts):
    value = parts[0]
    for r in range(1, len(parts)):
        value = jnp.where(rank == r, parts[r], value)
    return value


def pack_small_kernel(where_ref, query_ref, key_ref, value_ref, out_ref, gain_ref, tokens_ref,
                      seg_ref, cot_ref, small_ref, *slab_refs, ranks, lanes, lanes_all):
    slab_refs, cot_slabs = slab_refs[:len(slab_refs) // 2], slab_refs[len(slab_refs) // 2:]
    for k, ref in enumerate(cot_slabs):
        ref[...] = cot_ref[where_ref[1] ^ k, 0]
    rank, m = where_ref[2], where_ref[1]
    shard, width = query_ref.shape
    own_cols = width // ranks
    if lanes_all != own_cols:
        small_ref[...] = jnp.zeros_like(small_ref)
    for n, ref in enumerate((query_ref, key_ref, value_ref)):
        for low in range(0, own_cols, lanes):
            size = min(lanes, own_cols - low)
            at = (low // lanes * 3 + n) * lanes
            small_ref[0:shard, at:at + size] = pick(
                rank, [ref[:, r * own_cols + low:r * own_cols + low + size] for r in range(ranks)])
    small_ref[0:shard, 3 * lanes_all:] = pick(
        rank, [out_ref[:, r * own_cols:(r + 1) * own_cols] for r in range(ranks)])
    small_ref[shard:, :] = jnp.zeros_like(small_ref[shard:, :])
    small_ref[shard:, 0:shard] = gain_ref[...]
    span = tokens_ref.shape[2]
    for k, ref in enumerate(slab_refs):
        ref[0:span, :] = tokens_ref[m ^ k, 0]
        ref[span:, :] = jnp.zeros_like(ref[span:, :])
        row = seg_ref[pl.ds(m ^ k, 1), :].astype(F32)
        ref[span:, 0:span] = jnp.broadcast_to(row, (16, span)).astype(BF)


def pack_small(where, query, key, value, out, gains, tokens, segments, cot, ranks, lanes,
               lanes_all):
    shard, width = query.shape
    groups, _, span, _ = tokens.shape
    cols = 3 * lanes_all + width // ranks
    inputs = hbm(query, key, value, out, gains, tokens, segments, cot)
    shapes = [(shard + 16, cols)] + [(span + 16, width)] * groups + [(span, width)] * groups
    return pl.pallas_call(
        lambda *refs: pack_small_kernel(*refs, ranks=ranks, lanes=lanes, lanes_all=lanes_all),
        grid=(1,),
        in_specs=[SMEM_SPEC] + whole_specs(*inputs),
        out_specs=[pl.BlockSpec(shape, lambda i: (0, 0)) for shape in shapes],
        out_shape=[pltpu.HBM(shape, BF) for shape in shapes],
        compiler_params=pltpu.CompilerParams(vmem_limit_bytes=24 << 20),
        cost_estimate=SMALL_COST,
        name="pack_small",
    )(where, *inputs)


def pack_kernel(where_ref, gate_ref, up_ref, down_ref, out_ref, gu, *, fsdp, ranks):
    rank = where_ref[2]
    shard, cols = gu.shape
    part = down_ref.shape[0] // ranks
    for n, ref in enumerate((gate_ref, up_ref)):
        for j in range(fsdp):
            low = (n * fsdp + j) * part
            gu[:, low:low + part] = pick(
                rank, [ref[:, (j * ranks + r) * part:(j * ranks + r + 1) * part]
                       for r in range(ranks)])
    chunks = cols // 256
    for c in range(chunks):
        out_ref[c * shard:(c + 1) * shard, :] = gu[:, c * 256:(c + 1) * 256]
    rows = pl.ds(pl.multiple_of(rank * part, 16), part)
    for c in range(down_ref.shape[1] // 256):
        at = chunks * shard + c * part
        out_ref[at:at + part, :] = down_ref[rows, c * 256:(c + 1) * 256]


def pack(where, gate, up, down, fsdp, ranks):
    shard, ff = gate.shape
    cols = 2 * ff // ranks
    rows = cols // 256 * shard + down.shape[1] // 256 * (down.shape[0] // ranks)
    inputs = hbm(gate, up, down)
    return pl.pallas_call(
        lambda *refs: pack_kernel(*refs, fsdp=fsdp, ranks=ranks),
        grid=(1,),
        in_specs=[SMEM_SPEC] + whole_specs(*inputs),
        out_specs=pl.BlockSpec((rows, 256), lambda i: (0, 0)),
        out_shape=pltpu.HBM((rows, 256), BF),
        scratch_shapes=[pltpu.VMEM((shard, cols), BF)],
        compiler_params=pltpu.CompilerParams(vmem_limit_bytes=24 << 20),
        cost_estimate=SMALL_COST,
        name="pack",
    )(where, *inputs)


def arrange_kernel(gu_ref, hidden_ref, grad_ref, out_ref, down, sems):
    fsdp = out_ref.shape[0]
    shard, part = gu_ref.shape[0] // fsdp, hidden_ref.shape[1] // fsdp
    chunks = gu_ref.shape[1] // 256
    copies = []

    def send(source, j, low, rows):
        copies.append(pltpu.make_async_copy(
            source, out_ref.at[j, low:low + rows, :], sems.at[len(copies)]))
        copies[-1].start()

    for c in range(chunks):
        for j in range(fsdp):
            send(gu_ref.at[j * shard:(j + 1) * shard, c * 256:(c + 1) * 256], j, c * shard, shard)
    for c in range(grad_ref.shape[1] // 256):
        down[c] = dot(hidden_ref[...], grad_ref[:, c * 256:(c + 1) * 256], ((0,), (0,))).astype(BF)
        for j in range(fsdp):
            send(down.at[c, j * part:(j + 1) * part, :], j, chunks * shard + c * part, part)
    for copy in copies:
        copy.wait()


def arrange(gu, hidden, grad, fsdp):
    shard, ff, width = gu.shape[0] // fsdp, hidden.shape[1], grad.shape[1]
    rows = gu.shape[1] // 256 * shard + width // 256 * (ff // fsdp)
    return pl.pallas_call(
        arrange_kernel,
        in_specs=[VMEM_SPEC] * 3,
        out_specs=HBM_SPEC,
        out_shape=pltpu.HBM((fsdp, rows, 256), BF),
        scratch_shapes=[pltpu.VMEM((width // 256, ff, 256), BF),
                        pltpu.SemaphoreType.DMA(((gu.shape[1] + width) // 256 * fsdp,))],
        compiler_params=pltpu.CompilerParams(vmem_limit_bytes=16 << 20),
        cost_estimate=SMALL_COST,
        name="arrange",
    )(*vmem(gu, hidden, grad))


def finish_kernel(where_ref, keep_ref, part_ref, got_ref, *out_refs, ranks):
    groups, span, _ = keep_ref.shape
    for k, ref in enumerate(out_refs):
        group = where_ref[1] ^ k
        row = (group * ranks + where_ref[2]) * span
        own = part_ref[pl.ds(pl.multiple_of(row, span), span), :].astype(F32)
        ref[...] = (keep_ref[group] + own + got_ref[group].astype(F32)).astype(BF)


def finish(where, keep, part, got, ranks):
    groups, span, width = keep.shape
    return pl.pallas_call(
        lambda *refs: finish_kernel(*refs, ranks=ranks),
        in_specs=[SMEM_SPEC] + [VMEM_SPEC] * 3,
        out_specs=[VMEM_SPEC] * groups,
        out_shape=[jax.ShapeDtypeStruct((span, width), BF)] * groups,
        compiler_params=pltpu.CompilerParams(vmem_limit_bytes=24 << 20),
        cost_estimate=SMALL_COST,
        name="finish",
    )(where, keep, part, got)


def stack_kernel(where_ref, *refs):
    out_ref = refs[-1]
    for k, ref in enumerate(refs[:-1]):
        out_ref[where_ref[1] ^ k, 0] = ref[...]


def stack(where, slabs):
    span, width = slabs[0].shape
    return pl.pallas_call(
        stack_kernel,
        in_specs=[SMEM_SPEC] + [VMEM_SPEC] * len(slabs),
        out_specs=VMEM_SPEC,
        out_shape=jax.ShapeDtypeStruct((len(slabs), 1, span, width), BF),
        compiler_params=pltpu.CompilerParams(vmem_limit_bytes=16 << 20),
        cost_estimate=SMALL_COST,
        name="stack",
    )(where, *slabs)


def attend_back_kernel(seg_ref, g_ref, w_out_ref, q_ref, k_ref, v_ref, att_ref, lse_ref,
                       cos_ref, sin_ref, d_ref, grad_ref, k_sum, v_sum,
                       *, block, window, scale, head_size):
    tokens = g_ref.shape[0]
    half = head_size // 2
    lanes = 2 * head_size
    lane = lax.broadcasted_iota(jnp.int32, (1, lanes), 1)
    first = lane < head_size
    starts = start_row(seg_ref)
    k_sum[...] = jnp.zeros_like(k_sum)
    v_sum[...] = jnp.zeros_like(v_sum)
    for low in range(0, tokens, block):
        rows = pl.ds(low, block)
        grad_ref[rows, :] = dot(g_ref[rows, :], w_out_ref[...], ((1,), (1,))).astype(BF)
    small = block // 2
    for low in range(0, tokens, small):
        begin = first_key(low, small, window)
        end = low + small
        count = end - begin
        q = q_ref[low:end, :] * jnp.asarray(scale, BF)
        grad = grad_ref[low:end, :]
        product = (grad.astype(F32) * att_ref[low:end, :].astype(F32)).T
        zero = jnp.zeros_like(q)
        q_two = jnp.concatenate([jnp.where(first, q, zero), jnp.where(first, zero, q)], axis=0)
        grad_two = jnp.concatenate(
            [jnp.where(first, grad, zero), jnp.where(first, zero, grad)], axis=0)
        k = k_ref[begin:end, :]
        scores = dot(k, q_two, ((1,), (1,)))
        prob_grad = dot(v_ref[begin:end, :], grad_two, ((1,), (1,)))
        key_index = lax.broadcasted_iota(jnp.int32, (count, small), 0) + begin
        query_index = lax.broadcasted_iota(jnp.int32, (count, small), 1) + low
        visible = (key_index.astype(F32) >= starts[:, low:end]) & (key_index <= query_index)
        visible = jnp.concatenate([visible, visible], axis=1)
        lse = jnp.concatenate([lse_ref[0, h:h + 1, low:end] for h in range(2)], axis=1)
        row_dots = jnp.concatenate(
            [jnp.sum(product[h * head_size:(h + 1) * head_size], axis=0, keepdims=True)
             for h in range(2)], axis=1)
        weights = jnp.where(visible, jnp.exp(scores - lse), 0.0)
        score_low = (weights * (prob_grad - row_dots)).astype(BF)
        v_sum[begin:end, :] += dot(weights.astype(BF), grad_two)
        k_sum[begin:end, :] += dot(score_low, q_two)
        dq = dot(score_low, k, ((0,), (0,))) * scale
        dq = jnp.where(first, dq[:small], dq[small:])
        d_ref[low:end, :lanes] = (
            dq * cos_ref[low:end, :] - turn(dq, half) * sin_ref[low:end, :]).astype(BF)
    for low in range(0, tokens, block):
        rows = pl.ds(low, block)
        dk = k_sum[rows, :]
        d_ref[rows, lanes:2 * lanes] = (
            dk * cos_ref[rows, :] - turn(dk, half) * sin_ref[rows, :]).astype(BF)
        d_ref[rows, 2 * lanes:] = v_sum[rows, :].astype(BF)

def attend_back(seg, g, w_out, q, k, v, att, lse, cosine, sine, window, head_size):
    tokens, width = g.shape
    lanes = 2 * head_size
    pairs = q.shape[1] // lanes
    kernel = lambda *refs: attend_back_kernel(
        *refs, block=256, window=window, scale=1.0 / math.sqrt(head_size), head_size=head_size)
    column = pl.BlockSpec((tokens, lanes), lambda p: (0, p))
    inputs = hbm(seg) + vmem(g) + hbm(w_out, q, k, v, att, lse, cosine, sine)
    return pl.pallas_call(
        kernel,
        grid=(pairs,),
        in_specs=whole_specs(seg) + [
            VMEM_SPEC,
            pl.BlockSpec((lanes, width), lambda p: (p, 0)),
            column, column, column, column,
            pl.BlockSpec((1, 8, tokens), lambda p: (p, 0, 0)),
        ] + whole_specs(cosine, sine),
        out_specs=pl.BlockSpec((tokens, 3 * lanes), lambda p: (0, p)),
        out_shape=jax.ShapeDtypeStruct((tokens, 3 * lanes * pairs), BF),
        scratch_shapes=[
            pltpu.VMEM((tokens, lanes), BF),
            pltpu.VMEM((tokens, lanes), F32),
            pltpu.VMEM((tokens, lanes), F32),
        ],
        compiler_params=pltpu.CompilerParams(vmem_limit_bytes=28 << 20),
        cost_estimate=SMALL_COST,
        name="attend_back",
    )(*inputs)


def join_kernel(rank_ref, own_ref, other_ref, *out_refs, moves, plain):
    swapped = rank_ref[0] == 1
    own, other = own_ref[...], other_ref[...]
    halves = (jnp.where(swapped, other, own), jnp.where(swapped, own, other))
    for out, half, (rows, cols), (to_rows, to_cols) in moves:
        out_refs[out][to_rows, to_cols] = halves[half][rows, cols].astype(F32)
    for out, (rows, cols) in plain:
        out_refs[out][...] = own[rows, cols].astype(F32)


def join(rank, own, other, moves, plain, shapes):
    kernel = lambda *refs: join_kernel(*refs, moves=moves, plain=plain)
    return pl.pallas_call(
        kernel,
        in_specs=[
            pl.BlockSpec(memory_space=pltpu.SMEM),
            pl.BlockSpec(memory_space=pltpu.VMEM),
            pl.BlockSpec(memory_space=pltpu.VMEM),
        ],
        out_specs=[pl.BlockSpec(memory_space=pltpu.VMEM)] * len(shapes),
        out_shape=[jax.ShapeDtypeStruct(shape, F32) for shape in shapes],
        compiler_params=pltpu.CompilerParams(vmem_limit_bytes=32 << 20),
        name="join",
    )(rank.reshape(1), own, other)


def join_all_kernel(all_ref, *refs, moves):
    outs = (len(refs) - 2) // 2
    out_refs, whole_ref, blocks, sems = refs[:outs], refs[outs], refs[outs + 1:-1], refs[-1]
    groups, ranks, rows, _ = all_ref.shape
    for h in range(ranks):
        for m in range(groups):
            whole_ref[h, m * rows:(m + 1) * rows, :] = all_ref[m, h]
    copies = []
    for n in range(outs):
        for out, half, (rows, cols), (to_rows, to_cols) in moves:
            if out == n:
                blocks[out][to_rows, to_cols] = whole_ref[half, rows, cols].astype(F32)
        copies.append(pltpu.make_async_copy(blocks[n], out_refs[n], sems.at[n]))
        copies[-1].start()
    for copy in copies:
        copy.wait()


def join_all(parts, moves, shapes):
    groups, ranks, rows, cols = parts.shape
    parts, = hbm(parts)
    return pl.pallas_call(
        lambda *refs: join_all_kernel(*refs, moves=moves),
        grid=(1,),
        in_specs=whole_specs(parts),
        out_specs=[HBM_SPEC] * len(shapes),
        out_shape=[pltpu.HBM(shape, F32) for shape in shapes],
        scratch_shapes=[pltpu.VMEM((ranks, groups * rows, cols), BF)]
        + [pltpu.VMEM(shape, F32) for shape in shapes]
        + [pltpu.SemaphoreType.DMA((len(shapes),))],
        compiler_params=pltpu.CompilerParams(vmem_limit_bytes=24 << 20),
        cost_estimate=SMALL_COST,
        name="join_all",
    )(parts)


def make_body(groups, ranks, fsdp, square):
    F = ("y", "x") if square else ("f",)
    swap = [(0, 1), (1, 0)]
    pairs = square and ranks == 2 and groups == 4

    def hop(value, k):
        return lax.ppermute(value, "m", [(i, i ^ k) for i in range(groups)])

    def after(value, *earlier):
        return lax.optimization_barrier((value,) + earlier)[0]

    def between(slabs, value):
        hops, value = lax.optimization_barrier((slabs[1:], value))
        return slabs[:1] + hops, value

    def spread(slabs):
        return [hop(slab, k) if k else slab for k, slab in enumerate(slabs)]

    def both_ranks(where, slabs, span):
        if ranks == 2:
            return slabs + [lax.ppermute(slab, "r", swap) for slab in slabs]
        rows = lax.all_gather(stack(where, slabs)[:, 0], "r", axis=1)
        return [rows[:, :, :span].reshape(-1, rows.shape[-1]), rows]

    def share(part):
        if ranks == 2:
            other = lax.ppermute(part, "r", swap)
            mine_first = lax.axis_index("r") == 0
            return jnp.stack(
                [jnp.where(mine_first, part, other), jnp.where(mine_first, other, part)], axis=1)
        return lax.all_gather(part, "r", axis=1)

    def exchange(part):
        if ranks == 2:
            return part, lax.ppermute(part, "r", swap)
        return lax.psum(part, "r"), jnp.zeros_like(part)

    def gather_rows(part, wait=()):
        if not square:
            whole = lax.all_gather(part, F, axis=0, tiled=True)
            return [whole], [(None, 0, 0)], (), ()
        count = part.shape[0]
        rows = (count // 2) // 16 * 16
        send = after(part, *wait) if wait else part
        from_x = lax.ppermute(send, "x", swap)
        from_y = lax.ppermute(send, "y", swap)
        far_a = lax.ppermute(from_y[:rows], "x", swap)
        far_b = lax.ppermute(from_x[rows:], "y", swap)
        pieces = [(0, 0, count), (1, 0, count), (2, 0, count), (3, 0, rows), (3, rows, count - rows)]
        return [part, from_x, from_y, far_a, far_b], pieces, (from_x, from_y), (far_a, far_b)

    def add(*parts):
        return sum(part.astype(F32) for part in parts).astype(BF)

    def take(grad, k):
        return lax.dynamic_index_in_dim(grad, lax.axis_index(F) ^ k, 0, keepdims=False)

    def half_rows(grad):
        return (grad.shape[1] // 2) // 16 * 16

    def round_one(grad):
        far, rows = take(grad, 3), half_rows(grad)
        return lax.ppermute(far[:rows], "x", swap), lax.ppermute(far[rows:], "y", swap)

    def second_terms(grad, low, high):
        to_x, to_y, rows = take(grad, 1), take(grad, 2), half_rows(grad)
        to_x = jnp.concatenate([to_x[:rows], add(to_x[rows:], high)], axis=0)
        to_y = jnp.concatenate([add(to_y[:rows], low), to_y[rows:]], axis=0)
        return to_x, to_y

    def round_two(to_x, to_y):
        return lax.ppermute(to_x, "x", swap), lax.ppermute(to_y, "y", swap)

    def halve(owned, bit, axis):
        half = owned.shape[axis] // 2
        side = (lax.axis_index("m") // bit) % 2
        return (lax.dynamic_slice_in_dim(owned, (1 - side) * half, half, axis),
                lax.dynamic_slice_in_dim(owned, side * half, half, axis))

    def join_halves(owned, other, bit, axis):
        first = (lax.axis_index("m") // bit) % 2 == 0
        return jnp.concatenate(
            [jnp.where(first, owned, other), jnp.where(first, other, owned)], axis=axis)

    def reduce(grad):
        return lax.psum(lax.psum_scatter(grad, F, scatter_dimension=0, tiled=False), "m")

    def body(tokens, segments, w_query, w_key, w_value, w_out, w_gate, w_up, w_down,
             gain_attn, gain_ffn, cotangent):
        micro, _, span, width = tokens.shape
        head_size = width // HEADS
        seq_tokens = span * groups * ranks
        window = seq_tokens // 2
        rank = lax.axis_index("r")
        own_cols = width // ranks
        shard = w_query.shape[0]
        down_rows = w_down.shape[0]
        part_rows = down_rows // ranks
        ff = w_gate.shape[1]
        half_ff = ff // ranks

        lanes = 2 * head_size
        lanes_all = -(-own_cols // lanes) * lanes
        spare = lanes_all - own_cols
        block = span * ranks
        f_index = lax.axis_index(F)
        own_at, other_at, other_rank = (
            at.astype(jnp.uint32) for at in (rank * own_cols, (1 - rank) * own_cols, 1 - rank))
        where = jnp.stack([f_index, lax.axis_index("m"), rank])
        small_cols = 3 * lanes_all + own_cols
        gains_in = jnp.pad(jnp.stack([gain_attn, gain_ffn]), ((0, 14), (0, 0)))
        stack_own = pack(where, w_gate, w_up, w_down, fsdp, ranks)
        stack_all = lax.all_gather(stack_own, F, axis=0)
        cosine, sine = rotary_tables(seq_tokens, head_size, 2)
        small, *slabs = pack_small(
            after(where, stack_own), w_query, w_key, w_value, w_out, gains_in, tokens,
            segments[:, 0], cotangent, ranks, lanes, lanes_all)
        token_slabs, cot_slabs = slabs[:groups], slabs[groups:]
        token_slabs = spread(token_slabs)
        small_refs, small_pieces, near, far = gather_rows(small)
        if square:
            cot_slabs = cot_slabs[:1] + [after(slab, *token_slabs) for slab in cot_slabs[1:]]
        cot_slabs = spread(cot_slabs)
        if square:
            token_slabs = token_slabs[:1] + [
                after(slab, cosine, sine) for slab in token_slabs[1:]]
        token_refs = both_ranks(where, token_slabs, span)
        if ranks != 2:
            seg = token_refs[1][:, :, span, :span].reshape(1, seq_tokens).astype(F32)
            token_refs = [token_refs[0], seg]
        if square:
            own, from_x, from_y, far_a, far_b = small_refs
            at = far_a.shape[0]
            ends = [own, from_x, from_y, jnp.concatenate([far_a, far_b[:shard - at]], axis=0)]
            tails = [v[shard:shard + 2, :shard] for v in (own, from_x, from_y)]
            tails.append(far_b[shard - at:shard - at + 2, :shard])
            gains = jnp.zeros((fsdp, 2, shard), BF)
            out_cols = jnp.zeros((width, own_cols), BF)
            for offset in range(4):
                to = (f_index ^ offset) * shard
                gains = lax.dynamic_update_index_in_dim(gains, tails[offset], f_index ^ offset, 0)
                out_cols = lax.dynamic_update_slice_in_dim(
                    out_cols, ends[offset][:shard, 3 * lanes_all:], to, 0)
            gains = gains.transpose(1, 0, 2).reshape(2, width)
            small_pieces = [(o, f, min(n, shard - f)) for o, f, n in small_pieces]
            qkv_refs = small_refs
        else:
            whole = small_refs[0].reshape(fsdp, shard + 16, small_cols)
            gains = whole[:, shard:shard + 2, :shard].transpose(1, 0, 2).reshape(2, width)
            out_cols = whole[:, :shard, 3 * lanes_all:].reshape(width, own_cols)
            qkv_refs = [whole[:, :shard, :3 * lanes_all].reshape(width, 3 * lanes_all)]
        gains = gains.astype(F32)
        gain_one = gains[0:1]
        if ranks == 2:
            give = lax.dynamic_slice_in_dim(out_cols, (1 - rank) * own_cols, own_cols, 0)
            keep = lax.dynamic_slice_in_dim(out_cols, rank * own_cols, own_cols, 0)
            got = lax.ppermute(give, "r", swap)
            w_out_own = jnp.where(rank == 0, jnp.concatenate([keep, got], 1),
                                  jnp.concatenate([got, keep], 1))
        else:
            pieces = lax.all_to_all(out_cols, "r", 0, 0, tiled=True)
            pieces = pieces.reshape(ranks, own_cols, own_cols)
            w_out_own = jnp.concatenate([pieces[i] for i in range(ranks)], axis=1)
        w_out_even = jnp.pad(w_out_own, ((0, spare), (0, 0)))

        cosine, gains, gain_one, own_at, other_at, other_rank = lax.optimization_barrier(
            (cosine, gains, gain_one, own_at, other_at, other_rank))
        q, k, v, att, lse, w_qkv, x, seg = attend(
            where, cosine, sine, token_refs, ranks, qkv_refs, small_pieces, shard, lanes_all,
            window, head_size, width)
        if square:
            cot_slabs, att = between(cot_slabs, att)
        own, got = exchange(dot(att, w_out_even).astype(BF))
        cot_refs = both_ranks(where, cot_slabs, span)
        if ranks != 2:
            cot_refs = cot_refs[:1]
        total, middle_low, hidden_low, gate_back, silu, part, gu, down = forward(
            x, own, got, gain_one, stack_all, shard, part_rows, half_ff, 512)
        own, got = exchange(part)

        *out_slabs, ffn_grad_low, gu_grad_low, part, gain_ffn_grad = backward(
            where, total, own, got, gate_back, silu, gains, gu, down, cot_refs, block, groups, ranks)
        own, got = exchange(part)
        gu_w_grad = dot(middle_low, gu_grad_low, ((0,), (0,))).astype(BF)
        if ranks == 2:
            got, gu_w_grad = lax.optimization_barrier((got, gu_w_grad))
        stack_grad = arrange(gu_w_grad, hidden_low, ffn_grad_low, fsdp)
        stack_owned = lax.psum_scatter(stack_grad, F, scatter_dimension=0, tiled=False)
        own, got = after(own, stack_grad), after(got, stack_grad)
        branch_grad_low, branch_keep, gain_grads = norm_back(
            where[2:], total, ffn_grad_low, own, got, gain_one, gain_ffn_grad,
            fsdp, small_cols, block, span)
        out_w_grad = dot(att, branch_grad_low, ((0,), (0,)))[:own_cols].astype(BF)
        if ranks == 2:
            give = lax.dynamic_slice_in_dim(out_w_grad, other_at, own_cols, 1)
            keep = lax.dynamic_slice_in_dim(out_w_grad, own_at, own_cols, 1)
            got = lax.ppermute(give, "r", swap)
            out_cols_grad = jnp.where(rank == 0, jnp.concatenate([keep, got], 0),
                                      jnp.concatenate([got, keep], 0))
        else:
            rows = out_w_grad.reshape(own_cols, ranks, own_cols).transpose(1, 0, 2)
            out_cols_grad = lax.all_to_all(rows, "r", 0, 0, tiled=True).reshape(width, own_cols)
        branch_grad_low = after(branch_grad_low, out_cols_grad)
        d_qkv = attend_back(
            seg, branch_grad_low, w_out_even, q, k, v, att, lse, cosine, sine, window, head_size)
        if square:
            out_slabs, d_qkv = between(spread(out_slabs), d_qkv)
        else:
            out_slabs = spread(out_slabs)
        output = stack(where, out_slabs)
        qkv_w_grad = dot(x, d_qkv, ((0,), (0,))).astype(BF)
        small_grad = jnp.concatenate([qkv_w_grad, out_cols_grad], axis=1)
        small_grad = jnp.concatenate(
            [small_grad.reshape(fsdp, shard, small_cols), gain_grads], axis=1)
        if pairs:
            small_one = round_one(small_grad)
            d_qkv = after(d_qkv, small_grad)
        part = dot(d_qkv, w_qkv, ((1,), (1,))).astype(BF)
        if ranks == 2:
            rows = part.reshape(groups, ranks, span, width)
            give = lax.dynamic_index_in_dim(rows, other_rank, 1, keepdims=False)
            got = lax.ppermute(give, "r", swap)
        else:
            part = lax.psum(part, "r")
            got = jnp.zeros_like(branch_keep, BF)
        grad_slabs = list(finish(where, branch_keep, part, got, ranks))
        grad_slabs = spread(grad_slabs)
        if pairs:
            grad_slabs[:3], small_one = between(grad_slabs[:3], small_one)
            terms = second_terms(small_grad, *small_one)
            small_two, output, grad_slabs[3] = lax.optimization_barrier(
                (round_two(*terms), output, grad_slabs[3]))
            input_grad = stack(where, grad_slabs)
            stack_owned = after(stack_owned, *terms)
            quarter = lax.psum_scatter(stack_owned, "m", scatter_dimension=0, tiled=True)
            give, keep = halve(add(take(small_grad, 0), *small_two), 1, 1)
            got, quarter, input_grad = lax.optimization_barrier((hop(give, 1), quarter, input_grad))
            stack_parts = lax.all_gather(quarter, ("m", "r"), axis=0)
            stack_parts = stack_parts.reshape((groups, ranks) + quarter.shape)
            give, keep = halve(add(keep, got), 2, 1)
            owned = add(keep, hop(give, 2))
            owned = join_halves(owned, hop(owned, 2), 2, 1)
            small_sum = join_halves(owned, hop(owned, 1), 1, 1)
        else:
            stack_sum = lax.psum(stack_owned, "m")
            small_sum = reduce(small_grad)
            input_grad = stack(where, grad_slabs)
        if pairs:
            everything = slice(None)
            chunks = 2 * half_ff // 256
            stack_moves = [
                (n, h, (slice((n * fsdp + j) * shard, (n * fsdp + j + 1) * shard), everything),
                 (everything, slice(j * down_rows + h * part_rows, j * down_rows + (h + 1) * part_rows)))
                for n in range(2) for h in range(2) for j in range(fsdp)]
            stack_moves += [
                (2, h, (slice(chunks * shard + c * part_rows, chunks * shard + (c + 1) * part_rows),
                        everything),
                 (slice(h * part_rows, (h + 1) * part_rows), slice(c * 256, (c + 1) * 256)))
                for h in range(2) for c in range(width // 256)]
            small_moves = [
                (n, h, (slice(0, shard), slice((3 * p + n) * lanes, (3 * p + n + 1) * lanes)),
                 (everything, slice(h * own_cols + p * lanes, h * own_cols + (p + 1) * lanes)))
                for n in range(3) for h in range(2) for p in range(own_cols // lanes)]
            small_moves += [
                (3, h, (slice(0, shard), slice(3 * lanes_all, small_cols)),
                 (everything, slice(h * own_cols, (h + 1) * own_cols))) for h in range(2)]
            small_plain = [
                (4 + n, (slice(shard + n, shard + n + 1), slice(0, shard))) for n in range(2)]
            gate_w, up_w, down_grad = join_all(
                stack_parts, stack_moves, [(shard, ff)] * 2 + [(down_rows, width)])
            small_got, gate_w, up_w, down_grad = lax.optimization_barrier(
                (lax.ppermute(small_sum, "r", swap), gate_w, up_w, down_grad))
            query_w, key_w, value_w, out_w, gain_a, gain_f = join(
                rank, small_sum, small_got, small_moves, small_plain,
                [(shard, width)] * 4 + [(1, shard)] * 2)
        else:
            at = 2 * half_ff // 256 * shard
            down_sum = jnp.moveaxis(stack_sum[at:].reshape(-1, part_rows, 256), 0, 1)
            down_grad = jnp.moveaxis(share(down_sum.reshape(part_rows, width)), 1, 0)
            down_grad = down_grad.reshape(down_rows, width).astype(F32)
            gu_sum = jnp.moveaxis(stack_sum[:at].reshape(-1, shard, 256), 0, 1)
            gu_both = share(gu_sum.reshape(shard, 2 * fsdp, part_rows))
            gu_both = gu_both.reshape(shard, ranks, 2, fsdp, part_rows).astype(F32)
            gate_w, up_w = (
                gu_both[:, :, n].transpose(0, 2, 1, 3).reshape(shard, ff) for n in range(2))
            small_both = share(small_sum)[:shard].astype(F32)
            three = small_both[:, :, :3 * lanes_all].reshape(shard, ranks, -1, 3, lanes)
            query_w, key_w, value_w = (
                three[:, :, :, n].reshape(shard, ranks, lanes_all)[:, :, :own_cols].reshape(shard, width)
                for n in range(3))
            out_w = small_both[:, :, 3 * lanes_all:].reshape(shard, width)
            gain_a, gain_f = small_sum[shard, :shard].astype(F32), small_sum[shard + 1, :shard].astype(F32)
        return (output, input_grad, query_w, key_w, value_w, out_w,
                gate_w, up_w, down_grad, gain_a.reshape(shard), gain_f.reshape(shard))

    return body


def solution(mesh):
    def run(*args):
        groups = args[0].shape[0]
        seq, fsdp = mesh.shape["seq"], mesh.shape["fsdp"]
        ranks = seq // groups
        square = fsdp == 4
        names = ("m", "r") + (("y", "x") if square else ("f",))
        sizes = (groups, ranks) + ((2, 2) if square else (fsdp,))
        order = [mesh.axis_names.index(name) for name in ("seq", "fsdp")]
        inner = Mesh(mesh.devices.transpose(order).reshape(sizes), names)
        f = ("y", "x") if square else "f"
        s = ("m", "r")
        rows = P(f, None)
        data = P(None, f, s, None)
        in_specs = (data, P(None, f, s)) + (rows,) * 7 + (P(f), P(f), data)
        out_specs = (data, data) + (rows,) * 7 + (P(f), P(f))
        body = make_body(groups, ranks, fsdp, square)
        return jax.shard_map(
            body, mesh=inner, in_specs=in_specs, out_specs=out_specs, check_vma=False)(*args)

    return run
```
